32 devices in a mesh: expert: 8 (over y, x, core), shard: 4 (over z).
Axes of the slice: x: 2, y: 2, z: 4, core: 2. Of those that a mesh axis runs over, the one named last changes fastest.
Arguments:
- tokens: bfloat16 [16384, 768], P(('expert', 'shard')), may hold values from -6 to 6
- piece_start: int32 [32], P(('expert', 'shard')), may hold values from 0 to 256, as said below
- routes: int32 [16384, 2], P(('expert', 'shard')), may hold values from 0 to 15, all different within a row; in each aligned block of 512 rows (0 to 511, 512 to 1023, ...) at most 96 rows name the same one
- norm_gains: float32 [4, 768], replicated, may hold values from 0.5 to 1.5
- bias_tables: float32 [2, 12, 44], replicated, may hold values from -4 to 4
- qkv_weight: bfloat16 [2, 768, 2304], P(None, 'shard', 'expert'), may hold values from -0.21875 to 0.21875
- out_weight: bfloat16 [2, 768, 768], P(None, 'shard', 'expert'), may hold values from -1.25 to 1.25
- mlp_up: bfloat16 [768, 3072], P('shard', 'expert'), may hold values from -0.21875 to 0.21875
- mlp_down: bfloat16 [3072, 768], P('shard', 'expert'), may hold values from -0.15625 to 0.15625
- router: bfloat16 [768, 16], P('shard', 'expert'), may hold values from -0.3125 to 0.3125
- expert_up: bfloat16 [16, 768, 3072], P('expert', None, 'shard'), may hold values from -0.21875 to 0.21875
- expert_down: bfloat16 [16, 3072, 768], P('expert', 'shard'), may hold values from -0.15625 to 0.15625
- cotangent: bfloat16 [16384, 768], P(('expert', 'shard')), may hold values from -6 to 6
Outputs:
- output: bfloat16 [16384, 768], P(('expert', 'shard'))
- grad_input: float32 [16384, 768], P(('expert', 'shard'))
- grad_norm_gains: float32 [4, 768], replicated
- grad_bias_tables: float32 [2, 12, 44], replicated
- grad_qkv_weight: float32 [2, 768, 2304], P(None, 'shard', 'expert')
- grad_out_weight: float32 [2, 768, 768], P(None, 'shard', 'expert')
- grad_mlp_up: float32 [768, 3072], P('shard', 'expert')
- grad_mlp_down: float32 [3072, 768], P('shard', 'expert')
- grad_router: float32 [768, 16], P('shard', 'expert')
- grad_expert_up: float32 [16, 768, 3072], P('expert', None, 'shard')
- grad_expert_down: float32 [16, 3072, 768], P('expert', 'shard')
The draws below stay inside these ranges and needn't reach their ends.
Inputs may be any that keep to these rules, and one draw needn't show every extreme that they name: `routes`: in the rows of one device (aligned blocks of 512 tokens) no expert is named by more than 96 tokens; a token's two experts differ. Sequence s has one picture piece, positions piece_start[s] to piece_start[s] + 255.
All inputs are finite; a program needn't handle non-finite values.
Results may differ from the reference program's by a relative error of at most 0.025.
Values may be sent and summed in bfloat16 or wider, within the bound.
A program may use at most 320 MiB of HBM per device.

```python
import math
import jax
import jax.numpy as jnp
import numpy as np
from jax import lax

D = 768
HEADS = 12
FF = 3072
TOP = 2
PIECE = 256
NB = 44
TOK_DEV = 512
EXPERTS = 16
LENGTH = 512
SEQS = 32
TOKENS = 16384
CAP = 96
DEVICES = 32


def draw_piece_start(key, part):
    first_key = jax.random.fold_in(key, 11)
    second_key = jax.random.fold_in(key, 12)
    starts = jax.random.randint(first_key, (SEQS,), 0, LENGTH - PIECE + 1, dtype=jnp.int32)
    chosen = jax.random.randint(second_key, (), 0, SEQS, dtype=jnp.int32)
    positions = jnp.arange(SEQS, dtype=jnp.int32)
    starts = jnp.where(positions == chosen, LENGTH - PIECE, starts)
    starts = jnp.where(positions == (chosen + 1) % SEQS, 0, starts)
    return starts.astype(jnp.int32)


def with_spikes(entries, key, source, target, blocks, factor):
    owner, partner = [(jnp.arange(entries.shape[dim]) // (entries.shape[dim] // blocks)).reshape([-1 if axis == dim else 1 for axis in range(entries.ndim)]) for dim in (source, target)]
    chosen = jax.random.permutation(key, blocks)[partner]
    strong = (owner == chosen) | (owner == (partner + blocks // 2) % blocks)
    return jnp.where(strong, factor * entries, entries)


def levels(key, extent, shards, low, top_value):
    def one(axis_at, blocks):
        draws = jax.random.uniform(jax.random.fold_in(jax.random.fold_in(key, 6), axis_at), (blocks,), jnp.float32, low / len(shards), top_value / len(shards))
        return jnp.repeat(jnp.exp(draws), extent[axis_at] // blocks).reshape((-1,) + (1,) * (len(extent) - axis_at - 1))

    factor_of = one(*shards[0])
    for cut in shards[1:]:
        factor_of = factor_of * one(*cut)
    return factor_of


def routed_block(key, own, number, rows, count, top, bound, slope):
    ranking = jax.random.permutation(key, count)
    heavy_load, ordinary = portions_of(count, rows * top, bound, slope, True), portions_of(count, rows * top, bound, slope, False)
    places = jnp.arange(count)

    def named(sizes, rotation):
        used = int((sizes > 0).sum())
        fixed = max(1, used // 4)
        passed = fixed + (places - fixed + rotation * (used - fixed)) % max(1, count - fixed)
        return jnp.zeros((count,), jnp.int32).at[ranking[jnp.where(places < fixed, places, passed)]].set(jnp.asarray(sizes, jnp.int32))

    sizes = jnp.where(number % 4 == 0, named(heavy_load, number // 4), named(ordinary, number - number // 4 - 1))
    mixed = jax.random.permutation(jax.random.fold_in(own, 3), count)
    donor, receiver = mixed[0:count // 2 * 2:2], mixed[1:count // 2 * 2:2]
    margin = jnp.minimum(sizes[donor] - 1, bound - sizes[receiver]) // 2
    margin = jnp.where((donor == ranking[0]) | (receiver == ranking[0]) | (sizes[receiver] == 0), 0, jnp.maximum(margin, 0))
    passed = jax.random.randint(jax.random.fold_in(own, 4), (count // 2,), 0, 1 << 20) % (margin + 1)
    sizes = sizes.at[donor].add(-passed).at[receiver].add(passed)
    items = jnp.searchsorted(jnp.cumsum(sizes), jnp.arange(rows * top), side="right").astype(jnp.int32)
    table = items.reshape(top, rows).T
    table = table[jax.random.permutation(jax.random.fold_in(own, 1), rows)]
    rotation = jax.random.randint(jax.random.fold_in(own, 2), (rows, 1), 0, top)
    return jnp.take_along_axis(table, (jnp.arange(top)[None, :] + rotation) % top, axis=1)


def portions_of(amount, total, most, slope, full):
    loads = [(1 << 20) // math.isqrt(grade ** slope) + 1 for grade in range(1, amount + 1)]
    largest = most if full else min(most, max(-(-total // amount), total * loads[0] // sum(loads)))
    least = 1 if total - largest >= amount - 1 else 0
    counts, surplus = [largest] + [least] * (amount - 1), total - largest - least * (amount - 1)
    while surplus > 0:
        free = [i for i in range(1, amount) if counts[i] < largest] or [i for i in range(1, amount) if counts[i] < most]
        pool, budget = sum([loads[i] for i in free]), surplus
        for i in free:
            extra = min(most - counts[i], max(1, budget * loads[i] // pool), surplus)
            counts[i] = counts[i] + extra
            surplus = surplus - extra
    return np.array(counts)


def bell_draw(own_key, extent, scale, reach, pieces=(), held_as=jnp.bfloat16):
    level = levels(own_key, extent, pieces, -0.22, 0.18) if pieces else 1.0
    values = jax.random.normal(own_key, extent, jnp.float32) * scale * level
    return jnp.minimum(jnp.maximum(values, -reach), reach).astype(held_as)


def bell_draw_with(rng, extent, spread, most, cuts, heavy, kind=jnp.bfloat16):
    values = spread * jax.random.normal(rng, extent, jnp.float32)
    if cuts:
        values = values * levels(rng, extent, cuts, -0.22, 0.18)
    return jnp.clip(with_spikes(values, jax.random.fold_in(rng, 3), *heavy), -most, most).astype(kind)


def setup_inputs(seed: int = 0) -> dict:
    key_list = jax.random.split(jax.random.key(seed), 14)
    tokens = bell_draw(key_list[0], (TOKENS, D), 1.0, 6.0, ((0, 32),))
    piece_start = draw_piece_start(jax.random.fold_in(key_list[13], 71), 0)
    routes_keys = jax.random.split(jax.random.fold_in(key_list[2], 1), TOKENS // TOK_DEV)
    routes_turns = jax.random.permutation(jax.random.fold_in(key_list[2], 3), TOKENS // TOK_DEV)
    routes = jax.vmap(lambda own, number: routed_block(jax.random.fold_in(key_list[2], 2), own, number, TOK_DEV, EXPERTS, TOP, CAP, 1))(routes_keys, routes_turns).reshape((TOKENS, TOP))
    norm_gains = jnp.clip(1.0 + 0.1 * jax.random.normal(key_list[3], (4, D), jnp.float32), 0.5, 1.5)
    bias_tables = bell_draw(key_list[4], (2, HEADS, NB), 1.0, 4.0, (), jnp.float32)
    qkv_weight = bell_draw(key_list[5], (2, D, 3 * D), D ** -0.5, 0.21875, ((1, 4), (2, 8)))
    out_weight = bell_draw(key_list[6], (2, D, D), (D // 32) ** -0.5, 1.25, ((1, 4), (2, 8)))
    mlp_up = bell_draw(key_list[7], (D, FF), D ** -0.5, 0.21875, ((0, 4), (1, 8)))
    mlp_down = bell_draw(key_list[8], (FF, D), (FF // 2) ** -0.5, 0.15625, ((0, 4), (1, 8)))
    router = bell_draw(key_list[9], (D, EXPERTS), (D // 2) ** -0.5, 0.3125, ((0, 4), (1, 8)))
    expert_up = bell_draw(key_list[10], (EXPERTS, D, FF), D ** -0.5, 0.21875, ((0, 8), (2, 4)))
    expert_down = bell_draw(key_list[11], (EXPERTS, FF, D), (FF // 2) ** -0.5, 0.15625, ((0, 8), (1, 4)))
    cotangent = bell_draw_with(key_list[12], (TOKENS, D), 1.0, 6.0, ((0, 32),), (0, 1, 32, 2.75))
    return dict(tokens=tokens, piece_start=piece_start, routes=routes, norm_gains=norm_gains, bias_tables=bias_tables, qkv_weight=qkv_weight, out_weight=out_weight, mlp_up=mlp_up, mlp_down=mlp_down, router=router, expert_up=expert_up, expert_down=expert_down, cotangent=cotangent)


@jax.custom_vjp
def low(v):
    return lax.optimization_barrier(v.astype(jnp.bfloat16)).astype(jnp.float32)

@jax.custom_vjp
def low_back(v):
    return v

def low_keep(v):
    return (low(v), None)

def low_pass(kept, grad):
    return (grad,)

def back_keep(v):
    return (v, None)

def back_low(kept, grad):
    return (low(grad),)
low.defvjp(low_keep, low_pass)
low_back.defvjp(back_keep, back_low)
bucket_edges = (1, 2, 3, 4, 6, 8, 12, 16, 24, 32, 48, 64, 96, 128, 192, 256, 384, 512, 768, 1024, 1536)
norm_eps = 1e-06
far_below = -1e+30
highest = lax.Precision.HIGHEST

def product(left, right):
    return jnp.dot(left, right, precision=highest)

def normalize(field, gain):
    return field * lax.rsqrt(lax.optimization_barrier(jnp.mean(field * field, axis=-1, keepdims=True)) + norm_eps) * gain

def bucket_onehot(length, buckets):
    distance = jnp.arange(1 - length, length, dtype=jnp.int32)
    edge_list = jnp.array(bucket_edges, dtype=jnp.int32)
    magnitude = lax.optimization_barrier(jnp.sum((jnp.abs(distance)[:, None] >= edge_list[None, :]).astype(jnp.int32), axis=1, dtype=jnp.int32))
    bucket = magnitude + buckets // 2 * (distance > 0).astype(jnp.int32)
    return (bucket[:, None] == jnp.arange(buckets, dtype=jnp.int32)[None, :]).astype(jnp.float32)

def sequence_attention(qkv_rows, bias_vector, piece_first):
    length = qkv_rows.shape[0]
    model_width = qkv_rows.shape[1] // 3
    heads_view = qkv_rows.reshape(length, 3, HEADS, model_width // HEADS)
    queries = heads_view[:, 0]
    key_rows = heads_view[:, 1]
    value_rows = heads_view[:, 2]
    positions = jnp.arange(length, dtype=jnp.int32)
    offsets = positions[None, :] - positions[:, None] + (length - 1)
    raw = jnp.einsum('qhd,khd->hqk', queries, key_rows, precision=highest) * queries.shape[2] ** (-0.5)
    raw = low_back(raw + jnp.take(bias_vector, offsets, axis=1))
    inside = (positions >= piece_first) & (positions < piece_first + PIECE)
    keep_mask = (positions[None, :] <= positions[:, None]) | inside[:, None] & inside[None, :]
    scores = jnp.where(keep_mask[None, :, :], raw, far_below)
    weights = low(jax.nn.softmax(scores, axis=-1))
    mixed_rows = jnp.einsum('hqk,khd->qhd', weights, value_rows, precision=highest)
    return mixed_rows.reshape(length, model_width)

def attention_sublayer(residual, gain, qkv_full, out_full, table, piece_start):
    normed = low(normalize(residual, gain))
    qkv_rows = low(low_back(product(normed, qkv_full)))
    onehot = bucket_onehot(LENGTH, table.shape[1])
    bias_vector = product(table, onehot.T)
    group_size = math.gcd(SEQS, max(1, 4096 // LENGTH))
    grouped = qkv_rows.reshape(SEQS // group_size, group_size, LENGTH, qkv_rows.shape[1])
    starts = piece_start.reshape(SEQS // group_size, group_size)

    def one_group(member):
        rows_block, first_block = member
        return jax.vmap(lambda one_rows, one_first: sequence_attention(one_rows, bias_vector, one_first))(rows_block, first_block)
    mixed_rows = lax.map(jax.checkpoint(one_group), (grouped, starts))
    mixed_rows = low(low_back(mixed_rows.reshape(residual.shape[0], residual.shape[1])))
    return residual + low_back(product(mixed_rows, out_full))

def dense_sublayer(residual, gain, up_full, down_full):
    normed = low(normalize(residual, gain))
    hidden = low(jax.nn.gelu(low_back(product(normed, up_full))))
    return residual + low_back(product(hidden, down_full))

def expert_sublayer(residual, gain, router_full, up_experts, down_experts, routes):
    model_width = residual.shape[1]
    normed = low(normalize(residual, gain))
    logits = low_back(product(normed, router_full))
    gates = jax.nn.softmax(jnp.take_along_axis(logits, routes, axis=1), axis=1)
    experts_all = router_full.shape[1]
    choice_ids = routes.reshape(-1)
    onehot_ids = (choice_ids[:, None] == jnp.arange(experts_all, dtype=jnp.int32)[None, :]).astype(jnp.int32)
    ranks = jnp.cumsum(onehot_ids.reshape(DEVICES, -1, experts_all), axis=1, dtype=jnp.int32).reshape(-1, experts_all) - 1
    own_rank = lax.optimization_barrier(jnp.sum(ranks * onehot_ids, axis=1, dtype=jnp.int32))
    device_ids = jnp.arange(choice_ids.shape[0], dtype=jnp.int32) // (routes.shape[1] * TOK_DEV)
    slot_ids = (choice_ids * DEVICES + device_ids) * CAP + own_rank
    pair_rows = low_back(jnp.repeat(normed, routes.shape[1], axis=0))
    sectioned = jnp.zeros((experts_all * DEVICES * CAP, model_width), jnp.float32).at[slot_ids].set(pair_rows)
    sectioned = sectioned.reshape(experts_all, DEVICES * CAP, model_width)

    def one_expert(member):
        rows_in, up_one, down_one = member
        hidden = low(jax.nn.gelu(low_back(product(rows_in, up_one))))
        return low(low_back(product(hidden, down_one)))
    produced = lax.map(jax.checkpoint(one_expert), (sectioned, up_experts, down_experts))
    picked = produced.reshape(-1, model_width)[slot_ids].reshape(-1, routes.shape[1], model_width)
    return residual + lax.optimization_barrier(jnp.sum(gates[:, :, None] * picked, axis=1))

def forward(tokens, norm_gains, bias_tables, qkv_weight, out_weight, mlp_up, mlp_down, router, expert_up, expert_down, piece_start, routes):
    layer_one = attention_sublayer(tokens, norm_gains[0], qkv_weight[0], out_weight[0], bias_tables[0], piece_start)
    layer_two = dense_sublayer(layer_one, norm_gains[1], mlp_up, mlp_down)
    layer_three = attention_sublayer(layer_two, norm_gains[2], qkv_weight[1], out_weight[1], bias_tables[1], piece_start)
    return expert_sublayer(layer_three, norm_gains[3], router, expert_up, expert_down, routes)

def reference(tokens, piece_start, routes, norm_gains, bias_tables, qkv_weight, out_weight, mlp_up, mlp_down, router, expert_up, expert_down, cotangent):
    floats = (tokens.astype(jnp.float32), norm_gains.astype(jnp.float32), bias_tables.astype(jnp.float32), qkv_weight.astype(jnp.float32), out_weight.astype(jnp.float32), mlp_up.astype(jnp.float32), mlp_down.astype(jnp.float32), router.astype(jnp.float32), expert_up.astype(jnp.float32), expert_down.astype(jnp.float32))

    def closed(*members):
        return forward(*members, piece_start, routes)
    result, pullback = jax.vjp(closed, *floats)
    gradients = pullback(cotangent.astype(jnp.float32))
    return (result.astype(jnp.bfloat16), gradients[0], gradients[1], gradients[2], gradients[3], gradients[4], gradients[5], gradients[6], gradients[7], gradients[8], gradients[9])
```

```python
import jax
import jax.numpy as jnp
from jax import lax
from jax.experimental import pallas as pl
from jax.experimental.pallas import tpu as pltpu
from jax.sharding import PartitionSpec as P

PIECE = 256
norm_eps = 1e-06
far_below = -1e30
BF = jnp.bfloat16
F32 = jnp.float32
VMEM_BYTES = 56 * 1024 * 1024


def nn(a, b):
    return lax.dot_general(a, b, (((1,), (0,)), ((), ())), preferred_element_type=F32)


def nt(a, b):
    return lax.dot_general(a, b, (((1,), (1,)), ((), ())), preferred_element_type=F32)


def tn(a, b):
    return lax.dot_general(a, b, (((0,), (0,)), ((), ())), preferred_element_type=F32)


def inverse_rms(field):
    return lax.rsqrt(jnp.mean(field * field, axis=1, keepdims=True) + norm_eps)


def gelu_parts(u):
    cubic = 0.7978845608028654 * (u + 0.044715 * (u * u * u))
    bend = jnp.tanh(cubic)
    half = 0.5 * (1.0 + bend)
    slope = half + 0.5 * u * (1.0 - bend * bend) * (0.7978845608028654 * (1.0 + 0.134145 * (u * u)))
    return u * half, slope


def gelu_of(u):
    return 0.5 * u * (1.0 + jnp.tanh(0.7978845608028654 * (u + 0.044715 * (u * u * u))))


def fill_mask(piece_ref, mask_ref):
    length = mask_ref.shape[0]
    first = piece_ref[0]
    key_pos = lax.broadcasted_iota(jnp.int32, (length, length), 0)
    query_pos = lax.broadcasted_iota(jnp.int32, (length, length), 1)
    key_in = (key_pos >= first) & (key_pos < first + PIECE)
    query_in = (query_pos >= first) & (query_pos < first + PIECE)
    keep = (key_pos <= query_pos) | (key_in & query_in)
    mask_ref[...] = jnp.where(keep, 0.0, far_below)


def bias_strip(vector_row, strip_ref):
    wide = jnp.broadcast_to(vector_row, (128, vector_row.shape[1]))
    strip_ref[...] = pltpu.roll(wide, vector_row.shape[1] - 127, 1, stride=1, stride_axis=0)


def attend_kernel(
    piece_ref, x_ref, gain_ref, w_ref, wo_ref, vec_ref,
    out_ref, normed_ref, qkv_ref, mixed_ref, lse_ref,
    mask_ref, strip_ref, score_ref, prob_ref,
):
    length, width = x_ref.shape
    tiles = length // 128
    fill_mask(piece_ref, mask_ref)
    field = x_ref[...]
    normed_ref[...] = (field * inverse_rms(field) * gain_ref[...]).astype(BF)

    def project(c, _):
        cols = pl.ds(pl.multiple_of(c * 256, 256), 256)
        qkv_ref[:, cols] = nt(normed_ref[...], w_ref[cols, :]).astype(BF)
        return 0

    lax.fori_loop(0, 3 * width // 256, project, 0)
    lane_low = lax.broadcasted_iota(jnp.int32, (length, 128), 1) < 64
    row_low = lax.broadcasted_iota(jnp.int32, (128, length), 0) < 64

    def pair(hp, _):
        base = hp * 128
        q2 = qkv_ref[:, pl.ds(pl.multiple_of(base, 128), 128)] * jnp.asarray(0.125, BF)
        v2 = qkv_ref[:, pl.ds(pl.multiple_of(2 * width + base, 128), 128)]
        mixed = []
        for half in range(2):
            head = hp * 2 + half
            keep = lane_low if half == 0 else ~lane_low
            qm = jnp.where(keep, q2, jnp.zeros_like(q2))
            bias_strip(vec_ref[pl.ds(head, 1), :], strip_ref)
            peak = jnp.full((1, length), far_below, F32)
            for jt in range(tiles):
                rows = slice(jt * 128, jt * 128 + 128)
                k2 = qkv_ref[rows, pl.ds(pl.multiple_of(width + base, 128), 128)]
                at = 128 * (tiles - 1 - jt)
                s = nt(k2, qm) + strip_ref[:, at:at + length] + mask_ref[rows, :]
                score_ref[rows, :] = s
                peak = jnp.maximum(peak, jnp.max(s, axis=0, keepdims=True))
            total = jnp.zeros((1, length), F32)
            for jt in range(tiles):
                rows = slice(jt * 128, jt * 128 + 128)
                e = jnp.exp(score_ref[rows, :] - peak)
                total = total + jnp.sum(e, axis=0, keepdims=True)
                prob_ref[rows, :] = e.astype(BF)
            lse_ref[pl.ds(head, 1), :] = peak + jnp.log(total)
            mixed.append(tn(v2, prob_ref[...]) * (1.0 / total))
        both = jnp.where(row_low, mixed[0], mixed[1]).astype(BF)
        mixed_ref[:, pl.ds(pl.multiple_of(base, 128), 128)] = both.T
        return 0

    lax.fori_loop(0, width // 128, pair, 0)

    def back(c, _):
        cols = pl.ds(pl.multiple_of(c * 256, 256), 256)
        out_ref[:, cols] = x_ref[:, cols] + nt(mixed_ref[...], wo_ref[cols, :])
        return 0

    lax.fori_loop(0, width // 256, back, 0)


SMEM_SPEC = pl.BlockSpec(memory_space=pltpu.SMEM)
VMEM_SPEC = pl.BlockSpec(memory_space=pltpu.VMEM)


def attend(piece, x, gain, w, wo, vectors):
    length, width = x.shape
    heads = vectors.shape[0]
    span = vectors.shape[1]
    return pl.pallas_call(
        attend_kernel,
        out_shape=(
            jax.ShapeDtypeStruct((length, width), F32),
            jax.ShapeDtypeStruct((length, width), BF),
            jax.ShapeDtypeStruct((length, 3 * width), BF),
            jax.ShapeDtypeStruct((length, width), BF),
            jax.ShapeDtypeStruct((heads, length), F32),
        ),
        in_specs=[SMEM_SPEC] + [VMEM_SPEC] * 5,
        out_specs=[VMEM_SPEC] * 5,
        scratch_shapes=[
            pltpu.VMEM((length, length), F32),
            pltpu.VMEM((128, span), F32),
            pltpu.VMEM((length, length), F32),
            pltpu.VMEM((length, length), BF),
        ],
        compiler_params=pltpu.CompilerParams(vmem_limit_bytes=VMEM_BYTES),
        cost_estimate=pl.CostEstimate(
            flops=8 * length * width * width + 4 * length * length * width,
            bytes_accessed=20 * length * width + 8 * width * width,
            transcendentals=heads * length * length,
        ),
        name="attend",
    )(piece, x, gain, w, wo, vectors)


def attend_back_kernel(
    piece_ref, x_ref, gain_ref, w_ref, wo_ref, vec_ref, normed_ref, qkv_ref, mixed_ref, lse_ref, grad_ref,
    dx_ref, dw_ref, dwo_ref, dvec_ref, dgain_ref,
    mask_ref, strip_ref, sums_ref, prob_ref, ds_ref, low_ref, do_ref, dqkv_ref, delta_ref,
):
    length, width = x_ref.shape
    heads = vec_ref.shape[0]
    tiles = length // 128
    fill_mask(piece_ref, mask_ref)
    low_ref[...] = grad_ref[...].astype(BF)

    def out_back(c, _):
        cols = pl.ds(pl.multiple_of(c * 256, 256), 256)
        do_ref[:, cols] = nn(low_ref[...], wo_ref[:, cols]).astype(BF)
        dwo_ref[cols, :] = tn(low_ref[:, cols], mixed_ref[...]).astype(BF)
        return 0

    lax.fori_loop(0, width // 256, out_back, 0)
    pick = (
        lax.broadcasted_iota(jnp.int32, (delta_ref.shape[0], width), 1) // (width // heads)
        == lax.broadcasted_iota(jnp.int32, (delta_ref.shape[0], width), 0)
    ).astype(F32)
    delta_ref[...] = lax.dot_general(
        pick, do_ref[...].astype(F32) * mixed_ref[...].astype(F32), (((1,), (1,)), ((), ())),
        precision=lax.Precision.HIGHEST, preferred_element_type=F32,
    )
    lane_low = lax.broadcasted_iota(jnp.int32, (length, 128), 1) < 64
    lane_low_tile = lax.broadcasted_iota(jnp.int32, (128, 128), 1) < 64
    row_low = lax.broadcasted_iota(jnp.int32, (128, length), 0) < 64
    flip = (
        lax.broadcasted_iota(jnp.int32, (128, 128), 0) + lax.broadcasted_iota(jnp.int32, (128, 128), 1) == 127
    ).astype(F32)
    sums_ref[...] = jnp.zeros_like(sums_ref)

    def pair(hp, _):
        base = hp * 128
        q_cols = pl.ds(pl.multiple_of(base, 128), 128)
        k_cols = pl.ds(pl.multiple_of(width + base, 128), 128)
        v_cols = pl.ds(pl.multiple_of(2 * width + base, 128), 128)
        q2 = qkv_ref[:, q_cols] * jnp.asarray(0.125, BF)
        do2 = do_ref[:, q_cols]
        parts = []
        for half in range(2):
            head = hp * 2 + half
            keep = lane_low if half == 0 else ~lane_low
            qm = jnp.where(keep, q2, jnp.zeros_like(q2))
            dm = jnp.where(keep, do2, jnp.zeros_like(do2))
            bias_strip(vec_ref[pl.ds(head, 1), :], strip_ref)
            lse = lse_ref[pl.ds(head, 1), :]
            delta = delta_ref[pl.ds(head, 1), :]
            for jt in range(tiles):
                rows = slice(jt * 128, jt * 128 + 128)
                at = 128 * (tiles - 1 - jt)
                s = nt(qkv_ref[rows, k_cols], qm) + strip_ref[:, at:at + length] + mask_ref[rows, :]
                p = jnp.exp(s - lse)
                dp = nt(qkv_ref[rows, v_cols], dm)
                ds = (p * (dp - delta)).astype(BF)
                prob_ref[half, rows, :] = p.astype(BF)
                ds_ref[half, rows, :] = ds
                if jt == 0:
                    sums_ref[:, at:at + length] = ds.astype(F32)
                    sums_ref[:, 0:at] = jnp.zeros((128, at), F32)
                else:
                    sums_ref[:, at:at + length] += ds.astype(F32)
            turned = lax.dot_general(
                flip, sums_ref[...], (((1,), (0,)), ((), ())),
                precision=lax.Precision.HIGHEST, preferred_element_type=F32,
            )
            turned = pltpu.roll(turned, 0, 1, stride=1, stride_axis=0)
            dvec_ref[pl.ds(head, 1), :] = jnp.sum(turned, axis=0, keepdims=True)
            parts.append(tn(qkv_ref[:, k_cols], ds_ref[half]) * 0.125)
        both = jnp.where(row_low, parts[0], parts[1]).astype(BF)
        dqkv_ref[:, q_cols] = both.T
        for jt in range(tiles):
            rows = slice(jt * 128, jt * 128 + 128)
            dk = jnp.where(lane_low_tile, nn(ds_ref[0, rows, :], q2), nn(ds_ref[1, rows, :], q2))
            dqkv_ref[rows, k_cols] = dk.astype(BF)
            dv = jnp.where(lane_low_tile, nn(prob_ref[0, rows, :], do2), nn(prob_ref[1, rows, :], do2))
            dqkv_ref[rows, v_cols] = dv.astype(BF)
        return 0

    lax.fori_loop(0, width // 128, pair, 0)

    def weights_back(c, _):
        cols = pl.ds(pl.multiple_of(c * 256, 256), 256)
        dw_ref[cols, :] = tn(dqkv_ref[:, cols], normed_ref[...]).astype(BF)
        return 0

    lax.fori_loop(0, 3 * width // 256, weights_back, 0)

    def rows_back(c, _):
        cols = pl.ds(pl.multiple_of(c * 256, 256), 256)
        dx_ref[:, cols] = nn(dqkv_ref[...], w_ref[:, cols])
        return 0

    lax.fori_loop(0, width // 256, rows_back, 0)
    norm_back(x_ref, gain_ref, dx_ref, grad_ref, dx_ref, dgain_ref)


def norm_back(x_ref, gain_ref, upper_ref, base_ref, dx_ref, dgain_ref):
    field = x_ref[...]
    inverse = inverse_rms(field)
    unit = field * inverse
    upper = upper_ref[...]
    scaled = upper * gain_ref[...]
    dgain_ref[...] = jnp.sum(upper * unit, axis=0, keepdims=True)
    dx_ref[...] = base_ref[...] + inverse * (scaled - unit * jnp.mean(scaled * unit, axis=1, keepdims=True))


def attend_back(piece, x, gain, w, wo, vectors, normed, qkv, mixed, lse, grad):
    length, width = x.shape
    heads, span = vectors.shape
    return pl.pallas_call(
        attend_back_kernel,
        out_shape=(
            jax.ShapeDtypeStruct((length, width), F32),
            jax.ShapeDtypeStruct((3 * width, width), BF),
            jax.ShapeDtypeStruct((width, width), BF),
            jax.ShapeDtypeStruct((heads, span), F32),
            jax.ShapeDtypeStruct((1, width), F32),
        ),
        in_specs=[SMEM_SPEC] + [VMEM_SPEC] * 10,
        out_specs=[VMEM_SPEC] * 5,
        scratch_shapes=[
            pltpu.VMEM((length, length), F32),
            pltpu.VMEM((128, span), F32),
            pltpu.VMEM((128, span), F32),
            pltpu.VMEM((2, length, length), BF),
            pltpu.VMEM((2, length, length), BF),
            pltpu.VMEM((length, width), BF),
            pltpu.VMEM((length, width), BF),
            pltpu.VMEM((length, 3 * width), BF),
            pltpu.VMEM((16, length), F32),
        ],
        compiler_params=pltpu.CompilerParams(vmem_limit_bytes=VMEM_BYTES),
        cost_estimate=pl.CostEstimate(
            flops=16 * length * width * width + 10 * length * length * width,
            bytes_accessed=40 * length * width + 16 * width * width,
            transcendentals=heads * length * length,
        ),
        name="attend_back",
    )(piece, x, gain, w, wo, vectors, normed, qkv, mixed, lse, grad)


def mlp_kernel(x_ref, gain_ref, up_ref, down_ref, out_ref, normed_ref):
    field = x_ref[...]
    normed_ref[...] = (field * inverse_rms(field) * gain_ref[...]).astype(BF)
    out_ref[...] = field

    def chunk(c, _):
        at = pl.ds(pl.multiple_of(c * 512, 512), 512)
        hidden = gelu_of(nt(normed_ref[...], up_ref[at, :])).astype(BF)
        out_ref[...] += nt(hidden, down_ref[:, at])
        return 0

    lax.fori_loop(0, up_ref.shape[0] // 512, chunk, 0)


def mlp(x, gain, up, down):
    length, width = x.shape
    hidden = up.shape[0]
    return pl.pallas_call(
        mlp_kernel,
        out_shape=(jax.ShapeDtypeStruct((length, width), F32), jax.ShapeDtypeStruct((length, width), BF)),
        in_specs=[VMEM_SPEC] * 4,
        out_specs=[VMEM_SPEC] * 2,
        compiler_params=pltpu.CompilerParams(vmem_limit_bytes=VMEM_BYTES),
        cost_estimate=pl.CostEstimate(
            flops=4 * length * width * hidden, bytes_accessed=10 * length * width + 4 * width * hidden,
            transcendentals=length * hidden,
        ),
        name="mlp",
    )(x, gain, up, down)


def mlp_back_kernel(x_ref, gain_ref, up_ref, down_ref, normed_ref, grad_ref,
                    dx_ref, dup_ref, ddown_ref, dgain_ref, low_ref, acc_ref):
    low_ref[...] = grad_ref[...].astype(BF)
    acc_ref[...] = jnp.zeros_like(acc_ref)

    def chunk(c, _):
        at = pl.ds(pl.multiple_of(c * 512, 512), 512)
        hidden, slope = gelu_parts(nt(normed_ref[...], up_ref[at, :]))
        pre_grad = (nn(low_ref[...], down_ref[:, at]) * slope).astype(BF)
        ddown_ref[:, at] = tn(low_ref[...], hidden.astype(BF)).astype(BF)
        dup_ref[at, :] = tn(pre_grad, normed_ref[...]).astype(BF)
        acc_ref[...] += nn(pre_grad, up_ref[at, :])
        return 0

    lax.fori_loop(0, up_ref.shape[0] // 512, chunk, 0)
    norm_back(x_ref, gain_ref, acc_ref, grad_ref, dx_ref, dgain_ref)


def mlp_back(x, gain, up, down, normed, grad):
    length, width = x.shape
    hidden = up.shape[0]
    return pl.pallas_call(
        mlp_back_kernel,
        out_shape=(
            jax.ShapeDtypeStruct((length, width), F32),
            jax.ShapeDtypeStruct((hidden, width), BF),
            jax.ShapeDtypeStruct((width, hidden), BF),
            jax.ShapeDtypeStruct((1, width), F32),
        ),
        in_specs=[VMEM_SPEC] * 6,
        out_specs=[VMEM_SPEC] * 4,
        scratch_shapes=[pltpu.VMEM((length, width), BF), pltpu.VMEM((length, width), F32)],
        compiler_params=pltpu.CompilerParams(vmem_limit_bytes=VMEM_BYTES),
        cost_estimate=pl.CostEstimate(
            flops=10 * length * width * hidden, bytes_accessed=16 * length * width + 8 * width * hidden,
            transcendentals=length * hidden,
        ),
        name="mlp_back",
    )(x, gain, up, down, normed, grad)


def experts_kernel(
    x_ref, c_ref, gate_ref, up_ref, down_ref,
    y_ref, dx_ref, dgate_ref, own_up_ref, own_down_ref, peer_up_ref, peer_down_ref,
    y_sum, dx_sum, dgate_sum, up_sum, down_sum,
):
    part = pl.program_id(1)
    sources, _, span, width = x_ref.shape
    group = max(1, 384 // span)
    rows = group * span
    up_sum[...] = jnp.zeros_like(up_sum)
    down_sum[...] = jnp.zeros_like(down_sum)

    @pl.when(part == 0)
    def _():
        y_sum[...] = jnp.zeros_like(y_sum)
        dx_sum[...] = jnp.zeros_like(dx_sum)
        dgate_sum[...] = jnp.zeros_like(dgate_sum)

    def tile(i, _):
        at = pl.ds(i * group, group)
        x = x_ref[at, 0].reshape(rows, width)
        c = c_ref[at, 0].reshape(rows, width)
        gate = gate_ref[at, 0].reshape(rows, 1)
        hidden, slope = gelu_parts(nn(x, up_ref[...]))
        hidden = hidden.astype(BF)
        back = nt(c, down_ref[...])
        pre_grad = (gate * back * slope).astype(BF)
        dgate_sum[at] += jnp.sum(hidden.astype(F32) * back, axis=1, keepdims=True).reshape(group, span, 1)
        y_sum[at] += nn(hidden, down_ref[...]).reshape(group, span, width)
        dx_sum[at] += nt(pre_grad, up_ref[...]).reshape(group, span, width)
        up_sum[...] += tn(x, pre_grad)
        down_sum[...] += tn(hidden, (gate * c.astype(F32)).astype(BF))
        return 0

    lax.fori_loop(0, sources // group, tile, 0)

    @pl.when(part == 0)
    def _():
        own_up_ref[...] = up_sum[...]
        own_down_ref[...] = down_sum[...]

    @pl.when(part == 1)
    def _():
        peer_up_ref[...] = up_sum[...].astype(BF)
        peer_down_ref[...] = down_sum[...].astype(BF)
        y_ref[:, 0] = (gate_ref[:, 0] * y_sum[...]).astype(BF)
        dx_ref[:, 0] = dx_sum[...].astype(BF)
        dgate_ref[:, 0] = dgate_sum[...]


def run_experts(x, c, gate, up, down):
    sources, local, span, width = x.shape
    hidden = up.shape[3]
    lean = sources * span > 2048
    once = dict(pipeline_mode=pl.Buffered(1)) if lean else {}
    row_spec = pl.BlockSpec((sources, 1, span, width), lambda e, j: (0, e, 0, 0), **once)
    row_out_spec = pl.BlockSpec((sources, 1, span, width), lambda e, j: (0, e, 0, 0), pipeline_mode=pl.Buffered(1))
    gate_spec = pl.BlockSpec((sources, 1, span, 1), lambda e, j: (0, e, 0, 0), **once)
    sq = pl.Squeezed()
    up_spec = pl.BlockSpec((sq, sq, width, hidden), lambda e, j: (j, e, 0, 0))
    down_spec = pl.BlockSpec((sq, sq, hidden, width), lambda e, j: (j, e, 0, 0))
    gup_spec = pl.BlockSpec((sq, width, hidden), lambda e, j: (e, 0, 0))
    gdown_spec = pl.BlockSpec((sq, hidden, width), lambda e, j: (e, 0, 0))
    rows = local * sources * span
    return pl.pallas_call(
        experts_kernel,
        grid=(local, 2),
        out_shape=(
            jax.ShapeDtypeStruct(x.shape, BF),
            jax.ShapeDtypeStruct(x.shape, BF),
            jax.ShapeDtypeStruct(gate.shape, F32),
            jax.ShapeDtypeStruct((local, width, hidden), F32),
            jax.ShapeDtypeStruct((local, hidden, width), F32),
            jax.ShapeDtypeStruct((local, width, hidden), BF),
            jax.ShapeDtypeStruct((local, hidden, width), BF),
        ),
        in_specs=[row_spec, row_spec, gate_spec, up_spec, down_spec],
        out_specs=[row_out_spec, row_out_spec, gate_spec, gup_spec, gdown_spec, gup_spec, gdown_spec],
        scratch_shapes=[
            pltpu.VMEM((sources, span, width), F32),
            pltpu.VMEM((sources, span, width), F32),
            pltpu.VMEM((sources, span, 1), F32),
            pltpu.VMEM((width, hidden), F32),
            pltpu.VMEM((hidden, width), F32),
        ],
        compiler_params=pltpu.CompilerParams(vmem_limit_bytes=VMEM_BYTES),
        cost_estimate=pl.CostEstimate(
            flops=24 * rows * width * hidden, bytes_accessed=16 * rows * width, transcendentals=2 * rows * hidden,
        ),
        name="experts",
    )(x, c, gate, up, down)


def spread_kernel(slot_ref, rows_ref, out_ref):
    experts, zones, capacity, width = out_ref.shape
    length = rows_ref.shape[1]
    take = max(1, 384 // capacity)

    def chunk(i, _):
        for zone in range(zones):
            place = lax.broadcasted_iota(jnp.int32, (take * capacity, length), 0) + i * (take * capacity)
            hit = (place == slot_ref[zone, 0:1, :]) | (place == slot_ref[zone, 1:2, :])
            picked = nn(jnp.where(hit, 1.0, 0.0).astype(BF), rows_ref[zone])
            out_ref[pl.ds(i * take, take), zone] = picked.reshape(take, capacity, width).astype(BF)
        return 0

    lax.fori_loop(0, experts // take, chunk, 0)


def spread(slot_rows, rows, experts, capacity):
    zones, length, width = rows.shape
    return pl.pallas_call(
        spread_kernel,
        out_shape=jax.ShapeDtypeStruct((experts, zones, capacity, width), BF),
        in_specs=[VMEM_SPEC] * 2,
        out_specs=VMEM_SPEC,
        compiler_params=pltpu.CompilerParams(vmem_limit_bytes=VMEM_BYTES),
        cost_estimate=pl.CostEstimate(
            flops=2 * zones * experts * capacity * length * width,
            bytes_accessed=2 * zones * (experts * capacity + length) * width, transcendentals=0,
        ),
        name="spread",
    )(slot_rows, rows)


def collect_kernel(slot_ref, rows_ref, out_ref):
    experts, zones, capacity, width = rows_ref.shape
    length = out_ref.shape[1]
    take = max(1, 384 // capacity)
    out_ref[...] = jnp.zeros_like(out_ref)

    def chunk(i, _):
        for zone in range(zones):
            place = lax.broadcasted_iota(jnp.int32, (length, take * capacity), 1) + i * (take * capacity)
            hit = (place == slot_ref[:, 2 * zone:2 * zone + 1]) | (place == slot_ref[:, 2 * zone + 1:2 * zone + 2])
            rows = rows_ref[pl.ds(i * take, take), zone].reshape(take * capacity, width)
            out_ref[zone] += nn(jnp.where(hit, 1.0, 0.0).astype(BF), rows)
        return 0

    lax.fori_loop(0, experts // take, chunk, 0)


def collect(slot_columns, rows):
    experts, zones, capacity, width = rows.shape
    length = slot_columns.shape[0]
    return pl.pallas_call(
        collect_kernel,
        out_shape=jax.ShapeDtypeStruct((zones, length, width), F32),
        in_specs=[VMEM_SPEC] * 2,
        out_specs=VMEM_SPEC,
        compiler_params=pltpu.CompilerParams(vmem_limit_bytes=VMEM_BYTES),
        cost_estimate=pl.CostEstimate(
            flops=2 * zones * experts * capacity * length * width,
            bytes_accessed=2 * zones * (experts * capacity + 2 * length) * width, transcendentals=0,
        ),
        name="collect",
    )(slot_columns, rows)


bucket_edges = (1, 2, 3, 4, 6, 8, 12, 16, 24, 32, 48, 64, 96, 128, 192, 256, 384, 512, 768, 1024, 1536)


def bucket_onehot(length, buckets):
    distance = (length - 1) - jnp.arange(2 * length, dtype=jnp.int32)
    edge_list = jnp.array(bucket_edges, dtype=jnp.int32)
    magnitude = jnp.sum(
        (jnp.abs(distance)[:, None] >= edge_list[None, :]).astype(jnp.int32), axis=1, dtype=jnp.int32
    )
    bucket = magnitude + buckets // 2 * (distance > 0).astype(jnp.int32)
    real = jnp.arange(2 * length)[:, None] < 2 * length - 1
    hit = (bucket[:, None] == jnp.arange(buckets, dtype=jnp.int32)[None, :]) & real
    return hit.astype(F32)


def expert_slots(routes, experts_all, capacity):
    pairs = routes.reshape(-1)
    onehot = pairs[:, None] == jnp.arange(experts_all, dtype=jnp.int32)[None, :]
    count = pairs.shape[0]
    before = jnp.arange(count)[:, None] > jnp.arange(count)[None, :]
    ranks = jnp.dot(before.astype(BF), onehot.astype(BF), preferred_element_type=F32)
    own = jnp.sum(jnp.where(onehot, ranks, 0.0), axis=1).astype(jnp.int32)
    return (pairs * capacity + own).reshape(routes.shape)


def shift_from(value, distance):
    size = lax.axis_size("shard")
    return lax.ppermute(value, "shard", [((z + distance) % size, z) for z in range(size)])


def shift_to(value, distance):
    size = lax.axis_size("shard")
    return lax.ppermute(value, "shard", [(z, (z + distance) % size) for z in range(size)])


def swap_pair(value):
    return lax.ppermute(value, "shard", [(z, z ^ 1) for z in range(lax.axis_size("shard"))])


def total_over_mesh(value):
    for name in ("shard", "expert"):
        size = lax.axis_size(name)
        step = 1
        while step < size:
            value = value + lax.ppermute(value, name, [(i, i ^ step) for i in range(size)])
            step *= 2
    return value


def exchange(value):
    return lax.all_to_all(value, "expert", split_axis=0, concat_axis=0, tiled=True)


def gather_rows(value, name):
    return lax.all_gather(value, name, axis=0, tiled=True)


def scatter_rows(value, name):
    return lax.psum_scatter(value, name, scatter_dimension=0, tiled=True)


def per_device(
    tokens, piece_start, routes, norm_gains, bias_tables, qkv_weight, out_weight, mlp_up, mlp_down, router,
    expert_up, expert_down, cotangent,
):
    length, width = tokens.shape
    owners = lax.axis_size("expert")
    zones = lax.axis_size("shard") // 2
    local = expert_up.shape[0]
    experts_all = local * owners
    capacity = 3 * routes.shape[1] * length // (2 * experts_all)
    qkv_cols, out_cols = qkv_weight.shape[2], out_weight.shape[2]
    router_pad = 16

    def router_block(part):
        return jnp.pad(part, ((0, 0), (0, router_pad - part.shape[1])))

    first = gather_rows(jnp.concatenate([qkv_weight[0], out_weight[0]], axis=1), "shard").T
    middle = gather_rows(mlp_up, "shard").T
    lower = gather_rows(mlp_down, "shard").T
    last = gather_rows(
        jnp.concatenate([qkv_weight[1], out_weight[1], router_block(router)], axis=1), "shard"
    ).T
    first = gather_rows(first, "expert").reshape(owners, qkv_cols + out_cols, width)
    up_full = gather_rows(middle, "expert")
    down_full = gather_rows(lower, "expert")
    last = gather_rows(last, "expert").reshape(owners, qkv_cols + out_cols + router_pad, width)

    def qkv_of(block):
        return block[:, :qkv_cols].reshape(-1, width)

    def out_of(block):
        return block[:, qkv_cols:qkv_cols + out_cols].reshape(-1, width)

    router_full = last[:, qkv_cols + out_cols:qkv_cols + out_cols + router.shape[1]].reshape(experts_all, width)

    up_pair = jnp.stack([expert_up, swap_pair(expert_up)])
    down_pair = jnp.stack([expert_down, swap_pair(expert_down)])

    slots = expert_slots(routes, experts_all, capacity)
    zone_slots = [slots] + [shift_from(slots, 2 * d) for d in range(1, zones)]
    slot_columns = jnp.concatenate(zone_slots, axis=1)
    slot_rows = slot_columns.T.reshape(zones, routes.shape[1], length)

    def dispatch(rows):
        own = [rows] + [shift_from(rows, 2 * d) for d in range(1, zones)]
        packed = spread(slot_rows, jnp.stack(own), experts_all, capacity)
        return exchange(packed.reshape(owners, local, zones * capacity, width))

    def undo(rows):
        back = exchange(rows).reshape(experts_all, zones, capacity, width)
        return collect(slot_columns, back)

    cotangent_rows = dispatch(cotangent)

    onehot = bucket_onehot(length, bias_tables.shape[2])
    vectors = lax.dot_general(
        bias_tables, onehot, (((2,), (1,)), ((), ())), precision=lax.Precision.HIGHEST
    )
    gains = [norm_gains[i:i + 1] for i in range(4)]
    x0 = tokens.astype(F32)
    x1, ah0, qkv0, o0, lse0 = attend(piece_start, x0, gains[0], qkv_of(first), out_of(first), vectors[0])
    x2, mh = mlp(x1, gains[1], up_full, down_full)
    x3, ah1, qkv1, o1, lse1 = attend(piece_start, x2, gains[2], qkv_of(last), out_of(last), vectors[1])

    unit3 = x3 * inverse_rms(x3)
    eh = (unit3 * gains[3]).astype(BF)
    logits = nt(eh, router_full)
    expert_ids = jnp.arange(experts_all, dtype=jnp.int32)
    chosen = routes[:, :, None] == expert_ids[None, None, :]
    gates = jax.nn.softmax(jnp.sum(jnp.where(chosen, logits[:, None, :], 0.0), axis=2), axis=1)

    eh_rows = dispatch(eh)
    slot_ids = jnp.arange(experts_all * capacity, dtype=jnp.int32)

    def gate_slots(zone):
        zone_gates = gates if zone == 0 else shift_from(gates, 2 * zone)
        hit = zone_slots[zone][:, :, None] == slot_ids[None, None, :]
        return jnp.sum(jnp.where(hit, zone_gates[:, :, None], 0.0), axis=(0, 1)).reshape(experts_all, capacity)

    gate_rows = exchange(
        jnp.stack([gate_slots(d) for d in range(zones)], axis=1).reshape(owners, local, zones * capacity)
    )
    y_rows, dx_rows, dgate_rows, own_up, own_down, peer_up, peer_down = run_experts(
        eh_rows, cotangent_rows, gate_rows[..., None], up_pair, down_pair
    )
    grad_up = own_up + swap_pair(peer_up).astype(F32)
    grad_down = own_down + swap_pair(peer_down).astype(F32)

    dx_back = undo(dx_rows)
    dgate_back = exchange(dgate_rows[..., 0]).reshape(experts_all, zones, capacity)
    token_grad = dx_back[0]
    gate_grad = 0.0
    for d in range(zones):
        hit = zone_slots[d][:, :, None] == slot_ids[None, None, :]
        part = jnp.sum(jnp.where(hit, dgate_back[:, d].reshape(-1)[None, None, :], 0.0), axis=2)
        gate_grad = gate_grad + (part if d == 0 else shift_to(part, 2 * d))
    for d in range(1, zones):
        token_grad = token_grad + shift_to(dx_back[d].astype(BF), 2 * d).astype(F32)
    y_back = undo(y_rows)
    final = x3 + y_back[0]
    for d in range(1, zones):
        final = final + shift_to(y_back[d].astype(BF), 2 * d).astype(F32)
    output = final.astype(BF)

    c = cotangent.astype(F32)
    dchoice = gates * (gate_grad - jnp.sum(gates * gate_grad, axis=1, keepdims=True))
    dlogits = jnp.sum(jnp.where(chosen, dchoice[:, :, None], 0.0), axis=1).astype(BF)
    grad_router = tn(dlogits, eh)
    deh = token_grad + nn(dlogits, router_full)
    scaled = deh * gains[3]
    dx3 = c + inverse_rms(x3) * (scaled - unit3 * jnp.mean(scaled * unit3, axis=1, keepdims=True))
    dgain3 = jnp.sum(deh * unit3, axis=0)[None]

    dx2, dqkv1, dout1, dvec1, dgain2 = attend_back(
        piece_start, x2, gains[2], qkv_of(last), out_of(last), vectors[1], ah1, qkv1, o1, lse1, dx3
    )
    dx1, dup, ddown, dgain1 = mlp_back(x1, gains[1], up_full, down_full, mh, dx2)
    dx0, dqkv0, dout0, dvec0, dgain0 = attend_back(
        piece_start, x0, gains[0], qkv_of(first), out_of(first), vectors[0], ah0, qkv0, o0, lse0, dx1
    )

    def reduce_block(parts):
        block = jnp.concatenate([p.reshape(owners, -1, p.shape[-1]) for p in parts], axis=1)
        rows = block.shape[1]
        mine = scatter_rows(block.reshape(owners * rows, block.shape[2]), "expert")
        return scatter_rows(mine.T, "shard").astype(F32)

    router_rows = jnp.pad(
        grad_router.astype(BF).reshape(owners, local, width), ((0, 0), (0, router_pad - local), (0, 0))
    )
    last_grad = reduce_block([dqkv1, dout1, router_rows])
    grad_mlp_up = reduce_block([dup])
    grad_mlp_down = reduce_block([ddown])
    first_grad = reduce_block([dqkv0, dout0])
    grad_qkv = jnp.stack([first_grad[:, :qkv_cols], last_grad[:, :qkv_cols]])
    grad_out = jnp.stack([first_grad[:, qkv_cols:], last_grad[:, qkv_cols:qkv_cols + out_cols]])
    grad_router_out = last_grad[:, qkv_cols + out_cols:qkv_cols + out_cols + local]

    dtables = lax.dot_general(
        jnp.stack([dvec0, dvec1]), onehot, (((2,), (0,)), ((), ())), precision=lax.Precision.HIGHEST
    )
    dgains = jnp.concatenate([dgain0, dgain1, dgain2, dgain3])
    small = total_over_mesh(jnp.concatenate([dgains.reshape(-1), dtables.reshape(-1)]))
    return (
        output,
        dx0,
        small[:dgains.size].reshape(dgains.shape),
        small[dgains.size:].reshape(dtables.shape),
        grad_qkv,
        grad_out,
        grad_mlp_up,
        grad_mlp_down,
        grad_router_out,
        grad_up,
        grad_down,
    )


def solution(mesh):
    both = P(("expert", "shard"), None)
    split3, split2 = P(None, "shard", "expert"), P("shard", "expert")
    up_spec, down_spec = P("expert", None, "shard"), P("expert", "shard", None)
    in_specs = (
        both, P(("expert", "shard")), both, P(), P(), split3, split3, split2, split2, split2, up_spec, down_spec, both
    )
    out_specs = (both, both, P(), P(), split3, split3, split2, split2, split2, up_spec, down_spec)
    return jax.shard_map(per_device, mesh=mesh, in_specs=in_specs, out_specs=out_specs, check_vma=False)
```

```python
import jax
import jax.numpy as jnp
from jax import lax
from jax.experimental import pallas as pl
from jax.experimental.pallas import tpu as pltpu
from jax.sharding import PartitionSpec as P

PIECE = 256
norm_eps = 1e-06
far_below = -1e30
BF = jnp.bfloat16
F32 = jnp.float32
VMEM_BYTES = 56 * 1024 * 1024


def nn(a, b):
    return lax.dot_general(a, b, (((1,), (0,)), ((), ())), preferred_element_type=F32)


def nt(a, b):
    return lax.dot_general(a, b, (((1,), (1,)), ((), ())), preferred_element_type=F32)


def tn(a, b):
    return lax.dot_general(a, b, (((0,), (0,)), ((), ())), preferred_element_type=F32)


def inverse_rms(field):
    return lax.rsqrt(jnp.mean(field * field, axis=1, keepdims=True) + norm_eps)


def gelu_parts(u):
    cubic = 0.7978845608028654 * (u + 0.044715 * (u * u * u))
    bend = jnp.tanh(cubic)
    half = 0.5 * (1.0 + bend)
    slope = half + 0.5 * u * (1.0 - bend * bend) * (0.7978845608028654 * (1.0 + 0.134145 * (u * u)))
    return u * half, slope


def gelu_of(u):
    return 0.5 * u * (1.0 + jnp.tanh(0.7978845608028654 * (u + 0.044715 * (u * u * u))))


def fill_mask(piece_ref, mask_ref):
    length = mask_ref.shape[0]
    first = piece_ref[0]
    key_pos = lax.broadcasted_iota(jnp.int32, (length, length), 0)
    query_pos = lax.broadcasted_iota(jnp.int32, (length, length), 1)
    key_in = (key_pos >= first) & (key_pos < first + PIECE)
    query_in = (query_pos >= first) & (query_pos < first + PIECE)
    keep = (key_pos <= query_pos) | (key_in & query_in)
    mask_ref[...] = jnp.where(keep, 0.0, far_below)


def bias_strip(vector_row, strip_ref):
    wide = jnp.broadcast_to(vector_row, (128, vector_row.shape[1]))
    strip_ref[...] = pltpu.roll(wide, vector_row.shape[1] - 127, 1, stride=1, stride_axis=0)


def flatten(blocks_ref, flat_ref):
    rows = blocks_ref.shape[1]
    for i in range(blocks_ref.shape[0]):
        flat_ref[i * rows:i * rows + rows, :] = blocks_ref[i]


def unflatten(flat_ref, blocks_ref, start):
    count = blocks_ref.shape[0]
    rows = flat_ref.shape[0] // count
    for i in range(count):
        blocks_ref[i, start:start + rows, :] = flat_ref[i * rows:i * rows + rows, :]


def weight_specs(weights):
    packed, qkv_rows, out_rows = weights
    if isinstance(packed, tuple):
        return list(packed), [VMEM_SPEC, VMEM_SPEC]
    return [packed], [VMEM_SPEC]


def weight_views(weights, refs):
    packed, qkv_rows, out_rows = weights
    if isinstance(packed, tuple):
        return refs[0], refs[1], refs[2:]
    return refs[0].at[:, 0:qkv_rows, :], refs[0].at[:, qkv_rows:qkv_rows + out_rows, :], refs[1:]


def attend_kernel(
    weights, piece_ref, x_ref, gain_ref, *refs
):
    w_ref, wo_ref, refs = weight_views(weights, refs)
    (vec_ref, out_ref, normed_ref, qkv_ref, mixed_ref, lse_ref,
     mask_ref, strip_ref, score_ref, prob_ref, flat_ref, flat_out_ref) = refs
    length, width = x_ref.shape
    flatten(w_ref, flat_ref)
    flatten(wo_ref, flat_out_ref)
    tiles = length // 128
    fill_mask(piece_ref, mask_ref)
    field = x_ref[...]
    normed_ref[...] = (field * inverse_rms(field) * gain_ref[...]).astype(BF)

    def project(c, _):
        cols = pl.ds(pl.multiple_of(c * 256, 256), 256)
        qkv_ref[:, cols] = nt(normed_ref[...], flat_ref[cols, :]).astype(BF)
        return 0

    lax.fori_loop(0, 3 * width // 256, project, 0)
    lane_low = lax.broadcasted_iota(jnp.int32, (length, 128), 1) < 64
    row_low = lax.broadcasted_iota(jnp.int32, (128, length), 0) < 64

    def pair(hp, _):
        base = hp * 128
        q2 = qkv_ref[:, pl.ds(pl.multiple_of(base, 128), 128)] * jnp.asarray(0.125, BF)
        v2 = qkv_ref[:, pl.ds(pl.multiple_of(2 * width + base, 128), 128)]
        mixed = []
        for half in range(2):
            head = hp * 2 + half
            keep = lane_low if half == 0 else ~lane_low
            qm = jnp.where(keep, q2, jnp.zeros_like(q2))
            bias_strip(vec_ref[pl.ds(head, 1), :], strip_ref)
            peak = jnp.full((1, length), far_below, F32)
            for jt in range(tiles):
                rows = slice(jt * 128, jt * 128 + 128)
                k2 = qkv_ref[rows, pl.ds(pl.multiple_of(width + base, 128), 128)]
                at = 128 * (tiles - 1 - jt)
                s = nt(k2, qm) + strip_ref[:, at:at + length] + mask_ref[rows, :]
                score_ref[rows, :] = s
                peak = jnp.maximum(peak, jnp.max(s, axis=0, keepdims=True))
            total = jnp.zeros((1, length), F32)
            for jt in range(tiles):
                rows = slice(jt * 128, jt * 128 + 128)
                e = jnp.exp(score_ref[rows, :] - peak)
                total = total + jnp.sum(e, axis=0, keepdims=True)
                prob_ref[rows, :] = e.astype(BF)
            lse_ref[pl.ds(head, 1), :] = peak + jnp.log(total)
            mixed.append(tn(v2, prob_ref[...]) * (1.0 / total))
        both = jnp.where(row_low, mixed[0], mixed[1]).astype(BF)
        mixed_ref[:, pl.ds(pl.multiple_of(base, 128), 128)] = both.T
        return 0

    lax.fori_loop(0, width // 128, pair, 0)

    def back(c, _):
        cols = pl.ds(pl.multiple_of(c * 256, 256), 256)
        out_ref[:, cols] = x_ref[:, cols] + nt(mixed_ref[...], flat_out_ref[cols, :])
        return 0

    lax.fori_loop(0, width // 256, back, 0)


SMEM_SPEC = pl.BlockSpec(memory_space=pltpu.SMEM)
VMEM_SPEC = pl.BlockSpec(memory_space=pltpu.VMEM)


def attend(piece, x, gain, weights, vectors):
    length, width = x.shape
    w_args, w_specs = weight_specs(weights)
    heads = vectors.shape[0]
    span = vectors.shape[1]
    return pl.pallas_call(
        lambda *refs: attend_kernel(weights, *refs),
        out_shape=(
            jax.ShapeDtypeStruct((length, width), F32),
            jax.ShapeDtypeStruct((length, width), BF),
            jax.ShapeDtypeStruct((length, 3 * width), BF),
            jax.ShapeDtypeStruct((length, width), BF),
            jax.ShapeDtypeStruct((heads, length), F32),
        ),
        in_specs=[SMEM_SPEC] + [VMEM_SPEC] * 2 + w_specs + [VMEM_SPEC],
        out_specs=[VMEM_SPEC] * 5,
        scratch_shapes=[
            pltpu.VMEM((length, length), F32),
            pltpu.VMEM((128, span), F32),
            pltpu.VMEM((length, length), F32),
            pltpu.VMEM((length, length), BF),
            pltpu.VMEM((3 * width, width), BF),
            pltpu.VMEM((width, width), BF),
        ],
        compiler_params=pltpu.CompilerParams(vmem_limit_bytes=VMEM_BYTES),
        cost_estimate=pl.CostEstimate(
            flops=8 * length * width * width + 4 * length * length * width,
            bytes_accessed=20 * length * width + 8 * width * width,
            transcendentals=heads * length * length,
        ),
        name="attend",
    )(piece, x, gain, *w_args, vectors)


def attend_back_kernel(
    tail, weights, piece_ref, x_ref, gain_ref, *refs
):
    w_ref, wo_ref, refs = weight_views(weights, refs)
    (vec_ref, normed_ref, qkv_ref, mixed_ref, lse_ref, grad_ref), refs = refs[:6], refs[6:]
    tail_ref, refs = (refs[0], refs[1:]) if tail else (None, refs)
    grad_refs, refs = (refs[1:len(refs) - 14], refs[:1] + refs[len(refs) - 14:])
    (dx_ref, dvec_ref, dgain_ref,
     mask_ref, strip_ref, sums_ref, prob_ref, ds_ref, low_ref, do_ref, dqkv_ref, delta_ref,
     flat_ref, flat_out_ref, dw_ref) = refs
    flatten(w_ref, flat_ref)
    flatten(wo_ref, flat_out_ref)
    length, width = x_ref.shape
    heads = vec_ref.shape[0]
    tiles = length // 128
    fill_mask(piece_ref, mask_ref)
    low_ref[...] = grad_ref[...].astype(BF)

    def out_back(c, _):
        cols = pl.ds(pl.multiple_of(c * 256, 256), 256)
        do_ref[:, cols] = nn(low_ref[...], flat_out_ref[:, cols]).astype(BF)
        return 0

    lax.fori_loop(0, width // 256, out_back, 0)

    def out_weights_back(c, _):
        cols = pl.ds(pl.multiple_of(c * 256, 256), 256)
        flat_out_ref[cols, :] = tn(low_ref[:, cols], mixed_ref[...]).astype(BF)
        return 0

    lax.fori_loop(0, width // 256, out_weights_back, 0)
    pick = (
        lax.broadcasted_iota(jnp.int32, (delta_ref.shape[0], width), 1) // (width // heads)
        == lax.broadcasted_iota(jnp.int32, (delta_ref.shape[0], width), 0)
    ).astype(F32)
    delta_ref[...] = lax.dot_general(
        pick, do_ref[...].astype(F32) * mixed_ref[...].astype(F32), (((1,), (1,)), ((), ())),
        precision=lax.Precision.HIGHEST, preferred_element_type=F32,
    )
    lane_low = lax.broadcasted_iota(jnp.int32, (length, 128), 1) < 64
    lane_low_tile = lax.broadcasted_iota(jnp.int32, (128, 128), 1) < 64
    row_low = lax.broadcasted_iota(jnp.int32, (128, length), 0) < 64
    flip = (
        lax.broadcasted_iota(jnp.int32, (128, 128), 0) + lax.broadcasted_iota(jnp.int32, (128, 128), 1) == 127
    ).astype(F32)
    sums_ref[...] = jnp.zeros_like(sums_ref)

    def pair(hp, _):
        base = hp * 128
        q_cols = pl.ds(pl.multiple_of(base, 128), 128)
        k_cols = pl.ds(pl.multiple_of(width + base, 128), 128)
        v_cols = pl.ds(pl.multiple_of(2 * width + base, 128), 128)
        q2 = qkv_ref[:, q_cols] * jnp.asarray(0.125, BF)
        do2 = do_ref[:, q_cols]
        parts = []
        for half in range(2):
            head = hp * 2 + half
            keep = lane_low if half == 0 else ~lane_low
            qm = jnp.where(keep, q2, jnp.zeros_like(q2))
            dm = jnp.where(keep, do2, jnp.zeros_like(do2))
            bias_strip(vec_ref[pl.ds(head, 1), :], strip_ref)
            lse = lse_ref[pl.ds(head, 1), :]
            delta = delta_ref[pl.ds(head, 1), :]
            for jt in range(tiles):
                rows = slice(jt * 128, jt * 128 + 128)
                at = 128 * (tiles - 1 - jt)
                s = nt(qkv_ref[rows, k_cols], qm) + strip_ref[:, at:at + length] + mask_ref[rows, :]
                p = jnp.exp(s - lse)
                dp = nt(qkv_ref[rows, v_cols], dm)
                ds = (p * (dp - delta)).astype(BF)
                prob_ref[half, rows, :] = p.astype(BF)
                ds_ref[half, rows, :] = ds
                if jt == 0:
                    sums_ref[:, at:at + length] = ds.astype(F32)
                    sums_ref[:, 0:at] = jnp.zeros((128, at), F32)
                else:
                    sums_ref[:, at:at + length] += ds.astype(F32)
            turned = lax.dot_general(
                flip, sums_ref[...], (((1,), (0,)), ((), ())),
                precision=lax.Precision.HIGHEST, preferred_element_type=F32,
            )
            turned = pltpu.roll(turned, 0, 1, stride=1, stride_axis=0)
            dvec_ref[pl.ds(head, 1), :] = jnp.sum(turned, axis=0, keepdims=True)
            parts.append(tn(qkv_ref[:, k_cols], ds_ref[half]) * 0.125)
        both = jnp.where(row_low, parts[0], parts[1]).astype(BF)
        dqkv_ref[:, q_cols] = both.T
        for jt in range(tiles):
            rows = slice(jt * 128, jt * 128 + 128)
            dk = jnp.where(lane_low_tile, nn(ds_ref[0, rows, :], q2), nn(ds_ref[1, rows, :], q2))
            dqkv_ref[rows, k_cols] = dk.astype(BF)
            dv = jnp.where(lane_low_tile, nn(prob_ref[0, rows, :], do2), nn(prob_ref[1, rows, :], do2))
            dqkv_ref[rows, v_cols] = dv.astype(BF)
        return 0

    lax.fori_loop(0, width // 128, pair, 0)

    def weights_back(c, _):
        cols = pl.ds(pl.multiple_of(c * 256, 256), 256)
        dw_ref[cols, :] = tn(dqkv_ref[:, cols], normed_ref[...]).astype(BF)
        return 0

    lax.fori_loop(0, 3 * width // 256, weights_back, 0)

    def rows_back(c, _):
        cols = pl.ds(pl.multiple_of(c * 256, 256), 256)
        dx_ref[:, cols] = nn(dqkv_ref[...], flat_ref[:, cols])
        return 0

    lax.fori_loop(0, width // 256, rows_back, 0)
    qkv_rows = w_ref.shape[1]
    unflatten(dw_ref, grad_refs[0], 0)
    unflatten(flat_out_ref, grad_refs[-1], qkv_rows if len(grad_refs) == 1 else 0)
    if tail:
        start = qkv_rows + wo_ref.shape[1]
        for i in range(tail_ref.shape[0]):
            grad_refs[0][i, start:, :] = tail_ref[i]
    norm_back(x_ref, gain_ref, dx_ref, grad_ref, dx_ref, dgain_ref)


def norm_back(x_ref, gain_ref, upper_ref, base_ref, dx_ref, dgain_ref):
    field = x_ref[...]
    inverse = inverse_rms(field)
    unit = field * inverse
    upper = upper_ref[...]
    scaled = upper * gain_ref[...]
    dgain_ref[...] = jnp.sum(upper * unit, axis=0, keepdims=True)
    dx_ref[...] = base_ref[...] + inverse * (scaled - unit * jnp.mean(scaled * unit, axis=1, keepdims=True))


def attend_back(piece, x, gain, weights, vectors, normed, qkv, mixed, lse, grad, tail=None):
    length, width = x.shape
    heads, span = vectors.shape
    w_args, w_specs = weight_specs(weights)
    packed = weights[0]
    grad_shapes = packed if isinstance(packed, tuple) else (packed,)
    tails = () if tail is None else (tail,)
    return pl.pallas_call(
        lambda *refs: attend_back_kernel(bool(tails), weights, *refs),
        out_shape=(jax.ShapeDtypeStruct((length, width), F32),)
        + tuple(jax.ShapeDtypeStruct(g.shape, BF) for g in grad_shapes)
        + (
            jax.ShapeDtypeStruct((heads, span), F32),
            jax.ShapeDtypeStruct((1, width), F32),
        ),
        in_specs=[SMEM_SPEC] + [VMEM_SPEC] * 2 + w_specs + [VMEM_SPEC] * (6 + len(tails)),
        out_specs=[VMEM_SPEC] * (3 + len(grad_shapes)),
        scratch_shapes=[
            pltpu.VMEM((length, length), F32),
            pltpu.VMEM((128, span), F32),
            pltpu.VMEM((128, span), F32),
            pltpu.VMEM((2, length, length), BF),
            pltpu.VMEM((2, length, length), BF),
            pltpu.VMEM((length, width), BF),
            pltpu.VMEM((length, width), BF),
            pltpu.VMEM((length, 3 * width), BF),
            pltpu.VMEM((16, length), F32),
            pltpu.VMEM((3 * width, width), BF),
            pltpu.VMEM((width, width), BF),
            pltpu.VMEM((3 * width, width), BF),
        ],
        compiler_params=pltpu.CompilerParams(vmem_limit_bytes=VMEM_BYTES),
        cost_estimate=pl.CostEstimate(
            flops=16 * length * width * width + 10 * length * length * width,
            bytes_accessed=40 * length * width + 16 * width * width,
            transcendentals=heads * length * length,
        ),
        name="attend_back",
    )(piece, x, gain, *w_args, vectors, normed, qkv, mixed, lse, grad, *tails)


def mlp_chunk(c, parts, zones, up_ref, down_ref):
    hidden, width = up_ref.shape
    piece = hidden // (parts * zones)
    rows = [
        up_ref[pl.ds(pl.multiple_of(z * parts * piece + c * piece, 16), piece), :] for z in range(zones)
    ]
    span = down_ref.shape[1] // parts
    down = down_ref[:, pl.ds(pl.multiple_of(c * span, 16), span), :].reshape(-1, down_ref.shape[2])
    return jnp.concatenate(rows, axis=0), down


def mlp_kernel(parts, zones, x_ref, gain_ref, up_ref, down_ref, out_ref, normed_ref):
    field = x_ref[...]
    normed_ref[...] = (field * inverse_rms(field) * gain_ref[...]).astype(BF)
    out_ref[...] = field

    def chunk(c, _):
        up, down = mlp_chunk(c, parts, zones, up_ref, down_ref)
        hidden = gelu_of(nt(normed_ref[...], up)).astype(BF)
        out_ref[...] += nt(hidden, down)
        return 0

    lax.fori_loop(0, parts, chunk, 0)


def mlp(x, gain, up, down, parts, zones):
    length, width = x.shape
    hidden = up.shape[0]
    return pl.pallas_call(
        lambda *refs: mlp_kernel(parts, zones, *refs),
        out_shape=(jax.ShapeDtypeStruct((length, width), F32), jax.ShapeDtypeStruct((length, width), BF)),
        in_specs=[VMEM_SPEC] * 4,
        out_specs=[VMEM_SPEC] * 2,
        compiler_params=pltpu.CompilerParams(vmem_limit_bytes=VMEM_BYTES),
        cost_estimate=pl.CostEstimate(
            flops=4 * length * width * hidden, bytes_accessed=10 * length * width + 4 * width * hidden,
            transcendentals=length * hidden,
        ),
        name="mlp",
    )(x, gain, up, down)


def mlp_back_kernel(parts, zones, x_ref, gain_ref, up_ref, down_ref, normed_ref, grad_ref,
                    dx_ref, dup_ref, ddown_ref, dgain_ref, low_ref, acc_ref):
    low_ref[...] = grad_ref[...].astype(BF)
    acc_ref[...] = jnp.zeros_like(acc_ref)

    piece = up_ref.shape[0] // (parts * zones)
    span = down_ref.shape[1] // parts

    def chunk(c, _):
        up, down = mlp_chunk(c, parts, zones, up_ref, down_ref)
        hidden, slope = gelu_parts(nt(normed_ref[...], up))
        pre_grad = (nn(low_ref[...], down) * slope).astype(BF)
        ddown = tn(low_ref[...], hidden.astype(BF)).astype(BF)
        ddown_ref[:, pl.ds(pl.multiple_of(c * span, 16), span), :] = ddown.reshape(-1, span, ddown.shape[1])
        dup = tn(pre_grad, normed_ref[...]).astype(BF)
        for z in range(zones):
            at = pl.ds(pl.multiple_of(z * parts * piece + c * piece, 16), piece)
            dup_ref[at, :] = dup[z * piece:z * piece + piece, :]
        acc_ref[...] += nn(pre_grad, up)
        return 0

    lax.fori_loop(0, parts, chunk, 0)
    norm_back(x_ref, gain_ref, acc_ref, grad_ref, dx_ref, dgain_ref)


def mlp_back(x, gain, up, down, normed, grad, parts, zones):
    length, width = x.shape
    hidden = up.shape[0]
    return pl.pallas_call(
        lambda *refs: mlp_back_kernel(parts, zones, *refs),
        out_shape=(
            jax.ShapeDtypeStruct((length, width), F32),
            jax.ShapeDtypeStruct((hidden, width), BF),
            jax.ShapeDtypeStruct(down.shape, BF),
            jax.ShapeDtypeStruct((1, width), F32),
        ),
        in_specs=[VMEM_SPEC] * 6,
        out_specs=[VMEM_SPEC] * 4,
        scratch_shapes=[pltpu.VMEM((length, width), BF), pltpu.VMEM((length, width), F32)],
        compiler_params=pltpu.CompilerParams(vmem_limit_bytes=VMEM_BYTES),
        cost_estimate=pl.CostEstimate(
            flops=10 * length * width * hidden, bytes_accessed=16 * length * width + 8 * width * hidden,
            transcendentals=length * hidden,
        ),
        name="mlp_back",
    )(x, gain, up, down, normed, grad)


def experts_kernel(
    x_ref, c_ref, gate_ref, up_ref, down_ref,
    y_ref, dx_ref, dgate_ref, own_up_ref, own_down_ref, peer_up_ref, peer_down_ref,
    y_sum, dx_sum, dgate_sum, up_sum, down_sum,
):
    part = pl.program_id(1)
    sources, _, span, width = x_ref.shape
    group = max(1, 384 // span)
    rows = group * span
    up_sum[...] = jnp.zeros_like(up_sum)
    down_sum[...] = jnp.zeros_like(down_sum)

    @pl.when(part == 0)
    def _():
        y_sum[...] = jnp.zeros_like(y_sum)
        dx_sum[...] = jnp.zeros_like(dx_sum)
        dgate_sum[...] = jnp.zeros_like(dgate_sum)

    def tile(i, _):
        at = pl.ds(i * group, group)
        x = x_ref[at, 0].reshape(rows, width)
        c = c_ref[at, 0].reshape(rows, width)
        gate = gate_ref[at, 0].reshape(rows, 1)
        hidden, slope = gelu_parts(nn(x, up_ref[...]))
        hidden = hidden.astype(BF)
        back = nt(c, down_ref[...])
        pre_grad = (gate * back * slope).astype(BF)
        dgate_sum[at] += jnp.sum(hidden.astype(F32) * back, axis=1, keepdims=True).reshape(group, span, 1)
        y_sum[at] += nn(hidden, down_ref[...]).reshape(group, span, width)
        dx_sum[at] += nt(pre_grad, up_ref[...]).reshape(group, span, width)
        up_sum[...] += tn(x, pre_grad)
        down_sum[...] += tn(hidden, (gate * c.astype(F32)).astype(BF))
        return 0

    lax.fori_loop(0, sources // group, tile, 0)

    @pl.when(part == 0)
    def _():
        own_up_ref[...] = up_sum[...]
        own_down_ref[...] = down_sum[...]

    @pl.when(part == 1)
    def _():
        peer_up_ref[...] = up_sum[...].astype(BF)
        peer_down_ref[...] = down_sum[...].astype(BF)
        y_ref[:, 0] = (gate_ref[:, 0] * y_sum[...]).astype(BF)
        dx_ref[:, 0] = dx_sum[...].astype(BF)
        dgate_ref[:, 0] = dgate_sum[...]


def run_experts(x, c, gate, up, down):
    sources, local, span, width = x.shape
    hidden = up.shape[3]
    lean = sources * span > 2048
    once = dict(pipeline_mode=pl.Buffered(1)) if lean else {}
    row_spec = pl.BlockSpec((sources, 1, span, width), lambda e, j: (0, e, 0, 0), **once)
    row_out_spec = pl.BlockSpec((sources, 1, span, width), lambda e, j: (0, e, 0, 0), pipeline_mode=pl.Buffered(1))
    gate_spec = pl.BlockSpec((sources, 1, span, 1), lambda e, j: (0, e, 0, 0), **once)
    sq = pl.Squeezed()
    up_spec = pl.BlockSpec((sq, sq, width, hidden), lambda e, j: (j, e, 0, 0))
    down_spec = pl.BlockSpec((sq, sq, hidden, width), lambda e, j: (j, e, 0, 0))
    gup_spec = pl.BlockSpec((sq, width, hidden), lambda e, j: (e, 0, 0))
    gdown_spec = pl.BlockSpec((sq, hidden, width), lambda e, j: (e, 0, 0))
    rows = local * sources * span
    return pl.pallas_call(
        experts_kernel,
        grid=(local, 2),
        out_shape=(
            jax.ShapeDtypeStruct(x.shape, BF),
            jax.ShapeDtypeStruct(x.shape, BF),
            jax.ShapeDtypeStruct(gate.shape, F32),
            jax.ShapeDtypeStruct((local, width, hidden), F32),
            jax.ShapeDtypeStruct((local, hidden, width), F32),
            jax.ShapeDtypeStruct((local, width, hidden), BF),
            jax.ShapeDtypeStruct((local, hidden, width), BF),
        ),
        in_specs=[row_spec, row_spec, gate_spec, up_spec, down_spec],
        out_specs=[row_out_spec, row_out_spec, gate_spec, gup_spec, gdown_spec, gup_spec, gdown_spec],
        scratch_shapes=[
            pltpu.VMEM((sources, span, width), F32),
            pltpu.VMEM((sources, span, width), F32),
            pltpu.VMEM((sources, span, 1), F32),
            pltpu.VMEM((width, hidden), F32),
            pltpu.VMEM((hidden, width), F32),
        ],
        compiler_params=pltpu.CompilerParams(vmem_limit_bytes=VMEM_BYTES),
        cost_estimate=pl.CostEstimate(
            flops=24 * rows * width * hidden, bytes_accessed=16 * rows * width, transcendentals=2 * rows * hidden,
        ),
        name="experts",
    )(x, c, gate, up, down)


def spread_kernel(slot_ref, rows_ref, out_ref):
    experts, zones, capacity, width = out_ref.shape
    length = rows_ref.shape[1]
    take = max(1, 384 // capacity)

    def chunk(i, _):
        for zone in range(zones):
            place = lax.broadcasted_iota(jnp.int32, (take * capacity, length), 0) + i * (take * capacity)
            hit = (place == slot_ref[zone, 0:1, :]) | (place == slot_ref[zone, 1:2, :])
            picked = nn(jnp.where(hit, 1.0, 0.0).astype(BF), rows_ref[zone])
            out_ref[pl.ds(i * take, take), zone] = picked.reshape(take, capacity, width).astype(BF)
        return 0

    lax.fori_loop(0, experts // take, chunk, 0)


def spread(slot_rows, rows, experts, capacity):
    zones, length, width = rows.shape
    return pl.pallas_call(
        spread_kernel,
        out_shape=jax.ShapeDtypeStruct((experts, zones, capacity, width), BF),
        in_specs=[VMEM_SPEC] * 2,
        out_specs=VMEM_SPEC,
        compiler_params=pltpu.CompilerParams(vmem_limit_bytes=VMEM_BYTES),
        cost_estimate=pl.CostEstimate(
            flops=2 * zones * experts * capacity * length * width,
            bytes_accessed=2 * zones * (experts * capacity + length) * width, transcendentals=0,
        ),
        name="spread",
    )(slot_rows, rows)


def collect_kernel(slot_ref, rows_ref, out_ref):
    experts, zones, capacity, width = rows_ref.shape
    length = out_ref.shape[1]
    take = max(1, 384 // capacity)
    out_ref[...] = jnp.zeros_like(out_ref)

    def chunk(i, _):
        for zone in range(zones):
            place = lax.broadcasted_iota(jnp.int32, (length, take * capacity), 1) + i * (take * capacity)
            hit = (place == slot_ref[:, 2 * zone:2 * zone + 1]) | (place == slot_ref[:, 2 * zone + 1:2 * zone + 2])
            rows = rows_ref[pl.ds(i * take, take), zone].reshape(take * capacity, width)
            out_ref[zone] += nn(jnp.where(hit, 1.0, 0.0).astype(BF), rows)
        return 0

    lax.fori_loop(0, experts // take, chunk, 0)


def collect(slot_columns, rows):
    experts, zones, capacity, width = rows.shape
    length = slot_columns.shape[0]
    return pl.pallas_call(
        collect_kernel,
        out_shape=jax.ShapeDtypeStruct((zones, length, width), F32),
        in_specs=[VMEM_SPEC] * 2,
        out_specs=VMEM_SPEC,
        compiler_params=pltpu.CompilerParams(vmem_limit_bytes=VMEM_BYTES),
        cost_estimate=pl.CostEstimate(
            flops=2 * zones * experts * capacity * length * width,
            bytes_accessed=2 * zones * (experts * capacity + 2 * length) * width, transcendentals=0,
        ),
        name="collect",
    )(slot_columns, rows)


MESH = pl.DeviceIdType.MESH


def flip(index, mask):
    bit = 1
    while bit <= mask:
        if mask & bit:
            index = index + bit - 2 * bit * ((index // bit) % 2)
        bit *= 2
    return index


def masks_of(bits):
    found = [0]
    for bit in bits:
        found = found + [m | bit for m in found]
    return found


def bits_below(size):
    found, bit = [], 1
    while bit < size:
        found.append(bit)
        bit *= 2
    return found


def halves_of(rows):
    cut = rows // 2 // 16 * 16
    return ((0, cut), (cut, rows - cut))


def routes_of(chips):
    bits = bits_below(chips)
    cut = len(bits) // 2
    return (bits, bits[cut:] + bits[:cut])


def greet(owner, zone, owners, zones):
    barrier = pltpu.get_barrier_semaphore()
    peers = [(flip(owner, bit), zone) for bit in bits_below(owners)]
    peers += [(owner, flip(zone, d)) for d in range(1, zones)]
    for peer in peers:
        pl.semaphore_signal(barrier, inc=1, device_id=peer, device_id_type=MESH)
    pl.semaphore_wait(barrier, len(peers))


def sender(send_sem, recv_sem):
    used = [0]

    def send(source, target, device):
        at = used[0]
        used[0] += 1
        copy = pltpu.make_async_remote_copy(
            source, target, send_sem.at[at], recv_sem.at[at], device_id=device, device_id_type=MESH
        )
        copy.start()
        return copy

    return send


def gather_copies(owners, zones):
    chips = owners // 2
    return zones - 1 + 2 * (chips - 1) + 2 * chips


def gather_kernel(owners, zones, used_rows, *refs):
    count = len(used_rows)
    blocks, outs = refs[:count], refs[count:2 * count]
    slabs, turned = refs[2 * count:3 * count], refs[3 * count:4 * count]
    send_sem, recv_sem, local_sem = refs[4 * count:]
    owner, zone = lax.axis_index("expert"), lax.axis_index("shard")
    greet(owner, zone, owners, zones)
    send = sender(send_sem, recv_sem)
    chips = owners // 2
    pending, finals = [], []

    def across(g):
        slabs[g][zone] = blocks[g][...]
        return [send(blocks[g], slabs[g].at[zone], (owner, flip(zone, d))) for d in range(1, zones)]

    def place(g, index, half):
        start, size = halves_of(used_rows[g])[half]
        return outs[g].at[index, pl.ds(start, size), :]

    def onward(g, half, index):
        finals.append(send(place(g, index, half), place(g, index, half), (flip(owner, 1), zone)))

    def start_rows(g, copies):
        for copy in copies:
            copy.wait_recv()
        pending.extend(copies)
        slab = slabs[g]
        turned[g][...] = slab[...].reshape(slab.shape[0] * slab.shape[1], slab.shape[2]).T
        local = pltpu.make_async_copy(
            turned[g].at[pl.ds(0, used_rows[g]), :], outs[g].at[owner], local_sem.at[g]
        )
        local.start()
        firsts = []
        for half, order in enumerate(routes_of(chips)):
            start, size = halves_of(used_rows[g])[half]
            source = turned[g].at[pl.ds(start, size), :]
            firsts.append([send(source, place(g, owner, half), (flip(owner, 2 * order[0]), zone))])
            finals.append(send(source, place(g, owner, half), (flip(owner, 1), zone)))
        return firsts, local

    def finish_rows(g, state, step):
        firsts, local = state
        if step == 0:
            local.wait()
        for half, order in enumerate(routes_of(chips)):
            for copy in firsts[half]:
                copy.wait_recv()
            pending.extend(firsts[half])
            done = masks_of(order[:step])
            arrived = [m | order[step] for m in done]
            if step + 1 < len(order):
                device = (flip(owner, 2 * order[step + 1]), zone)
                firsts[half] = [
                    send(place(g, flip(owner, 2 * m), half), place(g, flip(owner, 2 * m), half), device)
                    for m in done + arrived
                ]
            for m in arrived:
                onward(g, half, flip(owner, 2 * m))
        return firsts, local

    steps = len(routes_of(chips)[0])
    moving = {0: across(0)}
    states = {}
    for g in range(count):
        states[g] = start_rows(g, moving[g])
        if g + 1 < count:
            moving[g + 1] = across(g + 1)
        if g > 0:
            for step in range(1, steps):
                states[g - 1] = finish_rows(g - 1, states[g - 1], step)
        states[g] = finish_rows(g, states[g], 0)
    for step in range(1, steps):
        states[count - 1] = finish_rows(count - 1, states[count - 1], step)
    for copy in finals:
        copy.wait_recv()
    for copy in pending + finals:
        copy.wait_send()


def gather_weights(blocks, used_rows, owners, zones):
    count = len(blocks)
    depth = zones * blocks[0].shape[0]
    copies = count * gather_copies(owners, zones)
    return pl.pallas_call(
        lambda *refs: gather_kernel(owners, zones, used_rows, *refs),
        out_shape=tuple(jax.ShapeDtypeStruct((owners, used, depth), BF) for used in used_rows),
        in_specs=[VMEM_SPEC] * count,
        out_specs=tuple([pl.BlockSpec(memory_space=pl.ANY)] * count),
        scratch_shapes=[pltpu.VMEM((zones,) + b.shape, BF) for b in blocks]
        + [pltpu.VMEM((b.shape[1], depth), BF) for b in blocks]
        + [pltpu.SemaphoreType.DMA((copies,)), pltpu.SemaphoreType.DMA((copies,)), pltpu.SemaphoreType.DMA((count,))],
        compiler_params=pltpu.CompilerParams(
            vmem_limit_bytes=24 * 1024 * 1024, collective_id=1, has_side_effects=True
        ),
        name="gather_weights",
    )(*blocks)


def reduce_copies(owners, zones):
    return 1 + 2 * (owners // 2 - 1) + zones - 1


def add_rows(into, other):
    return (into.astype(F32) + other.astype(F32)).astype(BF)


def reduce_kernel(owners, zones, used_rows, *refs):
    count = len(used_rows)
    parts, small = refs[:count], refs[count]
    outs, small_out = refs[count + 1:2 * count + 1], refs[2 * count + 1]
    scratch = refs[2 * count + 2:]
    keep, near, far = scratch[:count], scratch[count:2 * count], scratch[2 * count:3 * count]
    slabs, incoming = scratch[3 * count:4 * count], scratch[4 * count:5 * count]
    small_mine, small_other, send_sem, recv_sem, local_sem = scratch[5 * count:]
    owner, zone = lax.axis_index("expert"), lax.axis_index("shard")
    chip, core = owner // 2, owner % 2
    greet(owner, zone, owners, zones)
    send = sender(send_sem, recv_sem)
    chips = owners // 2
    orders = routes_of(chips)
    steps = len(orders[0])
    sent = []
    small_peers = [(flip(owner, bit), zone) for bit in bits_below(owners)]
    small_peers += [(owner, flip(zone, bit)) for bit in bits_below(zones)]
    small_mine[0] = small[...]

    def small_start(i):
        return send(small_mine.at[i], small_other.at[i], small_peers[i])

    def small_finish(i, copy):
        copy.wait_recv()
        sent.append(copy)
        small_mine[i + 1] = small_mine[i] + small_other[i]

    def begin(g):
        local = pltpu.make_async_copy(parts[g].at[:, core], keep[g], local_sem.at[g])
        local.start()
        return send(parts[g].at[:, 1 - core], near[g], (flip(owner, 1), zone)), local

    def window(g, half):
        start, size = halves_of(used_rows[g])[half]
        return pl.ds(start, size)

    def push(g, step):
        copies = []
        for half, order in enumerate(orders):
            bit, rest = order[step], masks_of(order[step + 1:])
            device = (flip(owner, 2 * bit), zone)
            for i, m in enumerate(rest):
                slot = chips - 2 * len(rest) + i
                copies.append(send(
                    keep[g].at[flip(chip, bit | m), window(g, half), :], far[g].at[slot, window(g, half), :], device
                ))
        return copies

    def absorb(g, step, copies):
        for copy in copies:
            copy.wait_recv()
        sent.extend(copies)
        for half, order in enumerate(orders):
            rest = masks_of(order[step + 1:])
            for i, m in enumerate(rest):
                slot = chips - 2 * len(rest) + i
                index = flip(chip, m)
                keep[g][index, window(g, half), :] = add_rows(
                    keep[g][index, window(g, half), :], far[g][slot, window(g, half), :]
                )

    def stage_near(g, state):
        copy, local = state
        local.wait()
        copy.wait_recv()
        sent.append(copy)

        def one(h, _):
            keep[g][h] = add_rows(keep[g][h], near[g][h])
            return 0

        lax.fori_loop(0, chips, one, 0)
        return push(g, 0)

    def stage_zone(g):
        slab = slabs[g]
        spare = slab.shape[2] - used_rows[g]
        own = keep[g][chip]
        if spare:
            own = jnp.concatenate([own, jnp.zeros((spare, own.shape[1]), BF)], axis=0)
        slab[...] = own.T.reshape(slab.shape)
        return [
            send(slab.at[flip(zone, d)], incoming[g].at[d - 1], (owner, flip(zone, d))) for d in range(1, zones)
        ]

    def stage_end(g, copies):
        total = slabs[g][zone].astype(F32)
        for d in range(1, zones):
            copies[d - 1].wait_recv()
            total = total + incoming[g][d - 1].astype(F32)
        sent.extend(copies)
        outs[g][...] = total

    begun = [begin(g) for g in range(count)]
    small_copy = small_start(0)
    state = {}
    stages = steps + 2
    turn = 0
    for t in range(count + stages - 1):
        for g in reversed(range(count)):
            at = t - g
            if at == 0:
                state[g] = stage_near(g, begun[g])
            elif 1 <= at <= steps:
                absorb(g, at - 1, state[g])
                state[g] = push(g, at) if at < steps else stage_zone(g)
            elif at == steps + 1:
                stage_end(g, state[g])
        if turn < len(small_peers):
            small_finish(turn, small_copy)
            turn += 1
            if turn < len(small_peers):
                small_copy = small_start(turn)
    while turn < len(small_peers):
        small_finish(turn, small_copy)
        turn += 1
        if turn < len(small_peers):
            small_copy = small_start(turn)
    small_out[...] = small_mine[len(small_peers)]
    for copy in sent:
        copy.wait_send()


def reduce_grads(parts, small, owners, zones):
    count = len(parts)
    used_rows = tuple(p.shape[1] for p in parts)
    depth = parts[0].shape[2]
    chips = owners // 2
    parts = [p.reshape(chips, 2, p.shape[1], depth) for p in parts]
    wide = [-(-used // 128) * 128 for used in used_rows]
    rounds = len(bits_below(owners)) + len(bits_below(zones))
    copies = count * reduce_copies(owners, zones) + rounds
    return pl.pallas_call(
        lambda *refs: reduce_kernel(owners, zones, used_rows, *refs),
        out_shape=tuple(jax.ShapeDtypeStruct((depth // zones, w), F32) for w in wide)
        + (jax.ShapeDtypeStruct(small.shape, F32),),
        in_specs=[pl.BlockSpec(memory_space=pl.ANY)] * count + [VMEM_SPEC],
        out_specs=tuple([VMEM_SPEC] * (count + 1)),
        scratch_shapes=[pltpu.VMEM((chips, used, depth), BF) for used in used_rows]
        + [pltpu.VMEM((chips, used, depth), BF) for used in used_rows]
        + [pltpu.VMEM((chips - 1, used, depth), BF) for used in used_rows]
        + [pltpu.VMEM((zones, depth // zones, w), BF) for w in wide]
        + [pltpu.VMEM((zones - 1, depth // zones, w), BF) for w in wide]
        + [pltpu.VMEM((rounds + 1,) + small.shape, F32), pltpu.VMEM((rounds,) + small.shape, F32)]
        + [pltpu.SemaphoreType.DMA((copies,)), pltpu.SemaphoreType.DMA((copies,)), pltpu.SemaphoreType.DMA((count,))],
        compiler_params=pltpu.CompilerParams(
            vmem_limit_bytes=VMEM_BYTES, collective_id=2, has_side_effects=True
        ),
        name="reduce_grads",
    )(*parts, small)


bucket_edges = (1, 2, 3, 4, 6, 8, 12, 16, 24, 32, 48, 64, 96, 128, 192, 256, 384, 512, 768, 1024, 1536)


def bucket_onehot(length, buckets):
    distance = (length - 1) - jnp.arange(2 * length, dtype=jnp.int32)
    edge_list = jnp.array(bucket_edges, dtype=jnp.int32)
    magnitude = jnp.sum(
        (jnp.abs(distance)[:, None] >= edge_list[None, :]).astype(jnp.int32), axis=1, dtype=jnp.int32
    )
    bucket = magnitude + buckets // 2 * (distance > 0).astype(jnp.int32)
    real = jnp.arange(2 * length)[:, None] < 2 * length - 1
    hit = (bucket[:, None] == jnp.arange(buckets, dtype=jnp.int32)[None, :]) & real
    return hit.astype(F32)


def expert_slots(routes, experts_all, capacity):
    pairs = routes.reshape(-1)
    onehot = pairs[:, None] == jnp.arange(experts_all, dtype=jnp.int32)[None, :]
    count = pairs.shape[0]
    before = jnp.arange(count)[:, None] > jnp.arange(count)[None, :]
    ranks = jnp.dot(before.astype(BF), onehot.astype(BF), preferred_element_type=F32)
    own = jnp.sum(jnp.where(onehot, ranks, 0.0), axis=1).astype(jnp.int32)
    return (pairs * capacity + own).reshape(routes.shape)


def shift_from(value, distance):
    size = lax.axis_size("shard")
    return lax.ppermute(value, "shard", [((z + distance) % size, z) for z in range(size)])


def shift_to(value, distance):
    size = lax.axis_size("shard")
    return lax.ppermute(value, "shard", [(z, (z + distance) % size) for z in range(size)])


def swap_pair(value):
    return lax.ppermute(value, "shard", [(z, z ^ 1) for z in range(lax.axis_size("shard"))])


def exchange(value):
    return lax.all_to_all(value, "expert", split_axis=0, concat_axis=0, tiled=True)


def per_device(
    tokens, piece_start, routes, norm_gains, bias_tables, qkv_weight, out_weight, mlp_up, mlp_down, router,
    expert_up, expert_down, cotangent,
):
    length, width = tokens.shape
    owners = lax.axis_size("expert")
    zones = lax.axis_size("shard") // 2
    local = expert_up.shape[0]
    experts_all = local * owners
    capacity = 3 * routes.shape[1] * length // (2 * experts_all)
    qkv_cols, out_cols = qkv_weight.shape[2], out_weight.shape[2]
    zones_all = 2 * zones
    router_pad = 16
    parts = mlp_down.shape[0] // qkv_weight.shape[1]
    aligned = qkv_cols % 16 == 0 and out_cols % 16 == 0 and qkv_cols % out_cols == 0

    def padded(block):
        return jnp.pad(block, ((0, 0), (0, -block.shape[1] % 128)))

    down_block = mlp_down.reshape(parts, -1, mlp_down.shape[1]).transpose(1, 0, 2).reshape(qkv_weight.shape[1], -1)
    router_block = jnp.pad(router, ((0, 0), (0, router_pad - router.shape[1])))
    first, up_full, down_full, last = gather_weights(
        [
            padded(jnp.concatenate([qkv_weight[0], out_weight[0]], axis=1)),
            padded(mlp_up),
            padded(down_block),
            padded(jnp.concatenate([qkv_weight[1], out_weight[1], router_block], axis=1)),
        ],
        (qkv_cols + out_cols, mlp_up.shape[1], parts * mlp_down.shape[1], qkv_cols + out_cols + router_pad),
        owners, zones_all,
    )

    def layer_weights(block):
        if aligned:
            return (block, qkv_cols, out_cols)
        flat = (block[:, :qkv_cols].reshape(1, -1, width), block[:, qkv_cols:qkv_cols + out_cols].reshape(1, -1, width))
        return (flat, 3 * width, width)

    up_full = up_full.reshape(-1, width)
    if mlp_down.shape[1] % 16:
        down_full = down_full.reshape(owners, parts, -1, width).transpose(1, 0, 2, 3).reshape(1, -1, width)
    router_full = last[:, qkv_cols + out_cols:qkv_cols + out_cols + router.shape[1]].reshape(experts_all, width)

    first, cotangent_late, down_late = lax.optimization_barrier((first, cotangent, expert_down))
    weights0, weights1 = layer_weights(first), layer_weights(last)
    up_other, down_other = swap_pair(expert_up), swap_pair(down_late)

    slots = expert_slots(routes, experts_all, capacity)
    zone_slots = [slots] + [shift_from(slots, 2 * d) for d in range(1, zones)]
    slot_columns = jnp.concatenate(zone_slots, axis=1)
    slot_rows = slot_columns.T.reshape(zones, routes.shape[1], length)

    def dispatch(rows):
        own = [rows] + [shift_from(rows, 2 * d) for d in range(1, zones)]
        packed = spread(slot_rows, jnp.stack(own), experts_all, capacity)
        return exchange(packed.reshape(owners, local, zones * capacity, width))

    def undo(rows):
        back = exchange(rows).reshape(experts_all, zones, capacity, width)
        return collect(slot_columns, back)

    cotangent_rows = dispatch(cotangent_late)

    onehot = bucket_onehot(length, bias_tables.shape[2])
    vectors = lax.dot_general(
        bias_tables, onehot, (((2,), (1,)), ((), ())), precision=lax.Precision.HIGHEST
    )
    gains = [norm_gains[i:i + 1] for i in range(4)]
    x0 = tokens.astype(F32)
    x1, ah0, qkv0, o0, lse0 = attend(piece_start, x0, gains[0], weights0, vectors[0])
    x1, up_other = lax.optimization_barrier((x1, up_other))
    x2, mh = mlp(x1, gains[1], up_full, down_full, parts, zones_all)
    x3, ah1, qkv1, o1, lse1 = attend(piece_start, x2, gains[2], weights1, vectors[1])

    x3, down_other, cotangent_rows = lax.optimization_barrier((x3, down_other, cotangent_rows))
    up_pair = jnp.stack([expert_up, up_other])
    down_pair = jnp.stack([expert_down, down_other])
    unit3 = x3 * inverse_rms(x3)
    eh = (unit3 * gains[3]).astype(BF)
    logits = nt(eh, router_full)
    expert_ids = jnp.arange(experts_all, dtype=jnp.int32)
    chosen = routes[:, :, None] == expert_ids[None, None, :]
    gates = jax.nn.softmax(jnp.sum(jnp.where(chosen, logits[:, None, :], 0.0), axis=2), axis=1)

    eh_rows = dispatch(eh)
    slot_ids = jnp.arange(experts_all * capacity, dtype=jnp.int32)

    def gate_slots(zone):
        zone_gates = gates if zone == 0 else shift_from(gates, 2 * zone)
        hit = zone_slots[zone][:, :, None] == slot_ids[None, None, :]
        return jnp.sum(jnp.where(hit, zone_gates[:, :, None], 0.0), axis=(0, 1)).reshape(experts_all, capacity)

    gate_rows = exchange(
        jnp.stack([gate_slots(d) for d in range(zones)], axis=1).reshape(owners, local, zones * capacity)
    )
    y_rows, dx_rows, dgate_rows, own_up, own_down, peer_up, peer_down = run_experts(
        eh_rows, cotangent_rows, gate_rows[..., None], up_pair, down_pair
    )
    peer_up, peer_down = swap_pair(peer_up), swap_pair(peer_down)

    dx_back = undo(dx_rows)
    dgate_back = exchange(dgate_rows[..., 0]).reshape(experts_all, zones, capacity)
    token_grad = dx_back[0]
    gate_grad = 0.0
    for d in range(zones):
        hit = zone_slots[d][:, :, None] == slot_ids[None, None, :]
        part = jnp.sum(jnp.where(hit, dgate_back[:, d].reshape(-1)[None, None, :], 0.0), axis=2)
        gate_grad = gate_grad + (part if d == 0 else shift_to(part, 2 * d))
    for d in range(1, zones):
        token_grad = token_grad + shift_to(dx_back[d].astype(BF), 2 * d).astype(F32)
    c = cotangent.astype(F32)
    dchoice = gates * (gate_grad - jnp.sum(gates * gate_grad, axis=1, keepdims=True))
    dlogits = jnp.sum(jnp.where(chosen, dchoice[:, :, None], 0.0), axis=1).astype(BF)
    grad_router = tn(dlogits, eh)
    deh = token_grad + nn(dlogits, router_full)
    scaled = deh * gains[3]
    dx3 = c + inverse_rms(x3) * (scaled - unit3 * jnp.mean(scaled * unit3, axis=1, keepdims=True))
    dgain3 = jnp.sum(deh * unit3, axis=0)[None]

    router_rows = jnp.pad(
        grad_router.astype(BF).reshape(owners, local, width), ((0, 0), (0, router_pad - local), (0, 0))
    )

    def layer_grads(results, tail=None):
        grads = results[1:-2]
        if not aligned:
            pieces = [g.reshape(owners, -1, width) for g in grads] + ([] if tail is None else [tail])
            grads = [jnp.concatenate(pieces, axis=1)]
        return results[0], grads[0], results[-2], results[-1]

    dx2, last_part, dvec1, dgain2 = layer_grads(
        attend_back(
            piece_start, x2, gains[2], weights1, vectors[1], ah1, qkv1, o1, lse1, dx3, router_rows if aligned else None
        ),
        router_rows,
    )
    dx2, y_rows = lax.optimization_barrier((dx2, y_rows))
    y_back = undo(y_rows)
    final = x3 + y_back[0]
    for d in range(1, zones):
        final = final + shift_to(y_back[d].astype(BF), 2 * d).astype(F32)
    output = final.astype(BF)
    dx1, up_part, down_part, dgain1 = mlp_back(x1, gains[1], up_full, down_full, mh, dx2, parts, zones_all)
    dx0, first_part, dvec0, dgain0 = layer_grads(
        attend_back(piece_start, x0, gains[0], weights0, vectors[0], ah0, qkv0, o0, lse0, dx1)
    )
    dx0, output, peer_up, peer_down = lax.optimization_barrier((dx0, output, peer_up, peer_down))
    grad_up = own_up + peer_up.astype(F32)
    grad_down = own_down + peer_down.astype(F32)
    if mlp_down.shape[1] % 16:
        down_part = down_part.reshape(parts, owners, -1, width).transpose(1, 0, 2, 3)
    dtables = lax.dot_general(
        jnp.stack([dvec0, dvec1]), onehot, (((2,), (0,)), ((), ())), precision=lax.Precision.HIGHEST
    )
    dgains = jnp.concatenate([dgain0, dgain1, dgain2, dgain3])
    small = jnp.concatenate([dgains.reshape(-1), dtables.reshape(-1)])
    small = jnp.pad(small, (0, -small.size % 1024)).reshape(-1, 128)
    last_grad, up_grad, down_grad, first_grad, small = reduce_grads(
        [
            last_part, up_part.reshape(owners, -1, width), down_part.reshape(owners, -1, width), first_part
        ],
        small, owners, zones_all,
    )
    small = small.reshape(-1)
    grad_qkv = jnp.stack([first_grad[:, :qkv_cols], last_grad[:, :qkv_cols]])
    grad_out = jnp.stack(
        [first_grad[:, qkv_cols:qkv_cols + out_cols], last_grad[:, qkv_cols:qkv_cols + out_cols]]
    )
    grad_router_out = last_grad[:, qkv_cols + out_cols:qkv_cols + out_cols + local]
    grad_mlp_up = up_grad[:, :mlp_up.shape[1]]
    down_cols = mlp_down.shape[1]
    grad_mlp_down = down_grad[:, :parts * down_cols].reshape(-1, parts, down_cols).transpose(1, 0, 2)
    grad_mlp_down = grad_mlp_down.reshape(mlp_down.shape)
    return (
        output,
        dx0,
        small[:dgains.size].reshape(dgains.shape),
        small[dgains.size:dgains.size + dtables.size].reshape(dtables.shape),
        grad_qkv,
        grad_out,
        grad_mlp_up,
        grad_mlp_down,
        grad_router_out,
        grad_up,
        grad_down,
    )


def solution(mesh):
    both = P(("expert", "shard"), None)
    split3, split2 = P(None, "shard", "expert"), P("shard", "expert")
    up_spec, down_spec = P("expert", None, "shard"), P("expert", "shard", None)
    in_specs = (
        both, P(("expert", "shard")), both, P(), P(), split3, split3, split2, split2, split2, up_spec, down_spec, both
    )
    out_specs = (both, both, P(), P(), split3, split3, split2, split2, split2, up_spec, down_spec)
    return jax.shard_map(per_device, mesh=mesh, in_specs=in_specs, out_specs=out_specs, check_vma=False)
```

```python
import jax
import jax.numpy as jnp
from jax import lax
from jax.experimental import pallas as pl
from jax.experimental.pallas import tpu as pltpu
from jax.sharding import PartitionSpec as P

PIECE = 256
norm_eps = 1e-06
far_below = -1e30
BF = jnp.bfloat16
F32 = jnp.float32
VMEM_BYTES = 56 * 1024 * 1024


def nn(a, b):
    return lax.dot_general(a, b, (((1,), (0,)), ((), ())), preferred_element_type=F32)


def nt(a, b):
    return lax.dot_general(a, b, (((1,), (1,)), ((), ())), preferred_element_type=F32)


def tn(a, b):
    return lax.dot_general(a, b, (((0,), (0,)), ((), ())), preferred_element_type=F32)


def inverse_rms(field):
    return lax.rsqrt(jnp.mean(field * field, axis=1, keepdims=True) + norm_eps)


def gelu_parts(u):
    cubic = 0.7978845608028654 * (u + 0.044715 * (u * u * u))
    bend = jnp.tanh(cubic)
    half = 0.5 * (1.0 + bend)
    slope = half + 0.5 * u * (1.0 - bend * bend) * (0.7978845608028654 * (1.0 + 0.134145 * (u * u)))
    return u * half, slope


def gelu_of(u):
    return 0.5 * u * (1.0 + jnp.tanh(0.7978845608028654 * (u + 0.044715 * (u * u * u))))


def fill_mask(piece_ref, mask_ref):
    length = mask_ref.shape[0]
    first = piece_ref[0]
    key_pos = lax.broadcasted_iota(jnp.int32, (length, length), 0)
    query_pos = lax.broadcasted_iota(jnp.int32, (length, length), 1)
    key_in = (key_pos >= first) & (key_pos < first + PIECE)
    query_in = (query_pos >= first) & (query_pos < first + PIECE)
    keep = (key_pos <= query_pos) | (key_in & query_in)
    mask_ref[...] = jnp.where(keep, 0.0, far_below)


def bias_strip(vector_row, strip_ref):
    wide = jnp.broadcast_to(vector_row, (128, vector_row.shape[1]))
    strip_ref[...] = pltpu.roll(wide, vector_row.shape[1] - 127, 1, stride=1, stride_axis=0)


def flatten(blocks_ref, flat_ref):
    rows = blocks_ref.shape[1]
    for i in range(blocks_ref.shape[0]):
        flat_ref[i * rows:i * rows + rows, :] = blocks_ref[i]


def unflatten(flat_ref, blocks_ref, start):
    count = blocks_ref.shape[0]
    rows = flat_ref.shape[0] // count
    for i in range(count):
        blocks_ref[i, start:start + rows, :] = flat_ref[i * rows:i * rows + rows, :]


def weight_specs(weights):
    packed, qkv_rows, out_rows = weights
    if isinstance(packed, tuple):
        return list(packed), [VMEM_SPEC, VMEM_SPEC]
    return [packed], [VMEM_SPEC]


def weight_views(weights, refs):
    packed, qkv_rows, out_rows = weights
    if isinstance(packed, tuple):
        return refs[0], refs[1], refs[2:]
    return refs[0].at[:, 0:qkv_rows, :], refs[0].at[:, qkv_rows:qkv_rows + out_rows, :], refs[1:]


def attend_kernel(
    weights, piece_ref, x_ref, gain_ref, *refs
):
    w_ref, wo_ref, refs = weight_views(weights, refs)
    (vec_ref, out_ref, normed_ref, qkv_ref, mixed_ref, lse_ref,
     mask_ref, strip_ref, score_ref, prob_ref, flat_ref, flat_out_ref) = refs
    length, width = x_ref.shape
    flatten(w_ref, flat_ref)
    flatten(wo_ref, flat_out_ref)
    tiles = length // 128
    fill_mask(piece_ref, mask_ref)
    field = x_ref[...]
    normed_ref[...] = (field * inverse_rms(field) * gain_ref[...]).astype(BF)

    def project(c, _):
        cols = pl.ds(pl.multiple_of(c * 256, 256), 256)
        qkv_ref[:, cols] = nt(normed_ref[...], flat_ref[cols, :]).astype(BF)
        return 0

    lax.fori_loop(0, 3 * width // 256, project, 0)
    lane_low = lax.broadcasted_iota(jnp.int32, (length, 128), 1) < 64
    row_low = lax.broadcasted_iota(jnp.int32, (128, length), 0) < 64

    def pair(hp, _):
        base = hp * 128
        q2 = qkv_ref[:, pl.ds(pl.multiple_of(base, 128), 128)] * jnp.asarray(0.125, BF)
        v2 = qkv_ref[:, pl.ds(pl.multiple_of(2 * width + base, 128), 128)]
        mixed = []
        for half in range(2):
            head = hp * 2 + half
            keep = lane_low if half == 0 else ~lane_low
            qm = jnp.where(keep, q2, jnp.zeros_like(q2))
            bias_strip(vec_ref[pl.ds(head, 1), :], strip_ref)
            peak = jnp.full((1, length), far_below, F32)
            for jt in range(tiles):
                rows = slice(jt * 128, jt * 128 + 128)
                k2 = qkv_ref[rows, pl.ds(pl.multiple_of(width + base, 128), 128)]
                at = 128 * (tiles - 1 - jt)
                s = nt(k2, qm) + strip_ref[:, at:at + length] + mask_ref[rows, :]
                score_ref[rows, :] = s
                peak = jnp.maximum(peak, jnp.max(s, axis=0, keepdims=True))
            total = jnp.zeros((1, length), F32)
            for jt in range(tiles):
                rows = slice(jt * 128, jt * 128 + 128)
                e = jnp.exp(score_ref[rows, :] - peak)
                total = total + jnp.sum(e, axis=0, keepdims=True)
                prob_ref[rows, :] = e.astype(BF)
            lse_ref[pl.ds(head, 1), :] = peak + jnp.log(total)
            mixed.append(tn(v2, prob_ref[...]) * (1.0 / total))
        both = jnp.where(row_low, mixed[0], mixed[1]).astype(BF)
        mixed_ref[:, pl.ds(pl.multiple_of(base, 128), 128)] = both.T
        return 0

    lax.fori_loop(0, width // 128, pair, 0)

    def back(c, _):
        cols = pl.ds(pl.multiple_of(c * 256, 256), 256)
        out_ref[:, cols] = x_ref[:, cols] + nt(mixed_ref[...], flat_out_ref[cols, :])
        return 0

    lax.fori_loop(0, width // 256, back, 0)


SMEM_SPEC = pl.BlockSpec(memory_space=pltpu.SMEM)
VMEM_SPEC = pl.BlockSpec(memory_space=pltpu.VMEM)


def attend(piece, x, gain, weights, vectors):
    length, width = x.shape
    w_args, w_specs = weight_specs(weights)
    heads = vectors.shape[0]
    span = vectors.shape[1]
    return pl.pallas_call(
        lambda *refs: attend_kernel(weights, *refs),
        out_shape=(
            jax.ShapeDtypeStruct((length, width), F32),
            jax.ShapeDtypeStruct((length, width), BF),
            jax.ShapeDtypeStruct((length, 3 * width), BF),
            jax.ShapeDtypeStruct((length, width), BF),
            jax.ShapeDtypeStruct((heads, length), F32),
        ),
        in_specs=[SMEM_SPEC] + [VMEM_SPEC] * 2 + w_specs + [VMEM_SPEC],
        out_specs=[VMEM_SPEC] * 5,
        scratch_shapes=[
            pltpu.VMEM((length, length), F32),
            pltpu.VMEM((128, span), F32),
            pltpu.VMEM((length, length), F32),
            pltpu.VMEM((length, length), BF),
            pltpu.VMEM((3 * width, width), BF),
            pltpu.VMEM((width, width), BF),
        ],
        compiler_params=pltpu.CompilerParams(vmem_limit_bytes=VMEM_BYTES),
        cost_estimate=pl.CostEstimate(
            flops=8 * length * width * width + 4 * length * length * width,
            bytes_accessed=20 * length * width + 8 * width * width,
            transcendentals=heads * length * length,
        ),
        name="attend",
    )(piece, x, gain, *w_args, vectors)


def attend_back_kernel(
    tail, weights, piece_ref, x_ref, gain_ref, *refs
):
    w_ref, wo_ref, refs = weight_views(weights, refs)
    (vec_ref, normed_ref, qkv_ref, mixed_ref, lse_ref, grad_ref), refs = refs[:6], refs[6:]
    tail_ref, refs = (refs[0], refs[1:]) if tail else (None, refs)
    grad_refs, refs = (refs[1:len(refs) - 14], refs[:1] + refs[len(refs) - 14:])
    (dx_ref, dvec_ref, dgain_ref,
     mask_ref, strip_ref, sums_ref, prob_ref, ds_ref, low_ref, do_ref, dqkv_ref, delta_ref,
     flat_ref, flat_out_ref, dw_ref) = refs
    flatten(w_ref, flat_ref)
    flatten(wo_ref, flat_out_ref)
    length, width = x_ref.shape
    heads = vec_ref.shape[0]
    tiles = length // 128
    fill_mask(piece_ref, mask_ref)
    low_ref[...] = grad_ref[...].astype(BF)

    def out_back(c, _):
        cols = pl.ds(pl.multiple_of(c * 256, 256), 256)
        do_ref[:, cols] = nn(low_ref[...], flat_out_ref[:, cols]).astype(BF)
        return 0

    lax.fori_loop(0, width // 256, out_back, 0)

    def out_weights_back(c, _):
        cols = pl.ds(pl.multiple_of(c * 256, 256), 256)
        flat_out_ref[cols, :] = tn(low_ref[:, cols], mixed_ref[...]).astype(BF)
        return 0

    lax.fori_loop(0, width // 256, out_weights_back, 0)
    pick = (
        lax.broadcasted_iota(jnp.int32, (delta_ref.shape[0], width), 1) // (width // heads)
        == lax.broadcasted_iota(jnp.int32, (delta_ref.shape[0], width), 0)
    ).astype(F32)
    delta_ref[...] = lax.dot_general(
        pick, do_ref[...].astype(F32) * mixed_ref[...].astype(F32), (((1,), (1,)), ((), ())),
        precision=lax.Precision.HIGHEST, preferred_element_type=F32,
    )
    lane_low = lax.broadcasted_iota(jnp.int32, (length, 128), 1) < 64
    lane_low_tile = lax.broadcasted_iota(jnp.int32, (128, 128), 1) < 64
    row_low = lax.broadcasted_iota(jnp.int32, (128, length), 0) < 64
    flip = (
        lax.broadcasted_iota(jnp.int32, (128, 128), 0) + lax.broadcasted_iota(jnp.int32, (128, 128), 1) == 127
    ).astype(F32)
    sums_ref[...] = jnp.zeros_like(sums_ref)

    def pair(hp, _):
        base = hp * 128
        q_cols = pl.ds(pl.multiple_of(base, 128), 128)
        k_cols = pl.ds(pl.multiple_of(width + base, 128), 128)
        v_cols = pl.ds(pl.multiple_of(2 * width + base, 128), 128)
        q2 = qkv_ref[:, q_cols] * jnp.asarray(0.125, BF)
        do2 = do_ref[:, q_cols]
        parts = []
        for half in range(2):
            head = hp * 2 + half
            keep = lane_low if half == 0 else ~lane_low
            qm = jnp.where(keep, q2, jnp.zeros_like(q2))
            dm = jnp.where(keep, do2, jnp.zeros_like(do2))
            bias_strip(vec_ref[pl.ds(head, 1), :], strip_ref)
            lse = lse_ref[pl.ds(head, 1), :]
            delta = delta_ref[pl.ds(head, 1), :]
            for jt in range(tiles):
                rows = slice(jt * 128, jt * 128 + 128)
                at = 128 * (tiles - 1 - jt)
                s = nt(qkv_ref[rows, k_cols], qm) + strip_ref[:, at:at + length] + mask_ref[rows, :]
                p = jnp.exp(s - lse)
                dp = nt(qkv_ref[rows, v_cols], dm)
                ds = (p * (dp - delta)).astype(BF)
                prob_ref[half, rows, :] = p.astype(BF)
                ds_ref[half, rows, :] = ds
                if jt == 0:
                    sums_ref[:, at:at + length] = ds.astype(F32)
                    sums_ref[:, 0:at] = jnp.zeros((128, at), F32)
                else:
                    sums_ref[:, at:at + length] += ds.astype(F32)
            turned = lax.dot_general(
                flip, sums_ref[...], (((1,), (0,)), ((), ())),
                precision=lax.Precision.HIGHEST, preferred_element_type=F32,
            )
            turned = pltpu.roll(turned, 0, 1, stride=1, stride_axis=0)
            dvec_ref[pl.ds(head, 1), :] = jnp.sum(turned, axis=0, keepdims=True)
            parts.append(tn(qkv_ref[:, k_cols], ds_ref[half]) * 0.125)
        both = jnp.where(row_low, parts[0], parts[1]).astype(BF)
        dqkv_ref[:, q_cols] = both.T
        for jt in range(tiles):
            rows = slice(jt * 128, jt * 128 + 128)
            dk = jnp.where(lane_low_tile, nn(ds_ref[0, rows, :], q2), nn(ds_ref[1, rows, :], q2))
            dqkv_ref[rows, k_cols] = dk.astype(BF)
            dv = jnp.where(lane_low_tile, nn(prob_ref[0, rows, :], do2), nn(prob_ref[1, rows, :], do2))
            dqkv_ref[rows, v_cols] = dv.astype(BF)
        return 0

    lax.fori_loop(0, width // 128, pair, 0)

    def weights_back(c, _):
        cols = pl.ds(pl.multiple_of(c * 256, 256), 256)
        dw_ref[cols, :] = tn(dqkv_ref[:, cols], normed_ref[...]).astype(BF)
        return 0

    lax.fori_loop(0, 3 * width // 256, weights_back, 0)

    def rows_back(c, _):
        cols = pl.ds(pl.multiple_of(c * 256, 256), 256)
        dx_ref[:, cols] = nn(dqkv_ref[...], flat_ref[:, cols])
        return 0

    lax.fori_loop(0, width // 256, rows_back, 0)
    qkv_rows = w_ref.shape[1]
    unflatten(dw_ref, grad_refs[0], 0)
    unflatten(flat_out_ref, grad_refs[-1], qkv_rows if len(grad_refs) == 1 else 0)
    if tail:
        start = qkv_rows + wo_ref.shape[1]
        for i in range(tail_ref.shape[0]):
            grad_refs[0][i, start:, :] = tail_ref[i]
    norm_back(x_ref, gain_ref, dx_ref, grad_ref, dx_ref, dgain_ref)


def norm_back(x_ref, gain_ref, upper_ref, base_ref, dx_ref, dgain_ref):
    field = x_ref[...]
    inverse = inverse_rms(field)
    unit = field * inverse
    upper = upper_ref[...]
    scaled = upper * gain_ref[...]
    dgain_ref[...] = jnp.sum(upper * unit, axis=0, keepdims=True)
    dx_ref[...] = base_ref[...] + inverse * (scaled - unit * jnp.mean(scaled * unit, axis=1, keepdims=True))


def attend_back(piece, x, gain, weights, vectors, normed, qkv, mixed, lse, grad, tail=None):
    length, width = x.shape
    heads, span = vectors.shape
    w_args, w_specs = weight_specs(weights)
    packed = weights[0]
    grad_shapes = packed if isinstance(packed, tuple) else (packed,)
    tails = () if tail is None else (tail,)
    return pl.pallas_call(
        lambda *refs: attend_back_kernel(bool(tails), weights, *refs),
        out_shape=(jax.ShapeDtypeStruct((length, width), F32),)
        + tuple(jax.ShapeDtypeStruct(g.shape, BF) for g in grad_shapes)
        + (
            jax.ShapeDtypeStruct((heads, span), F32),
            jax.ShapeDtypeStruct((1, width), F32),
        ),
        in_specs=[SMEM_SPEC] + [VMEM_SPEC] * 2 + w_specs + [VMEM_SPEC] * (6 + len(tails)),
        out_specs=[VMEM_SPEC] * (3 + len(grad_shapes)),
        scratch_shapes=[
            pltpu.VMEM((length, length), F32),
            pltpu.VMEM((128, span), F32),
            pltpu.VMEM((128, span), F32),
            pltpu.VMEM((2, length, length), BF),
            pltpu.VMEM((2, length, length), BF),
            pltpu.VMEM((length, width), BF),
            pltpu.VMEM((length, width), BF),
            pltpu.VMEM((length, 3 * width), BF),
            pltpu.VMEM((16, length), F32),
            pltpu.VMEM((3 * width, width), BF),
            pltpu.VMEM((width, width), BF),
            pltpu.VMEM((3 * width, width), BF),
        ],
        compiler_params=pltpu.CompilerParams(vmem_limit_bytes=VMEM_BYTES),
        cost_estimate=pl.CostEstimate(
            flops=16 * length * width * width + 10 * length * length * width,
            bytes_accessed=40 * length * width + 16 * width * width,
            transcendentals=heads * length * length,
        ),
        name="attend_back",
    )(piece, x, gain, *w_args, vectors, normed, qkv, mixed, lse, grad, *tails)


def mlp_chunk(c, parts, zones, up_ref, down_ref):
    hidden, width = up_ref.shape
    piece = hidden // (parts * zones)
    rows = [
        up_ref[pl.ds(pl.multiple_of(z * parts * piece + c * piece, 16), piece), :] for z in range(zones)
    ]
    span = down_ref.shape[1] // parts
    down = down_ref[:, pl.ds(pl.multiple_of(c * span, 16), span), :].reshape(-1, down_ref.shape[2])
    return jnp.concatenate(rows, axis=0), down


def mlp_kernel(parts, zones, x_ref, gain_ref, up_ref, down_ref, out_ref, normed_ref):
    field = x_ref[...]
    normed_ref[...] = (field * inverse_rms(field) * gain_ref[...]).astype(BF)
    out_ref[...] = field

    def chunk(c, _):
        up, down = mlp_chunk(c, parts, zones, up_ref, down_ref)
        hidden = gelu_of(nt(normed_ref[...], up)).astype(BF)
        out_ref[...] += nt(hidden, down)
        return 0

    lax.fori_loop(0, parts, chunk, 0)


def mlp(x, gain, up, down, parts, zones):
    length, width = x.shape
    hidden = up.shape[0]
    return pl.pallas_call(
        lambda *refs: mlp_kernel(parts, zones, *refs),
        out_shape=(jax.ShapeDtypeStruct((length, width), F32), jax.ShapeDtypeStruct((length, width), BF)),
        in_specs=[VMEM_SPEC] * 4,
        out_specs=[VMEM_SPEC] * 2,
        compiler_params=pltpu.CompilerParams(vmem_limit_bytes=VMEM_BYTES),
        cost_estimate=pl.CostEstimate(
            flops=4 * length * width * hidden, bytes_accessed=10 * length * width + 4 * width * hidden,
            transcendentals=length * hidden,
        ),
        name="mlp",
    )(x, gain, up, down)


def mlp_back_kernel(parts, zones, x_ref, gain_ref, up_ref, down_ref, normed_ref, grad_ref,
                    dx_ref, dup_ref, ddown_ref, dgain_ref, low_ref, acc_ref):
    low_ref[...] = grad_ref[...].astype(BF)
    acc_ref[...] = jnp.zeros_like(acc_ref)

    piece = up_ref.shape[0] // (parts * zones)
    span = down_ref.shape[1] // parts

    def chunk(c, _):
        up, down = mlp_chunk(c, parts, zones, up_ref, down_ref)
        hidden, slope = gelu_parts(nt(normed_ref[...], up))
        pre_grad = (nn(low_ref[...], down) * slope).astype(BF)
        ddown = tn(low_ref[...], hidden.astype(BF)).astype(BF)
        ddown_ref[:, pl.ds(pl.multiple_of(c * span, 16), span), :] = ddown.reshape(-1, span, ddown.shape[1])
        dup = tn(pre_grad, normed_ref[...]).astype(BF)
        for z in range(zones):
            at = pl.ds(pl.multiple_of(z * parts * piece + c * piece, 16), piece)
            dup_ref[at, :] = dup[z * piece:z * piece + piece, :]
        acc_ref[...] += nn(pre_grad, up)
        return 0

    lax.fori_loop(0, parts, chunk, 0)
    norm_back(x_ref, gain_ref, acc_ref, grad_ref, dx_ref, dgain_ref)


def mlp_back(x, gain, up, down, normed, grad, parts, zones):
    length, width = x.shape
    hidden = up.shape[0]
    return pl.pallas_call(
        lambda *refs: mlp_back_kernel(parts, zones, *refs),
        out_shape=(
            jax.ShapeDtypeStruct((length, width), F32),
            jax.ShapeDtypeStruct((hidden, width), BF),
            jax.ShapeDtypeStruct(down.shape, BF),
            jax.ShapeDtypeStruct((1, width), F32),
        ),
        in_specs=[VMEM_SPEC] * 6,
        out_specs=[VMEM_SPEC] * 4,
        scratch_shapes=[pltpu.VMEM((length, width), BF), pltpu.VMEM((length, width), F32)],
        compiler_params=pltpu.CompilerParams(vmem_limit_bytes=VMEM_BYTES),
        cost_estimate=pl.CostEstimate(
            flops=10 * length * width * hidden, bytes_accessed=16 * length * width + 8 * width * hidden,
            transcendentals=length * hidden,
        ),
        name="mlp_back",
    )(x, gain, up, down, normed, grad)


MESH = pl.DeviceIdType.MESH


def flip(index, mask):
    bit = 1
    while bit <= mask:
        if mask & bit:
            index = index + bit - 2 * bit * ((index // bit) % 2)
        bit *= 2
    return index


def masks_of(bits):
    found = [0]
    for bit in bits:
        found = found + [m | bit for m in found]
    return found


def bits_below(size):
    found, bit = [], 1
    while bit < size:
        found.append(bit)
        bit *= 2
    return found


def halves_of(rows):
    cut = rows // 2 // 16 * 16
    return ((0, cut), (cut, rows - cut))


def routes_of(chips):
    bits = bits_below(chips)
    cut = len(bits) // 2
    return (bits, bits[cut:] + bits[:cut])


def greet(owner, zone, owners, zones):
    barrier = pltpu.get_barrier_semaphore()
    peers = [(flip(owner, bit), zone) for bit in bits_below(owners)]
    peers += [(owner, flip(zone, d)) for d in range(1, zones)]
    for peer in peers:
        pl.semaphore_signal(barrier, inc=1, device_id=peer, device_id_type=MESH)
    pl.semaphore_wait(barrier, len(peers))


def sender(send_sem, recv_sem):
    used = [0]

    def send(source, target, device):
        at = used[0]
        used[0] += 1
        copy = pltpu.make_async_remote_copy(
            source, target, send_sem.at[at], recv_sem.at[at], device_id=device, device_id_type=MESH
        )
        copy.start()
        return copy

    return send


def gather_copies(owners, zones):
    chips = owners // 2
    return zones - 1 + 2 * (chips - 1) + 2 * chips


def gather_kernel(owners, zones, used_rows, experts, capacity, *refs):
    count = len(used_rows)
    blocks, (late_ref, route_ref), refs = refs[:count], refs[count:count + 2], refs[count + 2:]
    outs, (near_ref, slot_ref), refs = refs[:count], refs[count:count + 2], refs[count + 2:]
    slabs, turned = refs[:count], refs[count:2 * count]
    slot_in_ref, send_sem, recv_sem, local_sem = refs[2 * count:]
    owner, zone = lax.axis_index("expert"), lax.axis_index("shard")
    greet(owner, zone, owners, zones)
    send = sender(send_sem, recv_sem)
    chips = owners // 2
    pending, finals = [], []

    def across(g):
        slabs[g][zone] = blocks[g][...]
        return [send(blocks[g], slabs[g].at[zone], (owner, flip(zone, d))) for d in range(1, zones)]

    def place(g, index, half):
        start, size = halves_of(used_rows[g])[half]
        return outs[g].at[index, pl.ds(start, size), :]

    def onward(g, half, index):
        finals.append(send(place(g, index, half), place(g, index, half), (flip(owner, 1), zone)))

    def start_rows(g, copies):
        for copy in copies:
            copy.wait_recv()
        pending.extend(copies)
        slab = slabs[g]
        turned[g][...] = slab[...].reshape(slab.shape[0] * slab.shape[1], slab.shape[2]).T
        local = pltpu.make_async_copy(
            turned[g].at[pl.ds(0, used_rows[g]), :], outs[g].at[owner], local_sem.at[g]
        )
        local.start()
        firsts = []
        for half, order in enumerate(routes_of(chips)):
            start, size = halves_of(used_rows[g])[half]
            source = turned[g].at[pl.ds(start, size), :]
            firsts.append([send(source, place(g, owner, half), (flip(owner, 2 * order[0]), zone))])
            finals.append(send(source, place(g, owner, half), (flip(owner, 1), zone)))
        return firsts, local

    def finish_rows(g, state, step):
        firsts, local = state
        if step == 0:
            local.wait()
        for half, order in enumerate(routes_of(chips)):
            for copy in firsts[half]:
                copy.wait_recv()
            pending.extend(firsts[half])
            done = masks_of(order[:step])
            arrived = [m | order[step] for m in done]
            if step + 1 < len(order):
                device = (flip(owner, 2 * order[step + 1]), zone)
                firsts[half] = [
                    send(place(g, flip(owner, 2 * m), half), place(g, flip(owner, 2 * m), half), device)
                    for m in done + arrived
                ]
            for m in arrived:
                onward(g, half, flip(owner, 2 * m))
        return firsts, local

    steps = len(routes_of(chips)[0])
    moving = {0: across(0)}
    states = {}
    slot_ref[0] = token_slots(route_ref[...], experts, capacity)
    slot_copies = []
    for d in range(1, zones // 2):
        device = (owner, (zone + zones - 2 * d) % zones)
        slot_copies.append(send(slot_ref.at[0], slot_in_ref.at[d - 1], device))
    for g in range(count):
        states[g] = start_rows(g, moving[g])
        if g + 1 < count:
            moving[g + 1] = across(g + 1)
        else:
            for d in range(1, zones // 2):
                device = (owner, (zone + zones - 2 * d) % zones)
                finals.append(send(late_ref, near_ref.at[d - 1], device))
        if g > 0:
            for step in range(1, steps):
                states[g - 1] = finish_rows(g - 1, states[g - 1], step)
        states[g] = finish_rows(g, states[g], 0)
    for step in range(1, steps):
        states[count - 1] = finish_rows(count - 1, states[count - 1], step)
    for d in range(1, zones // 2):
        slot_copies[d - 1].wait_recv()
        slot_ref[d] = slot_in_ref[d - 1]
    for copy in finals:
        copy.wait_recv()
    for copy in pending + finals + slot_copies:
        copy.wait_send()


def gather_weights(blocks, used_rows, late, route_rows, owners, zones, experts, capacity):
    count = len(blocks)
    depth = zones * blocks[0].shape[0]
    groups = zones // 2
    copies = count * gather_copies(owners, zones) + 2 * (groups - 1)
    length = route_rows.shape[1]
    any_spec = pl.BlockSpec(memory_space=pltpu.HBM)
    return pl.pallas_call(
        lambda *refs: gather_kernel(owners, zones, used_rows, experts, capacity, *refs),
        out_shape=tuple(jax.ShapeDtypeStruct((owners, used, depth), BF) for used in used_rows)
        + (
            jax.ShapeDtypeStruct((groups - 1,) + late.shape, late.dtype),
            jax.ShapeDtypeStruct((groups, 8, length), F32),
        ),
        in_specs=[VMEM_SPEC] * count + [any_spec, VMEM_SPEC],
        out_specs=tuple([any_spec] * (count + 1)) + (VMEM_SPEC,),
        scratch_shapes=[pltpu.VMEM((zones,) + b.shape, BF) for b in blocks]
        + [pltpu.VMEM((b.shape[1], depth), BF) for b in blocks]
        + [pltpu.VMEM((groups - 1, 8, length), F32)]
        + [pltpu.SemaphoreType.DMA((copies,)), pltpu.SemaphoreType.DMA((copies,)), pltpu.SemaphoreType.DMA((count,))],
        compiler_params=pltpu.CompilerParams(
            vmem_limit_bytes=24 * 1024 * 1024, collective_id=1, has_side_effects=True
        ),
        name="gather_weights",
    )(*blocks, late, route_rows)


def reduce_copies(owners, zones):
    return 1 + 2 * (owners // 2 - 1) + zones - 1


def add_rows(into, other):
    return (into.astype(F32) + other.astype(F32)).astype(BF)


def reduce_kernel(owners, zones, used_rows, *refs):
    count = len(used_rows)
    parts, small = refs[:count], refs[count]
    outs, small_out = refs[count + 1:2 * count + 1], refs[2 * count + 1]
    scratch = refs[2 * count + 2:]
    keep, near, far = scratch[:count], scratch[count:2 * count], scratch[2 * count:3 * count]
    slabs, incoming = scratch[3 * count:4 * count], scratch[4 * count:5 * count]
    small_mine, small_other, send_sem, recv_sem, local_sem = scratch[5 * count:]
    owner, zone = lax.axis_index("expert"), lax.axis_index("shard")
    chip, core = owner // 2, owner % 2
    greet(owner, zone, owners, zones)
    send = sender(send_sem, recv_sem)
    chips = owners // 2
    orders = routes_of(chips)
    steps = len(orders[0])
    sent = []
    small_peers = [(flip(owner, bit), zone) for bit in bits_below(owners)]
    small_peers += [(owner, flip(zone, bit)) for bit in bits_below(zones)]
    small_mine[0] = small[...]

    def small_start(i):
        return send(small_mine.at[i], small_other.at[i], small_peers[i])

    def small_finish(i, copy):
        copy.wait_recv()
        sent.append(copy)
        small_mine[i + 1] = small_mine[i] + small_other[i]

    def begin(g):
        local = pltpu.make_async_copy(parts[g].at[:, core], keep[g], local_sem.at[g])
        local.start()
        return send(parts[g].at[:, 1 - core], near[g], (flip(owner, 1), zone)), local

    def window(g, half):
        start, size = halves_of(used_rows[g])[half]
        return pl.ds(start, size)

    def push(g, step):
        copies = []
        for half, order in enumerate(orders):
            bit, rest = order[step], masks_of(order[step + 1:])
            device = (flip(owner, 2 * bit), zone)
            for i, m in enumerate(rest):
                slot = chips - 2 * len(rest) + i
                copies.append(send(
                    keep[g].at[flip(chip, bit | m), window(g, half), :], far[g].at[slot, window(g, half), :], device
                ))
        return copies

    def absorb(g, step, copies):
        for copy in copies:
            copy.wait_recv()
        sent.extend(copies)
        for half, order in enumerate(orders):
            rest = masks_of(order[step + 1:])
            for i, m in enumerate(rest):
                slot = chips - 2 * len(rest) + i
                index = flip(chip, m)
                keep[g][index, window(g, half), :] = add_rows(
                    keep[g][index, window(g, half), :], far[g][slot, window(g, half), :]
                )

    def stage_near(g, state):
        copy, local = state
        local.wait()
        copy.wait_recv()
        sent.append(copy)

        def one(h, _):
            keep[g][h] = add_rows(keep[g][h], near[g][h])
            return 0

        lax.fori_loop(0, chips, one, 0)
        return push(g, 0)

    def stage_zone(g):
        slab = slabs[g]
        spare = slab.shape[2] - used_rows[g]
        own = keep[g][chip]
        if spare:
            own = jnp.concatenate([own, jnp.zeros((spare, own.shape[1]), BF)], axis=0)
        slab[...] = own.T.reshape(slab.shape)
        return [
            send(slab.at[flip(zone, d)], incoming[g].at[d - 1], (owner, flip(zone, d))) for d in range(1, zones)
        ]

    def stage_end(g, copies):
        total = slabs[g][zone].astype(F32)
        for d in range(1, zones):
            copies[d - 1].wait_recv()
            total = total + incoming[g][d - 1].astype(F32)
        sent.extend(copies)
        outs[g][...] = total

    begun = [begin(g) for g in range(count)]
    small_copy = small_start(0)
    state = {}
    stages = steps + 2
    turn = 0
    for t in range(count + stages - 1):
        for g in reversed(range(count)):
            at = t - g
            if at == 0:
                state[g] = stage_near(g, begun[g])
            elif 1 <= at <= steps:
                absorb(g, at - 1, state[g])
                state[g] = push(g, at) if at < steps else stage_zone(g)
            elif at == steps + 1:
                stage_end(g, state[g])
        if turn < len(small_peers):
            small_finish(turn, small_copy)
            turn += 1
            if turn < len(small_peers):
                small_copy = small_start(turn)
    while turn < len(small_peers):
        small_finish(turn, small_copy)
        turn += 1
        if turn < len(small_peers):
            small_copy = small_start(turn)
    small_out[...] = small_mine[len(small_peers)]
    for copy in sent:
        copy.wait_send()


def reduce_grads(parts, small, owners, zones):
    count = len(parts)
    used_rows = tuple(p.shape[1] for p in parts)
    depth = parts[0].shape[2]
    chips = owners // 2
    parts = [p.reshape(chips, 2, p.shape[1], depth) for p in parts]
    wide = [-(-used // 128) * 128 for used in used_rows]
    rounds = len(bits_below(owners)) + len(bits_below(zones))
    copies = count * reduce_copies(owners, zones) + rounds
    return pl.pallas_call(
        lambda *refs: reduce_kernel(owners, zones, used_rows, *refs),
        out_shape=tuple(jax.ShapeDtypeStruct((depth // zones, w), F32) for w in wide)
        + (jax.ShapeDtypeStruct(small.shape, F32),),
        in_specs=[pl.BlockSpec(memory_space=pltpu.HBM)] * count + [VMEM_SPEC],
        out_specs=tuple([VMEM_SPEC] * (count + 1)),
        scratch_shapes=[pltpu.VMEM((chips, used, depth), BF) for used in used_rows]
        + [pltpu.VMEM((chips, used, depth), BF) for used in used_rows]
        + [pltpu.VMEM((chips - 1, used, depth), BF) for used in used_rows]
        + [pltpu.VMEM((zones, depth // zones, w), BF) for w in wide]
        + [pltpu.VMEM((zones - 1, depth // zones, w), BF) for w in wide]
        + [pltpu.VMEM((rounds + 1,) + small.shape, F32), pltpu.VMEM((rounds,) + small.shape, F32)]
        + [pltpu.SemaphoreType.DMA((copies,)), pltpu.SemaphoreType.DMA((copies,)), pltpu.SemaphoreType.DMA((count,))],
        compiler_params=pltpu.CompilerParams(
            vmem_limit_bytes=VMEM_BYTES, collective_id=2, has_side_effects=True
        ),
        name="reduce_grads",
    )(*parts, small)


def three_pieces(row):
    top = row.astype(BF)
    rest = row - top.astype(F32)
    middle = rest.astype(BF)
    low = (rest - middle.astype(F32)).astype(BF)
    return jnp.concatenate([top, middle, low, jnp.zeros((5, row.shape[1]), BF)], axis=0)


def sum_pieces(rows):
    return rows[0:1] + rows[1:2] + rows[2:3]


def token_slots(route_rows, experts, capacity):
    length = route_rows.shape[1]
    ids = lax.broadcasted_iota(jnp.int32, (experts, length), 0)
    first, second = route_rows[0:1] == ids, route_rows[1:2] == ids
    named = jnp.where(first | second, 1.0, 0.0).astype(BF)
    earlier = (
        lax.broadcasted_iota(jnp.int32, (length, length), 0) < lax.broadcasted_iota(jnp.int32, (length, length), 1)
    )
    place = nn(named, jnp.where(earlier, 1.0, 0.0).astype(BF)) + (ids * capacity).astype(F32)
    rows = [jnp.sum(jnp.where(hit, place, 0.0), axis=0, keepdims=True) for hit in (first, second)]
    return jnp.concatenate(rows + [jnp.zeros((6, length), F32)], axis=0)


def slot_hits(slots, start, count):
    place = lax.broadcasted_iota(jnp.int32, (count, slots.shape[1]), 0).astype(F32) + start.astype(F32)
    one, zero = jnp.asarray(1.0, F32), jnp.asarray(0.0, F32)
    return [jnp.where(place == slots[k:k + 1], one, zero).astype(BF) for k in range(2)]


def greet_plane(owner, zone, owners, zones):
    barrier = pltpu.get_barrier_semaphore()
    peers = [(flip(owner, mask), zone) for mask in range(1, owners)]
    peers += [(owner, (zone + d) % zones) for d in range(2, zones, 2)] + [(owner, flip(zone, 1))]
    for peer in peers:
        pl.semaphore_signal(barrier, inc=1, device_id=peer, device_id_type=MESH)
    pl.semaphore_wait(barrier, len(peers))


def peer_order(owners):
    return list(range(2, owners)) + [1, 0]


def softmax_pair(logits, route_rows):
    ids = lax.broadcasted_iota(jnp.int32, logits.shape, 0)
    a, b = [jnp.sum(jnp.where(route_rows[k:k + 1] == ids, logits, 0.0), axis=0, keepdims=True) for k in range(2)]
    peak = jnp.maximum(a, b)
    ea, eb = jnp.exp(a - peak), jnp.exp(b - peak)
    return ea / (ea + eb), eb / (ea + eb)


def send_rows_kernel(
    owners, zones, capacity, x_ref, gain_ref, router_ref, route_ref, slot_ref, slices_ref,
    normed_ref, gates_ref, rows_ref, gate_ref, other_ref,
    near_ref, near_gates_ref, packed_ref, tags_ref, tags_in_ref, send_sem, recv_sem, local_sem,
):
    owner, zone = lax.axis_index("expert"), lax.axis_index("shard")
    tags_ref[...] = jnp.zeros_like(tags_ref)
    greet_plane(owner, zone, owners, zones)
    send = sender(send_sem, recv_sem)
    groups = zones // 2
    local = rows_ref.shape[1]
    span = local * capacity
    field = x_ref[...]
    normed_ref[...] = (field * inverse_rms(field) * gain_ref[...]).astype(BF)
    cut = normed_ref.shape[1] // 2
    lanes = [pl.ds(0, cut), pl.ds(cut, cut)]
    copies = {}
    for half in range(2):
        for d in range(1, groups):
            device = (owner, (zone + zones - 2 * d) % zones)
            copies[d, half] = send(normed_ref.at[:, lanes[half]], near_ref.at[d - 1, :, lanes[half]], device)
    gates = softmax_pair(nt(router_ref[...], normed_ref[...]), route_ref[...])
    gates_ref[...] = jnp.concatenate(list(gates) + [jnp.zeros((6, gates[0].shape[1]), F32)], axis=0)
    for d in range(1, groups):
        copies[d, 2] = send(gates_ref, near_gates_ref.at[d - 1], (owner, (zone + zones - 2 * d) % zones))
    arrivals, stays = [], []
    for part in range(local):
        arrivals.append(send(slices_ref.at[part], other_ref.at[part], (owner, flip(zone, 1))))
    def ship(d, mask, target, half):
        columns = slice(None) if half is None else lanes[half]
        for part in range(local):
            source = packed_ref.at[d, mask, pl.ds(part * capacity, capacity), columns]
            place = rows_ref.at[owner, part, pl.ds(d * capacity, capacity), columns]
            if mask:
                arrivals.append(send(source, place, (target, zone)))
            else:
                at = (2 * d + (half or 0)) * local + part
                copy = pltpu.make_async_copy(source, place, local_sem.at[at])
                copy.start()
                stays.append(copy)

    for d in range(groups):
        for half in (None,) if d == 0 else (0, 1):
            if d:
                copies[d, half].wait_recv()
                if half == 0:
                    copies[d, 2].wait_recv()
            rows = normed_ref if d == 0 else near_ref.at[d - 1]
            weights = gates_ref[...] if d == 0 else near_gates_ref[d - 1]
            pieces = [three_pieces(weights[k:k + 1]) for k in range(2)]
            slots = slot_ref[d]
            for mask in peer_order(owners):
                target = flip(owner, mask)
                hits = slot_hits(slots, target * span, span)
                both = hits[0] + hits[1]
                if half is None:
                    packed_ref[d, mask] = nn(both, rows[...]).astype(BF)
                else:
                    packed_ref[d, mask, :, lanes[half]] = nn(both, rows[:, lanes[half]]).astype(BF)
                ship(d, mask, target, half)
                if half == 1:
                    continue
                tag = sum_pieces(nt(pieces[0], hits[0]) + nt(pieces[1], hits[1]))
                tags_ref[d, mask, :, 0:span] = jnp.broadcast_to(tag, (8, span))
                if mask:
                    arrivals.append(send(tags_ref.at[d, mask], tags_in_ref.at[d, owner], (target, zone)))
                else:
                    tags_in_ref[d, owner] = tags_ref[d, mask]
    for copy in arrivals:
        copy.wait_recv()
    for d in range(groups):
        for source in range(owners):
            column = tags_in_ref[d, source].T
            for part in range(local):
                gate_ref[source, part, d * capacity:(d + 1) * capacity, :] = column[
                    part * capacity:(part + 1) * capacity, 0:1
                ]
    for copy in stays:
        copy.wait()
    for copy in list(copies.values()) + arrivals:
        copy.wait_send()


def send_rows(x, gain, router, route_rows, slot_rows, slices, owners, zones, local, capacity):
    length, width = x.shape
    groups = zones // 2
    span = local * capacity
    any_spec = pl.BlockSpec(memory_space=pltpu.HBM)
    wide = -(-span // 128) * 128
    copies = local + 3 * (groups - 1) + (owners - 1) * (local + 1 + (groups - 1) * (2 * local + 1))
    return pl.pallas_call(
        lambda *refs: send_rows_kernel(owners, zones, capacity, *refs),
        out_shape=(
            jax.ShapeDtypeStruct((length, width), BF),
            jax.ShapeDtypeStruct((8, length), F32),
            jax.ShapeDtypeStruct((owners, local, groups * capacity, width), BF),
            jax.ShapeDtypeStruct((owners, local, groups * capacity, 1), F32),
            jax.ShapeDtypeStruct(slices.shape, slices.dtype),
        ),
        in_specs=[VMEM_SPEC] * 5 + [any_spec],
        out_specs=(VMEM_SPEC, VMEM_SPEC, any_spec, VMEM_SPEC, any_spec),
        scratch_shapes=[
            pltpu.VMEM((groups - 1, length, width), BF),
            pltpu.VMEM((groups - 1, 8, length), F32),
            pltpu.VMEM((groups, owners, span, width), BF),
            pltpu.VMEM((groups, owners, 8, wide), F32),
            pltpu.VMEM((groups, owners, 8, wide), F32),
            pltpu.SemaphoreType.DMA((copies,)),
            pltpu.SemaphoreType.DMA((copies,)),
            pltpu.SemaphoreType.DMA((2 * groups * local,)),
        ],
        compiler_params=pltpu.CompilerParams(
            vmem_limit_bytes=40 * 1024 * 1024, collective_id=3, has_side_effects=True
        ),
        name="send_rows",
    )(x, gain, router, route_rows, slot_rows, slices)


def return_rows_kernel(
    owners, zones, capacity,
    rows_ref, dgate_ref, slot_ref, gates_ref, route_ref, x_ref, gain_ref, router_ref, normed_ref, top_ref,
    dx_ref, dgain_ref, drouter_ref,
    back_ref, tags_ref, tags_in_ref, part_ref, part_in_ref, mark_ref, mark_in_ref, sum_ref, send_sem, recv_sem, local_sem,
):
    owner, zone = lax.axis_index("expert"), lax.axis_index("shard")
    tags_ref[...] = jnp.zeros_like(tags_ref)
    greet_plane(owner, zone, owners, zones)
    send = sender(send_sem, recv_sem)
    groups = zones // 2
    local = rows_ref.shape[1]
    span = local * capacity
    chip = owner // 2
    cut = back_ref.shape[3] // 2
    lanes = [pl.ds(0, cut), pl.ds(cut, cut)]
    arrivals, stays, sent = {}, {}, []

    def ship(d, half):
        window = pl.ds(d * capacity, capacity)
        columns = slice(None) if half is None else lanes[half]
        for mask in peer_order(owners):
            target = flip(owner, mask)
            for part in range(local):
                source = rows_ref.at[target, part, window, columns]
                place = back_ref.at[d, owner, pl.ds(part * capacity, capacity), columns]
                if mask:
                    arrivals.setdefault((d, half, mask), []).append(send(source, place, (target, zone)))
                else:
                    at = (2 * d + (half or 0)) * local + part
                    copy = pltpu.make_async_copy(source, place, local_sem.at[at])
                    copy.start()
                    stays.setdefault((d, half), []).append(copy)

    def ship_tags(d):
        for mask in peer_order(owners):
            target = flip(owner, mask)
            columns = [dgate_ref[target, part, d * capacity:(d + 1) * capacity, :] for part in range(local)]
            column = jnp.concatenate(columns, axis=0)
            tags_ref[d, mask, :, 0:span] = jnp.broadcast_to(column, (span, 128)).T[0:8]
            if mask:
                arrivals.setdefault((d, "tags", mask), []).append(
                    send(tags_ref.at[d, mask], tags_in_ref.at[d, owner], (target, zone))
                )
            else:
                tags_in_ref[d, owner] = tags_ref[d, mask]

    def collect_zone(d, half):
        slots = slot_ref[d]
        columns = slice(None) if half is None else lanes[half]
        marks = [jnp.zeros((1, slots.shape[1]), F32) for _ in range(2)]
        for turn, hop in enumerate(list(range(1, owners // 2)) + [0]):
            for mask in (2 * hop, 2 * hop + 1):
                waits = arrivals.get((d, half, mask), [])
                if half != 1:
                    waits = waits + arrivals.get((d, "tags", mask), [])
                for copy in waits:
                    copy.wait_recv()
                if mask == 0:
                    for copy in stays[d, half]:
                        copy.wait()
            peer = flip(chip, hop)
            hits = slot_hits(slots, peer * (2 * span), 2 * span)
            rows = back_ref[d, pl.ds(2 * peer, 2), :, columns]
            added = tn(hits[0] + hits[1], rows.reshape(2 * span, rows.shape[2]))
            if turn == 0:
                sum_ref[:, columns] = added
            else:
                sum_ref[:, columns] += added
            if half == 1:
                continue
            tag = tags_in_ref[d, pl.ds(2 * peer, 2)]
            tag = jnp.concatenate([tag[0, 0:1, 0:span], tag[1, 0:1, 0:span]], axis=1)
            pieces = three_pieces(tag)
            for k in range(2):
                marks[k] = marks[k] + sum_pieces(nn(pieces, hits[k]))
        return marks

    for d in range(1, groups):
        ship(d, 0)
        ship_tags(d)
    incoming = {d: [] for d in range(1, groups)}
    for half in range(2):
        for d in range(1, groups):
            for mask in peer_order(owners):
                for copy in arrivals.get((d, half, mask), []):
                    copy.wait_send()
            if half == 0:
                ship(d, 1)
        if half == 1:
            ship(0, None)
            ship_tags(0)
        for d in range(1, groups):
            device = (owner, (zone + 2 * d) % zones)
            marks = collect_zone(d, half)
            part_ref[d - 1, :, lanes[half]] = sum_ref[:, lanes[half]].astype(BF)
            incoming[d].append(
                send(part_ref.at[d - 1, :, lanes[half]], part_in_ref.at[d - 1, :, lanes[half]], device)
            )
            if half == 0:
                mark_ref[d - 1] = jnp.concatenate(marks + [jnp.zeros((6, marks[0].shape[1]), F32)], axis=0)
                incoming[d].append(send(mark_ref.at[d - 1], mark_in_ref.at[d - 1], device))
    marks = collect_zone(0, None)
    for d in range(1, groups):
        for copy in incoming[d]:
            copy.wait_recv()
            sent.append(copy)
        sum_ref[...] += part_in_ref[d - 1].astype(F32)
        marks = [marks[k] + mark_in_ref[d - 1, k:k + 1, :] for k in range(2)]
    gates = [gates_ref[k:k + 1, :] for k in range(2)]
    mean = gates[0] * marks[0] + gates[1] * marks[1]
    ids = lax.broadcasted_iota(jnp.int32, (router_ref.shape[0], mean.shape[1]), 0)
    dlogits = jnp.zeros(ids.shape, F32)
    for k in range(2):
        dlogits = dlogits + jnp.where(route_ref[k:k + 1, :] == ids, gates[k] * (marks[k] - mean), 0.0)
    dlogits = dlogits.astype(BF)
    drouter_ref[...] = nn(dlogits, normed_ref[...])
    sum_ref[...] += tn(dlogits, router_ref[...])
    field = x_ref[...]
    inverse = inverse_rms(field)
    unit = field * inverse
    upper = sum_ref[...]
    scaled = upper * gain_ref[...]
    dgain_ref[...] = jnp.sum(upper * unit, axis=0, keepdims=True)
    dx_ref[...] = top_ref[...].astype(F32) + inverse * (
        scaled - unit * jnp.mean(scaled * unit, axis=1, keepdims=True)
    )
    for (d, half, _), copies in arrivals.items():
        if d == 0 or half == "tags":
            sent.extend(copies)
    for copy in sent:
        copy.wait_send()


def return_rows(rows, dgate, slot_rows, gates, route_rows, x, gain, router, normed, top, zones, capacity):
    length, width = x.shape
    owners, local = rows.shape[:2]
    groups = zones // 2
    span = local * capacity
    wide = -(-span // 128) * 128
    copies = 3 * (groups - 1) + (owners - 1) * (local + 1 + (groups - 1) * (2 * local + 1))
    return pl.pallas_call(
        lambda *refs: return_rows_kernel(owners, zones, capacity, *refs),
        out_shape=(
            jax.ShapeDtypeStruct((length, width), F32),
            jax.ShapeDtypeStruct((1, width), F32),
            jax.ShapeDtypeStruct(router.shape, F32),
        ),
        in_specs=[pl.BlockSpec(memory_space=pltpu.HBM)] + [VMEM_SPEC] * 9,
        out_specs=[VMEM_SPEC] * 3,
        scratch_shapes=[
            pltpu.VMEM((groups, owners, span, width), BF),
            pltpu.VMEM((groups, owners, 8, wide), F32),
            pltpu.VMEM((groups, owners, 8, wide), F32),
            pltpu.VMEM((groups - 1, length, width), BF),
            pltpu.VMEM((groups - 1, length, width), BF),
            pltpu.VMEM((groups - 1, 8, length), F32),
            pltpu.VMEM((groups - 1, 8, length), F32),
            pltpu.VMEM((length, width), F32),
            pltpu.SemaphoreType.DMA((copies,)),
            pltpu.SemaphoreType.DMA((copies,)),
            pltpu.SemaphoreType.DMA((2 * groups * local,)),
        ],
        compiler_params=pltpu.CompilerParams(
            vmem_limit_bytes=40 * 1024 * 1024, collective_id=4, has_side_effects=True
        ),
        name="return_rows",
    )(rows, dgate, slot_rows, gates, route_rows, x, gain, router, normed, top)


def experts_kernel(
    x_ref, c_ref, gate_ref, own_up_in, own_down_in, peer_up_in, peer_down_in,
    y_ref, dx_ref, dgate_ref, own_up_ref, own_down_ref, peer_up_ref, peer_down_ref,
    hidden_ref, pre_ref, dey_ref,
):
    sources, _, span, width = x_ref.shape
    size = own_up_in.shape[1]
    group = max(1, 384 // span)
    rows = group * span

    @pl.loop(0, sources // group)
    def _(i):
        at = pl.ds(i * group, group)
        rows_at = pl.ds(pl.multiple_of(i * rows, 16), rows)
        x = x_ref[at, 0].reshape(rows, width)
        c = c_ref[at, 0].reshape(rows, width)
        gate = gate_ref[at, 0].reshape(rows, 1)
        dey_ref[rows_at, :] = (gate * c.astype(F32)).astype(BF)
        dgate = jnp.zeros((rows, 1), F32)
        for part, (up_ref, down_ref) in enumerate(((own_up_in, own_down_in), (peer_up_in, peer_down_in))):
            cols = slice(part * size, part * size + size)
            hidden, slope = gelu_parts(nn(x, up_ref[...]))
            hidden = hidden.astype(BF)
            hidden_ref[rows_at, cols] = hidden
            back = nt(c, down_ref[...])
            dgate = dgate + jnp.sum(hidden.astype(F32) * back, axis=1, keepdims=True)
            pre_ref[rows_at, cols] = (gate * back * slope).astype(BF)
        y = nn(hidden_ref[rows_at, 0:size], own_down_in[...]) + nn(hidden_ref[rows_at, size:], peer_down_in[...])
        y_ref[at, 0] = (gate * y).astype(BF).reshape(group, span, width)
        dx = nt(pre_ref[rows_at, 0:size], own_up_in[...]) + nt(pre_ref[rows_at, size:], peer_up_in[...])
        dx_ref[at, 0] = dx.astype(BF).reshape(group, span, width)
        dgate_ref[at, 0] = dgate.reshape(group, span, 1)

    step = 256 if width % 256 == 0 else 128

    @pl.loop(0, width // step)
    def _(i):
        at = pl.ds(pl.multiple_of(i * step, step), step)
        x = x_ref[:, 0, :, at].reshape(sources * span, step)
        own_up_ref[at, :] = tn(x, pre_ref[:, 0:size])
        peer_up_ref[at, :] = tn(x, pre_ref[:, size:]).astype(BF)

    step = 256 if size % 256 == 0 else 128

    @pl.loop(0, size // step)
    def _(i):
        at = pl.ds(pl.multiple_of(i * step, step), step)
        own_down_ref[at, :] = tn(hidden_ref[:, at], dey_ref[...])
        peer_at = pl.ds(pl.multiple_of(i * step + size, step), step)
        peer_down_ref[at, :] = tn(hidden_ref[:, peer_at], dey_ref[...]).astype(BF)


def run_experts(x, c, gate, own_up, own_down, peer_up, peer_down):
    sources, local, span, width = x.shape
    hidden = own_up.shape[2]
    lean = sources * span > 2048
    once = dict(pipeline_mode=pl.Buffered(1)) if lean else {}
    row_spec = pl.BlockSpec((sources, 1, span, width), lambda e: (0, e, 0, 0), **once)
    gate_spec = pl.BlockSpec((sources, 1, span, 1), lambda e: (0, e, 0, 0), **once)
    late_spec = pl.BlockSpec((sources, 1, span, width), lambda e: (0, e, 0, 0), pipeline_mode=pl.Buffered(1))
    sq = pl.Squeezed()
    gup_spec = pl.BlockSpec((sq, width, hidden), lambda e: (e, 0, 0))
    gdown_spec = pl.BlockSpec((sq, hidden, width), lambda e: (e, 0, 0))
    rows = local * sources * span
    return pl.pallas_call(
        experts_kernel,
        grid=(local,),
        out_shape=(
            jax.ShapeDtypeStruct(x.shape, BF),
            jax.ShapeDtypeStruct(x.shape, BF),
            jax.ShapeDtypeStruct(gate.shape, F32),
            jax.ShapeDtypeStruct((local, width, hidden), F32),
            jax.ShapeDtypeStruct((local, hidden, width), F32),
            jax.ShapeDtypeStruct((local, width, hidden), BF),
            jax.ShapeDtypeStruct((local, hidden, width), BF),
        ),
        in_specs=[row_spec, late_spec, gate_spec, gup_spec, gdown_spec, gup_spec, gdown_spec],
        out_specs=[late_spec, row_spec, gate_spec, gup_spec, gdown_spec, gup_spec, gdown_spec],
        scratch_shapes=[
            pltpu.VMEM((sources * span, 2 * hidden), BF),
            pltpu.VMEM((sources * span, 2 * hidden), BF),
            pltpu.VMEM((sources * span, width), BF),
        ],
        compiler_params=pltpu.CompilerParams(vmem_limit_bytes=60 * 1024 * 1024),
        cost_estimate=pl.CostEstimate(
            flops=24 * rows * width * hidden, bytes_accessed=16 * rows * width, transcendentals=2 * rows * hidden,
        ),
        name="experts",
    )(x, c, gate, own_up, own_down, peer_up, peer_down)


def spread_kernel(slot_ref, rows_ref, out_ref):
    experts, zones, capacity, width = out_ref.shape
    take = max(1, 384 // capacity)

    def chunk(i, _):
        for zone in range(zones):
            hits = slot_hits(slot_ref[zone], i * (take * capacity), take * capacity)
            picked = nn(hits[0] + hits[1], rows_ref[zone])
            out_ref[pl.ds(i * take, take), zone] = picked.reshape(take, capacity, width).astype(BF)
        return 0

    lax.fori_loop(0, experts // take, chunk, 0)


def spread(slot_rows, rows, experts, capacity):
    zones, length, width = rows.shape
    return pl.pallas_call(
        spread_kernel,
        out_shape=jax.ShapeDtypeStruct((experts, zones, capacity, width), BF),
        in_specs=[VMEM_SPEC] * 2,
        out_specs=VMEM_SPEC,
        compiler_params=pltpu.CompilerParams(vmem_limit_bytes=VMEM_BYTES),
        cost_estimate=pl.CostEstimate(
            flops=2 * zones * experts * capacity * length * width,
            bytes_accessed=2 * zones * (experts * capacity + length) * width, transcendentals=0,
        ),
        name="spread",
    )(slot_rows, rows)


def collect_kernel(slot_ref, rows_ref, out_ref):
    experts, zones, capacity, width = rows_ref.shape
    length = out_ref.shape[1]
    take = max(1, 384 // capacity)
    out_ref[...] = jnp.zeros_like(out_ref)

    def chunk(i, _):
        for zone in range(zones):
            hits = slot_hits(slot_ref[zone], i * (take * capacity), take * capacity)
            rows = rows_ref[pl.ds(i * take, take), zone].reshape(take * capacity, width)
            out_ref[zone] += tn(hits[0] + hits[1], rows)
        return 0

    lax.fori_loop(0, experts // take, chunk, 0)


def collect(slot_rows, rows):
    experts, zones, capacity, width = rows.shape
    length = slot_rows.shape[2]
    return pl.pallas_call(
        collect_kernel,
        out_shape=jax.ShapeDtypeStruct((zones, length, width), F32),
        in_specs=[VMEM_SPEC] * 2,
        out_specs=VMEM_SPEC,
        compiler_params=pltpu.CompilerParams(vmem_limit_bytes=VMEM_BYTES),
        cost_estimate=pl.CostEstimate(
            flops=2 * zones * experts * capacity * length * width,
            bytes_accessed=2 * zones * (experts * capacity + 2 * length) * width, transcendentals=0,
        ),
        name="collect",
    )(slot_rows, rows)


bucket_edges = (1, 2, 3, 4, 6, 8, 12, 16, 24, 32, 48, 64, 96, 128, 192, 256, 384, 512, 768, 1024, 1536)


def bucket_onehot(length, buckets):
    distance = (length - 1) - jnp.arange(2 * length, dtype=jnp.int32)
    edge_list = jnp.array(bucket_edges, dtype=jnp.int32)
    magnitude = jnp.sum(
        (jnp.abs(distance)[:, None] >= edge_list[None, :]).astype(jnp.int32), axis=1, dtype=jnp.int32
    )
    bucket = magnitude + buckets // 2 * (distance > 0).astype(jnp.int32)
    real = jnp.arange(2 * length)[:, None] < 2 * length - 1
    hit = (bucket[:, None] == jnp.arange(buckets, dtype=jnp.int32)[None, :]) & real
    return hit.astype(F32)


def shift_from(value, distance):
    size = lax.axis_size("shard")
    return lax.ppermute(value, "shard", [((z + distance) % size, z) for z in range(size)])


def shift_to(value, distance):
    size = lax.axis_size("shard")
    return lax.ppermute(value, "shard", [(z, (z + distance) % size) for z in range(size)])


def swap_pair(value):
    return lax.ppermute(value, "shard", [(z, z ^ 1) for z in range(lax.axis_size("shard"))])


def exchange(value):
    return lax.all_to_all(value, "expert", split_axis=0, concat_axis=0, tiled=True)


def per_device(
    tokens, piece_start, routes, norm_gains, bias_tables, qkv_weight, out_weight, mlp_up, mlp_down, router,
    expert_up, expert_down, cotangent,
):
    length, width = tokens.shape
    owners = lax.axis_size("expert")
    zones = lax.axis_size("shard") // 2
    local = expert_up.shape[0]
    experts_all = local * owners
    capacity = 3 * routes.shape[1] * length // (2 * experts_all)
    qkv_cols, out_cols = qkv_weight.shape[2], out_weight.shape[2]
    zones_all = 2 * zones
    router_pad = 16
    parts = mlp_down.shape[0] // qkv_weight.shape[1]
    aligned = qkv_cols % 16 == 0 and out_cols % 16 == 0 and qkv_cols % out_cols == 0

    def padded(block):
        return jnp.pad(block, ((0, 0), (0, -block.shape[1] % 128)))

    down_block = mlp_down.reshape(parts, -1, mlp_down.shape[1]).transpose(1, 0, 2).reshape(qkv_weight.shape[1], -1)
    router_block = jnp.pad(router, ((0, 0), (0, router_pad - router.shape[1])))
    route_rows = routes.T
    first, up_full, down_full, last, cotangent_near, slot_rows = gather_weights(
        [
            padded(jnp.concatenate([qkv_weight[0], out_weight[0]], axis=1)),
            padded(mlp_up),
            padded(down_block),
            padded(jnp.concatenate([qkv_weight[1], out_weight[1], router_block], axis=1)),
        ],
        (qkv_cols + out_cols, mlp_up.shape[1], parts * mlp_down.shape[1], qkv_cols + out_cols + router_pad),
        cotangent, route_rows, owners, zones_all, experts_all, capacity,
    )

    def layer_weights(block):
        if aligned:
            return (block, qkv_cols, out_cols)
        flat = (block[:, :qkv_cols].reshape(1, -1, width), block[:, qkv_cols:qkv_cols + out_cols].reshape(1, -1, width))
        return (flat, 3 * width, width)

    up_full = up_full.reshape(-1, width)
    if mlp_down.shape[1] % 16:
        down_full = down_full.reshape(owners, parts, -1, width).transpose(1, 0, 2, 3).reshape(1, -1, width)
    router_full = last[:, qkv_cols + out_cols:qkv_cols + out_cols + router.shape[1]].reshape(experts_all, width)

    first, up_late = lax.optimization_barrier((first, expert_up))
    weights0, weights1 = layer_weights(first), layer_weights(last)
    up_other = swap_pair(up_late)
    direct = capacity % 16 == 0

    def dispatch(rows):
        packed = spread(slot_rows, rows, experts_all, capacity)
        return exchange(packed.reshape(owners, local, zones * capacity, width))

    def undo(rows):
        back = exchange(rows).reshape(experts_all, zones, capacity, width)
        return collect(slot_rows, back)

    cotangent_rows = dispatch(jnp.concatenate([cotangent[None], cotangent_near]))

    onehot = bucket_onehot(length, bias_tables.shape[2])
    vectors = lax.dot_general(
        bias_tables, onehot, (((2,), (1,)), ((), ())), precision=lax.Precision.HIGHEST
    )
    gains = [norm_gains[i:i + 1] for i in range(4)]
    x0 = tokens.astype(F32)
    x1, ah0, qkv0, o0, lse0 = attend(piece_start, x0, gains[0], weights0, vectors[0])
    x2, mh = mlp(x1, gains[1], up_full, down_full, parts, zones_all)
    x3, ah1, qkv1, o1, lse1 = attend(piece_start, x2, gains[2], weights1, vectors[1])

    x3, up_other, cotangent_rows = lax.optimization_barrier((x3, up_other, cotangent_rows))
    if direct:
        eh, gates, eh_rows, gate_rows, down_other = send_rows(
            x3, gains[3], router_full, route_rows, slot_rows, expert_down, owners, zones_all, local, capacity
        )
    else:
        down_other = swap_pair(expert_down)
        eh = (x3 * inverse_rms(x3) * gains[3]).astype(BF)
        gates = jnp.concatenate(softmax_pair(nt(router_full, eh), route_rows))
        eh_rows = dispatch(jnp.stack([eh] + [shift_from(eh, 2 * d) for d in range(1, zones)]))
        slot_ids = jnp.arange(experts_all * capacity, dtype=jnp.int32).astype(F32)
        marks = [slot_rows[d, :2][None] == slot_ids[:, None, None] for d in range(zones)]

        def gate_slots(d):
            held = gates if d == 0 else shift_from(gates, 2 * d)
            return jnp.sum(jnp.where(marks[d], held[None], 0.0), axis=(1, 2)).reshape(experts_all, capacity)

        gate_rows = exchange(
            jnp.stack([gate_slots(d) for d in range(zones)], axis=1).reshape(owners, local, zones * capacity)
        )[..., None]
    y_rows, dx_rows, dgate_rows, own_up, own_down, peer_up, peer_down = run_experts(
        eh_rows, cotangent_rows, gate_rows, expert_up, expert_down, up_other, down_other
    )
    peer_up, peer_down = swap_pair(peer_up), swap_pair(peer_down)

    if direct:
        dx3, dgain3, grad_router = return_rows(
            dx_rows, dgate_rows, slot_rows, gates, route_rows, x3, gains[3], router_full, eh, cotangent,
            zones_all, capacity,
        )
    else:
        dx_back = undo(dx_rows)
        dgate_back = exchange(dgate_rows[..., 0]).reshape(experts_all, zones, capacity)
        token_grad, gate_grad = dx_back[0], 0.0
        for d in range(zones):
            part = jnp.sum(jnp.where(marks[d], dgate_back[:, d].reshape(-1)[:, None, None], 0.0), axis=0)
            gate_grad = gate_grad + (part if d == 0 else shift_to(part, 2 * d))
        for d in range(1, zones):
            token_grad = token_grad + shift_to(dx_back[d].astype(BF), 2 * d).astype(F32)
        dchoice = gates * (gate_grad - jnp.sum(gates * gate_grad, axis=0, keepdims=True))
        chosen = route_rows[:, None, :] == jnp.arange(experts_all, dtype=jnp.int32)[None, :, None]
        dlogits = jnp.sum(jnp.where(chosen, dchoice[:, None, :], 0.0), axis=0).astype(BF)
        grad_router = nn(dlogits, eh)
        deh = token_grad + tn(dlogits, router_full)
        unit3 = x3 * inverse_rms(x3)
        scaled = deh * gains[3]
        dx3 = cotangent.astype(F32) + inverse_rms(x3) * (
            scaled - unit3 * jnp.mean(scaled * unit3, axis=1, keepdims=True)
        )
        dgain3 = jnp.sum(deh * unit3, axis=0)[None]
    router_rows = jnp.pad(
        grad_router.astype(BF).reshape(owners, local, width), ((0, 0), (0, router_pad - local), (0, 0))
    )

    def layer_grads(results, tail=None):
        grads = results[1:-2]
        if not aligned:
            pieces = [g.reshape(owners, -1, width) for g in grads] + ([] if tail is None else [tail])
            grads = [jnp.concatenate(pieces, axis=1)]
        return results[0], grads[0], results[-2], results[-1]

    dx2, last_part, dvec1, dgain2 = layer_grads(
        attend_back(
            piece_start, x2, gains[2], weights1, vectors[1], ah1, qkv1, o1, lse1, dx3, router_rows if aligned else None
        ),
        router_rows,
    )
    dx2, y_rows = lax.optimization_barrier((dx2, y_rows))
    y_back = undo(y_rows)
    final = x3 + y_back[0]
    for d in range(1, zones):
        final = final + shift_to(y_back[d].astype(BF), 2 * d).astype(F32)
    output = final.astype(BF)
    dx1, up_part, down_part, dgain1 = mlp_back(x1, gains[1], up_full, down_full, mh, dx2, parts, zones_all)
    dx0, first_part, dvec0, dgain0 = layer_grads(
        attend_back(piece_start, x0, gains[0], weights0, vectors[0], ah0, qkv0, o0, lse0, dx1)
    )
    dx0, output, peer_up, peer_down = lax.optimization_barrier((dx0, output, peer_up, peer_down))
    grad_up = own_up + peer_up.astype(F32)
    grad_down = own_down + peer_down.astype(F32)
    if mlp_down.shape[1] % 16:
        down_part = down_part.reshape(parts, owners, -1, width).transpose(1, 0, 2, 3)
    dtables = lax.dot_general(
        jnp.stack([dvec0, dvec1]), onehot, (((2,), (0,)), ((), ())), precision=lax.Precision.HIGHEST
    )
    dgains = jnp.concatenate([dgain0, dgain1, dgain2, dgain3])
    small = jnp.concatenate([dgains.reshape(-1), dtables.reshape(-1)])
    small = jnp.pad(small, (0, -small.size % 1024)).reshape(-1, 128)
    last_grad, up_grad, down_grad, first_grad, small = reduce_grads(
        [
            last_part, up_part.reshape(owners, -1, width), down_part.reshape(owners, -1, width), first_part
        ],
        small, owners, zones_all,
    )
    small = small.reshape(-1)
    grad_qkv = jnp.stack([first_grad[:, :qkv_cols], last_grad[:, :qkv_cols]])
    grad_out = jnp.stack(
        [first_grad[:, qkv_cols:qkv_cols + out_cols], last_grad[:, qkv_cols:qkv_cols + out_cols]]
    )
    grad_router_out = last_grad[:, qkv_cols + out_cols:qkv_cols + out_cols + local]
    grad_mlp_up = up_grad[:, :mlp_up.shape[1]]
    down_cols = mlp_down.shape[1]
    grad_mlp_down = down_grad[:, :parts * down_cols].reshape(-1, parts, down_cols).transpose(1, 0, 2)
    grad_mlp_down = grad_mlp_down.reshape(mlp_down.shape)
    return (
        output,
        dx0,
        small[:dgains.size].reshape(dgains.shape),
        small[dgains.size:dgains.size + dtables.size].reshape(dtables.shape),
        grad_qkv,
        grad_out,
        grad_mlp_up,
        grad_mlp_down,
        grad_router_out,
        grad_up,
        grad_down,
    )


def solution(mesh):
    both = P(("expert", "shard"), None)
    split3, split2 = P(None, "shard", "expert"), P("shard", "expert")
    up_spec, down_spec = P("expert", None, "shard"), P("expert", "shard", None)
    in_specs = (
        both, P(("expert", "shard")), both, P(), P(), split3, split3, split2, split2, split2, up_spec, down_spec, both
    )
    out_specs = (both, both, P(), P(), split3, split3, split2, split2, split2, up_spec, down_spec)
    return jax.shard_map(per_device, mesh=mesh, in_specs=in_specs, out_specs=out_specs, check_vma=False)
```

```python
import jax
import jax.numpy as jnp
from jax import lax
from jax.experimental import pallas as pl
from jax.experimental.pallas import tpu as pltpu
from jax.sharding import PartitionSpec as P

PIECE = 256
norm_eps = 1e-06
far_below = -1e30
BF = jnp.bfloat16
F32 = jnp.float32
VMEM_BYTES = 56 * 1024 * 1024


def nn(a, b):
    return lax.dot_general(a, b, (((1,), (0,)), ((), ())), preferred_element_type=F32)


def nt(a, b):
    return lax.dot_general(a, b, (((1,), (1,)), ((), ())), preferred_element_type=F32)


def tn(a, b):
    return lax.dot_general(a, b, (((0,), (0,)), ((), ())), preferred_element_type=F32)


def inverse_rms(field):
    return lax.rsqrt(jnp.mean(field * field, axis=1, keepdims=True) + norm_eps)


def gelu_parts(u):
    cubic = 0.7978845608028654 * (u + 0.044715 * (u * u * u))
    bend = jnp.tanh(cubic)
    half = 0.5 * (1.0 + bend)
    slope = half + 0.5 * u * (1.0 - bend * bend) * (0.7978845608028654 * (1.0 + 0.134145 * (u * u)))
    return u * half, slope


def gelu_of(u):
    return 0.5 * u * (1.0 + jnp.tanh(0.7978845608028654 * (u + 0.044715 * (u * u * u))))


def fill_mask(piece_ref, mask_ref):
    length = mask_ref.shape[0]
    first = piece_ref[0]
    key_pos = lax.broadcasted_iota(jnp.int32, (length, length), 0)
    query_pos = lax.broadcasted_iota(jnp.int32, (length, length), 1)
    key_in = (key_pos >= first) & (key_pos < first + PIECE)
    query_in = (query_pos >= first) & (query_pos < first + PIECE)
    keep = (key_pos <= query_pos) | (key_in & query_in)
    mask_ref[...] = jnp.where(keep, 0.0, far_below)


def bias_strip(vector_row, strip_ref):
    wide = jnp.broadcast_to(vector_row, (128, vector_row.shape[1]))
    strip_ref[...] = pltpu.roll(wide, vector_row.shape[1] - 127, 1, stride=1, stride_axis=0)


def flatten(blocks_ref, flat_ref, sems):
    rows = blocks_ref.shape[1]
    copies = [
        pltpu.make_async_copy(blocks_ref.at[i], flat_ref.at[pl.ds(i * rows, rows), :], sems.at[i])
        for i in range(blocks_ref.shape[0])
    ]
    for copy in copies:
        copy.start()
    return copies


def arrive(copies):
    for copy in copies:
        copy.wait()


def unflatten(flat_ref, blocks_ref, start):
    count = blocks_ref.shape[0]
    rows = flat_ref.shape[0] // count
    for i in range(count):
        blocks_ref[i, start:start + rows, :] = flat_ref[i * rows:i * rows + rows, :]


def weight_specs(weights):
    packed, qkv_rows, out_rows = weights
    if isinstance(packed, tuple):
        return list(packed), [HBM_SPEC, HBM_SPEC]
    return [packed], [HBM_SPEC]


def weight_sems(weights):
    packed = weights[0]
    count = 1 if isinstance(packed, tuple) else packed.shape[0]
    return [pltpu.SemaphoreType.DMA((count,)), pltpu.SemaphoreType.DMA((count,))]


def weight_views(weights, refs):
    packed, qkv_rows, out_rows = weights
    if isinstance(packed, tuple):
        return refs[0], refs[1], refs[2:]
    return refs[0].at[:, 0:qkv_rows, :], refs[0].at[:, qkv_rows:qkv_rows + out_rows, :], refs[1:]


def attend_kernel(
    weights, piece_ref, x_ref, gain_ref, *refs
):
    w_ref, wo_ref, refs = weight_views(weights, refs)
    (vec_ref, out_ref, normed_ref, qkv_ref, mixed_ref, lse_ref,
     mask_ref, strip_ref, score_ref, prob_ref, flat_ref, flat_out_ref, w_sem, wo_sem) = refs
    length, width = x_ref.shape
    w_copies = flatten(w_ref, flat_ref, w_sem)
    wo_copies = flatten(wo_ref, flat_out_ref, wo_sem)
    tiles = length // 128
    fill_mask(piece_ref, mask_ref)
    field = x_ref[...]
    normed_ref[...] = (field * inverse_rms(field) * gain_ref[...]).astype(BF)

    arrive(w_copies)

    def project(c, _):
        cols = pl.ds(pl.multiple_of(c * 256, 256), 256)
        qkv_ref[:, cols] = nt(normed_ref[...], flat_ref[cols, :]).astype(BF)
        return 0

    lax.fori_loop(0, 3 * width // 256, project, 0)
    lane_low = lax.broadcasted_iota(jnp.int32, (length, 128), 1) < 64
    row_low = lax.broadcasted_iota(jnp.int32, (128, length), 0) < 64

    def pair(hp, _):
        base = hp * 128
        q2 = qkv_ref[:, pl.ds(pl.multiple_of(base, 128), 128)] * jnp.asarray(0.125, BF)
        v2 = qkv_ref[:, pl.ds(pl.multiple_of(2 * width + base, 128), 128)]
        mixed = []
        for half in range(2):
            head = hp * 2 + half
            keep = lane_low if half == 0 else ~lane_low
            qm = jnp.where(keep, q2, jnp.zeros_like(q2))
            bias_strip(vec_ref[pl.ds(head, 1), :], strip_ref)
            peak = jnp.full((1, length), far_below, F32)
            for jt in range(tiles):
                rows = slice(jt * 128, jt * 128 + 128)
                k2 = qkv_ref[rows, pl.ds(pl.multiple_of(width + base, 128), 128)]
                at = 128 * (tiles - 1 - jt)
                s = nt(k2, qm) + strip_ref[:, at:at + length] + mask_ref[rows, :]
                score_ref[rows, :] = s
                peak = jnp.maximum(peak, jnp.max(s, axis=0, keepdims=True))
            total = jnp.zeros((1, length), F32)
            for jt in range(tiles):
                rows = slice(jt * 128, jt * 128 + 128)
                e = jnp.exp(score_ref[rows, :] - peak)
                total = total + jnp.sum(e, axis=0, keepdims=True)
                prob_ref[rows, :] = e.astype(BF)
            lse_ref[pl.ds(head, 1), :] = peak + jnp.log(total)
            mixed.append(tn(v2, prob_ref[...]) * (1.0 / total))
        both = jnp.where(row_low, mixed[0], mixed[1]).astype(BF)
        mixed_ref[:, pl.ds(pl.multiple_of(base, 128), 128)] = both.T
        return 0

    lax.fori_loop(0, width // 128, pair, 0)

    arrive(wo_copies)

    def back(c, _):
        cols = pl.ds(pl.multiple_of(c * 256, 256), 256)
        out_ref[:, cols] = x_ref[:, cols] + nt(mixed_ref[...], flat_out_ref[cols, :])
        return 0

    lax.fori_loop(0, width // 256, back, 0)


HBM_SPEC = pl.BlockSpec(memory_space=pltpu.HBM)
SMEM_SPEC = pl.BlockSpec(memory_space=pltpu.SMEM)
VMEM_SPEC = pl.BlockSpec(memory_space=pltpu.VMEM)


def attend(piece, x, gain, weights, vectors):
    length, width = x.shape
    w_args, w_specs = weight_specs(weights)
    heads = vectors.shape[0]
    span = vectors.shape[1]
    return pl.pallas_call(
        lambda *refs: attend_kernel(weights, *refs),
        out_shape=(
            jax.ShapeDtypeStruct((length, width), F32),
            jax.ShapeDtypeStruct((length, width), BF),
            jax.ShapeDtypeStruct((length, 3 * width), BF),
            jax.ShapeDtypeStruct((length, width), BF),
            jax.ShapeDtypeStruct((heads, length), F32),
        ),
        in_specs=[SMEM_SPEC] + [VMEM_SPEC] * 2 + w_specs + [VMEM_SPEC],
        out_specs=[VMEM_SPEC] * 5,
        scratch_shapes=[
            pltpu.VMEM((length, length), F32),
            pltpu.VMEM((128, span), F32),
            pltpu.VMEM((length, length), F32),
            pltpu.VMEM((length, length), BF),
            pltpu.VMEM((3 * width, width), BF),
            pltpu.VMEM((width, width), BF),
        ] + weight_sems(weights),
        compiler_params=pltpu.CompilerParams(vmem_limit_bytes=VMEM_BYTES),
        cost_estimate=pl.CostEstimate(
            flops=8 * length * width * width + 4 * length * length * width,
            bytes_accessed=20 * length * width + 8 * width * width,
            transcendentals=heads * length * length,
        ),
        name="attend",
    )(piece, x, gain, *w_args, vectors)


def attend_back_kernel(
    tail, weights, ride, piece_ref, x_ref, gain_ref, *refs
):
    ride_refs, refs = (refs[len(refs) - ride.scratch:], refs[:len(refs) - ride.scratch]) if ride else ((), refs)
    w_ref, wo_ref, refs = weight_views(weights, refs)
    (vec_ref, normed_ref, qkv_ref, mixed_ref, lse_ref, grad_ref), refs = refs[:6], refs[6:]
    tail_ref, refs = (refs[0], refs[1:]) if tail else (None, refs)
    rides_in, refs = (refs[:ride.inputs], refs[ride.inputs:]) if ride else ((), refs)
    rides_out, refs = (refs[:ride.outputs], refs[ride.outputs:]) if ride else ((), refs)
    grad_refs, refs = (refs[1:len(refs) - 15], refs[:1] + refs[len(refs) - 15:])
    (dx_ref, dvec_ref, dgain_ref,
     mask_ref, strip_ref, sums_ref, prob_ref, ds_ref, low_ref, do_ref, dqkv_ref, delta_ref,
     flat_ref, flat_out_ref, w_sem, wo_sem) = refs
    wo_copies = flatten(wo_ref, flat_out_ref, wo_sem)
    w_copies = flatten(w_ref, flat_ref, w_sem)
    turns, rows_turn, end = (
        ride.board(rides_in, rides_out, ride_refs, dx_ref, low_ref) if ride else ([], None, None)
    )
    length, width = x_ref.shape
    heads = vec_ref.shape[0]
    tiles = length // 128
    fill_mask(piece_ref, mask_ref)
    low_ref[...] = grad_ref[...].astype(BF)

    arrive(wo_copies)

    def out_back(c, _):
        cols = pl.ds(pl.multiple_of(c * 256, 256), 256)
        do_ref[:, cols] = nn(low_ref[...], flat_out_ref[:, cols]).astype(BF)
        return 0

    lax.fori_loop(0, width // 256, out_back, 0)

    def out_weights_back(c, _):
        cols = pl.ds(pl.multiple_of(c * 256, 256), 256)
        flat_out_ref[cols, :] = tn(low_ref[:, cols], mixed_ref[...]).astype(BF)
        return 0

    lax.fori_loop(0, width // 256, out_weights_back, 0)
    pick = (
        lax.broadcasted_iota(jnp.int32, (delta_ref.shape[0], width), 1) // (width // heads)
        == lax.broadcasted_iota(jnp.int32, (delta_ref.shape[0], width), 0)
    ).astype(F32)
    delta_ref[...] = lax.dot_general(
        pick, do_ref[...].astype(F32) * mixed_ref[...].astype(F32), (((1,), (1,)), ((), ())),
        precision=lax.Precision.HIGHEST, preferred_element_type=F32,
    )
    lane_low = lax.broadcasted_iota(jnp.int32, (length, 128), 1) < 64
    lane_low_tile = lax.broadcasted_iota(jnp.int32, (128, 128), 1) < 64
    row_low = lax.broadcasted_iota(jnp.int32, (128, length), 0) < 64
    flip = (
        lax.broadcasted_iota(jnp.int32, (128, 128), 0) + lax.broadcasted_iota(jnp.int32, (128, 128), 1) == 127
    ).astype(F32)
    sums_ref[...] = jnp.zeros_like(sums_ref)

    def pair(hp, _):
        if rows_turn is not None:
            pl.when(hp == 0)(rows_turn)
        for at, turn in enumerate(turns):
            pl.when(hp == min(1 + 3 * at, width // 128 - 1))(turn)
        base = hp * 128
        q_cols = pl.ds(pl.multiple_of(base, 128), 128)
        k_cols = pl.ds(pl.multiple_of(width + base, 128), 128)
        v_cols = pl.ds(pl.multiple_of(2 * width + base, 128), 128)
        q2 = qkv_ref[:, q_cols] * jnp.asarray(0.125, BF)
        do2 = do_ref[:, q_cols]
        parts = []
        for half in range(2):
            head = hp * 2 + half
            keep = lane_low if half == 0 else ~lane_low
            qm = jnp.where(keep, q2, jnp.zeros_like(q2))
            dm = jnp.where(keep, do2, jnp.zeros_like(do2))
            bias_strip(vec_ref[pl.ds(head, 1), :], strip_ref)
            lse = lse_ref[pl.ds(head, 1), :]
            delta = delta_ref[pl.ds(head, 1), :]
            for jt in range(tiles):
                rows = slice(jt * 128, jt * 128 + 128)
                at = 128 * (tiles - 1 - jt)
                s = nt(qkv_ref[rows, k_cols], qm) + strip_ref[:, at:at + length] + mask_ref[rows, :]
                p = jnp.exp(s - lse)
                dp = nt(qkv_ref[rows, v_cols], dm)
                ds = (p * (dp - delta)).astype(BF)
                prob_ref[half, rows, :] = p.astype(BF)
                ds_ref[half, rows, :] = ds
                if jt == 0:
                    sums_ref[:, at:at + length] = ds.astype(F32)
                    sums_ref[:, 0:at] = jnp.zeros((128, at), F32)
                else:
                    sums_ref[:, at:at + length] += ds.astype(F32)
            turned = lax.dot_general(
                flip, sums_ref[...], (((1,), (0,)), ((), ())),
                precision=lax.Precision.HIGHEST, preferred_element_type=F32,
            )
            turned = pltpu.roll(turned, 0, 1, stride=1, stride_axis=0)
            dvec_ref[pl.ds(head, 1), :] = jnp.sum(turned, axis=0, keepdims=True)
            parts.append(tn(qkv_ref[:, k_cols], ds_ref[half]) * 0.125)
        both = jnp.where(row_low, parts[0], parts[1]).astype(BF)
        dqkv_ref[:, q_cols] = both.T
        for jt in range(tiles):
            rows = slice(jt * 128, jt * 128 + 128)
            dk = jnp.where(lane_low_tile, nn(ds_ref[0, rows, :], q2), nn(ds_ref[1, rows, :], q2))
            dqkv_ref[rows, k_cols] = dk.astype(BF)
            dv = jnp.where(lane_low_tile, nn(prob_ref[0, rows, :], do2), nn(prob_ref[1, rows, :], do2))
            dqkv_ref[rows, v_cols] = dv.astype(BF)
        return 0

    lax.fori_loop(0, width // 128, pair, 0)

    arrive(w_copies)

    def rows_back(c, _):
        cols = pl.ds(pl.multiple_of(c * 256, 256), 256)
        dx_ref[:, cols] = nn(dqkv_ref[...], flat_ref[:, cols])
        return 0

    lax.fori_loop(0, width // 256, rows_back, 0)
    def weights_back(c, _):
        cols = pl.ds(pl.multiple_of(c * 256, 256), 256)
        flat_ref[cols, :] = tn(dqkv_ref[:, cols], normed_ref[...]).astype(BF)
        return 0

    lax.fori_loop(0, 3 * width // 256, weights_back, 0)

    qkv_rows = w_ref.shape[1]
    unflatten(flat_ref, grad_refs[0], 0)
    unflatten(flat_out_ref, grad_refs[-1], qkv_rows if len(grad_refs) == 1 else 0)
    if tail:
        start = qkv_rows + wo_ref.shape[1]
        for i in range(tail_ref.shape[0]):
            grad_refs[0][i, start:, :] = tail_ref[i]
    norm_back(x_ref, gain_ref, dx_ref, grad_ref, dx_ref, dgain_ref)
    if ride:
        end()


def norm_back(x_ref, gain_ref, upper_ref, base_ref, dx_ref, dgain_ref):
    field = x_ref[...]
    inverse = inverse_rms(field)
    unit = field * inverse
    upper = upper_ref[...]
    scaled = upper * gain_ref[...]
    dgain_ref[...] = jnp.sum(upper * unit, axis=0, keepdims=True)
    dx_ref[...] = base_ref[...] + inverse * (scaled - unit * jnp.mean(scaled * unit, axis=1, keepdims=True))


def attend_back(piece, x, gain, weights, vectors, normed, qkv, mixed, lse, grad, tail=None, ride=None):
    length, width = x.shape
    heads, span = vectors.shape
    w_args, w_specs = weight_specs(weights)
    packed = weights[0]
    grad_shapes = packed if isinstance(packed, tuple) else (packed,)
    tails = () if tail is None else (tail,)
    return pl.pallas_call(
        lambda *refs: attend_back_kernel(bool(tails), weights, ride, *refs),
        out_shape=(tuple(ride.out_shape) if ride else ())
        + (jax.ShapeDtypeStruct((length, width), F32),)
        + tuple(jax.ShapeDtypeStruct(g.shape, BF) for g in grad_shapes)
        + (
            jax.ShapeDtypeStruct((heads, span), F32),
            jax.ShapeDtypeStruct((1, width), F32),
        ),
        in_specs=[SMEM_SPEC] + [VMEM_SPEC] * 2 + w_specs + [VMEM_SPEC] * (6 + len(tails)) + (ride.in_specs if ride else []),
        out_specs=(ride.out_specs if ride else []) + [VMEM_SPEC] * (3 + len(grad_shapes)),
        scratch_shapes=[
            pltpu.VMEM((length, length), F32),
            pltpu.VMEM((128, span), F32),
            pltpu.VMEM((128, span), F32),
            pltpu.VMEM((2, length, length), BF),
            pltpu.VMEM((2, length, length), BF),
            pltpu.VMEM((length, width), BF),
            pltpu.VMEM((length, width), BF),
            pltpu.VMEM((length, 3 * width), BF),
            pltpu.VMEM((16, length), F32),
            pltpu.VMEM((3 * width, width), BF),
            pltpu.VMEM((width, width), BF),
        ] + weight_sems(weights) + (ride.scratch_shapes if ride else []),
        compiler_params=ride.params if ride else pltpu.CompilerParams(vmem_limit_bytes=VMEM_BYTES),
        cost_estimate=pl.CostEstimate(
            flops=16 * length * width * width + 10 * length * length * width,
            bytes_accessed=40 * length * width + 16 * width * width,
            transcendentals=heads * length * length,
        ),
        name="attend_back",
    )(piece, x, gain, *w_args, vectors, normed, qkv, mixed, lse, grad, *tails, *(ride.args if ride else []))


def mlp_chunk(c, parts, zones, up_ref, down_ref):
    hidden, width = up_ref.shape
    piece = hidden // (parts * zones)
    rows = [
        up_ref[pl.ds(pl.multiple_of(z * parts * piece + c * piece, 16), piece), :] for z in range(zones)
    ]
    span = down_ref.shape[1] // parts
    down = down_ref[:, pl.ds(pl.multiple_of(c * span, 16), span), :].reshape(-1, down_ref.shape[2])
    return jnp.concatenate(rows, axis=0), down


def mlp_loads(parts, zones, up_hbm, down_hbm, up_ref, down_ref, sems):
    piece = up_ref.shape[0] // (parts * zones)
    span = down_ref.shape[1] // parts
    loads = []
    for c in range(parts):
        chunk = [
            pltpu.make_async_copy(
                up_hbm.at[pl.ds((z * parts + c) * piece, piece), :],
                up_ref.at[pl.ds((z * parts + c) * piece, piece), :], sems.at[c, z],
            )
            for z in range(zones)
        ]
        columns = pl.ds(c * span, span)
        chunk.append(
            pltpu.make_async_copy(down_hbm.at[:, columns, :], down_ref.at[:, columns, :], sems.at[c, zones])
        )
        loads.append(chunk)
    for chunk in loads:
        for copy in chunk:
            copy.start()
    return loads


def mlp_kernel(parts, zones, x_ref, gain_ref, up_hbm, down_hbm, out_ref, normed_ref, up_ref, down_ref, sems):
    loads = mlp_loads(parts, zones, up_hbm, down_hbm, up_ref, down_ref, sems)
    field = x_ref[...]
    normed_ref[...] = (field * inverse_rms(field) * gain_ref[...]).astype(BF)
    out_ref[...] = field

    def chunk(c, _):
        for at, copies in enumerate(loads):
            pl.when(c == at)(lambda copies=copies: arrive(copies))
        up, down = mlp_chunk(c, parts, zones, up_ref, down_ref)
        hidden = gelu_of(nt(normed_ref[...], up)).astype(BF)
        out_ref[...] += nt(hidden, down)
        return 0

    lax.fori_loop(0, parts, chunk, 0)


def mlp(x, gain, up, down, parts, zones):
    length, width = x.shape
    hidden = up.shape[0]
    return pl.pallas_call(
        lambda *refs: mlp_kernel(parts, zones, *refs),
        out_shape=(jax.ShapeDtypeStruct((length, width), F32), jax.ShapeDtypeStruct((length, width), BF)),
        in_specs=[VMEM_SPEC] * 2 + [HBM_SPEC] * 2,
        out_specs=[VMEM_SPEC] * 2,
        scratch_shapes=[
            pltpu.VMEM(up.shape, BF), pltpu.VMEM(down.shape, BF), pltpu.SemaphoreType.DMA((parts, zones + 1))
        ],
        compiler_params=pltpu.CompilerParams(vmem_limit_bytes=VMEM_BYTES),
        cost_estimate=pl.CostEstimate(
            flops=4 * length * width * hidden, bytes_accessed=10 * length * width + 4 * width * hidden,
            transcendentals=length * hidden,
        ),
        name="mlp",
    )(x, gain, up, down)


def mlp_back_kernel(parts, zones, x_ref, gain_ref, up_hbm, down_hbm, normed_ref, grad_ref,
                    dx_ref, dup_ref, ddown_ref, dgain_ref, low_ref, acc_ref, up_ref, down_ref, sems):
    loads = mlp_loads(parts, zones, up_hbm, down_hbm, up_ref, down_ref, sems)
    low_ref[...] = grad_ref[...].astype(BF)
    acc_ref[...] = jnp.zeros_like(acc_ref)

    piece = up_ref.shape[0] // (parts * zones)
    span = down_ref.shape[1] // parts

    def chunk(c, _):
        for at, copies in enumerate(loads):
            pl.when(c == at)(lambda copies=copies: arrive(copies))
        up, down = mlp_chunk(c, parts, zones, up_ref, down_ref)
        hidden, slope = gelu_parts(nt(normed_ref[...], up))
        pre_grad = (nn(low_ref[...], down) * slope).astype(BF)
        ddown = tn(low_ref[...], hidden.astype(BF)).astype(BF)
        ddown_ref[:, pl.ds(pl.multiple_of(c * span, 16), span), :] = ddown.reshape(-1, span, ddown.shape[1])
        dup = tn(pre_grad, normed_ref[...]).astype(BF)
        for z in range(zones):
            at = pl.ds(pl.multiple_of(z * parts * piece + c * piece, 16), piece)
            dup_ref[at, :] = dup[z * piece:z * piece + piece, :]
        acc_ref[...] += nn(pre_grad, up)
        return 0

    lax.fori_loop(0, parts, chunk, 0)
    norm_back(x_ref, gain_ref, acc_ref, grad_ref, dx_ref, dgain_ref)


def mlp_back(x, gain, up, down, normed, grad, parts, zones):
    length, width = x.shape
    hidden = up.shape[0]
    return pl.pallas_call(
        lambda *refs: mlp_back_kernel(parts, zones, *refs),
        out_shape=(
            jax.ShapeDtypeStruct((length, width), F32),
            jax.ShapeDtypeStruct((hidden, width), BF),
            jax.ShapeDtypeStruct(down.shape, BF),
            jax.ShapeDtypeStruct((1, width), F32),
        ),
        in_specs=[VMEM_SPEC] * 2 + [HBM_SPEC] * 2 + [VMEM_SPEC] * 2,
        out_specs=[VMEM_SPEC] * 4,
        scratch_shapes=[
            pltpu.VMEM((length, width), BF), pltpu.VMEM((length, width), F32),
            pltpu.VMEM(up.shape, BF), pltpu.VMEM(down.shape, BF), pltpu.SemaphoreType.DMA((parts, zones + 1)),
        ],
        compiler_params=pltpu.CompilerParams(vmem_limit_bytes=VMEM_BYTES),
        cost_estimate=pl.CostEstimate(
            flops=10 * length * width * hidden, bytes_accessed=16 * length * width + 8 * width * hidden,
            transcendentals=length * hidden,
        ),
        name="mlp_back",
    )(x, gain, up, down, normed, grad)


MESH = pl.DeviceIdType.MESH


def flip(index, mask):
    bit = 1
    while bit <= mask:
        if mask & bit:
            index = index + bit - 2 * bit * ((index // bit) % 2)
        bit *= 2
    return index


def masks_of(bits):
    found = [0]
    for bit in bits:
        found = found + [m | bit for m in found]
    return found


def bits_below(size):
    found, bit = [], 1
    while bit < size:
        found.append(bit)
        bit *= 2
    return found


def halves_of(rows):
    cut = rows // 2 // 16 * 16
    return ((0, cut), (cut, rows - cut))


def routes_of(chips):
    bits = bits_below(chips)
    cut = len(bits) // 2
    return (bits, bits[cut:] + bits[:cut])


def greet(owner, zone, owners, zones):
    barrier = pltpu.get_barrier_semaphore()
    peers = [(flip(owner, bit), zone) for bit in bits_below(owners)]
    peers += [(owner, flip(zone, d)) for d in range(1, zones)]
    for peer in peers:
        pl.semaphore_signal(barrier, inc=1, device_id=peer, device_id_type=MESH)
    pl.semaphore_wait(barrier, len(peers))


def sender(send_sem, recv_sem):
    used = [0]

    def send(source, target, device):
        at = used[0]
        used[0] += 1
        copy = pltpu.make_async_remote_copy(
            source, target, send_sem.at[at], recv_sem.at[at], device_id=device, device_id_type=MESH
        )
        copy.start()
        return copy

    return send


def gather_copies(owners, zones):
    chips = owners // 2
    return zones - 1 + 2 * (chips - 1) + 2 * chips


def gather_kernel(owners, zones, used_rows, experts, capacity, *refs):
    count = len(used_rows)
    blocks, (late_ref, route_ref), refs = refs[:count], refs[count:count + 2], refs[count + 2:]
    outs, (slot_ref, spread_ref), refs = refs[:count], refs[count:count + 2], refs[count + 2:]
    slabs, turned = refs[:count], refs[count:2 * count]
    direct = capacity % 16 == 0
    near_ref, refs = (refs[2 * count], refs[:2 * count] + refs[2 * count + 1:]) if direct else (spread_ref, refs)
    slot_in_ref, send_sem, recv_sem, local_sem = refs[2 * count:]
    owner, zone = lax.axis_index("expert"), lax.axis_index("shard")
    greet(owner, zone, owners, zones)
    send = sender(send_sem, recv_sem)
    chips = owners // 2
    pending, finals = [], []

    def across(g):
        slabs[g][zone] = blocks[g][...]
        return [send(blocks[g], slabs[g].at[zone], (owner, flip(zone, d))) for d in range(1, zones)]

    def place(g, index, half):
        start, size = halves_of(used_rows[g])[half]
        return outs[g].at[index, pl.ds(start, size), :]

    def onward(g, half, index):
        finals.append(send(place(g, index, half), place(g, index, half), (flip(owner, 1), zone)))

    def start_rows(g, copies):
        for copy in copies:
            copy.wait_recv()
        pending.extend(copies)
        slab = slabs[g]
        turned[g][...] = slab[...].reshape(slab.shape[0] * slab.shape[1], slab.shape[2]).T
        local = pltpu.make_async_copy(
            turned[g].at[pl.ds(0, used_rows[g]), :], outs[g].at[owner], local_sem.at[g]
        )
        local.start()
        firsts = []
        for half, order in enumerate(routes_of(chips)):
            start, size = halves_of(used_rows[g])[half]
            source = turned[g].at[pl.ds(start, size), :]
            firsts.append([send(source, place(g, owner, half), (flip(owner, 2 * order[0]), zone))])
            finals.append(send(source, place(g, owner, half), (flip(owner, 1), zone)))
        return firsts, local

    def finish_rows(g, state, step):
        firsts, local = state
        if step == 0:
            local.wait()
        for half, order in enumerate(routes_of(chips)):
            for copy in firsts[half]:
                copy.wait_recv()
            pending.extend(firsts[half])
            done = masks_of(order[:step])
            arrived = [m | order[step] for m in done]
            if step + 1 < len(order):
                device = (flip(owner, 2 * order[step + 1]), zone)
                firsts[half] = [
                    send(place(g, flip(owner, 2 * m), half), place(g, flip(owner, 2 * m), half), device)
                    for m in done + arrived
                ]
            for m in arrived:
                onward(g, half, flip(owner, 2 * m))
        return firsts, local

    steps = len(routes_of(chips)[0])
    moving = {0: across(0)}
    states = {}
    slot_ref[0] = token_slots(route_ref[...], experts, capacity)
    near_copies = []

    def spread_zone(d):
        if not direct:
            return
        take = max(1, 384 // capacity)
        rows = late_ref if d == 0 else near_ref.at[d - 1]

        def chunk(i, _):
            hits = slot_hits(slot_ref[d], i * (take * capacity), take * capacity)
            picked = nn(hits[0] + hits[1], rows[...]).reshape(take, capacity, rows.shape[1])
            spread_ref[pl.ds(i * take, take), d] = picked.astype(BF)
            return 0

        lax.fori_loop(0, experts // take, chunk, 0)

    for g in range(count):
        states[g] = start_rows(g, moving[g])
        if g + 1 < count:
            moving[g + 1] = across(g + 1)
        if g == count - 1:
            for d in range(1, zones // 2):
                device = (owner, (zone + zones - 2 * d) % zones)
                near_copies.append(send(slot_ref.at[0], slot_in_ref.at[d - 1], device))
                near_copies.append(send(late_ref, near_ref.at[d - 1], device))
        if g == 1:
            spread_zone(0)
        if g > 0:
            for step in range(1, steps):
                states[g - 1] = finish_rows(g - 1, states[g - 1], step)
        states[g] = finish_rows(g, states[g], 0)
    for step in range(1, steps):
        states[count - 1] = finish_rows(count - 1, states[count - 1], step)
    for copy in near_copies:
        copy.wait_recv()
    for d in range(1, zones // 2):
        slot_ref[d] = slot_in_ref[d - 1]
        spread_zone(d)
    for copy in finals:
        copy.wait_recv()
    for copy in pending + finals + near_copies:
        copy.wait_send()


def gather_weights(blocks, used_rows, late, route_rows, owners, zones, experts, capacity):
    count = len(blocks)
    depth = zones * blocks[0].shape[0]
    groups = zones // 2
    copies = count * gather_copies(owners, zones) + 2 * (groups - 1)
    length = route_rows.shape[1]
    any_spec = pl.BlockSpec(memory_space=pltpu.HBM)
    direct = capacity % 16 == 0
    near_shape = (groups - 1,) + late.shape
    if direct:
        spread_shape, late_spec = (experts, groups, capacity, late.shape[1]), VMEM_SPEC
    else:
        spread_shape, late_spec = near_shape, any_spec
    return pl.pallas_call(
        lambda *refs: gather_kernel(owners, zones, used_rows, experts, capacity, *refs),
        out_shape=tuple(jax.ShapeDtypeStruct((owners, used, depth), BF) for used in used_rows)
        + (
            jax.ShapeDtypeStruct((groups, 8, length), F32),
            jax.ShapeDtypeStruct(spread_shape, BF),
        ),
        in_specs=[VMEM_SPEC] * count + [late_spec, VMEM_SPEC],
        out_specs=tuple([any_spec] * count) + (VMEM_SPEC, late_spec),
        scratch_shapes=[pltpu.VMEM((zones,) + b.shape, BF) for b in blocks]
        + [pltpu.VMEM((b.shape[1], depth), BF) for b in blocks]
        + ([pltpu.VMEM(near_shape, BF)] if direct else [])
        + [pltpu.VMEM((groups - 1, 8, length), F32)]
        + [pltpu.SemaphoreType.DMA((copies,)), pltpu.SemaphoreType.DMA((copies,)), pltpu.SemaphoreType.DMA((count,))],
        compiler_params=pltpu.CompilerParams(
            vmem_limit_bytes=61 * 1024 * 1024, collective_id=1, has_side_effects=True
        ),
        name="gather_weights",
    )(*blocks, late, route_rows)


def add_rows(into, other):
    return (into.astype(F32) + other.astype(F32)).astype(BF)


class Mail:
    def __init__(self, at, source, target, device, sems):
        self.at, self.source, self.target, self.device, self.sems = at, source, target, device, sems

    def make(self):
        return pltpu.make_async_remote_copy(
            self.source(), self.target(), self.sems[0].at[self.at], self.sems[1].at[self.at],
            device_id=self.device, device_id_type=MESH,
        )

    def start(self):
        self.make().start()
        return self

    def wait_recv(self):
        self.make().wait_recv()

    def wait_send(self):
        self.make().wait_send()


class Post:
    def __init__(self, send_sem, recv_sem):
        self.sems, self.mails = (send_sem, recv_sem), []

    def plan(self, source, target, device):
        mail = Mail(len(self.mails), source, target, device, self.sems)
        self.mails.append(mail)
        return mail

    def close(self):
        for mail in self.mails:
            mail.wait_send()


def cross_copies(owners):
    return 1 + 2 * (owners // 2 - 1)


def cross_scratch(owners, used, depth):
    chips = owners // 2
    return [
        pltpu.VMEM((chips, used, depth), BF),
        pltpu.VMEM((chips, used, depth), BF),
        pltpu.VMEM((chips - 1, used, depth), BF),
        pltpu.SemaphoreType.DMA,
    ]


def cross_plan(post, part, keep, near, far, local_sem, owner, zone, owners):
    chips = owners // 2
    chip, core = owner // 2, owner % 2
    used = keep.shape[1]
    orders = routes_of(chips)
    steps = len(orders[0])
    first = post.plan(lambda: part.at[:, 1 - core], lambda: near, (flip(owner, 1), zone))

    def window(half):
        start, size = halves_of(used)[half]
        return pl.ds(start, size)

    def slot_of(step, i):
        return chips - 2 * len(masks_of(orders[0][step + 1:])) + i

    pushes = []
    for step in range(steps):
        mails = []
        for half, order in enumerate(orders):
            bit, rest = order[step], masks_of(order[step + 1:])
            for i, m in enumerate(rest):
                index = flip(chip, bit | m)
                mails.append(post.plan(
                    lambda index=index, half=half: keep.at[index, window(half), :],
                    lambda i=i, half=half, step=step: far.at[slot_of(step, i), window(half), :],
                    (flip(owner, 2 * bit), zone),
                ))
        pushes.append(mails)

    def local():
        return pltpu.make_async_copy(part.at[:, core], keep, local_sem)

    def begin():
        local().start()
        first.start()

    def meet():
        local().wait()
        first.wait_recv()

        def one(h, _):
            keep[h] = add_rows(keep[h], near[h])
            return 0

        lax.fori_loop(0, chips, one, 0)
        for mail in pushes[0]:
            mail.start()

    def absorb(step):
        for mail in pushes[step]:
            mail.wait_recv()
        for half, order in enumerate(orders):
            for i, m in enumerate(masks_of(order[step + 1:])):
                index = flip(chip, m)
                keep[index, window(half), :] = add_rows(
                    keep[index, window(half), :], far[slot_of(step, i), window(half), :]
                )
        if step + 1 < steps:
            for mail in pushes[step + 1]:
                mail.start()

    stages = [meet] + [lambda step=step: absorb(step) for step in range(steps)]
    return begin, stages


def zone_scratch(zones, used, depth):
    wide = -(-used // 128) * 128
    return [pltpu.VMEM((zones, depth // zones, wide), BF), pltpu.VMEM((zones - 1, depth // zones, wide), BF)]


def zone_shape(zones, used, depth):
    return jax.ShapeDtypeStruct((depth // zones, -(-used // 128) * 128), F32)


def zone_plan(post, slab, incoming, out_ref, owner, zone, zones):
    mails = [
        post.plan(
            lambda d=d: slab.at[flip(zone, d)], lambda d=d: incoming.at[d - 1], (owner, flip(zone, d))
        )
        for d in range(1, zones)
    ]

    def start(own):
        spare = slab.shape[2] - own.shape[0]
        if spare:
            own = jnp.concatenate([own, jnp.zeros((spare, own.shape[1]), BF)], axis=0)
        slab[...] = own.T.reshape(slab.shape)
        for mail in mails:
            mail.start()

    def end():
        total = slab[zone].astype(F32)
        for d in range(1, zones):
            mails[d - 1].wait_recv()
            total = total + incoming[d - 1].astype(F32)
        out_ref[...] = total

    return start, end


class Ride:
    def __init__(self, parts, zoned, owns, rows, owners, zones, capacity, depth, collective_id):
        groups = zones // 2
        self.owners, self.zones, self.capacity, self.zoned, self.count = owners, zones, capacity, zoned, len(parts)
        self.owns = len(owns)
        self.with_rows = rows is not None
        hbm = pl.BlockSpec(memory_space=pltpu.HBM)
        self.args = [p.reshape(owners // 2, 2, p.shape[1], depth) for p in parts] + list(owns)
        self.in_specs = [hbm] * len(parts) + [VMEM_SPEC] * len(owns)
        self.out_shape = [zone_shape(zones, p.shape[1], depth) for p in parts[:zoned]]
        self.out_shape += [jax.ShapeDtypeStruct(p.shape[1:], BF) for p in parts[zoned:]]
        self.out_shape += [zone_shape(zones, o.shape[0], depth) for o in owns]
        self.scratch_shapes = []
        for p in parts:
            self.scratch_shapes += cross_scratch(owners, p.shape[1], depth)
        for p in parts[:zoned]:
            self.scratch_shapes += zone_scratch(zones, p.shape[1], depth)
        for o in owns:
            self.scratch_shapes += zone_scratch(zones, o.shape[0], depth)
        copies = len(parts) * cross_copies(owners) + (zoned + len(owns)) * (zones - 1)
        if self.with_rows:
            y, slot_rows = rows
            length = slot_rows.shape[2]
            self.args += [y, slot_rows]
            self.in_specs += [hbm, VMEM_SPEC]
            self.out_shape += [jax.ShapeDtypeStruct((groups - 1, length, depth), BF)]
            self.scratch_shapes += [
                pltpu.VMEM((groups - 1,) + y.shape[:2] + (capacity, depth), BF),
                pltpu.SemaphoreType.DMA((groups - 1,)),
                *[pltpu.VMEM((length, depth), BF)] * (groups - 2),
            ]
            copies += groups - 1
        self.out_specs = [VMEM_SPEC] * len(self.out_shape)
        self.scratch_shapes += [pltpu.SemaphoreType.DMA((copies,)), pltpu.SemaphoreType.DMA((copies,))]
        self.inputs, self.outputs, self.scratch = len(self.args), len(self.out_shape), len(self.scratch_shapes)
        self.params = pltpu.CompilerParams(
            vmem_limit_bytes=61 * 1024 * 1024, collective_id=collective_id, has_side_effects=True
        )

    def board(self, inputs, outputs, scratch, room, spare):
        owner, zone = lax.axis_index("expert"), lax.axis_index("shard")
        owners, zones, count, groups = self.owners, self.zones, self.count, self.zones // 2
        greet(owner, zone, owners, zones)
        post = Post(scratch[-2], scratch[-1])
        plans = [cross_plan(post, inputs[g], *scratch[4 * g:4 * g + 4], owner, zone, owners) for g in range(count)]
        keeps = [scratch[4 * g] for g in range(count)]
        for begin, _ in plans:
            begin()
        zone_plans = []
        for g in range(self.zoned):
            slab, incoming = scratch[4 * count + 2 * g:4 * count + 2 * g + 2]
            zone_plans.append(zone_plan(post, slab, incoming, outputs[g], owner, zone, zones))
        for i in range(self.owns):
            at = 4 * count + 2 * (self.zoned + i)
            start, end = zone_plan(post, scratch[at], scratch[at + 1], outputs[count + i], owner, zone, zones)
            start(inputs[count + i][...])
            zone_plans.append((start, end))
        y_mails = []
        if self.with_rows:
            y_ref, slot_ref = inputs[count + self.owns:count + self.owns + 2]
            at = 4 * count + 2 * (self.zoned + self.owns)
            y_rows, y_sem = scratch[at:at + 2]
            y_part = [spare, *scratch[at + 2:-2]]

            def load(d):
                window = pl.ds(d * self.capacity, self.capacity)
                return pltpu.make_async_copy(y_ref.at[:, :, window, :], y_rows.at[d - 1], y_sem.at[d - 1])

            for d in range(1, groups):
                load(d).start()
                y_mails.append(post.plan(
                    lambda d=d: y_part[d - 1], lambda d=d: outputs[-1].at[d - 1], (owner, (zone + 2 * d) % zones)
                ))

        def rows_turn():
            for d in range(1, groups):
                load(d).wait()
                collect_rows(y_rows.at[d - 1], slot_ref[d], room)
                y_part[d - 1][...] = room[...].astype(BF)
                y_mails[d - 1].start()

        turns = []
        for g in range(count):
            turns.append(lambda g=g: self.run([plans[g - 1][1][1]] if g else [], [plans[g][1][0]]))
        if count == 1:
            turns.append(lambda: self.run([plans[0][1][1]]))
        longest = len(plans[0][1]) if plans else 0

        def finish_part():
            for t in range(1, count + longest - 1):
                for g in reversed(range(count)):
                    at = t - g
                    if 1 <= at < longest and (at > 1 or (g == count - 1 and count > 1)):
                        plans[g][1][at]()
                        if at == longest - 1 and g < self.zoned:
                            zone_plans[g][0](keeps[g][owner // 2])
            for g in range(self.zoned, count):
                outputs[g][...] = keeps[g][owner // 2]
            for _, end in zone_plans:
                end()
            for mail in y_mails:
                mail.wait_recv()
            post.close()

        return turns, rows_turn if self.with_rows else None, finish_part

    def run(self, *groups):
        for acts in groups:
            for act in acts:
                act()


def collect_rows(rows_ref, slots, room):
    owners, local, capacity, width = rows_ref.shape
    span = 2 * local * capacity
    for h in range(owners // 2):
        hits = slot_hits(slots, jnp.int32(h * span), span)
        added = tn(hits[0] + hits[1], rows_ref[2 * h:2 * h + 2].reshape(span, width))
        if h == 0:
            room[...] = added
        else:
            room[...] += added


def finish_kernel(owners, zones, capacity, sizes, *refs):
    refs = list(refs)

    def take(count):
        found = refs[:count]
        del refs[:count]
        return found

    with_rows, chunks = sizes
    early_refs, (down_part, part, small) = take(2), take(3)
    own_refs, peer_refs = take(2), take(2)
    y_ref, slot_ref, x_ref, y_in = take(4) if with_rows else (None, None, None, None)
    *outs, small_out = take(5)
    sum_refs = take(2)
    y_out = take(1)[0] if with_rows else None
    cross_refs = [take(4) for _ in range(2)]
    zone_refs = [take(2) for _ in range(4)]
    small_mine, small_other = take(2)
    stages = [take(3) for _ in range(2)]
    add_sem = take(1)[0]
    if with_rows:
        y_rows, y_sum, y_sem = take(3)
    send_sem, recv_sem = take(2)
    owner, zone = lax.axis_index("expert"), lax.axis_index("shard")
    greet(owner, zone, owners, zones)
    post = Post(send_sem, recv_sem)
    plans = [
        cross_plan(post, p, *r, owner, zone, owners) for p, r in zip((down_part, part), cross_refs)
    ]
    for begin, _ in plans:
        begin()
    down, cross = [stages for _, stages in plans]
    if with_rows:
        y_copy = pltpu.make_async_copy(y_ref.at[:, :, pl.ds(0, capacity), :], y_rows, y_sem)
        y_copy.start()
    zone_starts, zone_ends = zip(
        *[zone_plan(post, r[0], r[1], out, owner, zone, zones) for r, out in zip(zone_refs, outs)]
    )
    for start, ref in zip(zone_starts, early_refs):
        start(ref[...])
    small_peers = [(flip(owner, bit), zone) for bit in bits_below(owners)]
    small_peers += [(owner, flip(zone, bit)) for bit in bits_below(zones)]
    small_mails = [
        post.plan(lambda i=i: small_mine.at[i], lambda i=i: small_other.at[i], peer)
        for i, peer in enumerate(small_peers)
    ]
    small_mine[0] = small[...]
    small_mails[0].start()

    def small_step(i):
        if i < len(small_mails):
            small_mails[i].wait_recv()
            small_mine[i + 1] = small_mine[i] + small_other[i]
            if i + 1 < len(small_mails):
                small_mails[i + 1].start()

    groups = zones // 2

    def add_stage(i):
        mine, theirs, total = stages[i]
        count = chunks[i]
        size = mine.shape[1]

        def loads(k):
            rows = pl.ds(k * size, size)
            return (
                pltpu.make_async_copy(own_refs[i].at[rows, :], mine.at[k % 2], add_sem.at[i, k % 2, 0]),
                pltpu.make_async_copy(peer_refs[i].at[rows, :], theirs.at[k % 2], add_sem.at[i, k % 2, 1]),
            )

        def store(k):
            return pltpu.make_async_copy(
                total.at[k % 2], sum_refs[i].at[pl.ds(k * size, size), :], add_sem.at[i, k % 2, 2]
            )

        for copy in loads(0):
            copy.start()
        for k in range(count):
            if k + 1 < count:
                for copy in loads(k + 1):
                    copy.start()
            for copy in loads(k):
                copy.wait()
            if k >= 2:
                store(k - 2).wait()
            total[k % 2] = mine[k % 2] + theirs[k % 2].astype(F32)
            store(k).start()
        for k in range(max(0, count - 2), count):
            store(k).wait()

    down[0]()
    small_step(0)
    add_stage(0)
    down[1]()
    cross[0]()
    small_step(1)
    if with_rows:
        y_copy.wait()
        collect_rows(y_rows, slot_ref[0], y_sum)
        total = x_ref[...] + y_sum[...]
        for d in range(1, groups):
            total = total + y_in[d - 1].astype(F32)
        y_out[...] = total.astype(BF)
    small_step(2)
    for act in down[2:]:
        act()
    zone_starts[2](cross_refs[0][0][owner // 2])
    for act in cross[1:-1]:
        act()
    zone_ends[0]()
    zone_ends[1]()
    small_step(3)
    cross[-1]()
    zone_starts[3](cross_refs[1][0][owner // 2])
    small_step(4)
    add_stage(1)
    for i in range(5, len(small_mails)):
        small_step(i)
    small_out[...] = small_mine[len(small_mails)]
    zone_ends[2]()
    zone_ends[3]()
    post.close()


def finish(early, down_part, first_part, small, owns, peers, owners, zones, capacity, rows=None):
    depth = first_part.shape[2]
    chips = owners // 2
    used = tuple(o.shape[0] for o in early) + (down_part.shape[1], first_part.shape[1])
    cross_parts = [p.reshape(chips, 2, p.shape[1], depth) for p in (down_part, first_part)]
    flat = [o.reshape(-1, o.shape[-1]) for o in owns]
    flat_peers = [p.reshape(-1, p.shape[-1]) for p in peers]
    chunk = 256
    chunks = tuple(f.shape[0] // chunk for f in flat)
    rounds = len(bits_below(owners)) + len(bits_below(zones))
    copies = 2 * cross_copies(owners) + 4 * (zones - 1) + rounds
    hbm = pl.BlockSpec(memory_space=pltpu.HBM)
    args = [*early, *cross_parts, small, *flat, *flat_peers]
    in_specs = [VMEM_SPEC, VMEM_SPEC, hbm, hbm, VMEM_SPEC] + [hbm] * 4
    out_shape = [zone_shape(zones, u, depth) for u in used] + [jax.ShapeDtypeStruct(small.shape, F32)]
    out_shape += [jax.ShapeDtypeStruct(f.shape, F32) for f in flat]
    out_specs = [VMEM_SPEC] * 5 + [hbm] * 2
    scratch = cross_scratch(owners, used[2], depth) + cross_scratch(owners, used[3], depth)
    for u in used:
        scratch += zone_scratch(zones, u, depth)
    scratch += [pltpu.VMEM((rounds + 1,) + small.shape, F32), pltpu.VMEM((rounds,) + small.shape, F32)]
    for f in flat:
        shape = (2, chunk, f.shape[1])
        scratch += [pltpu.VMEM(shape, F32), pltpu.VMEM(shape, BF), pltpu.VMEM(shape, F32)]
    scratch += [pltpu.SemaphoreType.DMA((2, 2, 3))]
    if rows is not None:
        y, slot_rows, x, y_near = rows
        args += [y, slot_rows, x, y_near]
        in_specs += [hbm, VMEM_SPEC, VMEM_SPEC, VMEM_SPEC]
        out_shape += [jax.ShapeDtypeStruct(x.shape, BF)]
        out_specs += [VMEM_SPEC]
        scratch += [
            pltpu.VMEM(y.shape[:2] + (capacity, depth), BF), pltpu.VMEM(x.shape, F32), pltpu.SemaphoreType.DMA,
        ]
    scratch += [pltpu.SemaphoreType.DMA((copies,)), pltpu.SemaphoreType.DMA((copies,))]
    sizes = (rows is not None, chunks)
    return pl.pallas_call(
        lambda *refs: finish_kernel(owners, zones, capacity, sizes, *refs),
        out_shape=tuple(out_shape),
        in_specs=in_specs,
        out_specs=tuple(out_specs),
        scratch_shapes=scratch,
        compiler_params=pltpu.CompilerParams(
            vmem_limit_bytes=61 * 1024 * 1024, collective_id=2, has_side_effects=True
        ),
        name="finish",
    )(*args)


def three_pieces(row):
    top = row.astype(BF)
    rest = row - top.astype(F32)
    middle = rest.astype(BF)
    low = (rest - middle.astype(F32)).astype(BF)
    return jnp.concatenate([top, middle, low, jnp.zeros((5, row.shape[1]), BF)], axis=0)


def sum_pieces(rows):
    return rows[0:1] + rows[1:2] + rows[2:3]


def token_slots(route_rows, experts, capacity):
    length = route_rows.shape[1]
    ids = lax.broadcasted_iota(jnp.int32, (experts, length), 0)
    first, second = route_rows[0:1] == ids, route_rows[1:2] == ids
    named = jnp.where(first | second, 1.0, 0.0).astype(BF)
    earlier = (
        lax.broadcasted_iota(jnp.int32, (length, length), 0) < lax.broadcasted_iota(jnp.int32, (length, length), 1)
    )
    place = nn(named, jnp.where(earlier, 1.0, 0.0).astype(BF)) + (ids * capacity).astype(F32)
    rows = [jnp.sum(jnp.where(hit, place, 0.0), axis=0, keepdims=True) for hit in (first, second)]
    return jnp.concatenate(rows + [jnp.zeros((6, length), F32)], axis=0)


def slot_hits(slots, start, count):
    place = lax.broadcasted_iota(jnp.int32, (count, slots.shape[1]), 0).astype(F32) + start.astype(F32)
    one, zero = jnp.asarray(1.0, F32), jnp.asarray(0.0, F32)
    return [jnp.where(place == slots[k:k + 1], one, zero).astype(BF) for k in range(2)]


def greet_plane(owner, zone, owners, zones):
    barrier = pltpu.get_barrier_semaphore()
    peers = [(flip(owner, mask), zone) for mask in range(1, owners)]
    peers += [(owner, (zone + d) % zones) for d in range(2, zones, 2)] + [(owner, flip(zone, 1))]
    for peer in peers:
        pl.semaphore_signal(barrier, inc=1, device_id=peer, device_id_type=MESH)
    pl.semaphore_wait(barrier, len(peers))


def peer_order(owners):
    return list(range(2, owners)) + [1, 0]


def softmax_pair(logits, route_rows):
    ids = lax.broadcasted_iota(jnp.int32, logits.shape, 0)
    a, b = [jnp.sum(jnp.where(route_rows[k:k + 1] == ids, logits, 0.0), axis=0, keepdims=True) for k in range(2)]
    peak = jnp.maximum(a, b)
    ea, eb = jnp.exp(a - peak), jnp.exp(b - peak)
    return ea / (ea + eb), eb / (ea + eb)


def send_rows_kernel(
    owners, zones, capacity, x_ref, gain_ref, router_ref, route_ref, slot_ref, slices_ref,
    normed_ref, gates_ref, rows_ref, gate_ref, other_ref,
    near_ref, near_gates_ref, packed_ref, tags_ref, tags_in_ref, send_sem, recv_sem, local_sem,
):
    owner, zone = lax.axis_index("expert"), lax.axis_index("shard")
    tags_ref[...] = jnp.zeros_like(tags_ref)
    greet_plane(owner, zone, owners, zones)
    send = sender(send_sem, recv_sem)
    groups = zones // 2
    local = rows_ref.shape[1]
    span = local * capacity
    field = x_ref[...]
    normed_ref[...] = (field * inverse_rms(field) * gain_ref[...]).astype(BF)
    cut = normed_ref.shape[1] // 2
    lanes = [pl.ds(0, cut), pl.ds(cut, cut)]
    copies = {}
    for half in range(2):
        for d in range(1, groups):
            device = (owner, (zone + zones - 2 * d) % zones)
            copies[d, half] = send(normed_ref.at[:, lanes[half]], near_ref.at[d - 1, :, lanes[half]], device)
    gates = softmax_pair(nt(router_ref[...], normed_ref[...]), route_ref[...])
    gates_ref[...] = jnp.concatenate(list(gates) + [jnp.zeros((6, gates[0].shape[1]), F32)], axis=0)
    for d in range(1, groups):
        copies[d, 2] = send(gates_ref, near_gates_ref.at[d - 1], (owner, (zone + zones - 2 * d) % zones))
    arrivals, stays = [], []
    for part in range(local):
        arrivals.append(send(slices_ref.at[part], other_ref.at[part], (owner, flip(zone, 1))))
    def ship(d, mask, target, half):
        columns = slice(None) if half is None else lanes[half]
        for part in range(local):
            source = packed_ref.at[d, mask, pl.ds(part * capacity, capacity), columns]
            place = rows_ref.at[owner, part, pl.ds(d * capacity, capacity), columns]
            if mask:
                arrivals.append(send(source, place, (target, zone)))
            else:
                at = (2 * d + (half or 0)) * local + part
                copy = pltpu.make_async_copy(source, place, local_sem.at[at])
                copy.start()
                stays.append(copy)

    for d in range(groups):
        for half in (None,) if d == 0 else (0, 1):
            if d:
                copies[d, half].wait_recv()
                if half == 0:
                    copies[d, 2].wait_recv()
            rows = normed_ref if d == 0 else near_ref.at[d - 1]
            weights = gates_ref[...] if d == 0 else near_gates_ref[d - 1]
            pieces = [three_pieces(weights[k:k + 1]) for k in range(2)]
            slots = slot_ref[d]
            for mask in peer_order(owners):
                target = flip(owner, mask)
                hits = slot_hits(slots, target * span, span)
                both = hits[0] + hits[1]
                if half is None:
                    packed_ref[d, mask] = nn(both, rows[...]).astype(BF)
                else:
                    packed_ref[d, mask, :, lanes[half]] = nn(both, rows[:, lanes[half]]).astype(BF)
                ship(d, mask, target, half)
                if half == 1:
                    continue
                tag = sum_pieces(nt(pieces[0], hits[0]) + nt(pieces[1], hits[1]))
                tags_ref[d, mask, :, 0:span] = jnp.broadcast_to(tag, (8, span))
                if mask:
                    arrivals.append(send(tags_ref.at[d, mask], tags_in_ref.at[d, owner], (target, zone)))
                else:
                    tags_in_ref[d, owner] = tags_ref[d, mask]
    for copy in arrivals:
        copy.wait_recv()
    for d in range(groups):
        for source in range(owners):
            column = tags_in_ref[d, source].T
            for part in range(local):
                gate_ref[source, part, d * capacity:(d + 1) * capacity, :] = column[
                    part * capacity:(part + 1) * capacity, 0:1
                ]
    for copy in stays:
        copy.wait()
    for copy in list(copies.values()) + arrivals:
        copy.wait_send()


def send_rows(x, gain, router, route_rows, slot_rows, slices, owners, zones, local, capacity):
    length, width = x.shape
    groups = zones // 2
    span = local * capacity
    any_spec = pl.BlockSpec(memory_space=pltpu.HBM)
    wide = -(-span // 128) * 128
    copies = local + 3 * (groups - 1) + (owners - 1) * (local + 1 + (groups - 1) * (2 * local + 1))
    return pl.pallas_call(
        lambda *refs: send_rows_kernel(owners, zones, capacity, *refs),
        out_shape=(
            jax.ShapeDtypeStruct((length, width), BF),
            jax.ShapeDtypeStruct((8, length), F32),
            jax.ShapeDtypeStruct((owners, local, groups * capacity, width), BF),
            jax.ShapeDtypeStruct((owners, local, groups * capacity, 1), F32),
            jax.ShapeDtypeStruct(slices.shape, slices.dtype),
        ),
        in_specs=[VMEM_SPEC] * 5 + [any_spec],
        out_specs=(VMEM_SPEC, VMEM_SPEC, any_spec, VMEM_SPEC, any_spec),
        scratch_shapes=[
            pltpu.VMEM((groups - 1, length, width), BF),
            pltpu.VMEM((groups - 1, 8, length), F32),
            pltpu.VMEM((groups, owners, span, width), BF),
            pltpu.VMEM((groups, owners, 8, wide), F32),
            pltpu.VMEM((groups, owners, 8, wide), F32),
            pltpu.SemaphoreType.DMA((copies,)),
            pltpu.SemaphoreType.DMA((copies,)),
            pltpu.SemaphoreType.DMA((2 * groups * local,)),
        ],
        compiler_params=pltpu.CompilerParams(
            vmem_limit_bytes=61 * 1024 * 1024, collective_id=3, has_side_effects=True
        ),
        name="send_rows",
    )(x, gain, router, route_rows, slot_rows, slices)


def return_rows_kernel(
    owners, zones, capacity,
    rows_ref, dgate_ref, slot_ref, gates_ref, route_ref, x_ref, gain_ref, router_ref, normed_ref, top_ref,
    dx_ref, dgain_ref, drouter_ref,
    back_ref, tags_ref, tags_in_ref, part_ref, part_in_ref, mark_ref, mark_in_ref, sum_ref, send_sem, recv_sem, local_sem,
):
    owner, zone = lax.axis_index("expert"), lax.axis_index("shard")
    tags_ref[...] = jnp.zeros_like(tags_ref)
    greet_plane(owner, zone, owners, zones)
    send = sender(send_sem, recv_sem)
    groups = zones // 2
    local = rows_ref.shape[1]
    span = local * capacity
    chip = owner // 2
    cut = back_ref.shape[3] // 2
    lanes = [pl.ds(0, cut), pl.ds(cut, cut)]
    arrivals, stays, sent = {}, {}, []

    def ship(d, half):
        window = pl.ds(d * capacity, capacity)
        columns = slice(None) if half is None else lanes[half]
        for mask in peer_order(owners):
            target = flip(owner, mask)
            for part in range(local):
                source = rows_ref.at[target, part, window, columns]
                place = back_ref.at[d, owner, pl.ds(part * capacity, capacity), columns]
                if mask:
                    arrivals.setdefault((d, half, mask), []).append(send(source, place, (target, zone)))
                else:
                    at = (2 * d + (half or 0)) * local + part
                    copy = pltpu.make_async_copy(source, place, local_sem.at[at])
                    copy.start()
                    stays.setdefault((d, half), []).append(copy)

    def ship_tags(d):
        for mask in peer_order(owners):
            target = flip(owner, mask)
            columns = [dgate_ref[target, part, d * capacity:(d + 1) * capacity, :] for part in range(local)]
            column = jnp.concatenate(columns, axis=0)
            tags_ref[d, mask, :, 0:span] = jnp.broadcast_to(column, (span, 128)).T[0:8]
            if mask:
                arrivals.setdefault((d, "tags", mask), []).append(
                    send(tags_ref.at[d, mask], tags_in_ref.at[d, owner], (target, zone))
                )
            else:
                tags_in_ref[d, owner] = tags_ref[d, mask]

    def collect_zone(d, half):
        slots = slot_ref[d]
        columns = slice(None) if half is None else lanes[half]
        marks = [jnp.zeros((1, slots.shape[1]), F32) for _ in range(2)]
        for turn, hop in enumerate(list(range(1, owners // 2)) + [0]):
            for mask in (2 * hop, 2 * hop + 1):
                waits = arrivals.get((d, half, mask), [])
                if half != 1:
                    waits = waits + arrivals.get((d, "tags", mask), [])
                for copy in waits:
                    copy.wait_recv()
                if mask == 0:
                    for copy in stays[d, half]:
                        copy.wait()
            peer = flip(chip, hop)
            hits = slot_hits(slots, peer * (2 * span), 2 * span)
            rows = back_ref[d, pl.ds(2 * peer, 2), :, columns]
            added = tn(hits[0] + hits[1], rows.reshape(2 * span, rows.shape[2]))
            if turn == 0:
                sum_ref[:, columns] = added
            else:
                sum_ref[:, columns] += added
            if half == 1:
                continue
            tag = tags_in_ref[d, pl.ds(2 * peer, 2)]
            tag = jnp.concatenate([tag[0, 0:1, 0:span], tag[1, 0:1, 0:span]], axis=1)
            pieces = three_pieces(tag)
            for k in range(2):
                marks[k] = marks[k] + sum_pieces(nn(pieces, hits[k]))
        return marks

    for d in range(1, groups):
        ship(d, 0)
        ship_tags(d)
    incoming = {d: [] for d in range(1, groups)}
    for half in range(2):
        for d in range(1, groups):
            for mask in peer_order(owners):
                for copy in arrivals.get((d, half, mask), []):
                    copy.wait_send()
            if half == 0:
                ship(d, 1)
        if half == 1:
            ship(0, None)
            ship_tags(0)
        for d in range(1, groups):
            device = (owner, (zone + 2 * d) % zones)
            marks = collect_zone(d, half)
            part_ref[d - 1, :, lanes[half]] = sum_ref[:, lanes[half]].astype(BF)
            incoming[d].append(
                send(part_ref.at[d - 1, :, lanes[half]], part_in_ref.at[d - 1, :, lanes[half]], device)
            )
            if half == 0:
                mark_ref[d - 1] = jnp.concatenate(marks + [jnp.zeros((6, marks[0].shape[1]), F32)], axis=0)
                incoming[d].append(send(mark_ref.at[d - 1], mark_in_ref.at[d - 1], device))
    marks = collect_zone(0, None)
    for d in range(1, groups):
        for copy in incoming[d]:
            copy.wait_recv()
            sent.append(copy)
        sum_ref[...] += part_in_ref[d - 1].astype(F32)
        marks = [marks[k] + mark_in_ref[d - 1, k:k + 1, :] for k in range(2)]
    gates = [gates_ref[k:k + 1, :] for k in range(2)]
    mean = gates[0] * marks[0] + gates[1] * marks[1]
    ids = lax.broadcasted_iota(jnp.int32, (router_ref.shape[0], mean.shape[1]), 0)
    dlogits = jnp.zeros(ids.shape, F32)
    for k in range(2):
        dlogits = dlogits + jnp.where(route_ref[k:k + 1, :] == ids, gates[k] * (marks[k] - mean), 0.0)
    dlogits = dlogits.astype(BF)
    drouter_ref[...] = nn(dlogits, normed_ref[...])
    sum_ref[...] += tn(dlogits, router_ref[...])
    field = x_ref[...]
    inverse = inverse_rms(field)
    unit = field * inverse
    upper = sum_ref[...]
    scaled = upper * gain_ref[...]
    dgain_ref[...] = jnp.sum(upper * unit, axis=0, keepdims=True)
    dx_ref[...] = top_ref[...].astype(F32) + inverse * (
        scaled - unit * jnp.mean(scaled * unit, axis=1, keepdims=True)
    )
    for (d, half, _), copies in arrivals.items():
        if d == 0 or half == "tags":
            sent.extend(copies)
    for copy in sent:
        copy.wait_send()


def return_rows(rows, dgate, slot_rows, gates, route_rows, x, gain, router, normed, top, zones, capacity):
    length, width = x.shape
    owners, local = rows.shape[:2]
    groups = zones // 2
    span = local * capacity
    wide = -(-span // 128) * 128
    copies = 3 * (groups - 1) + (owners - 1) * (local + 1 + (groups - 1) * (2 * local + 1))
    return pl.pallas_call(
        lambda *refs: return_rows_kernel(owners, zones, capacity, *refs),
        out_shape=(
            jax.ShapeDtypeStruct((length, width), F32),
            jax.ShapeDtypeStruct((1, width), F32),
            jax.ShapeDtypeStruct(router.shape, F32),
        ),
        in_specs=[pl.BlockSpec(memory_space=pltpu.HBM)] + [VMEM_SPEC] * 9,
        out_specs=[VMEM_SPEC] * 3,
        scratch_shapes=[
            pltpu.VMEM((groups, owners, span, width), BF),
            pltpu.VMEM((groups, owners, 8, wide), F32),
            pltpu.VMEM((groups, owners, 8, wide), F32),
            pltpu.VMEM((groups - 1, length, width), BF),
            pltpu.VMEM((groups - 1, length, width), BF),
            pltpu.VMEM((groups - 1, 8, length), F32),
            pltpu.VMEM((groups - 1, 8, length), F32),
            pltpu.VMEM((length, width), F32),
            pltpu.SemaphoreType.DMA((copies,)),
            pltpu.SemaphoreType.DMA((copies,)),
            pltpu.SemaphoreType.DMA((2 * groups * local,)),
        ],
        compiler_params=pltpu.CompilerParams(
            vmem_limit_bytes=61 * 1024 * 1024, collective_id=4, has_side_effects=True
        ),
        name="return_rows",
    )(rows, dgate, slot_rows, gates, route_rows, x, gain, router, normed, top)


def experts_kernel(
    x_ref, c_ref, gate_ref, own_up_in, own_down_in, peer_up_in, peer_down_in,
    y_ref, dx_ref, dgate_ref, own_up_ref, own_down_ref, peer_up_ref, peer_down_ref,
    hidden_ref, pre_ref, dey_ref,
):
    sources, _, span, width = x_ref.shape
    size = own_up_in.shape[1]
    group = max(1, 384 // span)
    rows = group * span

    @pl.loop(0, sources // group)
    def _(i):
        at = pl.ds(i * group, group)
        rows_at = pl.ds(pl.multiple_of(i * rows, 16), rows)
        x = x_ref[at, 0].reshape(rows, width)
        c = c_ref[at, 0].reshape(rows, width)
        gate = gate_ref[at, 0].reshape(rows, 1)
        dey_ref[rows_at, :] = (gate * c.astype(F32)).astype(BF)
        dgate = jnp.zeros((rows, 1), F32)
        for part, (up_ref, down_ref) in enumerate(((own_up_in, own_down_in), (peer_up_in, peer_down_in))):
            cols = slice(part * size, part * size + size)
            hidden, slope = gelu_parts(nn(x, up_ref[...]))
            hidden = hidden.astype(BF)
            hidden_ref[rows_at, cols] = hidden
            back = nt(c, down_ref[...])
            dgate = dgate + jnp.sum(hidden.astype(F32) * back, axis=1, keepdims=True)
            pre_ref[rows_at, cols] = (gate * back * slope).astype(BF)
        y = nn(hidden_ref[rows_at, 0:size], own_down_in[...]) + nn(hidden_ref[rows_at, size:], peer_down_in[...])
        y_ref[at, 0] = (gate * y).astype(BF).reshape(group, span, width)
        dx = nt(pre_ref[rows_at, 0:size], own_up_in[...]) + nt(pre_ref[rows_at, size:], peer_up_in[...])
        dx_ref[at, 0] = dx.astype(BF).reshape(group, span, width)
        dgate_ref[at, 0] = dgate.reshape(group, span, 1)

    step = 256 if width % 256 == 0 else 128

    @pl.loop(0, width // step)
    def _(i):
        at = pl.ds(pl.multiple_of(i * step, step), step)
        x = x_ref[:, 0, :, at].reshape(sources * span, step)
        own_up_ref[at, :] = tn(x, pre_ref[:, 0:size])
        peer_up_ref[at, :] = tn(x, pre_ref[:, size:]).astype(BF)

    step = 256 if size % 256 == 0 else 128

    @pl.loop(0, size // step)
    def _(i):
        at = pl.ds(pl.multiple_of(i * step, step), step)
        own_down_ref[at, :] = tn(hidden_ref[:, at], dey_ref[...])
        peer_at = pl.ds(pl.multiple_of(i * step + size, step), step)
        peer_down_ref[at, :] = tn(hidden_ref[:, peer_at], dey_ref[...]).astype(BF)


def run_experts(x, c, gate, own_up, own_down, peer_up, peer_down):
    sources, local, span, width = x.shape
    hidden = own_up.shape[2]
    lean = sources * span > 2048
    once = dict(pipeline_mode=pl.Buffered(1)) if lean else {}
    row_spec = pl.BlockSpec((sources, 1, span, width), lambda e: (0, e, 0, 0), **once)
    gate_spec = pl.BlockSpec((sources, 1, span, 1), lambda e: (0, e, 0, 0), **once)
    late_spec = pl.BlockSpec((sources, 1, span, width), lambda e: (0, e, 0, 0), pipeline_mode=pl.Buffered(1))
    sq = pl.Squeezed()
    gup_spec = pl.BlockSpec((sq, width, hidden), lambda e: (e, 0, 0))
    gdown_spec = pl.BlockSpec((sq, hidden, width), lambda e: (e, 0, 0))
    rows = local * sources * span
    return pl.pallas_call(
        experts_kernel,
        grid=(local,),
        out_shape=(
            jax.ShapeDtypeStruct(x.shape, BF),
            jax.ShapeDtypeStruct(x.shape, BF),
            jax.ShapeDtypeStruct(gate.shape, F32),
            jax.ShapeDtypeStruct((local, width, hidden), F32),
            jax.ShapeDtypeStruct((local, hidden, width), F32),
            jax.ShapeDtypeStruct((local, width, hidden), BF),
            jax.ShapeDtypeStruct((local, hidden, width), BF),
        ),
        in_specs=[row_spec, late_spec, gate_spec, gup_spec, gdown_spec, gup_spec, gdown_spec],
        out_specs=[late_spec, row_spec, gate_spec, gup_spec, gdown_spec, gup_spec, gdown_spec],
        scratch_shapes=[
            pltpu.VMEM((sources * span, 2 * hidden), BF),
            pltpu.VMEM((sources * span, 2 * hidden), BF),
            pltpu.VMEM((sources * span, width), BF),
        ],
        compiler_params=pltpu.CompilerParams(vmem_limit_bytes=60 * 1024 * 1024),
        cost_estimate=pl.CostEstimate(
            flops=24 * rows * width * hidden, bytes_accessed=16 * rows * width, transcendentals=2 * rows * hidden,
        ),
        name="experts",
    )(x, c, gate, own_up, own_down, peer_up, peer_down)


def spread_kernel(slot_ref, rows_ref, out_ref):
    experts, zones, capacity, width = out_ref.shape
    take = max(1, 384 // capacity)

    def chunk(i, _):
        for zone in range(zones):
            hits = slot_hits(slot_ref[zone], i * (take * capacity), take * capacity)
            picked = nn(hits[0] + hits[1], rows_ref[zone])
            out_ref[pl.ds(i * take, take), zone] = picked.reshape(take, capacity, width).astype(BF)
        return 0

    lax.fori_loop(0, experts // take, chunk, 0)


def spread(slot_rows, rows, experts, capacity):
    zones, length, width = rows.shape
    return pl.pallas_call(
        spread_kernel,
        out_shape=jax.ShapeDtypeStruct((experts, zones, capacity, width), BF),
        in_specs=[VMEM_SPEC] * 2,
        out_specs=VMEM_SPEC,
        compiler_params=pltpu.CompilerParams(vmem_limit_bytes=VMEM_BYTES),
        cost_estimate=pl.CostEstimate(
            flops=2 * zones * experts * capacity * length * width,
            bytes_accessed=2 * zones * (experts * capacity + length) * width, transcendentals=0,
        ),
        name="spread",
    )(slot_rows, rows)


def collect_kernel(first, slot_ref, rows_ref, out_ref):
    experts, zones, capacity, width = rows_ref.shape
    length = out_ref.shape[1]
    take = max(1, 384 // capacity)
    out_ref[...] = jnp.zeros_like(out_ref)

    def chunk(i, _):
        for zone in range(first, zones):
            hits = slot_hits(slot_ref[zone], i * (take * capacity), take * capacity)
            rows = rows_ref[pl.ds(i * take, take), zone].reshape(take * capacity, width)
            out_ref[zone - first] += tn(hits[0] + hits[1], rows)
        return 0

    lax.fori_loop(0, experts // take, chunk, 0)


def collect(slot_rows, rows, first=0):
    experts, zones, capacity, width = rows.shape
    length = slot_rows.shape[2]
    return pl.pallas_call(
        lambda *refs: collect_kernel(first, *refs),
        out_shape=jax.ShapeDtypeStruct((zones - first, length, width), F32),
        in_specs=[VMEM_SPEC] * 2,
        out_specs=VMEM_SPEC,
        compiler_params=pltpu.CompilerParams(vmem_limit_bytes=VMEM_BYTES),
        cost_estimate=pl.CostEstimate(
            flops=2 * zones * experts * capacity * length * width,
            bytes_accessed=2 * zones * (experts * capacity + 2 * length) * width, transcendentals=0,
        ),
        name="collect",
    )(slot_rows, rows)


bucket_edges = (1, 2, 3, 4, 6, 8, 12, 16, 24, 32, 48, 64, 96, 128, 192, 256, 384, 512, 768, 1024, 1536)


def bucket_onehot(length, buckets):
    distance = (length - 1) - jnp.arange(2 * length, dtype=jnp.int32)
    edge_list = jnp.array(bucket_edges, dtype=jnp.int32)
    magnitude = jnp.sum(
        (jnp.abs(distance)[:, None] >= edge_list[None, :]).astype(jnp.int32), axis=1, dtype=jnp.int32
    )
    bucket = magnitude + buckets // 2 * (distance > 0).astype(jnp.int32)
    real = jnp.arange(2 * length)[:, None] < 2 * length - 1
    hit = (bucket[:, None] == jnp.arange(buckets, dtype=jnp.int32)[None, :]) & real
    return hit.astype(F32)


def shift_from(value, distance):
    size = lax.axis_size("shard")
    return lax.ppermute(value, "shard", [((z + distance) % size, z) for z in range(size)])


def shift_to(value, distance):
    size = lax.axis_size("shard")
    return lax.ppermute(value, "shard", [(z, (z + distance) % size) for z in range(size)])


def swap_pair(value):
    return lax.ppermute(value, "shard", [(z, z ^ 1) for z in range(lax.axis_size("shard"))])


def exchange(value):
    return lax.all_to_all(value, "expert", split_axis=0, concat_axis=0, tiled=True)


def per_device(
    tokens, piece_start, routes, norm_gains, bias_tables, qkv_weight, out_weight, mlp_up, mlp_down, router,
    expert_up, expert_down, cotangent,
):
    length, width = tokens.shape
    owners = lax.axis_size("expert")
    zones = lax.axis_size("shard") // 2
    local = expert_up.shape[0]
    experts_all = local * owners
    capacity = 3 * routes.shape[1] * length // (2 * experts_all)
    qkv_cols, out_cols = qkv_weight.shape[2], out_weight.shape[2]
    zones_all = 2 * zones
    router_pad = 16
    direct = capacity % 16 == 0
    parts = mlp_down.shape[0] // qkv_weight.shape[1]
    aligned = qkv_cols % 16 == 0 and out_cols % 16 == 0 and qkv_cols % out_cols == 0

    def padded(block):
        return jnp.pad(block, ((0, 0), (0, -block.shape[1] % 128)))

    down_block = mlp_down.reshape(parts, -1, mlp_down.shape[1]).transpose(1, 0, 2).reshape(qkv_weight.shape[1], -1)
    router_block = jnp.pad(router, ((0, 0), (0, router_pad - router.shape[1])))
    route_rows = routes.T
    first, up_full, down_full, last, slot_rows, cotangent_rows = gather_weights(
        [
            padded(jnp.concatenate([qkv_weight[0], out_weight[0]], axis=1)),
            padded(mlp_up),
            padded(down_block),
            padded(jnp.concatenate([qkv_weight[1], out_weight[1], router_block], axis=1)),
        ],
        (qkv_cols + out_cols, mlp_up.shape[1], parts * mlp_down.shape[1], qkv_cols + out_cols + router_pad),
        cotangent, route_rows, owners, zones_all, experts_all, capacity,
    )

    def layer_weights(block):
        if aligned:
            return (block, qkv_cols, out_cols)
        flat = (block[:, :qkv_cols].reshape(1, -1, width), block[:, qkv_cols:qkv_cols + out_cols].reshape(1, -1, width))
        return (flat, 3 * width, width)

    up_full = up_full.reshape(-1, width)
    if mlp_down.shape[1] % 16:
        down_full = down_full.reshape(owners, parts, -1, width).transpose(1, 0, 2, 3).reshape(1, -1, width)
    router_full = last[:, qkv_cols + out_cols:qkv_cols + out_cols + router.shape[1]].reshape(experts_all, width)

    first, up_late = lax.optimization_barrier((first, expert_up))
    weights0, weights1 = layer_weights(first), layer_weights(last)
    up_other = swap_pair(up_late)

    def dispatch(rows):
        packed = spread(slot_rows, rows, experts_all, capacity)
        return exchange(packed.reshape(owners, local, zones * capacity, width))

    if direct:
        cotangent_rows = exchange(cotangent_rows.reshape(owners, local, zones * capacity, width))
    else:
        cotangent_rows = dispatch(jnp.concatenate([cotangent[None], cotangent_rows]))

    def undo(rows):
        back = exchange(rows).reshape(experts_all, zones, capacity, width)
        return collect(slot_rows, back)


    onehot = bucket_onehot(length, bias_tables.shape[2])
    vectors = lax.dot_general(
        bias_tables, onehot, (((2,), (1,)), ((), ())), precision=lax.Precision.HIGHEST
    )
    gains = [norm_gains[i:i + 1] for i in range(4)]
    x0 = tokens.astype(F32)
    x1, ah0, qkv0, o0, lse0 = attend(piece_start, x0, gains[0], weights0, vectors[0])
    x2, mh = mlp(x1, gains[1], up_full, down_full, parts, zones_all)
    x3, ah1, qkv1, o1, lse1 = attend(piece_start, x2, gains[2], weights1, vectors[1])

    x3, up_other, cotangent_rows = lax.optimization_barrier((x3, up_other, cotangent_rows))
    if direct:
        eh, gates, eh_rows, gate_rows, down_other = send_rows(
            x3, gains[3], router_full, route_rows, slot_rows, expert_down, owners, zones_all, local, capacity
        )
    else:
        down_other = swap_pair(expert_down)
        eh = (x3 * inverse_rms(x3) * gains[3]).astype(BF)
        gates = jnp.concatenate(softmax_pair(nt(router_full, eh), route_rows))
        eh_rows = dispatch(jnp.stack([eh] + [shift_from(eh, 2 * d) for d in range(1, zones)]))
        slot_ids = jnp.arange(experts_all * capacity, dtype=jnp.int32).astype(F32)
        marks = [slot_rows[d, :2][None] == slot_ids[:, None, None] for d in range(zones)]

        def gate_slots(d):
            held = gates if d == 0 else shift_from(gates, 2 * d)
            return jnp.sum(jnp.where(marks[d], held[None], 0.0), axis=(1, 2)).reshape(experts_all, capacity)

        gate_rows = exchange(
            jnp.stack([gate_slots(d) for d in range(zones)], axis=1).reshape(owners, local, zones * capacity)
        )[..., None]
    y_rows, dx_rows, dgate_rows, own_up, own_down, peer_up, peer_down = run_experts(
        eh_rows, cotangent_rows, gate_rows, expert_up, expert_down, up_other, down_other
    )
    if direct:
        dx3, dgain3, grad_router = return_rows(
            dx_rows, dgate_rows, slot_rows, gates, route_rows, x3, gains[3], router_full, eh, cotangent,
            zones_all, capacity,
        )
    else:
        dx_back = undo(dx_rows)
        dgate_back = exchange(dgate_rows[..., 0]).reshape(experts_all, zones, capacity)
        token_grad, gate_grad = dx_back[0], 0.0
        for d in range(zones):
            part = jnp.sum(jnp.where(marks[d], dgate_back[:, d].reshape(-1)[:, None, None], 0.0), axis=0)
            gate_grad = gate_grad + (part if d == 0 else shift_to(part, 2 * d))
        for d in range(1, zones):
            token_grad = token_grad + shift_to(dx_back[d].astype(BF), 2 * d).astype(F32)
        dchoice = gates * (gate_grad - jnp.sum(gates * gate_grad, axis=0, keepdims=True))
        chosen = route_rows[:, None, :] == jnp.arange(experts_all, dtype=jnp.int32)[None, :, None]
        dlogits = jnp.sum(jnp.where(chosen, dchoice[:, None, :], 0.0), axis=0).astype(BF)
        grad_router = nn(dlogits, eh)
        deh = token_grad + tn(dlogits, router_full)
        unit3 = x3 * inverse_rms(x3)
        scaled = deh * gains[3]
        dx3 = cotangent.astype(F32) + inverse_rms(x3) * (
            scaled - unit3 * jnp.mean(scaled * unit3, axis=1, keepdims=True)
        )
        dgain3 = jnp.sum(deh * unit3, axis=0)[None]
    router_rows = jnp.pad(
        grad_router.astype(BF).reshape(owners, local, width), ((0, 0), (0, router_pad - local), (0, 0))
    )

    def layer_grads(results, tail=None):
        grads = results[1:-2]
        if not aligned:
            pieces = [g.reshape(owners, -1, width) for g in grads] + ([] if tail is None else [tail])
            grads = [jnp.concatenate(pieces, axis=1)]
        return results[0], grads[0], results[-2], results[-1]

    dx3, y_rows = lax.optimization_barrier((dx3, y_rows))
    y_back = exchange(y_rows)
    dx2, last_part, dvec1, dgain2 = layer_grads(
        attend_back(
            piece_start, x2, gains[2], weights1, vectors[1], ah1, qkv1, o1, lse1, dx3, router_rows if aligned else None,
        ),
        router_rows,
    )
    peer_up = swap_pair(peer_up)
    dx2, peer_down = lax.optimization_barrier((dx2, peer_down))
    peer_down = swap_pair(peer_down)
    dx1, up_part, down_part, dgain1 = mlp_back(
        x1, gains[1], up_full, down_full, mh, dx2, parts, zones_all
    )
    if mlp_down.shape[1] % 16:
        down_part = down_part.reshape(parts, owners, -1, width).transpose(1, 0, 2, 3)
    dx1, y_back, peer_up = lax.optimization_barrier((dx1, y_back, peer_up))
    ride = Ride(
        [last_part, up_part.reshape(owners, -1, width)], 0, [], (y_back, slot_rows) if direct else None,
        owners, zones_all, capacity, width, 6,
    )
    last_own, up_own, *results = attend_back(
        piece_start, x0, gains[0], weights0, vectors[0], ah0, qkv0, o0, lse0, dx1, None, ride
    )
    y_near = results.pop(0) if direct else None
    dx0, first_part, dvec0, dgain0 = layer_grads(results)
    dx0, peer_down = lax.optimization_barrier((dx0, peer_down))
    dtables = lax.dot_general(
        jnp.stack([dvec0, dvec1]), onehot, (((2,), (0,)), ((), ())), precision=lax.Precision.HIGHEST
    )
    dgains = jnp.concatenate([dgain0, dgain1, dgain2, dgain3])
    small = jnp.concatenate([dgains.reshape(-1), dtables.reshape(-1)])
    small = jnp.pad(small, (0, -small.size % 1024)).reshape(-1, 128)
    last_grad, up_grad, down_grad, first_grad, small, grad_up, grad_down, *finals = finish(
        (last_own, up_own), down_part.reshape(owners, -1, width), first_part, small, (own_up, own_down), (peer_up, peer_down), owners, zones_all, capacity,
        (y_back, slot_rows, x3, y_near) if direct else None,
    )
    grad_up, grad_down = grad_up.reshape(own_up.shape), grad_down.reshape(own_down.shape)
    if direct:
        output = finals[0]
    else:
        y_zones = collect(slot_rows, y_back.reshape(experts_all, zones, capacity, width))
        output = x3 + y_zones[0]
        for d in range(1, zones):
            output = output + shift_to(y_zones[d].astype(BF), 2 * d).astype(F32)
        output = output.astype(BF)
    small = small.reshape(-1)
    grad_qkv = jnp.stack([first_grad[:, :qkv_cols], last_grad[:, :qkv_cols]])
    grad_out = jnp.stack(
        [first_grad[:, qkv_cols:qkv_cols + out_cols], last_grad[:, qkv_cols:qkv_cols + out_cols]]
    )
    grad_router_out = last_grad[:, qkv_cols + out_cols:qkv_cols + out_cols + local]
    grad_mlp_up = up_grad[:, :mlp_up.shape[1]]
    down_cols = mlp_down.shape[1]
    grad_mlp_down = down_grad[:, :parts * down_cols].reshape(-1, parts, down_cols).transpose(1, 0, 2)
    grad_mlp_down = grad_mlp_down.reshape(mlp_down.shape)
    return (
        output,
        dx0,
        small[:dgains.size].reshape(dgains.shape),
        small[dgains.size:dgains.size + dtables.size].reshape(dtables.shape),
        grad_qkv,
        grad_out,
        grad_mlp_up,
        grad_mlp_down,
        grad_router_out,
        grad_up,
        grad_down,
    )


def solution(mesh):
    both = P(("expert", "shard"), None)
    split3, split2 = P(None, "shard", "expert"), P("shard", "expert")
    up_spec, down_spec = P("expert", None, "shard"), P("expert", "shard", None)
    in_specs = (
        both, P(("expert", "shard")), both, P(), P(), split3, split3, split2, split2, split2, up_spec, down_spec, both
    )
    out_specs = (both, both, P(), P(), split3, split3, split2, split2, split2, up_spec, down_spec)
    return jax.shard_map(per_device, mesh=mesh, in_specs=in_specs, out_specs=out_specs, check_vma=False)
```

```python
import jax
import jax.numpy as jnp
from jax import lax
from jax.experimental import pallas as pl
from jax.experimental.pallas import tpu as pltpu
from jax.sharding import PartitionSpec as P

PIECE = 256
norm_eps = 1e-06
far_below = -1e30
BF = jnp.bfloat16
F32 = jnp.float32
VMEM_BYTES = 56 * 1024 * 1024


def nn(a, b):
    return lax.dot_general(a, b, (((1,), (0,)), ((), ())), preferred_element_type=F32)


def nt(a, b):
    return lax.dot_general(a, b, (((1,), (1,)), ((), ())), preferred_element_type=F32)


def tn(a, b):
    return lax.dot_general(a, b, (((0,), (0,)), ((), ())), preferred_element_type=F32)


def inverse_rms(field):
    return lax.rsqrt(jnp.mean(field * field, axis=1, keepdims=True) + norm_eps)


def gelu_parts(u):
    cubic = 0.7978845608028654 * (u + 0.044715 * (u * u * u))
    bend = jnp.tanh(cubic)
    half = 0.5 * (1.0 + bend)
    slope = half + 0.5 * u * (1.0 - bend * bend) * (0.7978845608028654 * (1.0 + 0.134145 * (u * u)))
    return u * half, slope


def gelu_of(u):
    return 0.5 * u * (1.0 + jnp.tanh(0.7978845608028654 * (u + 0.044715 * (u * u * u))))


def fill_mask(piece_ref, mask_ref):
    length = mask_ref.shape[0]
    first = piece_ref[0]
    key_pos = lax.broadcasted_iota(jnp.int32, (length, length), 0)
    query_pos = lax.broadcasted_iota(jnp.int32, (length, length), 1)
    key_in = (key_pos >= first) & (key_pos < first + PIECE)
    query_in = (query_pos >= first) & (query_pos < first + PIECE)
    keep = (key_pos <= query_pos) | (key_in & query_in)
    mask_ref[...] = jnp.where(keep, 0.0, far_below)


def bias_strip(vector_row, strip_ref):
    wide = jnp.broadcast_to(vector_row, (128, vector_row.shape[1]))
    strip_ref[...] = pltpu.roll(wide, vector_row.shape[1] - 127, 1, stride=1, stride_axis=0)


def flatten(blocks_ref, flat_ref, sems):
    rows = blocks_ref.shape[1]
    copies = [
        pltpu.make_async_copy(blocks_ref.at[i], flat_ref.at[pl.ds(i * rows, rows), :], sems.at[i])
        for i in range(blocks_ref.shape[0])
    ]
    for copy in copies:
        copy.start()
    return copies


def arrive(copies):
    for copy in copies:
        copy.wait()


def unflatten(flat_ref, blocks_ref, start):
    count = blocks_ref.shape[0]
    rows = flat_ref.shape[0] // count
    for i in range(count):
        blocks_ref[i, start:start + rows, :] = flat_ref[i * rows:i * rows + rows, :]


def weight_specs(weights):
    packed, qkv_rows, out_rows = weights
    if isinstance(packed, tuple):
        return list(packed), [HBM_SPEC, HBM_SPEC]
    return [packed], [HBM_SPEC]


def weight_sems(weights):
    packed = weights[0]
    count = 1 if isinstance(packed, tuple) else packed.shape[0]
    return [pltpu.SemaphoreType.DMA((count,)), pltpu.SemaphoreType.DMA((count,))]


def weight_views(weights, refs):
    packed, qkv_rows, out_rows = weights
    if isinstance(packed, tuple):
        return refs[0], refs[1], refs[2:]
    return refs[0].at[:, 0:qkv_rows, :], refs[0].at[:, qkv_rows:qkv_rows + out_rows, :], refs[1:]


def attend_kernel(
    weights, piece_ref, x_ref, gain_ref, *refs
):
    w_ref, wo_ref, refs = weight_views(weights, refs)
    (vec_ref, out_ref, normed_ref, qkv_ref, mixed_ref, lse_ref,
     mask_ref, strip_ref, score_ref, prob_ref, flat_ref, flat_out_ref, w_sem, wo_sem) = refs
    length, width = x_ref.shape
    w_copies = flatten(w_ref, flat_ref, w_sem)
    wo_copies = flatten(wo_ref, flat_out_ref, wo_sem)
    tiles = length // 128
    fill_mask(piece_ref, mask_ref)
    field = x_ref[...]
    normed_ref[...] = (field * inverse_rms(field) * gain_ref[...]).astype(BF)

    arrive(w_copies)

    def project(c, _):
        cols = pl.ds(pl.multiple_of(c * 256, 256), 256)
        qkv_ref[:, cols] = nt(normed_ref[...], flat_ref[cols, :]).astype(BF)
        return 0

    lax.fori_loop(0, 3 * width // 256, project, 0)
    lane_low = lax.broadcasted_iota(jnp.int32, (length, 128), 1) < 64
    row_low = lax.broadcasted_iota(jnp.int32, (128, length), 0) < 64

    def pair(hp, _):
        base = hp * 128
        q2 = qkv_ref[:, pl.ds(pl.multiple_of(base, 128), 128)] * jnp.asarray(0.125, BF)
        v2 = qkv_ref[:, pl.ds(pl.multiple_of(2 * width + base, 128), 128)]
        mixed = []
        for half in range(2):
            head = hp * 2 + half
            keep = lane_low if half == 0 else ~lane_low
            qm = jnp.where(keep, q2, jnp.zeros_like(q2))
            bias_strip(vec_ref[pl.ds(head, 1), :], strip_ref)
            peak = jnp.full((1, length), far_below, F32)
            for jt in range(tiles):
                rows = slice(jt * 128, jt * 128 + 128)
                k2 = qkv_ref[rows, pl.ds(pl.multiple_of(width + base, 128), 128)]
                at = 128 * (tiles - 1 - jt)
                s = nt(k2, qm) + strip_ref[:, at:at + length] + mask_ref[rows, :]
                score_ref[rows, :] = s
                peak = jnp.maximum(peak, jnp.max(s, axis=0, keepdims=True))
            total = jnp.zeros((1, length), F32)
            for jt in range(tiles):
                rows = slice(jt * 128, jt * 128 + 128)
                e = jnp.exp(score_ref[rows, :] - peak)
                total = total + jnp.sum(e, axis=0, keepdims=True)
                prob_ref[rows, :] = e.astype(BF)
            lse_ref[pl.ds(head, 1), :] = peak + jnp.log(total)
            mixed.append(tn(v2, prob_ref[...]) * (1.0 / total))
        both = jnp.where(row_low, mixed[0], mixed[1]).astype(BF)
        mixed_ref[:, pl.ds(pl.multiple_of(base, 128), 128)] = both.T
        return 0

    lax.fori_loop(0, width // 128, pair, 0)

    arrive(wo_copies)

    def back(c, _):
        cols = pl.ds(pl.multiple_of(c * 256, 256), 256)
        out_ref[:, cols] = x_ref[:, cols] + nt(mixed_ref[...], flat_out_ref[cols, :])
        return 0

    lax.fori_loop(0, width // 256, back, 0)


HBM_SPEC = pl.BlockSpec(memory_space=pltpu.HBM)
SMEM_SPEC = pl.BlockSpec(memory_space=pltpu.SMEM)
VMEM_SPEC = pl.BlockSpec(memory_space=pltpu.VMEM)


def attend(piece, x, gain, weights, vectors):
    length, width = x.shape
    w_args, w_specs = weight_specs(weights)
    heads = vectors.shape[0]
    span = vectors.shape[1]
    return pl.pallas_call(
        lambda *refs: attend_kernel(weights, *refs),
        out_shape=(
            jax.ShapeDtypeStruct((length, width), F32),
            jax.ShapeDtypeStruct((length, width), BF),
            jax.ShapeDtypeStruct((length, 3 * width), BF),
            jax.ShapeDtypeStruct((length, width), BF),
            jax.ShapeDtypeStruct((heads, length), F32),
        ),
        in_specs=[SMEM_SPEC] + [VMEM_SPEC] * 2 + w_specs + [VMEM_SPEC],
        out_specs=[VMEM_SPEC] * 5,
        scratch_shapes=[
            pltpu.VMEM((length, length), F32),
            pltpu.VMEM((128, span), F32),
            pltpu.VMEM((length, length), F32),
            pltpu.VMEM((length, length), BF),
            pltpu.VMEM((3 * width, width), BF),
            pltpu.VMEM((width, width), BF),
        ] + weight_sems(weights),
        compiler_params=pltpu.CompilerParams(vmem_limit_bytes=VMEM_BYTES),
        cost_estimate=pl.CostEstimate(
            flops=8 * length * width * width + 4 * length * length * width,
            bytes_accessed=20 * length * width + 8 * width * width,
            transcendentals=heads * length * length,
        ),
        name="attend",
    )(piece, x, gain, *w_args, vectors)


def attend_back_kernel(
    tail, weights, ride, piece_ref, x_ref, gain_ref, *refs
):
    ride_refs, refs = (refs[len(refs) - ride.scratch:], refs[:len(refs) - ride.scratch]) if ride else ((), refs)
    w_ref, wo_ref, refs = weight_views(weights, refs)
    (vec_ref, normed_ref, qkv_ref, mixed_ref, lse_ref, grad_ref), refs = refs[:6], refs[6:]
    tail_ref, refs = (refs[0], refs[1:]) if tail else (None, refs)
    rides_in, refs = (refs[:ride.inputs], refs[ride.inputs:]) if ride else ((), refs)
    rides_out, refs = (refs[:ride.outputs], refs[ride.outputs:]) if ride else ((), refs)
    grad_refs, refs = (refs[1:len(refs) - 15], refs[:1] + refs[len(refs) - 15:])
    (dx_ref, dvec_ref, dgain_ref,
     mask_ref, strip_ref, sums_ref, prob_ref, ds_ref, low_ref, do_ref, dqkv_ref, delta_ref,
     flat_ref, flat_out_ref, w_sem, wo_sem) = refs
    wo_copies = flatten(wo_ref, flat_out_ref, wo_sem)
    w_copies = flatten(w_ref, flat_ref, w_sem)
    turns, rows_turn, end = (
        ride.board(rides_in, rides_out, ride_refs, dx_ref, low_ref) if ride else ([], None, None)
    )
    length, width = x_ref.shape
    heads = vec_ref.shape[0]
    tiles = length // 128
    fill_mask(piece_ref, mask_ref)
    low_ref[...] = grad_ref[...].astype(BF)

    arrive(wo_copies)

    def out_back(c, _):
        cols = pl.ds(pl.multiple_of(c * 256, 256), 256)
        do_ref[:, cols] = nn(low_ref[...], flat_out_ref[:, cols]).astype(BF)
        return 0

    lax.fori_loop(0, width // 256, out_back, 0)

    def out_weights_back(c, _):
        cols = pl.ds(pl.multiple_of(c * 256, 256), 256)
        flat_out_ref[cols, :] = tn(low_ref[:, cols], mixed_ref[...]).astype(BF)
        return 0

    lax.fori_loop(0, width // 256, out_weights_back, 0)
    pick = (
        lax.broadcasted_iota(jnp.int32, (delta_ref.shape[0], width), 1) // (width // heads)
        == lax.broadcasted_iota(jnp.int32, (delta_ref.shape[0], width), 0)
    ).astype(F32)
    delta_ref[...] = lax.dot_general(
        pick, do_ref[...].astype(F32) * mixed_ref[...].astype(F32), (((1,), (1,)), ((), ())),
        precision=lax.Precision.HIGHEST, preferred_element_type=F32,
    )
    lane_low = lax.broadcasted_iota(jnp.int32, (length, 128), 1) < 64
    lane_low_tile = lax.broadcasted_iota(jnp.int32, (128, 128), 1) < 64
    row_low = lax.broadcasted_iota(jnp.int32, (128, length), 0) < 64
    flip = (
        lax.broadcasted_iota(jnp.int32, (128, 128), 0) + lax.broadcasted_iota(jnp.int32, (128, 128), 1) == 127
    ).astype(F32)
    sums_ref[...] = jnp.zeros_like(sums_ref)

    def pair(hp, _):
        if rows_turn is not None:
            pl.when(hp == 0)(rows_turn)
        for at, turn in enumerate(turns):
            pl.when(hp == min(1 + 3 * at, width // 128 - 1))(turn)
        base = hp * 128
        q_cols = pl.ds(pl.multiple_of(base, 128), 128)
        k_cols = pl.ds(pl.multiple_of(width + base, 128), 128)
        v_cols = pl.ds(pl.multiple_of(2 * width + base, 128), 128)
        q2 = qkv_ref[:, q_cols] * jnp.asarray(0.125, BF)
        do2 = do_ref[:, q_cols]
        parts = []
        for half in range(2):
            head = hp * 2 + half
            keep = lane_low if half == 0 else ~lane_low
            qm = jnp.where(keep, q2, jnp.zeros_like(q2))
            dm = jnp.where(keep, do2, jnp.zeros_like(do2))
            bias_strip(vec_ref[pl.ds(head, 1), :], strip_ref)
            lse = lse_ref[pl.ds(head, 1), :]
            delta = delta_ref[pl.ds(head, 1), :]
            for jt in range(tiles):
                rows = slice(jt * 128, jt * 128 + 128)
                at = 128 * (tiles - 1 - jt)
                s = nt(qkv_ref[rows, k_cols], qm) + strip_ref[:, at:at + length] + mask_ref[rows, :]
                p = jnp.exp(s - lse)
                dp = nt(qkv_ref[rows, v_cols], dm)
                ds = (p * (dp - delta)).astype(BF)
                prob_ref[half, rows, :] = p.astype(BF)
                ds_ref[half, rows, :] = ds
                if jt == 0:
                    sums_ref[:, at:at + length] = ds.astype(F32)
                    sums_ref[:, 0:at] = jnp.zeros((128, at), F32)
                else:
                    sums_ref[:, at:at + length] += ds.astype(F32)
            turned = lax.dot_general(
                flip, sums_ref[...], (((1,), (0,)), ((), ())),
                precision=lax.Precision.HIGHEST, preferred_element_type=F32,
            )
            turned = pltpu.roll(turned, 0, 1, stride=1, stride_axis=0)
            dvec_ref[pl.ds(head, 1), :] = jnp.sum(turned, axis=0, keepdims=True)
            parts.append(tn(qkv_ref[:, k_cols], ds_ref[half]) * 0.125)
        both = jnp.where(row_low, parts[0], parts[1]).astype(BF)
        dqkv_ref[:, q_cols] = both.T
        for jt in range(tiles):
            rows = slice(jt * 128, jt * 128 + 128)
            dk = jnp.where(lane_low_tile, nn(ds_ref[0, rows, :], q2), nn(ds_ref[1, rows, :], q2))
            dqkv_ref[rows, k_cols] = dk.astype(BF)
            dv = jnp.where(lane_low_tile, nn(prob_ref[0, rows, :], do2), nn(prob_ref[1, rows, :], do2))
            dqkv_ref[rows, v_cols] = dv.astype(BF)
        return 0

    lax.fori_loop(0, width // 128, pair, 0)

    arrive(w_copies)

    def rows_back(c, _):
        cols = pl.ds(pl.multiple_of(c * 256, 256), 256)
        dx_ref[:, cols] = nn(dqkv_ref[...], flat_ref[:, cols])
        return 0

    lax.fori_loop(0, width // 256, rows_back, 0)
    def weights_back(c, _):
        cols = pl.ds(pl.multiple_of(c * 256, 256), 256)
        flat_ref[cols, :] = tn(dqkv_ref[:, cols], normed_ref[...]).astype(BF)
        return 0

    lax.fori_loop(0, 3 * width // 256, weights_back, 0)

    qkv_rows = w_ref.shape[1]
    unflatten(flat_ref, grad_refs[0], 0)
    unflatten(flat_out_ref, grad_refs[-1], qkv_rows if len(grad_refs) == 1 else 0)
    if tail:
        start = qkv_rows + wo_ref.shape[1]
        for i in range(tail_ref.shape[0]):
            grad_refs[0][i, start:, :] = tail_ref[i]
    norm_back(x_ref, gain_ref, dx_ref, grad_ref, dx_ref, dgain_ref)
    if ride:
        end()


def norm_back(x_ref, gain_ref, upper_ref, base_ref, dx_ref, dgain_ref):
    field = x_ref[...]
    inverse = inverse_rms(field)
    unit = field * inverse
    upper = upper_ref[...]
    scaled = upper * gain_ref[...]
    dgain_ref[...] = jnp.sum(upper * unit, axis=0, keepdims=True)
    dx_ref[...] = base_ref[...] + inverse * (scaled - unit * jnp.mean(scaled * unit, axis=1, keepdims=True))


def attend_back(piece, x, gain, weights, vectors, normed, qkv, mixed, lse, grad, tail=None, ride=None):
    length, width = x.shape
    heads, span = vectors.shape
    w_args, w_specs = weight_specs(weights)
    packed = weights[0]
    grad_shapes = packed if isinstance(packed, tuple) else (packed,)
    tails = () if tail is None else (tail,)
    return pl.pallas_call(
        lambda *refs: attend_back_kernel(bool(tails), weights, ride, *refs),
        out_shape=(tuple(ride.out_shape) if ride else ())
        + (jax.ShapeDtypeStruct((length, width), F32),)
        + tuple(jax.ShapeDtypeStruct(g.shape, BF) for g in grad_shapes)
        + (
            jax.ShapeDtypeStruct((heads, span), F32),
            jax.ShapeDtypeStruct((1, width), F32),
        ),
        in_specs=[SMEM_SPEC] + [VMEM_SPEC] * 2 + w_specs + [VMEM_SPEC] * (6 + len(tails)) + (ride.in_specs if ride else []),
        out_specs=(ride.out_specs if ride else []) + [VMEM_SPEC] * (3 + len(grad_shapes)),
        scratch_shapes=[
            pltpu.VMEM((length, length), F32),
            pltpu.VMEM((128, span), F32),
            pltpu.VMEM((128, span), F32),
            pltpu.VMEM((2, length, length), BF),
            pltpu.VMEM((2, length, length), BF),
            pltpu.VMEM((length, width), BF),
            pltpu.VMEM((length, width), BF),
            pltpu.VMEM((length, 3 * width), BF),
            pltpu.VMEM((16, length), F32),
            pltpu.VMEM((3 * width, width), BF),
            pltpu.VMEM((width, width), BF),
        ] + weight_sems(weights) + (ride.scratch_shapes if ride else []),
        compiler_params=ride.params if ride else pltpu.CompilerParams(vmem_limit_bytes=VMEM_BYTES),
        cost_estimate=pl.CostEstimate(
            flops=16 * length * width * width + 10 * length * length * width,
            bytes_accessed=40 * length * width + 16 * width * width,
            transcendentals=heads * length * length,
        ),
        name="attend_back",
    )(piece, x, gain, *w_args, vectors, normed, qkv, mixed, lse, grad, *tails, *(ride.args if ride else []))


def mlp_chunk(c, parts, zones, up_ref, down_ref):
    hidden, width = up_ref.shape
    piece = hidden // (parts * zones)
    rows = [
        up_ref[pl.ds(pl.multiple_of(z * parts * piece + c * piece, 16), piece), :] for z in range(zones)
    ]
    span = down_ref.shape[1] // parts
    down = down_ref[:, pl.ds(pl.multiple_of(c * span, 16), span), :].reshape(-1, down_ref.shape[2])
    return jnp.concatenate(rows, axis=0), down


def mlp_loads(parts, zones, up_hbm, down_hbm, up_ref, down_ref, sems):
    piece = up_ref.shape[0] // (parts * zones)
    span = down_ref.shape[1] // parts
    loads = []
    for c in range(parts):
        chunk = [
            pltpu.make_async_copy(
                up_hbm.at[pl.ds((z * parts + c) * piece, piece), :],
                up_ref.at[pl.ds((z * parts + c) * piece, piece), :], sems.at[c, z],
            )
            for z in range(zones)
        ]
        columns = pl.ds(c * span, span)
        chunk.append(
            pltpu.make_async_copy(down_hbm.at[:, columns, :], down_ref.at[:, columns, :], sems.at[c, zones])
        )
        loads.append(chunk)
    for chunk in loads:
        for copy in chunk:
            copy.start()
    return loads


def mlp_kernel(parts, zones, x_ref, gain_ref, up_hbm, down_hbm, out_ref, normed_ref, up_ref, down_ref, sems):
    loads = mlp_loads(parts, zones, up_hbm, down_hbm, up_ref, down_ref, sems)
    field = x_ref[...]
    normed_ref[...] = (field * inverse_rms(field) * gain_ref[...]).astype(BF)
    out_ref[...] = field

    def chunk(c, _):
        for at, copies in enumerate(loads):
            pl.when(c == at)(lambda copies=copies: arrive(copies))
        up, down = mlp_chunk(c, parts, zones, up_ref, down_ref)
        hidden = gelu_of(nt(normed_ref[...], up)).astype(BF)
        out_ref[...] += nt(hidden, down)
        return 0

    lax.fori_loop(0, parts, chunk, 0)


def mlp(x, gain, up, down, parts, zones):
    length, width = x.shape
    hidden = up.shape[0]
    return pl.pallas_call(
        lambda *refs: mlp_kernel(parts, zones, *refs),
        out_shape=(jax.ShapeDtypeStruct((length, width), F32), jax.ShapeDtypeStruct((length, width), BF)),
        in_specs=[VMEM_SPEC] * 2 + [HBM_SPEC] * 2,
        out_specs=[VMEM_SPEC] * 2,
        scratch_shapes=[
            pltpu.VMEM(up.shape, BF), pltpu.VMEM(down.shape, BF), pltpu.SemaphoreType.DMA((parts, zones + 1))
        ],
        compiler_params=pltpu.CompilerParams(vmem_limit_bytes=VMEM_BYTES),
        cost_estimate=pl.CostEstimate(
            flops=4 * length * width * hidden, bytes_accessed=10 * length * width + 4 * width * hidden,
            transcendentals=length * hidden,
        ),
        name="mlp",
    )(x, gain, up, down)


def mlp_back_kernel(parts, zones, x_ref, gain_ref, up_hbm, down_hbm, normed_ref, grad_ref,
                    dx_ref, dup_ref, ddown_ref, dgain_ref, low_ref, acc_ref, up_ref, down_ref, sems):
    loads = mlp_loads(parts, zones, up_hbm, down_hbm, up_ref, down_ref, sems)
    low_ref[...] = grad_ref[...].astype(BF)
    acc_ref[...] = jnp.zeros_like(acc_ref)

    piece = up_ref.shape[0] // (parts * zones)
    span = down_ref.shape[1] // parts

    def chunk(c, _):
        for at, copies in enumerate(loads):
            pl.when(c == at)(lambda copies=copies: arrive(copies))
        up, down = mlp_chunk(c, parts, zones, up_ref, down_ref)
        hidden, slope = gelu_parts(nt(normed_ref[...], up))
        pre_grad = (nn(low_ref[...], down) * slope).astype(BF)
        ddown = tn(low_ref[...], hidden.astype(BF)).astype(BF)
        ddown_ref[:, pl.ds(pl.multiple_of(c * span, 16), span), :] = ddown.reshape(-1, span, ddown.shape[1])
        dup = tn(pre_grad, normed_ref[...]).astype(BF)
        for z in range(zones):
            at = pl.ds(pl.multiple_of(z * parts * piece + c * piece, 16), piece)
            dup_ref[at, :] = dup[z * piece:z * piece + piece, :]
        acc_ref[...] += nn(pre_grad, up)
        return 0

    lax.fori_loop(0, parts, chunk, 0)
    norm_back(x_ref, gain_ref, acc_ref, grad_ref, dx_ref, dgain_ref)


def mlp_back(x, gain, up, down, normed, grad, parts, zones):
    length, width = x.shape
    hidden = up.shape[0]
    return pl.pallas_call(
        lambda *refs: mlp_back_kernel(parts, zones, *refs),
        out_shape=(
            jax.ShapeDtypeStruct((length, width), F32),
            jax.ShapeDtypeStruct((hidden, width), BF),
            jax.ShapeDtypeStruct(down.shape, BF),
            jax.ShapeDtypeStruct((1, width), F32),
        ),
        in_specs=[VMEM_SPEC] * 2 + [HBM_SPEC] * 2 + [VMEM_SPEC] * 2,
        out_specs=[VMEM_SPEC] * 4,
        scratch_shapes=[
            pltpu.VMEM((length, width), BF), pltpu.VMEM((length, width), F32),
            pltpu.VMEM(up.shape, BF), pltpu.VMEM(down.shape, BF), pltpu.SemaphoreType.DMA((parts, zones + 1)),
        ],
        compiler_params=pltpu.CompilerParams(vmem_limit_bytes=VMEM_BYTES),
        cost_estimate=pl.CostEstimate(
            flops=10 * length * width * hidden, bytes_accessed=16 * length * width + 8 * width * hidden,
            transcendentals=length * hidden,
        ),
        name="mlp_back",
    )(x, gain, up, down, normed, grad)


MESH = pl.DeviceIdType.MESH


def flip(index, mask):
    bit = 1
    while bit <= mask:
        if mask & bit:
            index = index + bit - 2 * bit * ((index // bit) % 2)
        bit *= 2
    return index


def masks_of(bits):
    found = [0]
    for bit in bits:
        found = found + [m | bit for m in found]
    return found


def bits_below(size):
    found, bit = [], 1
    while bit < size:
        found.append(bit)
        bit *= 2
    return found


def halves_of(rows):
    cut = rows // 2 // 16 * 16
    return ((0, cut), (cut, rows - cut))


def routes_of(chips):
    bits = bits_below(chips)
    cut = len(bits) // 2
    return (bits, bits[cut:] + bits[:cut])


def greet(owner, zone, owners, zones):
    barrier = pltpu.get_barrier_semaphore()
    peers = [(flip(owner, bit), zone) for bit in bits_below(owners)]
    peers += [(owner, flip(zone, d)) for d in range(1, zones)]
    for peer in peers:
        pl.semaphore_signal(barrier, inc=1, device_id=peer, device_id_type=MESH)
    pl.semaphore_wait(barrier, len(peers))


def sender(send_sem, recv_sem):
    used = [0]

    def send(source, target, device):
        at = used[0]
        used[0] += 1
        copy = pltpu.make_async_remote_copy(
            source, target, send_sem.at[at], recv_sem.at[at], device_id=device, device_id_type=MESH
        )
        copy.start()
        return copy

    return send


def gather_copies(owners, zones):
    chips = owners // 2
    return zones - 1 + 2 * (chips - 1) + 2 * chips


def gather_kernel(owners, zones, used_rows, experts, capacity, *refs):
    count = len(used_rows)
    blocks, (late_ref, route_ref), refs = refs[:count], refs[count:count + 2], refs[count + 2:]
    outs, (slot_ref, spread_ref), refs = refs[:count], refs[count:count + 2], refs[count + 2:]
    slabs, turned = refs[:count], refs[count:2 * count]
    direct = capacity % 16 == 0
    near_ref, refs = (refs[2 * count], refs[:2 * count] + refs[2 * count + 1:]) if direct else (spread_ref, refs)
    slot_in_ref, send_sem, recv_sem, local_sem = refs[2 * count:]
    owner, zone = lax.axis_index("expert"), lax.axis_index("shard")
    greet(owner, zone, owners, zones)
    send = sender(send_sem, recv_sem)
    chips = owners // 2
    pending, finals = [], []

    def across(g):
        slabs[g][zone] = blocks[g][...]
        return [send(blocks[g], slabs[g].at[zone], (owner, flip(zone, d))) for d in range(1, zones)]

    def place(g, index, half):
        start, size = halves_of(used_rows[g])[half]
        return outs[g].at[index, pl.ds(start, size), :]

    def onward(g, half, index):
        finals.append(send(place(g, index, half), place(g, index, half), (flip(owner, 1), zone)))

    def start_rows(g, copies):
        for copy in copies:
            copy.wait_recv()
        pending.extend(copies)
        slab = slabs[g]
        turned[g][...] = slab[...].reshape(slab.shape[0] * slab.shape[1], slab.shape[2]).T
        local = pltpu.make_async_copy(
            turned[g].at[pl.ds(0, used_rows[g]), :], outs[g].at[owner], local_sem.at[g]
        )
        local.start()
        firsts = []
        for half, order in enumerate(routes_of(chips)):
            start, size = halves_of(used_rows[g])[half]
            source = turned[g].at[pl.ds(start, size), :]
            firsts.append([send(source, place(g, owner, half), (flip(owner, 2 * order[0]), zone))])
            finals.append(send(source, place(g, owner, half), (flip(owner, 1), zone)))
        return firsts, local

    def finish_rows(g, state, step):
        firsts, local = state
        if step == 0:
            local.wait()
        for half, order in enumerate(routes_of(chips)):
            for copy in firsts[half]:
                copy.wait_recv()
            pending.extend(firsts[half])
            done = masks_of(order[:step])
            arrived = [m | order[step] for m in done]
            if step + 1 < len(order):
                device = (flip(owner, 2 * order[step + 1]), zone)
                firsts[half] = [
                    send(place(g, flip(owner, 2 * m), half), place(g, flip(owner, 2 * m), half), device)
                    for m in done + arrived
                ]
            for m in arrived:
                onward(g, half, flip(owner, 2 * m))
        return firsts, local

    steps = len(routes_of(chips)[0])
    moving = {0: across(0)}
    states = {}
    slot_ref[0] = token_slots(route_ref[...], experts, capacity)
    near_copies = []

    def spread_zone(d):
        if not direct:
            return
        take = max(1, 384 // capacity)
        rows = late_ref if d == 0 else near_ref.at[d - 1]

        def chunk(i, _):
            hits = slot_hits(slot_ref[d], i * (take * capacity), take * capacity)
            picked = nn(hits[0] + hits[1], rows[...]).reshape(take, capacity, rows.shape[1])
            spread_ref[pl.ds(i * take, take), d] = picked.astype(BF)
            return 0

        lax.fori_loop(0, experts // take, chunk, 0)

    for g in range(count):
        states[g] = start_rows(g, moving[g])
        if g + 1 < count:
            moving[g + 1] = across(g + 1)
        if g == count - 1:
            for d in range(1, zones // 2):
                device = (owner, (zone + zones - 2 * d) % zones)
                near_copies.append(send(slot_ref.at[0], slot_in_ref.at[d - 1], device))
                near_copies.append(send(late_ref, near_ref.at[d - 1], device))
        if g == 1:
            spread_zone(0)
        if g > 0:
            for step in range(1, steps):
                states[g - 1] = finish_rows(g - 1, states[g - 1], step)
        states[g] = finish_rows(g, states[g], 0)
    for step in range(1, steps):
        states[count - 1] = finish_rows(count - 1, states[count - 1], step)
    for copy in near_copies:
        copy.wait_recv()
    for d in range(1, zones // 2):
        slot_ref[d] = slot_in_ref[d - 1]
        spread_zone(d)
    for copy in finals:
        copy.wait_recv()
    for copy in pending + finals + near_copies:
        copy.wait_send()


def gather_weights(blocks, used_rows, late, route_rows, owners, zones, experts, capacity):
    count = len(blocks)
    depth = zones * blocks[0].shape[0]
    groups = zones // 2
    copies = count * gather_copies(owners, zones) + 2 * (groups - 1)
    length = route_rows.shape[1]
    any_spec = pl.BlockSpec(memory_space=pltpu.HBM)
    direct = capacity % 16 == 0
    near_shape = (groups - 1,) + late.shape
    if direct:
        spread_shape, late_spec = (experts, groups, capacity, late.shape[1]), VMEM_SPEC
    else:
        spread_shape, late_spec = near_shape, any_spec
    return pl.pallas_call(
        lambda *refs: gather_kernel(owners, zones, used_rows, experts, capacity, *refs),
        out_shape=tuple(jax.ShapeDtypeStruct((owners, used, depth), BF) for used in used_rows)
        + (
            jax.ShapeDtypeStruct((groups, 8, length), F32),
            jax.ShapeDtypeStruct(spread_shape, BF),
        ),
        in_specs=[VMEM_SPEC] * count + [late_spec, VMEM_SPEC],
        out_specs=tuple([any_spec] * count) + (VMEM_SPEC, late_spec),
        scratch_shapes=[pltpu.VMEM((zones,) + b.shape, BF) for b in blocks]
        + [pltpu.VMEM((b.shape[1], depth), BF) for b in blocks]
        + ([pltpu.VMEM(near_shape, BF)] if direct else [])
        + [pltpu.VMEM((groups - 1, 8, length), F32)]
        + [pltpu.SemaphoreType.DMA((copies,)), pltpu.SemaphoreType.DMA((copies,)), pltpu.SemaphoreType.DMA((count,))],
        compiler_params=pltpu.CompilerParams(
            vmem_limit_bytes=61 * 1024 * 1024, collective_id=1, has_side_effects=True
        ),
        name="gather_weights",
    )(*blocks, late, route_rows)


def add_rows(into, other):
    return (into.astype(F32) + other.astype(F32)).astype(BF)


class Mail:
    def __init__(self, at, source, target, device, sems):
        self.at, self.source, self.target, self.device, self.sems = at, source, target, device, sems

    def make(self):
        return pltpu.make_async_remote_copy(
            self.source(), self.target(), self.sems[0].at[self.at], self.sems[1].at[self.at],
            device_id=self.device, device_id_type=MESH,
        )

    def start(self):
        self.make().start()
        return self

    def wait_recv(self):
        self.make().wait_recv()

    def wait_send(self):
        self.make().wait_send()


class Post:
    def __init__(self, send_sem, recv_sem):
        self.sems, self.mails = (send_sem, recv_sem), []

    def plan(self, source, target, device):
        mail = Mail(len(self.mails), source, target, device, self.sems)
        self.mails.append(mail)
        return mail

    def close(self):
        for mail in self.mails:
            mail.wait_send()


def cross_copies(owners):
    return 1 + 2 * (owners // 2 - 1)


def cross_scratch(owners, used, depth):
    chips = owners // 2
    return [
        pltpu.VMEM((chips, used, depth), BF),
        pltpu.VMEM((chips, used, depth), BF),
        pltpu.VMEM((chips - 1, used, depth), BF),
        pltpu.SemaphoreType.DMA,
    ]


def cross_plan(post, part, keep, near, far, local_sem, owner, zone, owners):
    chips = owners // 2
    chip, core = owner // 2, owner % 2
    used = keep.shape[1]
    orders = routes_of(chips)
    steps = len(orders[0])
    first = post.plan(lambda: part.at[:, 1 - core], lambda: near, (flip(owner, 1), zone))

    def window(half):
        start, size = halves_of(used)[half]
        return pl.ds(start, size)

    def slot_of(step, i):
        return chips - 2 * len(masks_of(orders[0][step + 1:])) + i

    pushes = []
    for step in range(steps):
        mails = []
        for half, order in enumerate(orders):
            bit, rest = order[step], masks_of(order[step + 1:])
            for i, m in enumerate(rest):
                index = flip(chip, bit | m)
                mails.append(post.plan(
                    lambda index=index, half=half: keep.at[index, window(half), :],
                    lambda i=i, half=half, step=step: far.at[slot_of(step, i), window(half), :],
                    (flip(owner, 2 * bit), zone),
                ))
        pushes.append(mails)

    def local():
        return pltpu.make_async_copy(part.at[:, core], keep, local_sem)

    def begin():
        local().start()
        first.start()

    def meet():
        local().wait()
        first.wait_recv()

        def one(h, _):
            keep[h] = add_rows(keep[h], near[h])
            return 0

        lax.fori_loop(0, chips, one, 0)
        for mail in pushes[0]:
            mail.start()

    def absorb(step):
        for mail in pushes[step]:
            mail.wait_recv()
        for half, order in enumerate(orders):
            for i, m in enumerate(masks_of(order[step + 1:])):
                index = flip(chip, m)
                keep[index, window(half), :] = add_rows(
                    keep[index, window(half), :], far[slot_of(step, i), window(half), :]
                )
        if step + 1 < steps:
            for mail in pushes[step + 1]:
                mail.start()

    stages = [meet] + [lambda step=step: absorb(step) for step in range(steps)]
    return begin, stages


def zone_scratch(zones, used, depth):
    wide = -(-used // 128) * 128
    return [pltpu.VMEM((zones, depth // zones, wide), BF), pltpu.VMEM((zones - 1, depth // zones, wide), BF)]


def zone_shape(zones, used, depth):
    return jax.ShapeDtypeStruct((depth // zones, -(-used // 128) * 128), F32)


def zone_plan(post, slab, incoming, out_ref, owner, zone, zones):
    mails = [
        post.plan(
            lambda d=d: slab.at[flip(zone, d)], lambda d=d: incoming.at[d - 1], (owner, flip(zone, d))
        )
        for d in range(1, zones)
    ]

    def start(own):
        spare = slab.shape[2] - own.shape[0]
        if spare:
            own = jnp.concatenate([own, jnp.zeros((spare, own.shape[1]), BF)], axis=0)
        slab[...] = own.T.reshape(slab.shape)
        for mail in mails:
            mail.start()

    def end():
        total = slab[zone].astype(F32)
        for d in range(1, zones):
            mails[d - 1].wait_recv()
            total = total + incoming[d - 1].astype(F32)
        out_ref[...] = total

    return start, end


class Ride:
    def __init__(self, parts, zoned, owns, rows, owners, zones, capacity, depth, collective_id):
        groups = zones // 2
        self.owners, self.zones, self.capacity, self.zoned, self.count = owners, zones, capacity, zoned, len(parts)
        self.owns = len(owns)
        self.with_rows = rows is not None
        hbm = pl.BlockSpec(memory_space=pltpu.HBM)
        self.args = [p.reshape(owners // 2, 2, p.shape[1], depth) for p in parts] + list(owns)
        self.in_specs = [hbm] * len(parts) + [VMEM_SPEC] * len(owns)
        self.out_shape = [zone_shape(zones, p.shape[1], depth) for p in parts[:zoned]]
        self.out_shape += [jax.ShapeDtypeStruct(p.shape[1:], BF) for p in parts[zoned:]]
        self.out_shape += [zone_shape(zones, o.shape[0], depth) for o in owns]
        self.scratch_shapes = []
        for p in parts:
            self.scratch_shapes += cross_scratch(owners, p.shape[1], depth)
        for p in parts[:zoned]:
            self.scratch_shapes += zone_scratch(zones, p.shape[1], depth)
        for o in owns:
            self.scratch_shapes += zone_scratch(zones, o.shape[0], depth)
        copies = len(parts) * cross_copies(owners) + (zoned + len(owns)) * (zones - 1)
        if self.with_rows:
            y, slot_rows = rows
            length = slot_rows.shape[2]
            self.args += [y, slot_rows]
            self.in_specs += [hbm, VMEM_SPEC]
            self.out_shape += [jax.ShapeDtypeStruct((groups - 1, length, depth), BF)]
            self.scratch_shapes += [
                pltpu.VMEM((groups - 1,) + y.shape[:2] + (capacity, depth), BF),
                pltpu.SemaphoreType.DMA((groups - 1,)),
                *[pltpu.VMEM((length, depth), BF)] * (groups - 2),
            ]
            copies += groups - 1
        self.out_specs = [VMEM_SPEC] * len(self.out_shape)
        self.scratch_shapes += [pltpu.SemaphoreType.DMA((copies,)), pltpu.SemaphoreType.DMA((copies,))]
        self.inputs, self.outputs, self.scratch = len(self.args), len(self.out_shape), len(self.scratch_shapes)
        self.params = pltpu.CompilerParams(
            vmem_limit_bytes=61 * 1024 * 1024, collective_id=collective_id, has_side_effects=True
        )

    def board(self, inputs, outputs, scratch, room, spare):
        owner, zone = lax.axis_index("expert"), lax.axis_index("shard")
        owners, zones, count, groups = self.owners, self.zones, self.count, self.zones // 2
        greet(owner, zone, owners, zones)
        post = Post(scratch[-2], scratch[-1])
        plans = [cross_plan(post, inputs[g], *scratch[4 * g:4 * g + 4], owner, zone, owners) for g in range(count)]
        keeps = [scratch[4 * g] for g in range(count)]
        for begin, _ in plans:
            begin()
        zone_plans = []
        for g in range(self.zoned):
            slab, incoming = scratch[4 * count + 2 * g:4 * count + 2 * g + 2]
            zone_plans.append(zone_plan(post, slab, incoming, outputs[g], owner, zone, zones))
        for i in range(self.owns):
            at = 4 * count + 2 * (self.zoned + i)
            start, end = zone_plan(post, scratch[at], scratch[at + 1], outputs[count + i], owner, zone, zones)
            start(inputs[count + i][...])
            zone_plans.append((start, end))
        y_mails = []
        if self.with_rows:
            y_ref, slot_ref = inputs[count + self.owns:count + self.owns + 2]
            at = 4 * count + 2 * (self.zoned + self.owns)
            y_rows, y_sem = scratch[at:at + 2]
            y_part = [spare, *scratch[at + 2:-2]]

            def load(d):
                window = pl.ds(d * self.capacity, self.capacity)
                return pltpu.make_async_copy(y_ref.at[:, :, window, :], y_rows.at[d - 1], y_sem.at[d - 1])

            for d in range(1, groups):
                load(d).start()
                y_mails.append(post.plan(
                    lambda d=d: y_part[d - 1], lambda d=d: outputs[-1].at[d - 1], (owner, (zone + 2 * d) % zones)
                ))

        def rows_turn():
            for d in range(1, groups):
                load(d).wait()
                collect_rows(y_rows.at[d - 1], slot_ref[d], room)
                y_part[d - 1][...] = room[...].astype(BF)
                y_mails[d - 1].start()

        turns = []
        for g in range(count):
            turns.append(lambda g=g: self.run([plans[g - 1][1][1]] if g else [], [plans[g][1][0]]))
        if count == 1:
            turns.append(lambda: self.run([plans[0][1][1]]))
        longest = len(plans[0][1]) if plans else 0

        def finish_part():
            for t in range(1, count + longest - 1):
                for g in reversed(range(count)):
                    at = t - g
                    if 1 <= at < longest and (at > 1 or (g == count - 1 and count > 1)):
                        plans[g][1][at]()
                        if at == longest - 1 and g < self.zoned:
                            zone_plans[g][0](keeps[g][owner // 2])
            for g in range(self.zoned, count):
                outputs[g][...] = keeps[g][owner // 2]
            for _, end in zone_plans:
                end()
            for mail in y_mails:
                mail.wait_recv()
            post.close()

        return turns, rows_turn if self.with_rows else None, finish_part

    def run(self, *groups):
        for acts in groups:
            for act in acts:
                act()


def collect_rows(rows_ref, slots, room):
    owners, local, capacity, width = rows_ref.shape
    span = 2 * local * capacity
    for h in range(owners // 2):
        hits = slot_hits(slots, jnp.int32(h * span), span)
        added = tn(hits[0] + hits[1], rows_ref[2 * h:2 * h + 2].reshape(span, width))
        if h == 0:
            room[...] = added
        else:
            room[...] += added


def finish_kernel(owners, zones, capacity, sizes, *refs):
    refs = list(refs)

    def take(count):
        found = refs[:count]
        del refs[:count]
        return found

    with_rows, chunks = sizes
    early_refs, (down_part, part, small) = take(2), take(3)
    own_refs, peer_refs = take(2), take(2)
    y_ref, slot_ref, x_ref, y_in = take(4) if with_rows else (None, None, None, None)
    *outs, small_out = take(5)
    sum_refs = take(2)
    y_out = take(1)[0] if with_rows else None
    cross_refs = [take(4) for _ in range(2)]
    zone_refs = [take(2) for _ in range(4)]
    small_mine, small_other = take(2)
    stages = [take(3) for _ in range(2)]
    add_sem = take(1)[0]
    if with_rows:
        y_rows, y_sum, y_sem = take(3)
    send_sem, recv_sem = take(2)
    owner, zone = lax.axis_index("expert"), lax.axis_index("shard")
    greet(owner, zone, owners, zones)
    post = Post(send_sem, recv_sem)
    plans = [
        cross_plan(post, p, *r, owner, zone, owners) for p, r in zip((down_part, part), cross_refs)
    ]
    for begin, _ in plans:
        begin()
    down, cross = [stages for _, stages in plans]
    if with_rows:
        y_copy = pltpu.make_async_copy(y_ref.at[:, :, pl.ds(0, capacity), :], y_rows, y_sem)
        y_copy.start()
    zone_starts, zone_ends = zip(
        *[zone_plan(post, r[0], r[1], out, owner, zone, zones) for r, out in zip(zone_refs, outs)]
    )
    for start, ref in zip(zone_starts, early_refs):
        start(ref[...])
    small_peers = [(flip(owner, bit), zone) for bit in bits_below(owners)]
    small_peers += [(owner, flip(zone, bit)) for bit in bits_below(zones)]
    small_mails = [
        post.plan(lambda i=i: small_mine.at[i], lambda i=i: small_other.at[i], peer)
        for i, peer in enumerate(small_peers)
    ]
    small_mine[0] = small[...]
    small_mails[0].start()

    def small_step(i):
        if i < len(small_mails):
            small_mails[i].wait_recv()
            small_mine[i + 1] = small_mine[i] + small_other[i]
            if i + 1 < len(small_mails):
                small_mails[i + 1].start()

    groups = zones // 2

    def add_stage(i):
        mine, theirs, total = stages[i]
        count = chunks[i]
        size = mine.shape[1]

        def loads(k):
            rows = pl.ds(k * size, size)
            return (
                pltpu.make_async_copy(own_refs[i].at[rows, :], mine.at[k % 2], add_sem.at[i, k % 2, 0]),
                pltpu.make_async_copy(peer_refs[i].at[rows, :], theirs.at[k % 2], add_sem.at[i, k % 2, 1]),
            )

        def store(k):
            return pltpu.make_async_copy(
                total.at[k % 2], sum_refs[i].at[pl.ds(k * size, size), :], add_sem.at[i, k % 2, 2]
            )

        for copy in loads(0):
            copy.start()
        for k in range(count):
            if k + 1 < count:
                for copy in loads(k + 1):
                    copy.start()
            for copy in loads(k):
                copy.wait()
            if k >= 2:
                store(k - 2).wait()
            total[k % 2] = mine[k % 2] + theirs[k % 2].astype(F32)
            store(k).start()
        for k in range(max(0, count - 2), count):
            store(k).wait()

    down[0]()
    small_step(0)
    add_stage(0)
    down[1]()
    cross[0]()
    small_step(1)
    if with_rows:
        y_copy.wait()
        collect_rows(y_rows, slot_ref[0], y_sum)
        total = x_ref[...] + y_sum[...]
        for d in range(1, groups):
            total = total + y_in[d - 1].astype(F32)
        y_out[...] = total.astype(BF)
    small_step(2)
    for act in down[2:]:
        act()
    zone_starts[2](cross_refs[0][0][owner // 2])
    for act in cross[1:-1]:
        act()
    zone_ends[0]()
    zone_ends[1]()
    small_step(3)
    cross[-1]()
    zone_starts[3](cross_refs[1][0][owner // 2])
    small_step(4)
    add_stage(1)
    for i in range(5, len(small_mails)):
        small_step(i)
    small_out[...] = small_mine[len(small_mails)]
    zone_ends[2]()
    zone_ends[3]()
    post.close()


def finish(early, down_part, first_part, small, owns, peers, owners, zones, capacity, rows=None):
    depth = first_part.shape[2]
    chips = owners // 2
    used = tuple(o.shape[0] for o in early) + (down_part.shape[1], first_part.shape[1])
    cross_parts = [p.reshape(chips, 2, p.shape[1], depth) for p in (down_part, first_part)]
    flat = [o.reshape(-1, o.shape[-1]) for o in owns]
    flat_peers = [p.reshape(-1, p.shape[-1]) for p in peers]
    chunk = 256
    chunks = tuple(f.shape[0] // chunk for f in flat)
    rounds = len(bits_below(owners)) + len(bits_below(zones))
    copies = 2 * cross_copies(owners) + 4 * (zones - 1) + rounds
    hbm = pl.BlockSpec(memory_space=pltpu.HBM)
    args = [*early, *cross_parts, small, *flat, *flat_peers]
    in_specs = [VMEM_SPEC, VMEM_SPEC, hbm, hbm, VMEM_SPEC] + [hbm] * 4
    out_shape = [zone_shape(zones, u, depth) for u in used] + [jax.ShapeDtypeStruct(small.shape, F32)]
    out_shape += [jax.ShapeDtypeStruct(f.shape, F32) for f in flat]
    out_specs = [VMEM_SPEC] * 5 + [hbm] * 2
    scratch = cross_scratch(owners, used[2], depth) + cross_scratch(owners, used[3], depth)
    for u in used:
        scratch += zone_scratch(zones, u, depth)
    scratch += [pltpu.VMEM((rounds + 1,) + small.shape, F32), pltpu.VMEM((rounds,) + small.shape, F32)]
    for f in flat:
        shape = (2, chunk, f.shape[1])
        scratch += [pltpu.VMEM(shape, F32), pltpu.VMEM(shape, BF), pltpu.VMEM(shape, F32)]
    scratch += [pltpu.SemaphoreType.DMA((2, 2, 3))]
    if rows is not None:
        y, slot_rows, x, y_near = rows
        args += [y, slot_rows, x, y_near]
        in_specs += [hbm, VMEM_SPEC, VMEM_SPEC, VMEM_SPEC]
        out_shape += [jax.ShapeDtypeStruct(x.shape, BF)]
        out_specs += [VMEM_SPEC]
        scratch += [
            pltpu.VMEM(y.shape[:2] + (capacity, depth), BF), pltpu.VMEM(x.shape, F32), pltpu.SemaphoreType.DMA,
        ]
    scratch += [pltpu.SemaphoreType.DMA((copies,)), pltpu.SemaphoreType.DMA((copies,))]
    sizes = (rows is not None, chunks)
    return pl.pallas_call(
        lambda *refs: finish_kernel(owners, zones, capacity, sizes, *refs),
        out_shape=tuple(out_shape),
        in_specs=in_specs,
        out_specs=tuple(out_specs),
        scratch_shapes=scratch,
        compiler_params=pltpu.CompilerParams(
            vmem_limit_bytes=61 * 1024 * 1024, collective_id=2, has_side_effects=True
        ),
        name="finish",
    )(*args)


def three_pieces(row):
    top = row.astype(BF)
    rest = row - top.astype(F32)
    middle = rest.astype(BF)
    low = (rest - middle.astype(F32)).astype(BF)
    return jnp.concatenate([top, middle, low, jnp.zeros((5, row.shape[1]), BF)], axis=0)


def sum_pieces(rows):
    return rows[0:1] + rows[1:2] + rows[2:3]


def token_slots(route_rows, experts, capacity):
    length = route_rows.shape[1]
    ids = lax.broadcasted_iota(jnp.int32, (experts, length), 0)
    first, second = route_rows[0:1] == ids, route_rows[1:2] == ids
    named = jnp.where(first | second, 1.0, 0.0).astype(BF)
    earlier = (
        lax.broadcasted_iota(jnp.int32, (length, length), 0) < lax.broadcasted_iota(jnp.int32, (length, length), 1)
    )
    place = nn(named, jnp.where(earlier, 1.0, 0.0).astype(BF)) + (ids * capacity).astype(F32)
    rows = [jnp.sum(jnp.where(hit, place, 0.0), axis=0, keepdims=True) for hit in (first, second)]
    return jnp.concatenate(rows + [jnp.zeros((6, length), F32)], axis=0)


def slot_hits(slots, start, count):
    place = lax.broadcasted_iota(jnp.int32, (count, slots.shape[1]), 0).astype(F32) + start.astype(F32)
    one, zero = jnp.asarray(1.0, F32), jnp.asarray(0.0, F32)
    return [jnp.where(place == slots[k:k + 1], one, zero).astype(BF) for k in range(2)]


def greet_plane(owner, zone, owners, zones):
    barrier = pltpu.get_barrier_semaphore()
    peers = [(flip(owner, mask), zone) for mask in range(1, owners)]
    peers += [(owner, (zone + d) % zones) for d in range(2, zones, 2)] + [(owner, flip(zone, 1))]
    for peer in peers:
        pl.semaphore_signal(barrier, inc=1, device_id=peer, device_id_type=MESH)
    pl.semaphore_wait(barrier, len(peers))


def peer_order(owners):
    return list(range(2, owners)) + [1, 0]


def softmax_pair(logits, route_rows):
    ids = lax.broadcasted_iota(jnp.int32, logits.shape, 0)
    a, b = [jnp.sum(jnp.where(route_rows[k:k + 1] == ids, logits, 0.0), axis=0, keepdims=True) for k in range(2)]
    peak = jnp.maximum(a, b)
    ea, eb = jnp.exp(a - peak), jnp.exp(b - peak)
    return ea / (ea + eb), eb / (ea + eb)


def send_rows_kernel(
    owners, zones, capacity, x_ref, gain_ref, router_ref, route_ref, slot_ref, slices_ref,
    normed_ref, gates_ref, rows_ref, gate_ref, other_ref,
    near_ref, near_gates_ref, packed_ref, tags_ref, tags_in_ref, send_sem, recv_sem, local_sem,
):
    owner, zone = lax.axis_index("expert"), lax.axis_index("shard")
    tags_ref[...] = jnp.zeros_like(tags_ref)
    greet_plane(owner, zone, owners, zones)
    send = sender(send_sem, recv_sem)
    groups = zones // 2
    local = rows_ref.shape[1]
    span = local * capacity
    field = x_ref[...]
    normed_ref[...] = (field * inverse_rms(field) * gain_ref[...]).astype(BF)
    cut = normed_ref.shape[1] // 2
    lanes = [pl.ds(0, cut), pl.ds(cut, cut)]
    copies = {}
    for half in range(2):
        for d in range(1, groups):
            device = (owner, (zone + zones - 2 * d) % zones)
            copies[d, half] = send(normed_ref.at[:, lanes[half]], near_ref.at[d - 1, :, lanes[half]], device)
    gates = softmax_pair(nt(router_ref[...], normed_ref[...]), route_ref[...])
    gates_ref[...] = jnp.concatenate(list(gates) + [jnp.zeros((6, gates[0].shape[1]), F32)], axis=0)
    for d in range(1, groups):
        copies[d, 2] = send(gates_ref, near_gates_ref.at[d - 1], (owner, (zone + zones - 2 * d) % zones))
    arrivals, stays = [], []
    for part in range(local):
        arrivals.append(send(slices_ref.at[part], other_ref.at[part], (owner, flip(zone, 1))))
    def ship(d, mask, target, half):
        columns = slice(None) if half is None else lanes[half]
        for part in range(local):
            source = packed_ref.at[d, mask, pl.ds(part * capacity, capacity), columns]
            place = rows_ref.at[owner, part, pl.ds(d * capacity, capacity), columns]
            if mask:
                arrivals.append(send(source, place, (target, zone)))
            else:
                at = (2 * d + (half or 0)) * local + part
                copy = pltpu.make_async_copy(source, place, local_sem.at[at])
                copy.start()
                stays.append(copy)

    for d in range(groups):
        for half in (None,) if d == 0 else (0, 1):
            if d:
                copies[d, half].wait_recv()
                if half == 0:
                    copies[d, 2].wait_recv()
            rows = normed_ref if d == 0 else near_ref.at[d - 1]
            weights = gates_ref[...] if d == 0 else near_gates_ref[d - 1]
            pieces = [three_pieces(weights[k:k + 1]) for k in range(2)]
            slots = slot_ref[d]
            for mask in peer_order(owners):
                target = flip(owner, mask)
                hits = slot_hits(slots, target * span, span)
                both = hits[0] + hits[1]
                if half is None:
                    packed_ref[d, mask] = nn(both, rows[...]).astype(BF)
                else:
                    packed_ref[d, mask, :, lanes[half]] = nn(both, rows[:, lanes[half]]).astype(BF)
                ship(d, mask, target, half)
                if half == 1:
                    continue
                tag = sum_pieces(nt(pieces[0], hits[0]) + nt(pieces[1], hits[1]))
                tags_ref[d, mask, :, 0:span] = jnp.broadcast_to(tag, (8, span))
                if mask:
                    arrivals.append(send(tags_ref.at[d, mask], tags_in_ref.at[d, owner], (target, zone)))
                else:
                    tags_in_ref[d, owner] = tags_ref[d, mask]
    for copy in arrivals:
        copy.wait_recv()
    for d in range(groups):
        for source in range(owners):
            column = tags_in_ref[d, source].T
            for part in range(local):
                gate_ref[source, part, d * capacity:(d + 1) * capacity, :] = column[
                    part * capacity:(part + 1) * capacity, 0:1
                ]
    for copy in stays:
        copy.wait()
    for copy in list(copies.values()) + arrivals:
        copy.wait_send()


def send_rows(x, gain, router, route_rows, slot_rows, slices, owners, zones, local, capacity):
    length, width = x.shape
    groups = zones // 2
    span = local * capacity
    any_spec = pl.BlockSpec(memory_space=pltpu.HBM)
    wide = -(-span // 128) * 128
    copies = local + 3 * (groups - 1) + (owners - 1) * (local + 1 + (groups - 1) * (2 * local + 1))
    return pl.pallas_call(
        lambda *refs: send_rows_kernel(owners, zones, capacity, *refs),
        out_shape=(
            jax.ShapeDtypeStruct((length, width), BF),
            jax.ShapeDtypeStruct((8, length), F32),
            jax.ShapeDtypeStruct((owners, local, groups * capacity, width), BF),
            jax.ShapeDtypeStruct((owners, local, groups * capacity, 1), F32),
            jax.ShapeDtypeStruct(slices.shape, slices.dtype),
        ),
        in_specs=[VMEM_SPEC] * 5 + [any_spec],
        out_specs=(VMEM_SPEC, VMEM_SPEC, any_spec, VMEM_SPEC, any_spec),
        scratch_shapes=[
            pltpu.VMEM((groups - 1, length, width), BF),
            pltpu.VMEM((groups - 1, 8, length), F32),
            pltpu.VMEM((groups, owners, span, width), BF),
            pltpu.VMEM((groups, owners, 8, wide), F32),
            pltpu.VMEM((groups, owners, 8, wide), F32),
            pltpu.SemaphoreType.DMA((copies,)),
            pltpu.SemaphoreType.DMA((copies,)),
            pltpu.SemaphoreType.DMA((2 * groups * local,)),
        ],
        compiler_params=pltpu.CompilerParams(
            vmem_limit_bytes=61 * 1024 * 1024, collective_id=3, has_side_effects=True
        ),
        name="send_rows",
    )(x, gain, router, route_rows, slot_rows, slices)


def return_rows_kernel(
    owners, zones, capacity,
    rows_ref, hidden_in, pre_in, dey_in, sent_in, own_down_in, peer_down_in,
    gate_cols_ref, dgate_ref, slot_ref, gates_ref, route_ref, x_ref, gain_ref, router_ref, normed_ref, top_ref,
    dx_ref, dgain_ref, drouter_ref, *refs,
):
    outs, y_out, refs = (refs[0:2], refs[2:4]), refs[4], refs[5:]
    (hidden_ref, pre_ref, dey_ref, sent_ref, own_ref, peer_ref, load_sem, store_sem), refs = refs[:8], refs[8:]
    (down_ref, y_ref, down_sem, y_sem), refs = refs[:4], refs[4:]
    (back_ref, tags_ref, tags_in_ref, part_ref, part_in_ref, mark_ref, mark_in_ref, sum_ref, send_sem, recv_sem,
     local_sem) = refs
    owner, zone = lax.axis_index("expert"), lax.axis_index("shard")
    tags_ref[...] = jnp.zeros_like(tags_ref)
    greet_plane(owner, zone, owners, zones)
    send = sender(send_sem, recv_sem)
    groups = zones // 2
    local = rows_ref.shape[1]
    span = local * capacity
    chip = owner // 2
    cut = back_ref.shape[3] // 2
    lanes = [pl.ds(0, cut), pl.ds(cut, cut)]
    arrivals, stays, sent = {}, {}, []

    def ship(d, half):
        window = pl.ds(d * capacity, capacity)
        columns = slice(None) if half is None else lanes[half]
        for mask in peer_order(owners):
            target = flip(owner, mask)
            for part in range(local):
                source = rows_ref.at[target, part, window, columns]
                place = back_ref.at[d, owner, pl.ds(part * capacity, capacity), columns]
                if mask:
                    arrivals.setdefault((d, half, mask), []).append(send(source, place, (target, zone)))
                else:
                    at = (2 * d + (half or 0)) * local + part
                    copy = pltpu.make_async_copy(source, place, local_sem.at[at])
                    copy.start()
                    stays.setdefault((d, half), []).append(copy)

    def ship_tags(d):
        for mask in peer_order(owners):
            target = flip(owner, mask)
            columns = [dgate_ref[target, part, d * capacity:(d + 1) * capacity, :] for part in range(local)]
            column = jnp.concatenate(columns, axis=0)
            tags_ref[d, mask, :, 0:span] = jnp.broadcast_to(column, (span, 128)).T[0:8]
            if mask:
                arrivals.setdefault((d, "tags", mask), []).append(
                    send(tags_ref.at[d, mask], tags_in_ref.at[d, owner], (target, zone))
                )
            else:
                tags_in_ref[d, owner] = tags_ref[d, mask]

    def collect_zone(d, half):
        slots = slot_ref[d]
        columns = slice(None) if half is None else lanes[half]
        marks = [jnp.zeros((1, slots.shape[1]), F32) for _ in range(2)]
        for turn, hop in enumerate(list(range(1, owners // 2)) + [0]):
            for mask in (2 * hop, 2 * hop + 1):
                waits = arrivals.get((d, half, mask), [])
                if half != 1:
                    waits = waits + arrivals.get((d, "tags", mask), [])
                for copy in waits:
                    copy.wait_recv()
                if mask == 0:
                    for copy in stays[d, half]:
                        copy.wait()
            peer = flip(chip, hop)
            hits = slot_hits(slots, peer * (2 * span), 2 * span)
            rows = back_ref[d, pl.ds(2 * peer, 2), :, columns]
            added = tn(hits[0] + hits[1], rows.reshape(2 * span, rows.shape[2]))
            if turn == 0:
                sum_ref[:, columns] = added
            else:
                sum_ref[:, columns] += added
            if half == 1:
                continue
            tag = tags_in_ref[d, pl.ds(2 * peer, 2)]
            tag = jnp.concatenate([tag[0, 0:1, 0:span], tag[1, 0:1, 0:span]], axis=1)
            pieces = three_pieces(tag)
            for k in range(2):
                marks[k] = marks[k] + sum_pieces(nn(pieces, hits[k]))
        return marks

    def load(e):
        return [
            pltpu.make_async_copy(source, target.at[e], load_sem.at[e, i])
            for i, (source, target) in enumerate((
                (hidden_in.at[e], hidden_ref), (pre_in.at[e], pre_ref), (dey_in.at[e], dey_ref),
                (sent_in.at[:, e], sent_ref),
            ))
        ]

    def stores(turn):
        e, kind, slot = turn // 2, turn % 2, turn % 2
        return [
            pltpu.make_async_copy(ref.at[slot], out[kind].at[e], store_sem.at[slot, i])
            for i, (ref, out) in enumerate(((own_ref, outs[0]), (peer_ref, outs[1])))
        ]

    size = hidden_ref.shape[2] // 2
    width = dey_ref.shape[2]

    def weight_turn(turn):
        e, kind = turn // 2, turn % 2
        if kind == 0:
            for copy in load(e):
                copy.wait()
        if turn >= 2:
            for copy in stores(turn - 2):
                copy.wait()
        total = width if kind == 0 else size
        step = 256 if total % 256 == 0 else 128
        columns = size if kind == 0 else width

        @pl.loop(0, total // step)
        def _(i):
            at = pl.ds(pl.multiple_of(i * step, step), step)
            if kind == 0:
                rows = sent_ref[e, :, :, at].reshape(-1, step)
                own_ref[turn % 2, at, 0:columns] = tn(rows, pre_ref[e, :, 0:size])
                peer_ref[turn % 2, at, 0:columns] = tn(rows, pre_ref[e, :, size:]).astype(BF)
            else:
                peer_at = pl.ds(pl.multiple_of(i * step + size, step), step)
                own_ref[turn % 2, at, :] = tn(hidden_ref[e, :, at], dey_ref[e])
                peer_ref[turn % 2, at, :] = tn(hidden_ref[e, :, peer_at], dey_ref[e]).astype(BF)

        for copy in stores(turn):
            copy.start()

    def down_load(e):
        return [
            pltpu.make_async_copy(source.at[e], down_ref.at[e, i], down_sem.at[e, i])
            for i, source in enumerate((own_down_in, peer_down_in))
        ]

    group = y_ref.shape[1]
    tiles = owners // group

    def y_store(e, i):
        return pltpu.make_async_copy(
            y_ref.at[i % 2], y_out.at[pl.ds(i * group, group), e], y_sem.at[i % 2]
        )

    def y_turn(e):
        for copy in down_load(e):
            copy.wait()
        rows = group * sent_ref.shape[2]

        @pl.loop(0, tiles)
        def _(i):
            pl.when(i >= 2)(lambda: y_store(e, i - 2).wait())
            at = pl.ds(pl.multiple_of(i * rows, 16), rows)
            y = nn(hidden_ref[e, at, 0:size], down_ref[e, 0]) + nn(hidden_ref[e, at, size:], down_ref[e, 1])
            y = gate_cols_ref[pl.ds(i * group, group), e].reshape(rows, 1) * y
            y_ref[i % 2] = y.astype(BF).reshape(group, sent_ref.shape[2], width)
            y_store(e, i).start()

        for i in range(max(0, tiles - 2), tiles):
            y_store(e, i).wait()

    turns = 2 * hidden_ref.shape[0]
    for e in range(hidden_ref.shape[0]):
        for copy in load(e) + down_load(e):
            copy.start()
    for d in range(1, groups):
        ship(d, 0)
        ship_tags(d)
    incoming = {d: [] for d in range(1, groups)}
    for half in range(2):
        for turn in ((0, 1), (2,))[half]:
            weight_turn(turn)
        if half == 1:
            y_turn(0)
        for d in range(1, groups):
            for mask in peer_order(owners):
                for copy in arrivals.get((d, half, mask), []):
                    copy.wait_send()
            if half == 0:
                ship(d, 1)
        if half == 1:
            ship(0, None)
            ship_tags(0)
        for d in range(1, groups):
            device = (owner, (zone + 2 * d) % zones)
            marks = collect_zone(d, half)
            part_ref[d - 1, :, lanes[half]] = sum_ref[:, lanes[half]].astype(BF)
            incoming[d].append(
                send(part_ref.at[d - 1, :, lanes[half]], part_in_ref.at[d - 1, :, lanes[half]], device)
            )
            if half == 0:
                mark_ref[d - 1] = jnp.concatenate(marks + [jnp.zeros((6, marks[0].shape[1]), F32)], axis=0)
                incoming[d].append(send(mark_ref.at[d - 1], mark_in_ref.at[d - 1], device))
    for turn in range(3, turns):
        weight_turn(turn)
    for e in range(1, hidden_ref.shape[0]):
        y_turn(e)
    marks = collect_zone(0, None)
    for d in range(1, groups):
        for copy in incoming[d]:
            copy.wait_recv()
            sent.append(copy)
        sum_ref[...] += part_in_ref[d - 1].astype(F32)
        marks = [marks[k] + mark_in_ref[d - 1, k:k + 1, :] for k in range(2)]
    gates = [gates_ref[k:k + 1, :] for k in range(2)]
    mean = gates[0] * marks[0] + gates[1] * marks[1]
    ids = lax.broadcasted_iota(jnp.int32, (router_ref.shape[0], mean.shape[1]), 0)
    dlogits = jnp.zeros(ids.shape, F32)
    for k in range(2):
        dlogits = dlogits + jnp.where(route_ref[k:k + 1, :] == ids, gates[k] * (marks[k] - mean), 0.0)
    dlogits = dlogits.astype(BF)
    drouter_ref[...] = nn(dlogits, normed_ref[...])
    sum_ref[...] += tn(dlogits, router_ref[...])
    field = x_ref[...]
    inverse = inverse_rms(field)
    unit = field * inverse
    upper = sum_ref[...]
    scaled = upper * gain_ref[...]
    dgain_ref[...] = jnp.sum(upper * unit, axis=0, keepdims=True)
    dx_ref[...] = top_ref[...].astype(F32) + inverse * (
        scaled - unit * jnp.mean(scaled * unit, axis=1, keepdims=True)
    )
    for (d, half, _), copies in arrivals.items():
        if d == 0 or half == "tags":
            sent.extend(copies)
    for turn in range(max(0, turns - 2), turns):
        for copy in stores(turn):
            copy.wait()
    for copy in sent:
        copy.wait_send()


def return_rows(rows, hidden, pre, dey, sent, own_down, peer_down, gate_cols, dgate, slot_rows, gates, route_rows, x, gain, router, normed, top, zones, capacity):
    length, width = x.shape
    owners, local = rows.shape[:2]
    groups = zones // 2
    size = hidden.shape[2] // 2
    span = local * capacity
    wide = -(-span // 128) * 128
    copies = 3 * (groups - 1) + (owners - 1) * (local + 1 + (groups - 1) * (2 * local + 1))
    return pl.pallas_call(
        lambda *refs: return_rows_kernel(owners, zones, capacity, *refs),
        out_shape=(
            jax.ShapeDtypeStruct((length, width), F32),
            jax.ShapeDtypeStruct((1, width), F32),
            jax.ShapeDtypeStruct(router.shape, F32),
            jax.ShapeDtypeStruct((local, width, size), F32),
            jax.ShapeDtypeStruct((local, size, width), F32),
            jax.ShapeDtypeStruct((local, width, size), BF),
            jax.ShapeDtypeStruct((local, size, width), BF),
            jax.ShapeDtypeStruct(sent.shape, BF),
        ),
        in_specs=[HBM_SPEC] * 7 + [VMEM_SPEC] * 10,
        out_specs=[VMEM_SPEC] * 3 + [HBM_SPEC] * 5,
        scratch_shapes=[
            pltpu.VMEM(hidden.shape, BF),
            pltpu.VMEM(pre.shape, BF),
            pltpu.VMEM(dey.shape, BF),
            pltpu.VMEM((local, owners) + sent.shape[2:], BF),
            pltpu.VMEM((2, max(width, size), width), F32),
            pltpu.VMEM((2, max(width, size), width), BF),
            pltpu.SemaphoreType.DMA((local, 4)),
            pltpu.SemaphoreType.DMA((2, 2)),
            pltpu.VMEM((local, 2, size, width), BF),
            pltpu.VMEM((2, max(1, 384 // sent.shape[2])) + sent.shape[2:], BF),
            pltpu.SemaphoreType.DMA((local, 2)),
            pltpu.SemaphoreType.DMA((2,)),
            pltpu.VMEM((groups, owners, span, width), BF),
            pltpu.VMEM((groups, owners, 8, wide), F32),
            pltpu.VMEM((groups, owners, 8, wide), F32),
            pltpu.VMEM((groups - 1, length, width), BF),
            pltpu.VMEM((groups - 1, length, width), BF),
            pltpu.VMEM((groups - 1, 8, length), F32),
            pltpu.VMEM((groups - 1, 8, length), F32),
            pltpu.VMEM((length, width), F32),
            pltpu.SemaphoreType.DMA((copies,)),
            pltpu.SemaphoreType.DMA((copies,)),
            pltpu.SemaphoreType.DMA((2 * groups * local,)),
        ],
        compiler_params=pltpu.CompilerParams(
            vmem_limit_bytes=61 * 1024 * 1024, collective_id=4, has_side_effects=True
        ),
        name="return_rows",
    )(rows, hidden, pre, dey, sent, own_down, peer_down, gate_cols, dgate, slot_rows, gates, route_rows, x, gain, router, normed, top)


def experts_kernel(
    x_ref, c_ref, gate_ref, own_up_in, own_down_in, peer_up_in, peer_down_in,
    y_ref, dx_ref, dgate_ref, own_up_ref, own_down_ref, peer_up_ref, peer_down_ref,
    hidden_ref, pre_ref, dey_ref,
):
    sources, _, span, width = x_ref.shape
    size = own_up_in.shape[1]
    group = max(1, 384 // span)
    rows = group * span

    @pl.loop(0, sources // group)
    def _(i):
        at = pl.ds(i * group, group)
        rows_at = pl.ds(pl.multiple_of(i * rows, 16), rows)
        x = x_ref[at, 0].reshape(rows, width)
        c = c_ref[at, 0].reshape(rows, width)
        gate = gate_ref[at, 0].reshape(rows, 1)
        dey_ref[rows_at, :] = (gate * c.astype(F32)).astype(BF)
        dgate = jnp.zeros((rows, 1), F32)
        for part, (up_ref, down_ref) in enumerate(((own_up_in, own_down_in), (peer_up_in, peer_down_in))):
            cols = slice(part * size, part * size + size)
            hidden, slope = gelu_parts(nn(x, up_ref[...]))
            hidden = hidden.astype(BF)
            hidden_ref[rows_at, cols] = hidden
            back = nt(c, down_ref[...])
            dgate = dgate + jnp.sum(hidden.astype(F32) * back, axis=1, keepdims=True)
            pre_ref[rows_at, cols] = (gate * back * slope).astype(BF)
        y = nn(hidden_ref[rows_at, 0:size], own_down_in[...]) + nn(hidden_ref[rows_at, size:], peer_down_in[...])
        y_ref[at, 0] = (gate * y).astype(BF).reshape(group, span, width)
        dx = nt(pre_ref[rows_at, 0:size], own_up_in[...]) + nt(pre_ref[rows_at, size:], peer_up_in[...])
        dx_ref[at, 0] = dx.astype(BF).reshape(group, span, width)
        dgate_ref[at, 0] = dgate.reshape(group, span, 1)

    step = 256 if width % 256 == 0 else 128

    @pl.loop(0, width // step)
    def _(i):
        at = pl.ds(pl.multiple_of(i * step, step), step)
        x = x_ref[:, 0, :, at].reshape(sources * span, step)
        own_up_ref[at, :] = tn(x, pre_ref[:, 0:size])
        peer_up_ref[at, :] = tn(x, pre_ref[:, size:]).astype(BF)

    step = 256 if size % 256 == 0 else 128

    @pl.loop(0, size // step)
    def _(i):
        at = pl.ds(pl.multiple_of(i * step, step), step)
        own_down_ref[at, :] = tn(hidden_ref[:, at], dey_ref[...])
        peer_at = pl.ds(pl.multiple_of(i * step + size, step), step)
        peer_down_ref[at, :] = tn(hidden_ref[:, peer_at], dey_ref[...]).astype(BF)


def experts_rows_kernel(
    x_ref, c_ref, gate_ref, own_up_in, own_down_in, peer_up_in, peer_down_in,
    dx_ref, dgate_ref, hidden_ref, pre_ref, dey_ref,
):
    group, _, span, width = x_ref.shape
    size = own_up_in.shape[1]
    rows = group * span
    x = x_ref[:, 0].reshape(rows, width)
    c = c_ref[:, 0].reshape(rows, width)
    gate = gate_ref[:, 0].reshape(rows, 1)
    dey_ref[...] = (gate * c.astype(F32)).astype(BF)
    dgate = jnp.zeros((rows, 1), F32)
    for part, (up_ref, down_ref) in enumerate(((own_up_in, own_down_in), (peer_up_in, peer_down_in))):
        cols = slice(part * size, part * size + size)
        hidden, slope = gelu_parts(nn(x, up_ref[...]))
        hidden = hidden.astype(BF)
        hidden_ref[:, cols] = hidden
        back = nt(c, down_ref[...])
        dgate = dgate + jnp.sum(hidden.astype(F32) * back, axis=1, keepdims=True)
        pre_ref[:, cols] = (gate * back * slope).astype(BF)
    dx = nt(pre_ref[:, 0:size], own_up_in[...]) + nt(pre_ref[:, size:], peer_up_in[...])
    dx_ref[:, 0] = dx.astype(BF).reshape(group, span, width)
    dgate_ref[:, 0] = dgate.reshape(group, span, 1)


def run_experts(x, c, gate, own_up, own_down, peer_up, peer_down):
    sources, local, span, width = x.shape
    hidden = own_up.shape[2]
    lean = sources * span > 2048
    once = dict(pipeline_mode=pl.Buffered(1)) if lean else {}
    row_spec = pl.BlockSpec((sources, 1, span, width), lambda e: (0, e, 0, 0), **once)
    gate_spec = pl.BlockSpec((sources, 1, span, 1), lambda e: (0, e, 0, 0), **once)
    late_spec = pl.BlockSpec((sources, 1, span, width), lambda e: (0, e, 0, 0), pipeline_mode=pl.Buffered(1))
    sq = pl.Squeezed()
    gup_spec = pl.BlockSpec((sq, width, hidden), lambda e: (e, 0, 0))
    gdown_spec = pl.BlockSpec((sq, hidden, width), lambda e: (e, 0, 0))
    rows = local * sources * span
    return pl.pallas_call(
        experts_kernel,
        grid=(local,),
        out_shape=(
            jax.ShapeDtypeStruct(x.shape, BF),
            jax.ShapeDtypeStruct(x.shape, BF),
            jax.ShapeDtypeStruct(gate.shape, F32),
            jax.ShapeDtypeStruct((local, width, hidden), F32),
            jax.ShapeDtypeStruct((local, hidden, width), F32),
            jax.ShapeDtypeStruct((local, width, hidden), BF),
            jax.ShapeDtypeStruct((local, hidden, width), BF),
        ),
        in_specs=[row_spec, late_spec, gate_spec, gup_spec, gdown_spec, gup_spec, gdown_spec],
        out_specs=[late_spec, row_spec, gate_spec, gup_spec, gdown_spec, gup_spec, gdown_spec],
        scratch_shapes=[
            pltpu.VMEM((sources * span, 2 * hidden), BF),
            pltpu.VMEM((sources * span, 2 * hidden), BF),
            pltpu.VMEM((sources * span, width), BF),
        ],
        compiler_params=pltpu.CompilerParams(vmem_limit_bytes=60 * 1024 * 1024),
        cost_estimate=pl.CostEstimate(
            flops=24 * rows * width * hidden, bytes_accessed=16 * rows * width, transcendentals=2 * rows * hidden,
        ),
        name="experts",
    )(x, c, gate, own_up, own_down, peer_up, peer_down)


def run_expert_rows(x, c, gate, own_up, own_down, peer_up, peer_down):
    sources, local, span, width = x.shape
    hidden = own_up.shape[2]
    group = max(1, 384 // span)
    rows = group * span
    tiles = sources // group
    row_spec = pl.BlockSpec((group, 1, span, width), lambda e, i: (i, e, 0, 0))
    gate_spec = pl.BlockSpec((group, 1, span, 1), lambda e, i: (i, e, 0, 0))
    sq = pl.Squeezed()
    up_spec = pl.BlockSpec((sq, width, hidden), lambda e, i: (e, 0, 0))
    down_spec = pl.BlockSpec((sq, hidden, width), lambda e, i: (e, 0, 0))
    wide_spec = pl.BlockSpec((sq, rows, 2 * hidden), lambda e, i: (e, i, 0))
    dey_spec = pl.BlockSpec((sq, rows, width), lambda e, i: (e, i, 0))
    everything = local * sources * span
    return pl.pallas_call(
        experts_rows_kernel,
        grid=(local, tiles),
        out_shape=(
            jax.ShapeDtypeStruct(x.shape, BF),
            jax.ShapeDtypeStruct(gate.shape, F32),
            jax.ShapeDtypeStruct((local, sources * span, 2 * hidden), BF),
            jax.ShapeDtypeStruct((local, sources * span, 2 * hidden), BF),
            jax.ShapeDtypeStruct((local, sources * span, width), BF),
        ),
        in_specs=[row_spec, row_spec, gate_spec, up_spec, down_spec, up_spec, down_spec],
        out_specs=[row_spec, gate_spec, wide_spec, wide_spec, dey_spec],
        compiler_params=pltpu.CompilerParams(vmem_limit_bytes=60 * 1024 * 1024),
        cost_estimate=pl.CostEstimate(
            flops=12 * everything * width * hidden, bytes_accessed=16 * everything * width,
            transcendentals=2 * everything * hidden,
        ),
        name="expert_rows",
    )(x, c, gate, own_up, own_down, peer_up, peer_down)


def spread_kernel(slot_ref, rows_ref, out_ref):
    experts, zones, capacity, width = out_ref.shape
    take = max(1, 384 // capacity)

    def chunk(i, _):
        for zone in range(zones):
            hits = slot_hits(slot_ref[zone], i * (take * capacity), take * capacity)
            picked = nn(hits[0] + hits[1], rows_ref[zone])
            out_ref[pl.ds(i * take, take), zone] = picked.reshape(take, capacity, width).astype(BF)
        return 0

    lax.fori_loop(0, experts // take, chunk, 0)


def spread(slot_rows, rows, experts, capacity):
    zones, length, width = rows.shape
    return pl.pallas_call(
        spread_kernel,
        out_shape=jax.ShapeDtypeStruct((experts, zones, capacity, width), BF),
        in_specs=[VMEM_SPEC] * 2,
        out_specs=VMEM_SPEC,
        compiler_params=pltpu.CompilerParams(vmem_limit_bytes=VMEM_BYTES),
        cost_estimate=pl.CostEstimate(
            flops=2 * zones * experts * capacity * length * width,
            bytes_accessed=2 * zones * (experts * capacity + length) * width, transcendentals=0,
        ),
        name="spread",
    )(slot_rows, rows)


def collect_kernel(first, slot_ref, rows_ref, out_ref):
    experts, zones, capacity, width = rows_ref.shape
    length = out_ref.shape[1]
    take = max(1, 384 // capacity)
    out_ref[...] = jnp.zeros_like(out_ref)

    def chunk(i, _):
        for zone in range(first, zones):
            hits = slot_hits(slot_ref[zone], i * (take * capacity), take * capacity)
            rows = rows_ref[pl.ds(i * take, take), zone].reshape(take * capacity, width)
            out_ref[zone - first] += tn(hits[0] + hits[1], rows)
        return 0

    lax.fori_loop(0, experts // take, chunk, 0)


def collect(slot_rows, rows, first=0):
    experts, zones, capacity, width = rows.shape
    length = slot_rows.shape[2]
    return pl.pallas_call(
        lambda *refs: collect_kernel(first, *refs),
        out_shape=jax.ShapeDtypeStruct((zones - first, length, width), F32),
        in_specs=[VMEM_SPEC] * 2,
        out_specs=VMEM_SPEC,
        compiler_params=pltpu.CompilerParams(vmem_limit_bytes=VMEM_BYTES),
        cost_estimate=pl.CostEstimate(
            flops=2 * zones * experts * capacity * length * width,
            bytes_accessed=2 * zones * (experts * capacity + 2 * length) * width, transcendentals=0,
        ),
        name="collect",
    )(slot_rows, rows)


bucket_edges = (1, 2, 3, 4, 6, 8, 12, 16, 24, 32, 48, 64, 96, 128, 192, 256, 384, 512, 768, 1024, 1536)


def bucket_onehot(length, buckets):
    distance = (length - 1) - jnp.arange(2 * length, dtype=jnp.int32)
    edge_list = jnp.array(bucket_edges, dtype=jnp.int32)
    magnitude = jnp.sum(
        (jnp.abs(distance)[:, None] >= edge_list[None, :]).astype(jnp.int32), axis=1, dtype=jnp.int32
    )
    bucket = magnitude + buckets // 2 * (distance > 0).astype(jnp.int32)
    real = jnp.arange(2 * length)[:, None] < 2 * length - 1
    hit = (bucket[:, None] == jnp.arange(buckets, dtype=jnp.int32)[None, :]) & real
    return hit.astype(F32)


def shift_from(value, distance):
    size = lax.axis_size("shard")
    return lax.ppermute(value, "shard", [((z + distance) % size, z) for z in range(size)])


def shift_to(value, distance):
    size = lax.axis_size("shard")
    return lax.ppermute(value, "shard", [(z, (z + distance) % size) for z in range(size)])


def swap_pair(value):
    return lax.ppermute(value, "shard", [(z, z ^ 1) for z in range(lax.axis_size("shard"))])


def exchange(value):
    return lax.all_to_all(value, "expert", split_axis=0, concat_axis=0, tiled=True)


def per_device(
    tokens, piece_start, routes, norm_gains, bias_tables, qkv_weight, out_weight, mlp_up, mlp_down, router,
    expert_up, expert_down, cotangent,
):
    length, width = tokens.shape
    owners = lax.axis_size("expert")
    zones = lax.axis_size("shard") // 2
    local = expert_up.shape[0]
    experts_all = local * owners
    capacity = 3 * routes.shape[1] * length // (2 * experts_all)
    qkv_cols, out_cols = qkv_weight.shape[2], out_weight.shape[2]
    zones_all = 2 * zones
    router_pad = 16
    direct = capacity % 16 == 0
    parts = mlp_down.shape[0] // qkv_weight.shape[1]
    aligned = qkv_cols % 16 == 0 and out_cols % 16 == 0 and qkv_cols % out_cols == 0

    def padded(block):
        return jnp.pad(block, ((0, 0), (0, -block.shape[1] % 128)))

    down_block = mlp_down.reshape(parts, -1, mlp_down.shape[1]).transpose(1, 0, 2).reshape(qkv_weight.shape[1], -1)
    router_block = jnp.pad(router, ((0, 0), (0, router_pad - router.shape[1])))
    route_rows = routes.T
    first, up_full, down_full, last, slot_rows, cotangent_rows = gather_weights(
        [
            padded(jnp.concatenate([qkv_weight[0], out_weight[0]], axis=1)),
            padded(mlp_up),
            padded(down_block),
            padded(jnp.concatenate([qkv_weight[1], out_weight[1], router_block], axis=1)),
        ],
        (qkv_cols + out_cols, mlp_up.shape[1], parts * mlp_down.shape[1], qkv_cols + out_cols + router_pad),
        cotangent, route_rows, owners, zones_all, experts_all, capacity,
    )

    def layer_weights(block):
        if aligned:
            return (block, qkv_cols, out_cols)
        flat = (block[:, :qkv_cols].reshape(1, -1, width), block[:, qkv_cols:qkv_cols + out_cols].reshape(1, -1, width))
        return (flat, 3 * width, width)

    up_full = up_full.reshape(-1, width)
    if mlp_down.shape[1] % 16:
        down_full = down_full.reshape(owners, parts, -1, width).transpose(1, 0, 2, 3).reshape(1, -1, width)
    router_full = last[:, qkv_cols + out_cols:qkv_cols + out_cols + router.shape[1]].reshape(experts_all, width)

    first, up_late = lax.optimization_barrier((first, expert_up))
    weights0, weights1 = layer_weights(first), layer_weights(last)
    up_other = swap_pair(up_late)

    def dispatch(rows):
        packed = spread(slot_rows, rows, experts_all, capacity)
        return exchange(packed.reshape(owners, local, zones * capacity, width))

    if direct:
        cotangent_rows = exchange(cotangent_rows.reshape(owners, local, zones * capacity, width))
    else:
        cotangent_rows = dispatch(jnp.concatenate([cotangent[None], cotangent_rows]))

    def undo(rows):
        back = exchange(rows).reshape(experts_all, zones, capacity, width)
        return collect(slot_rows, back)


    onehot = bucket_onehot(length, bias_tables.shape[2])
    vectors = lax.dot_general(
        bias_tables, onehot, (((2,), (1,)), ((), ())), precision=lax.Precision.HIGHEST
    )
    gains = [norm_gains[i:i + 1] for i in range(4)]
    x0 = tokens.astype(F32)
    x1, ah0, qkv0, o0, lse0 = attend(piece_start, x0, gains[0], weights0, vectors[0])
    x2, mh = mlp(x1, gains[1], up_full, down_full, parts, zones_all)
    x3, ah1, qkv1, o1, lse1 = attend(piece_start, x2, gains[2], weights1, vectors[1])

    x3, up_other, cotangent_rows = lax.optimization_barrier((x3, up_other, cotangent_rows))
    if direct:
        eh, gates, eh_rows, gate_rows, down_other = send_rows(
            x3, gains[3], router_full, route_rows, slot_rows, expert_down, owners, zones_all, local, capacity
        )
    else:
        down_other = swap_pair(expert_down)
        eh = (x3 * inverse_rms(x3) * gains[3]).astype(BF)
        gates = jnp.concatenate(softmax_pair(nt(router_full, eh), route_rows))
        eh_rows = dispatch(jnp.stack([eh] + [shift_from(eh, 2 * d) for d in range(1, zones)]))
        slot_ids = jnp.arange(experts_all * capacity, dtype=jnp.int32).astype(F32)
        marks = [slot_rows[d, :2][None] == slot_ids[:, None, None] for d in range(zones)]

        def gate_slots(d):
            held = gates if d == 0 else shift_from(gates, 2 * d)
            return jnp.sum(jnp.where(marks[d], held[None], 0.0), axis=(1, 2)).reshape(experts_all, capacity)

        gate_rows = exchange(
            jnp.stack([gate_slots(d) for d in range(zones)], axis=1).reshape(owners, local, zones * capacity)
        )[..., None]
    expert_weights = (expert_up, expert_down, up_other, down_other)
    if direct:
        dx_rows, dgate_rows, hidden_rows, pre_rows, dey_rows = run_expert_rows(
            eh_rows, cotangent_rows, gate_rows, *expert_weights
        )
        dx3, dgain3, grad_router, own_up, own_down, peer_up, peer_down, y_rows = return_rows(
            dx_rows, hidden_rows, pre_rows, dey_rows, eh_rows, expert_down, down_other, gate_rows, dgate_rows,
            slot_rows, gates, route_rows, x3, gains[3], router_full, eh, cotangent, zones_all, capacity,
        )
    else:
        y_rows, dx_rows, dgate_rows, own_up, own_down, peer_up, peer_down = run_experts(
            eh_rows, cotangent_rows, gate_rows, *expert_weights
        )
        dx_back = undo(dx_rows)
        dgate_back = exchange(dgate_rows[..., 0]).reshape(experts_all, zones, capacity)
        token_grad, gate_grad = dx_back[0], 0.0
        for d in range(zones):
            part = jnp.sum(jnp.where(marks[d], dgate_back[:, d].reshape(-1)[:, None, None], 0.0), axis=0)
            gate_grad = gate_grad + (part if d == 0 else shift_to(part, 2 * d))
        for d in range(1, zones):
            token_grad = token_grad + shift_to(dx_back[d].astype(BF), 2 * d).astype(F32)
        dchoice = gates * (gate_grad - jnp.sum(gates * gate_grad, axis=0, keepdims=True))
        chosen = route_rows[:, None, :] == jnp.arange(experts_all, dtype=jnp.int32)[None, :, None]
        dlogits = jnp.sum(jnp.where(chosen, dchoice[:, None, :], 0.0), axis=0).astype(BF)
        grad_router = nn(dlogits, eh)
        deh = token_grad + tn(dlogits, router_full)
        unit3 = x3 * inverse_rms(x3)
        scaled = deh * gains[3]
        dx3 = cotangent.astype(F32) + inverse_rms(x3) * (
            scaled - unit3 * jnp.mean(scaled * unit3, axis=1, keepdims=True)
        )
        dgain3 = jnp.sum(deh * unit3, axis=0)[None]
    router_rows = jnp.pad(
        grad_router.astype(BF).reshape(owners, local, width), ((0, 0), (0, router_pad - local), (0, 0))
    )

    def layer_grads(results, tail=None):
        grads = results[1:-2]
        if not aligned:
            pieces = [g.reshape(owners, -1, width) for g in grads] + ([] if tail is None else [tail])
            grads = [jnp.concatenate(pieces, axis=1)]
        return results[0], grads[0], results[-2], results[-1]

    dx3, y_rows = lax.optimization_barrier((dx3, y_rows))
    y_back = exchange(y_rows)
    dx2, last_part, dvec1, dgain2 = layer_grads(
        attend_back(
            piece_start, x2, gains[2], weights1, vectors[1], ah1, qkv1, o1, lse1, dx3, router_rows if aligned else None,
        ),
        router_rows,
    )
    peer_up = swap_pair(peer_up)
    dx2, peer_down = lax.optimization_barrier((dx2, peer_down))
    peer_down = swap_pair(peer_down)
    dx1, up_part, down_part, dgain1 = mlp_back(
        x1, gains[1], up_full, down_full, mh, dx2, parts, zones_all
    )
    if mlp_down.shape[1] % 16:
        down_part = down_part.reshape(parts, owners, -1, width).transpose(1, 0, 2, 3)
    dx1, y_back, peer_up = lax.optimization_barrier((dx1, y_back, peer_up))
    ride = Ride(
        [last_part, up_part.reshape(owners, -1, width)], 0, [], (y_back, slot_rows) if direct else None,
        owners, zones_all, capacity, width, 6,
    )
    last_own, up_own, *results = attend_back(
        piece_start, x0, gains[0], weights0, vectors[0], ah0, qkv0, o0, lse0, dx1, None, ride
    )
    y_near = results.pop(0) if direct else None
    dx0, first_part, dvec0, dgain0 = layer_grads(results)
    dx0, peer_down = lax.optimization_barrier((dx0, peer_down))
    dtables = lax.dot_general(
        jnp.stack([dvec0, dvec1]), onehot, (((2,), (0,)), ((), ())), precision=lax.Precision.HIGHEST
    )
    dgains = jnp.concatenate([dgain0, dgain1, dgain2, dgain3])
    small = jnp.concatenate([dgains.reshape(-1), dtables.reshape(-1)])
    small = jnp.pad(small, (0, -small.size % 1024)).reshape(-1, 128)
    last_grad, up_grad, down_grad, first_grad, small, grad_up, grad_down, *finals = finish(
        (last_own, up_own), down_part.reshape(owners, -1, width), first_part, small, (own_up, own_down), (peer_up, peer_down), owners, zones_all, capacity,
        (y_back, slot_rows, x3, y_near) if direct else None,
    )
    grad_up, grad_down = grad_up.reshape(own_up.shape), grad_down.reshape(own_down.shape)
    if direct:
        output = finals[0]
    else:
        y_zones = collect(slot_rows, y_back.reshape(experts_all, zones, capacity, width))
        output = x3 + y_zones[0]
        for d in range(1, zones):
            output = output + shift_to(y_zones[d].astype(BF), 2 * d).astype(F32)
        output = output.astype(BF)
    small = small.reshape(-1)
    grad_qkv = jnp.stack([first_grad[:, :qkv_cols], last_grad[:, :qkv_cols]])
    grad_out = jnp.stack(
        [first_grad[:, qkv_cols:qkv_cols + out_cols], last_grad[:, qkv_cols:qkv_cols + out_cols]]
    )
    grad_router_out = last_grad[:, qkv_cols + out_cols:qkv_cols + out_cols + local]
    grad_mlp_up = up_grad[:, :mlp_up.shape[1]]
    down_cols = mlp_down.shape[1]
    grad_mlp_down = down_grad[:, :parts * down_cols].reshape(-1, parts, down_cols).transpose(1, 0, 2)
    grad_mlp_down = grad_mlp_down.reshape(mlp_down.shape)
    return (
        output,
        dx0,
        small[:dgains.size].reshape(dgains.shape),
        small[dgains.size:dgains.size + dtables.size].reshape(dtables.shape),
        grad_qkv,
        grad_out,
        grad_mlp_up,
        grad_mlp_down,
        grad_router_out,
        grad_up,
        grad_down,
    )


def solution(mesh):
    both = P(("expert", "shard"), None)
    split3, split2 = P(None, "shard", "expert"), P("shard", "expert")
    up_spec, down_spec = P("expert", None, "shard"), P("expert", "shard", None)
    in_specs = (
        both, P(("expert", "shard")), both, P(), P(), split3, split3, split2, split2, split2, up_spec, down_spec, both
    )
    out_specs = (both, both, P(), P(), split3, split3, split2, split2, split2, up_spec, down_spec)
    return jax.shard_map(per_device, mesh=mesh, in_specs=in_specs, out_specs=out_specs, check_vma=False)
```

```python
import jax
import jax.numpy as jnp
from jax import lax
from jax.experimental import pallas as pl
from jax.experimental.pallas import tpu as pltpu
from jax.sharding import PartitionSpec as P

PIECE = 256
norm_eps = 1e-06
far_below = -1e30
BF = jnp.bfloat16
F32 = jnp.float32
VMEM_BYTES = 56 * 1024 * 1024


def nn(a, b):
    return lax.dot_general(a, b, (((1,), (0,)), ((), ())), preferred_element_type=F32)


def nt(a, b):
    return lax.dot_general(a, b, (((1,), (1,)), ((), ())), preferred_element_type=F32)


def tn(a, b):
    return lax.dot_general(a, b, (((0,), (0,)), ((), ())), preferred_element_type=F32)


def inverse_rms(field):
    return lax.rsqrt(jnp.mean(field * field, axis=1, keepdims=True) + norm_eps)


def gelu_parts(u):
    cubic = 0.7978845608028654 * (u + 0.044715 * (u * u * u))
    bend = jnp.tanh(cubic)
    half = 0.5 * (1.0 + bend)
    slope = half + 0.5 * u * (1.0 - bend * bend) * (0.7978845608028654 * (1.0 + 0.134145 * (u * u)))
    return u * half, slope


def gelu_of(u):
    return 0.5 * u * (1.0 + jnp.tanh(0.7978845608028654 * (u + 0.044715 * (u * u * u))))


def fill_mask(piece_ref, mask_ref):
    length = mask_ref.shape[0]
    first = piece_ref[0]
    key_pos = lax.broadcasted_iota(jnp.int32, (length, length), 0)
    query_pos = lax.broadcasted_iota(jnp.int32, (length, length), 1)
    key_in = (key_pos >= first) & (key_pos < first + PIECE)
    query_in = (query_pos >= first) & (query_pos < first + PIECE)
    keep = (key_pos <= query_pos) | (key_in & query_in)
    mask_ref[...] = jnp.where(keep, 0.0, far_below)


def bias_strip(vector_row, strip_ref):
    wide = jnp.broadcast_to(vector_row, (128, vector_row.shape[1]))
    strip_ref[...] = pltpu.roll(wide, vector_row.shape[1] - 127, 1, stride=1, stride_axis=0)


def flatten(blocks_ref, flat_ref, sems):
    rows = blocks_ref.shape[1]
    copies = [
        pltpu.make_async_copy(blocks_ref.at[i], flat_ref.at[pl.ds(i * rows, rows), :], sems.at[i])
        for i in range(blocks_ref.shape[0])
    ]
    for copy in copies:
        copy.start()
    return copies


def arrive(copies):
    for copy in copies:
        copy.wait()


def unflatten(flat_ref, blocks_ref, start):
    count = blocks_ref.shape[0]
    rows = flat_ref.shape[0] // count
    for i in range(count):
        blocks_ref[i, start:start + rows, :] = flat_ref[i * rows:i * rows + rows, :]


def weight_specs(weights):
    packed, qkv_rows, out_rows = weights
    if isinstance(packed, tuple):
        return list(packed), [HBM_SPEC, HBM_SPEC]
    return [packed], [HBM_SPEC]


def weight_sems(weights):
    packed = weights[0]
    count = 1 if isinstance(packed, tuple) else packed.shape[0]
    return [pltpu.SemaphoreType.DMA((count,)), pltpu.SemaphoreType.DMA((count,))]


def weight_views(weights, refs):
    packed, qkv_rows, out_rows = weights
    if isinstance(packed, tuple):
        return refs[0], refs[1], refs[2:]
    return refs[0].at[:, 0:qkv_rows, :], refs[0].at[:, qkv_rows:qkv_rows + out_rows, :], refs[1:]


def attend_kernel(
    weights, piece_ref, x_ref, gain_ref, *refs
):
    w_ref, wo_ref, refs = weight_views(weights, refs)
    (vec_ref, out_ref, normed_ref, qkv_ref, mixed_ref, lse_ref,
     mask_ref, strip_ref, score_ref, prob_ref, flat_ref, flat_out_ref, w_sem, wo_sem) = refs
    length, width = x_ref.shape
    w_copies = flatten(w_ref, flat_ref, w_sem)
    wo_copies = flatten(wo_ref, flat_out_ref, wo_sem)
    tiles = length // 128
    fill_mask(piece_ref, mask_ref)
    field = x_ref[...].astype(F32)
    normed_ref[...] = (field * inverse_rms(field) * gain_ref[...]).astype(BF)

    arrive(w_copies)

    def project(c, _):
        cols = pl.ds(pl.multiple_of(c * 256, 256), 256)
        qkv_ref[:, cols] = nt(normed_ref[...], flat_ref[cols, :]).astype(BF)
        return 0

    lax.fori_loop(0, 3 * width // 256, project, 0)
    lane_low = lax.broadcasted_iota(jnp.int32, (length, 128), 1) < 64
    row_low = lax.broadcasted_iota(jnp.int32, (128, length), 0) < 64

    def pair(hp, _):
        base = hp * 128
        q2 = qkv_ref[:, pl.ds(pl.multiple_of(base, 128), 128)] * jnp.asarray(0.125, BF)
        v2 = qkv_ref[:, pl.ds(pl.multiple_of(2 * width + base, 128), 128)]
        mixed = []
        for half in range(2):
            head = hp * 2 + half
            keep = lane_low if half == 0 else ~lane_low
            qm = jnp.where(keep, q2, jnp.zeros_like(q2))
            bias_strip(vec_ref[pl.ds(head, 1), :], strip_ref)
            peak = jnp.full((1, length), far_below, F32)
            for jt in range(tiles):
                rows = slice(jt * 128, jt * 128 + 128)
                k2 = qkv_ref[rows, pl.ds(pl.multiple_of(width + base, 128), 128)]
                at = 128 * (tiles - 1 - jt)
                s = nt(k2, qm) + strip_ref[:, at:at + length] + mask_ref[rows, :]
                score_ref[rows, :] = s
                peak = jnp.maximum(peak, jnp.max(s, axis=0, keepdims=True))
            total = jnp.zeros((1, length), F32)
            for jt in range(tiles):
                rows = slice(jt * 128, jt * 128 + 128)
                e = jnp.exp(score_ref[rows, :] - peak)
                total = total + jnp.sum(e, axis=0, keepdims=True)
                prob_ref[rows, :] = e.astype(BF)
            lse_ref[pl.ds(head, 1), :] = peak + jnp.log(total)
            mixed.append(tn(v2, prob_ref[...]) * (1.0 / total))
        both = jnp.where(row_low, mixed[0], mixed[1]).astype(BF)
        mixed_ref[:, pl.ds(pl.multiple_of(base, 128), 128)] = both.T
        return 0

    lax.fori_loop(0, width // 128, pair, 0)

    arrive(wo_copies)

    def back(c, _):
        cols = pl.ds(pl.multiple_of(c * 256, 256), 256)
        out_ref[:, cols] = x_ref[:, cols].astype(F32) + nt(mixed_ref[...], flat_out_ref[cols, :])
        return 0

    lax.fori_loop(0, width // 256, back, 0)


HBM_SPEC = pl.BlockSpec(memory_space=pltpu.HBM)
SMEM_SPEC = pl.BlockSpec(memory_space=pltpu.SMEM)
VMEM_SPEC = pl.BlockSpec(memory_space=pltpu.VMEM)


def attend(piece, x, gain, weights, vectors):
    length, width = x.shape
    w_args, w_specs = weight_specs(weights)
    heads = vectors.shape[0]
    span = vectors.shape[1]
    return pl.pallas_call(
        lambda *refs: attend_kernel(weights, *refs),
        out_shape=(
            jax.ShapeDtypeStruct((length, width), F32),
            jax.ShapeDtypeStruct((length, width), BF),
            jax.ShapeDtypeStruct((length, 3 * width), BF),
            jax.ShapeDtypeStruct((length, width), BF),
            jax.ShapeDtypeStruct((heads, length), F32),
        ),
        in_specs=[SMEM_SPEC] + [VMEM_SPEC] * 2 + w_specs + [VMEM_SPEC],
        out_specs=[VMEM_SPEC] * 5,
        scratch_shapes=[
            pltpu.VMEM((length, length), F32),
            pltpu.VMEM((128, span), F32),
            pltpu.VMEM((length, length), F32),
            pltpu.VMEM((length, length), BF),
            pltpu.VMEM((3 * width, width), BF),
            pltpu.VMEM((width, width), BF),
        ] + weight_sems(weights),
        compiler_params=pltpu.CompilerParams(vmem_limit_bytes=VMEM_BYTES),
        cost_estimate=pl.CostEstimate(
            flops=8 * length * width * width + 4 * length * length * width,
            bytes_accessed=20 * length * width + 8 * width * width,
            transcendentals=heads * length * length,
        ),
        name="attend",
    )(piece, x, gain, *w_args, vectors)


def attend_back_kernel(
    tail, weights, ride, piece_ref, x_ref, gain_ref, *refs
):
    ride_refs, refs = (refs[len(refs) - ride.scratch:], refs[:len(refs) - ride.scratch]) if ride else ((), refs)
    w_ref, wo_ref, refs = weight_views(weights, refs)
    (vec_ref, normed_ref, qkv_ref, mixed_ref, lse_ref, grad_ref), refs = refs[:6], refs[6:]
    tail_ref, refs = (refs[0], refs[1:]) if tail else (None, refs)
    rides_in, refs = (refs[:ride.inputs], refs[ride.inputs:]) if ride else ((), refs)
    rides_out, refs = (refs[:ride.outputs], refs[ride.outputs:]) if ride else ((), refs)
    grad_refs, refs = (refs[1:len(refs) - 15], refs[:1] + refs[len(refs) - 15:])
    (dx_ref, dvec_ref, dgain_ref,
     mask_ref, strip_ref, sums_ref, prob_ref, ds_ref, low_ref, do_ref, dqkv_ref, delta_ref,
     flat_ref, flat_out_ref, w_sem, wo_sem) = refs
    wo_copies = flatten(wo_ref, flat_out_ref, wo_sem)
    w_copies = flatten(w_ref, flat_ref, w_sem)
    turns, rows_turn, end = (
        ride.board(rides_in, rides_out, ride_refs, dx_ref, low_ref) if ride else ([], None, None)
    )
    length, width = x_ref.shape
    heads = vec_ref.shape[0]
    tiles = length // 128
    fill_mask(piece_ref, mask_ref)
    low_ref[...] = grad_ref[...].astype(BF)

    arrive(wo_copies)

    def out_back(c, _):
        cols = pl.ds(pl.multiple_of(c * 256, 256), 256)
        do_ref[:, cols] = nn(low_ref[...], flat_out_ref[:, cols]).astype(BF)
        return 0

    lax.fori_loop(0, width // 256, out_back, 0)

    def out_weights_back(c, _):
        cols = pl.ds(pl.multiple_of(c * 256, 256), 256)
        flat_out_ref[cols, :] = tn(low_ref[:, cols], mixed_ref[...]).astype(BF)
        return 0

    lax.fori_loop(0, width // 256, out_weights_back, 0)
    pick = (
        lax.broadcasted_iota(jnp.int32, (delta_ref.shape[0], width), 1) // (width // heads)
        == lax.broadcasted_iota(jnp.int32, (delta_ref.shape[0], width), 0)
    ).astype(F32)
    delta_ref[...] = lax.dot_general(
        pick, do_ref[...].astype(F32) * mixed_ref[...].astype(F32), (((1,), (1,)), ((), ())),
        precision=lax.Precision.HIGHEST, preferred_element_type=F32,
    )
    lane_low = lax.broadcasted_iota(jnp.int32, (length, 128), 1) < 64
    lane_low_tile = lax.broadcasted_iota(jnp.int32, (128, 128), 1) < 64
    row_low = lax.broadcasted_iota(jnp.int32, (128, length), 0) < 64
    flip = (
        lax.broadcasted_iota(jnp.int32, (128, 128), 0) + lax.broadcasted_iota(jnp.int32, (128, 128), 1) == 127
    ).astype(F32)
    sums_ref[...] = jnp.zeros_like(sums_ref)

    def pair(hp, _):
        for at, turn in enumerate(turns):
            pl.when(hp == min(3 * at, width // 128 - 1))(turn)
        if rows_turn is not None:
            pl.when(hp == 1)(rows_turn)
        base = hp * 128
        q_cols = pl.ds(pl.multiple_of(base, 128), 128)
        k_cols = pl.ds(pl.multiple_of(width + base, 128), 128)
        v_cols = pl.ds(pl.multiple_of(2 * width + base, 128), 128)
        q2 = qkv_ref[:, q_cols] * jnp.asarray(0.125, BF)
        do2 = do_ref[:, q_cols]
        parts = []
        for half in range(2):
            head = hp * 2 + half
            keep = lane_low if half == 0 else ~lane_low
            qm = jnp.where(keep, q2, jnp.zeros_like(q2))
            dm = jnp.where(keep, do2, jnp.zeros_like(do2))
            bias_strip(vec_ref[pl.ds(head, 1), :], strip_ref)
            lse = lse_ref[pl.ds(head, 1), :]
            delta = delta_ref[pl.ds(head, 1), :]
            for jt in range(tiles):
                rows = slice(jt * 128, jt * 128 + 128)
                at = 128 * (tiles - 1 - jt)
                s = nt(qkv_ref[rows, k_cols], qm) + strip_ref[:, at:at + length] + mask_ref[rows, :]
                p = jnp.exp(s - lse)
                dp = nt(qkv_ref[rows, v_cols], dm)
                ds = (p * (dp - delta)).astype(BF)
                prob_ref[half, rows, :] = p.astype(BF)
                ds_ref[half, rows, :] = ds
                if jt == 0:
                    sums_ref[:, at:at + length] = ds.astype(F32)
                    sums_ref[:, 0:at] = jnp.zeros((128, at), F32)
                else:
                    sums_ref[:, at:at + length] += ds.astype(F32)
            turned = lax.dot_general(
                flip, sums_ref[...], (((1,), (0,)), ((), ())),
                precision=lax.Precision.HIGHEST, preferred_element_type=F32,
            )
            turned = pltpu.roll(turned, 0, 1, stride=1, stride_axis=0)
            dvec_ref[pl.ds(head, 1), :] = jnp.sum(turned, axis=0, keepdims=True)
            parts.append(tn(qkv_ref[:, k_cols], ds_ref[half]) * 0.125)
        both = jnp.where(row_low, parts[0], parts[1]).astype(BF)
        dqkv_ref[:, q_cols] = both.T
        for jt in range(tiles):
            rows = slice(jt * 128, jt * 128 + 128)
            dk = jnp.where(lane_low_tile, nn(ds_ref[0, rows, :], q2), nn(ds_ref[1, rows, :], q2))
            dqkv_ref[rows, k_cols] = dk.astype(BF)
            dv = jnp.where(lane_low_tile, nn(prob_ref[0, rows, :], do2), nn(prob_ref[1, rows, :], do2))
            dqkv_ref[rows, v_cols] = dv.astype(BF)
        return 0

    lax.fori_loop(0, width // 128, pair, 0)

    arrive(w_copies)

    def rows_back(c, _):
        cols = pl.ds(pl.multiple_of(c * 256, 256), 256)
        dx_ref[:, cols] = nn(dqkv_ref[...], flat_ref[:, cols])
        return 0

    lax.fori_loop(0, width // 256, rows_back, 0)
    def weights_back(c, _):
        cols = pl.ds(pl.multiple_of(c * 256, 256), 256)
        flat_ref[cols, :] = tn(dqkv_ref[:, cols], normed_ref[...]).astype(BF)
        return 0

    lax.fori_loop(0, 3 * width // 256, weights_back, 0)

    qkv_rows = w_ref.shape[1]
    unflatten(flat_ref, grad_refs[0], 0)
    unflatten(flat_out_ref, grad_refs[-1], qkv_rows if len(grad_refs) == 1 else 0)
    if tail:
        start = qkv_rows + wo_ref.shape[1]
        for i in range(tail_ref.shape[0]):
            grad_refs[0][i, start:, :] = tail_ref[i]
    norm_back(x_ref, gain_ref, dx_ref, grad_ref, dx_ref, dgain_ref)
    if ride:
        end()


def norm_back(x_ref, gain_ref, upper_ref, base_ref, dx_ref, dgain_ref):
    field = x_ref[...].astype(F32)
    inverse = inverse_rms(field)
    unit = field * inverse
    upper = upper_ref[...]
    scaled = upper * gain_ref[...]
    dgain_ref[...] = jnp.sum(upper * unit, axis=0, keepdims=True)
    dx_ref[...] = base_ref[...] + inverse * (scaled - unit * jnp.mean(scaled * unit, axis=1, keepdims=True))


def attend_back(piece, x, gain, weights, vectors, normed, qkv, mixed, lse, grad, tail=None, ride=None):
    length, width = x.shape
    heads, span = vectors.shape
    w_args, w_specs = weight_specs(weights)
    packed = weights[0]
    grad_shapes = packed if isinstance(packed, tuple) else (packed,)
    tails = () if tail is None else (tail,)
    return pl.pallas_call(
        lambda *refs: attend_back_kernel(bool(tails), weights, ride, *refs),
        out_shape=(tuple(ride.out_shape) if ride else ())
        + (jax.ShapeDtypeStruct((length, width), F32),)
        + tuple(jax.ShapeDtypeStruct(g.shape, BF) for g in grad_shapes)
        + (
            jax.ShapeDtypeStruct((heads, span), F32),
            jax.ShapeDtypeStruct((1, width), F32),
        ),
        in_specs=[SMEM_SPEC] + [VMEM_SPEC] * 2 + w_specs + [VMEM_SPEC] * (6 + len(tails)) + (ride.in_specs if ride else []),
        out_specs=(ride.out_specs if ride else []) + [VMEM_SPEC] * (3 + len(grad_shapes)),
        scratch_shapes=[
            pltpu.VMEM((length, length), F32),
            pltpu.VMEM((128, span), F32),
            pltpu.VMEM((128, span), F32),
            pltpu.VMEM((2, length, length), BF),
            pltpu.VMEM((2, length, length), BF),
            pltpu.VMEM((length, width), BF),
            pltpu.VMEM((length, width), BF),
            pltpu.VMEM((length, 3 * width), BF),
            pltpu.VMEM((16, length), F32),
            pltpu.VMEM((3 * width, width), BF),
            pltpu.VMEM((width, width), BF),
        ] + weight_sems(weights) + (ride.scratch_shapes if ride else []),
        compiler_params=ride.params if ride else pltpu.CompilerParams(vmem_limit_bytes=VMEM_BYTES),
        cost_estimate=pl.CostEstimate(
            flops=16 * length * width * width + 10 * length * length * width,
            bytes_accessed=40 * length * width + 16 * width * width,
            transcendentals=heads * length * length,
        ),
        name="attend_back",
    )(piece, x, gain, *w_args, vectors, normed, qkv, mixed, lse, grad, *tails, *(ride.args if ride else []))


def mlp_chunk(c, parts, zones, up_ref, down_ref):
    hidden, width = up_ref.shape
    piece = hidden // (parts * zones)
    rows = [
        up_ref[pl.ds(pl.multiple_of(z * parts * piece + c * piece, 16), piece), :] for z in range(zones)
    ]
    span = down_ref.shape[1] // parts
    down = down_ref[:, pl.ds(pl.multiple_of(c * span, 16), span), :].reshape(-1, down_ref.shape[2])
    return jnp.concatenate(rows, axis=0), down


def mlp_loads(parts, zones, up_hbm, down_hbm, up_ref, down_ref, sems):
    piece = up_ref.shape[0] // (parts * zones)
    span = down_ref.shape[1] // parts
    loads = []
    for c in range(parts):
        chunk = [
            pltpu.make_async_copy(
                up_hbm.at[pl.ds((z * parts + c) * piece, piece), :],
                up_ref.at[pl.ds((z * parts + c) * piece, piece), :], sems.at[c, z],
            )
            for z in range(zones)
        ]
        columns = pl.ds(c * span, span)
        chunk.append(
            pltpu.make_async_copy(down_hbm.at[:, columns, :], down_ref.at[:, columns, :], sems.at[c, zones])
        )
        loads.append(chunk)
    for chunk in loads:
        for copy in chunk:
            copy.start()
    return loads


def mlp_kernel(parts, zones, x_ref, gain_ref, up_hbm, down_hbm, out_ref, normed_ref, up_ref, down_ref, sems):
    loads = mlp_loads(parts, zones, up_hbm, down_hbm, up_ref, down_ref, sems)
    field = x_ref[...].astype(F32)
    normed_ref[...] = (field * inverse_rms(field) * gain_ref[...]).astype(BF)
    out_ref[...] = field

    def chunk(c, _):
        for at, copies in enumerate(loads):
            pl.when(c == at)(lambda copies=copies: arrive(copies))
        up, down = mlp_chunk(c, parts, zones, up_ref, down_ref)
        hidden = gelu_of(nt(normed_ref[...], up)).astype(BF)
        out_ref[...] += nt(hidden, down)
        return 0

    lax.fori_loop(0, parts, chunk, 0)


def mlp(x, gain, up, down, parts, zones):
    length, width = x.shape
    hidden = up.shape[0]
    return pl.pallas_call(
        lambda *refs: mlp_kernel(parts, zones, *refs),
        out_shape=(jax.ShapeDtypeStruct((length, width), F32), jax.ShapeDtypeStruct((length, width), BF)),
        in_specs=[VMEM_SPEC] * 2 + [HBM_SPEC] * 2,
        out_specs=[VMEM_SPEC] * 2,
        scratch_shapes=[
            pltpu.VMEM(up.shape, BF), pltpu.VMEM(down.shape, BF), pltpu.SemaphoreType.DMA((parts, zones + 1))
        ],
        compiler_params=pltpu.CompilerParams(vmem_limit_bytes=VMEM_BYTES),
        cost_estimate=pl.CostEstimate(
            flops=4 * length * width * hidden, bytes_accessed=10 * length * width + 4 * width * hidden,
            transcendentals=length * hidden,
        ),
        name="mlp",
    )(x, gain, up, down)


def mlp_back_kernel(parts, zones, x_ref, gain_ref, up_hbm, down_hbm, normed_ref, grad_ref,
                    dx_ref, dup_ref, ddown_ref, dgain_ref, low_ref, acc_ref, up_ref, down_ref, sems):
    loads = mlp_loads(parts, zones, up_hbm, down_hbm, up_ref, down_ref, sems)
    low_ref[...] = grad_ref[...].astype(BF)
    acc_ref[...] = jnp.zeros_like(acc_ref)

    piece = up_ref.shape[0] // (parts * zones)
    span = down_ref.shape[1] // parts

    def chunk(c, _):
        for at, copies in enumerate(loads):
            pl.when(c == at)(lambda copies=copies: arrive(copies))
        up, down = mlp_chunk(c, parts, zones, up_ref, down_ref)
        hidden, slope = gelu_parts(nt(normed_ref[...], up))
        pre_grad = (nn(low_ref[...], down) * slope).astype(BF)
        ddown = tn(low_ref[...], hidden.astype(BF)).astype(BF)
        ddown_ref[:, pl.ds(pl.multiple_of(c * span, 16), span), :] = ddown.reshape(-1, span, ddown.shape[1])
        dup = tn(pre_grad, normed_ref[...]).astype(BF)
        for z in range(zones):
            at = pl.ds(pl.multiple_of(z * parts * piece + c * piece, 16), piece)
            dup_ref[at, :] = dup[z * piece:z * piece + piece, :]
        acc_ref[...] += nn(pre_grad, up)
        return 0

    lax.fori_loop(0, parts, chunk, 0)
    norm_back(x_ref, gain_ref, acc_ref, grad_ref, dx_ref, dgain_ref)


def mlp_back(x, gain, up, down, normed, grad, parts, zones):
    length, width = x.shape
    hidden = up.shape[0]
    return pl.pallas_call(
        lambda *refs: mlp_back_kernel(parts, zones, *refs),
        out_shape=(
            jax.ShapeDtypeStruct((length, width), F32),
            jax.ShapeDtypeStruct((hidden, width), BF),
            jax.ShapeDtypeStruct(down.shape, BF),
            jax.ShapeDtypeStruct((1, width), F32),
        ),
        in_specs=[VMEM_SPEC] * 2 + [HBM_SPEC] * 2 + [VMEM_SPEC] * 2,
        out_specs=[VMEM_SPEC] * 4,
        scratch_shapes=[
            pltpu.VMEM((length, width), BF), pltpu.VMEM((length, width), F32),
            pltpu.VMEM(up.shape, BF), pltpu.VMEM(down.shape, BF), pltpu.SemaphoreType.DMA((parts, zones + 1)),
        ],
        compiler_params=pltpu.CompilerParams(vmem_limit_bytes=VMEM_BYTES),
        cost_estimate=pl.CostEstimate(
            flops=10 * length * width * hidden, bytes_accessed=16 * length * width + 8 * width * hidden,
            transcendentals=length * hidden,
        ),
        name="mlp_back",
    )(x, gain, up, down, normed, grad)


MESH = pl.DeviceIdType.MESH


def flip(index, mask):
    bit = 1
    while bit <= mask:
        if mask & bit:
            index = index + bit - 2 * bit * ((index // bit) % 2)
        bit *= 2
    return index


def masks_of(bits):
    found = [0]
    for bit in bits:
        found = found + [m | bit for m in found]
    return found


def bits_below(size):
    found, bit = [], 1
    while bit < size:
        found.append(bit)
        bit *= 2
    return found


def halves_of(rows):
    cut = rows // 2 // 16 * 16
    return ((0, cut), (cut, rows - cut))


def routes_of(chips):
    bits = bits_below(chips)
    cut = len(bits) // 2
    return (bits, bits[cut:] + bits[:cut])


def greet(owner, zone, owners, zones):
    barrier = pltpu.get_barrier_semaphore()
    peers = [(flip(owner, bit), zone) for bit in bits_below(owners)]
    peers += [(owner, flip(zone, d)) for d in range(1, zones)]
    for peer in peers:
        pl.semaphore_signal(barrier, inc=1, device_id=peer, device_id_type=MESH)
    pl.semaphore_wait(barrier, len(peers))


def sender(send_sem, recv_sem):
    used = [0]

    def send(source, target, device):
        at = used[0]
        used[0] += 1
        copy = pltpu.make_async_remote_copy(
            source, target, send_sem.at[at], recv_sem.at[at], device_id=device, device_id_type=MESH
        )
        copy.start()
        return copy

    return send


def gather_copies(owners, zones):
    chips = owners // 2
    return zones - 1 + 2 * (chips - 1) + 2 * chips


def gather_kernel(owners, zones, used_rows, experts, capacity, *refs):
    count = len(used_rows)
    blocks, (late_ref, route_ref), refs = refs[:count], refs[count:count + 2], refs[count + 2:]
    outs, (slot_ref, spread_ref), refs = refs[:count], refs[count:count + 2], refs[count + 2:]
    slabs, turned = refs[:count], refs[count:2 * count]
    direct = capacity % 16 == 0
    near_ref, refs = (refs[2 * count], refs[:2 * count] + refs[2 * count + 1:]) if direct else (spread_ref, refs)
    slot_in_ref, send_sem, recv_sem, local_sem = refs[2 * count:]
    owner, zone = lax.axis_index("expert"), lax.axis_index("shard")
    greet(owner, zone, owners, zones)
    send = sender(send_sem, recv_sem)
    chips = owners // 2
    pending, finals = [], []

    def across(g):
        slabs[g][zone] = blocks[g][...]
        return [send(blocks[g], slabs[g].at[zone], (owner, flip(zone, d))) for d in range(1, zones)]

    def place(g, index, half):
        start, size = halves_of(used_rows[g])[half]
        return outs[g].at[index, pl.ds(start, size), :]

    def onward(g, half, index):
        finals.append(send(place(g, index, half), place(g, index, half), (flip(owner, 1), zone)))

    def start_rows(g, copies):
        for copy in copies:
            copy.wait_recv()
        pending.extend(copies)
        slab = slabs[g]
        turned[g][...] = slab[...].reshape(slab.shape[0] * slab.shape[1], slab.shape[2]).T
        local = pltpu.make_async_copy(
            turned[g].at[pl.ds(0, used_rows[g]), :], outs[g].at[owner], local_sem.at[g]
        )
        local.start()
        firsts = []
        for half, order in enumerate(routes_of(chips)):
            start, size = halves_of(used_rows[g])[half]
            source = turned[g].at[pl.ds(start, size), :]
            firsts.append([send(source, place(g, owner, half), (flip(owner, 2 * order[0]), zone))])
            finals.append(send(source, place(g, owner, half), (flip(owner, 1), zone)))
        return firsts, local

    def finish_rows(g, state, step):
        firsts, local = state
        if step == 0:
            local.wait()
        for half, order in enumerate(routes_of(chips)):
            for copy in firsts[half]:
                copy.wait_recv()
            pending.extend(firsts[half])
            done = masks_of(order[:step])
            arrived = [m | order[step] for m in done]
            if step + 1 < len(order):
                device = (flip(owner, 2 * order[step + 1]), zone)
                firsts[half] = [
                    send(place(g, flip(owner, 2 * m), half), place(g, flip(owner, 2 * m), half), device)
                    for m in done + arrived
                ]
            for m in arrived:
                onward(g, half, flip(owner, 2 * m))
        return firsts, local

    steps = len(routes_of(chips)[0])
    moving = {0: across(0)}
    states = {}
    slot_ref[0] = token_slots(route_ref[...], experts, capacity)
    near_copies = []

    def spread_zone(d):
        if not direct:
            return
        take = max(1, 384 // capacity)
        rows = late_ref if d == 0 else near_ref.at[d - 1]

        def chunk(i, _):
            hits = slot_hits(slot_ref[d], i * (take * capacity), take * capacity)
            picked = nn(hits[0] + hits[1], rows[...]).reshape(take, capacity, rows.shape[1])
            spread_ref[pl.ds(i * take, take), d] = picked.astype(BF)
            return 0

        lax.fori_loop(0, experts // take, chunk, 0)

    for g in range(count):
        states[g] = start_rows(g, moving[g])
        if g + 1 < count:
            moving[g + 1] = across(g + 1)
        if g == count - 1:
            for d in range(1, zones // 2):
                device = (owner, (zone + zones - 2 * d) % zones)
                near_copies.append(send(slot_ref.at[0], slot_in_ref.at[d - 1], device))
                near_copies.append(send(late_ref, near_ref.at[d - 1], device))
        if g == 1:
            spread_zone(0)
        if g > 0:
            for step in range(1, steps):
                states[g - 1] = finish_rows(g - 1, states[g - 1], step)
        states[g] = finish_rows(g, states[g], 0)
    for step in range(1, steps):
        states[count - 1] = finish_rows(count - 1, states[count - 1], step)
    for copy in near_copies:
        copy.wait_recv()
    for d in range(1, zones // 2):
        slot_ref[d] = slot_in_ref[d - 1]
        spread_zone(d)
    for copy in finals:
        copy.wait_recv()
    for copy in pending + finals + near_copies:
        copy.wait_send()


def gather_weights(blocks, used_rows, late, route_rows, owners, zones, experts, capacity):
    count = len(blocks)
    depth = zones * blocks[0].shape[0]
    groups = zones // 2
    copies = count * gather_copies(owners, zones) + 2 * (groups - 1)
    length = route_rows.shape[1]
    any_spec = pl.BlockSpec(memory_space=pltpu.HBM)
    direct = capacity % 16 == 0
    near_shape = (groups - 1,) + late.shape
    if direct:
        spread_shape, late_spec = (experts, groups, capacity, late.shape[1]), VMEM_SPEC
    else:
        spread_shape, late_spec = near_shape, any_spec
    return pl.pallas_call(
        lambda *refs: gather_kernel(owners, zones, used_rows, experts, capacity, *refs),
        out_shape=tuple(jax.ShapeDtypeStruct((owners, used, depth), BF) for used in used_rows)
        + (
            jax.ShapeDtypeStruct((groups, 8, length), F32),
            jax.ShapeDtypeStruct(spread_shape, BF),
        ),
        in_specs=[VMEM_SPEC] * count + [late_spec, VMEM_SPEC],
        out_specs=tuple([any_spec] * count) + (VMEM_SPEC, late_spec),
        scratch_shapes=[pltpu.VMEM((zones,) + b.shape, BF) for b in blocks]
        + [pltpu.VMEM((b.shape[1], depth), BF) for b in blocks]
        + ([pltpu.VMEM(near_shape, BF)] if direct else [])
        + [pltpu.VMEM((groups - 1, 8, length), F32)]
        + [pltpu.SemaphoreType.DMA((copies,)), pltpu.SemaphoreType.DMA((copies,)), pltpu.SemaphoreType.DMA((count,))],
        compiler_params=pltpu.CompilerParams(
            vmem_limit_bytes=61 * 1024 * 1024, collective_id=1, has_side_effects=True
        ),
        name="gather_weights",
    )(*blocks, late, route_rows)


def add_rows(into, other):
    return (into.astype(F32) + other.astype(F32)).astype(BF)


class Mail:
    def __init__(self, at, source, target, device, sems):
        self.at, self.source, self.target, self.device, self.sems = at, source, target, device, sems

    def make(self):
        return pltpu.make_async_remote_copy(
            self.source(), self.target(), self.sems[0].at[self.at], self.sems[1].at[self.at],
            device_id=self.device, device_id_type=MESH,
        )

    def start(self):
        self.make().start()
        return self

    def wait_recv(self):
        self.make().wait_recv()

    def wait_send(self):
        self.make().wait_send()


class Post:
    def __init__(self, send_sem, recv_sem):
        self.sems, self.mails = (send_sem, recv_sem), []

    def plan(self, source, target, device):
        mail = Mail(len(self.mails), source, target, device, self.sems)
        self.mails.append(mail)
        return mail

    def close(self):
        for mail in self.mails:
            mail.wait_send()


def cross_copies(owners):
    return 1 + 2 * (owners // 2 - 1)


def cross_scratch(owners, used, depth):
    chips = owners // 2
    return [
        pltpu.VMEM((chips, used, depth), BF),
        pltpu.VMEM((chips, used, depth), BF),
        pltpu.VMEM((chips - 1, used, depth), BF),
        pltpu.SemaphoreType.DMA,
    ]


def cross_plan(post, part, keep, near, far, local_sem, owner, zone, owners):
    chips = owners // 2
    chip, core = owner // 2, owner % 2
    used = keep.shape[1]
    orders = routes_of(chips)
    steps = len(orders[0])
    first = post.plan(lambda: part.at[:, 1 - core], lambda: near, (flip(owner, 1), zone))

    def window(half):
        start, size = halves_of(used)[half]
        return pl.ds(start, size)

    def slot_of(step, i):
        return chips - 2 * len(masks_of(orders[0][step + 1:])) + i

    pushes = []
    for step in range(steps):
        mails = []
        for half, order in enumerate(orders):
            bit, rest = order[step], masks_of(order[step + 1:])
            for i, m in enumerate(rest):
                index = flip(chip, bit | m)
                mails.append(post.plan(
                    lambda index=index, half=half: keep.at[index, window(half), :],
                    lambda i=i, half=half, step=step: far.at[slot_of(step, i), window(half), :],
                    (flip(owner, 2 * bit), zone),
                ))
        pushes.append(mails)

    def local():
        return pltpu.make_async_copy(part.at[:, core], keep, local_sem)

    def begin():
        local().start()
        first.start()

    def meet():
        local().wait()
        first.wait_recv()

        def one(h, _):
            keep[h] = add_rows(keep[h], near[h])
            return 0

        lax.fori_loop(0, chips, one, 0)
        for mail in pushes[0]:
            mail.start()

    def absorb(step):
        for mail in pushes[step]:
            mail.wait_recv()
        for half, order in enumerate(orders):
            for i, m in enumerate(masks_of(order[step + 1:])):
                index = flip(chip, m)
                keep[index, window(half), :] = add_rows(
                    keep[index, window(half), :], far[slot_of(step, i), window(half), :]
                )
        if step + 1 < steps:
            for mail in pushes[step + 1]:
                mail.start()

    stages = [meet] + [lambda step=step: absorb(step) for step in range(steps)]
    return begin, stages


def zone_scratch(zones, used, depth):
    wide = -(-used // 128) * 128
    return [pltpu.VMEM((zones, depth // zones, wide), BF), pltpu.VMEM((zones - 1, depth // zones, wide), BF)]


def zone_shape(zones, used, depth):
    return jax.ShapeDtypeStruct((depth // zones, -(-used // 128) * 128), F32)


def zone_plan(post, slab, incoming, out_ref, owner, zone, zones):
    mails = [
        post.plan(
            lambda d=d: slab.at[flip(zone, d)], lambda d=d: incoming.at[d - 1], (owner, flip(zone, d))
        )
        for d in range(1, zones)
    ]

    def start(own):
        spare = slab.shape[2] - own.shape[0]
        if spare:
            own = jnp.concatenate([own, jnp.zeros((spare, own.shape[1]), BF)], axis=0)
        slab[...] = own.T.reshape(slab.shape)
        for mail in mails:
            mail.start()

    def end():
        total = slab[zone].astype(F32)
        for d in range(1, zones):
            mails[d - 1].wait_recv()
            total = total + incoming[d - 1].astype(F32)
        out_ref[...] = total

    return start, end


class Ride:
    def __init__(self, parts, zoned, owns, rows, owners, zones, capacity, depth, collective_id):
        groups = zones // 2
        self.owners, self.zones, self.capacity, self.zoned, self.count = owners, zones, capacity, zoned, len(parts)
        self.owns = len(owns)
        self.with_rows = rows is not None
        hbm = pl.BlockSpec(memory_space=pltpu.HBM)
        self.args = [p.reshape(owners // 2, 2, p.shape[1], depth) for p in parts] + list(owns)
        self.in_specs = [hbm] * len(parts) + [VMEM_SPEC] * len(owns)
        self.out_shape = [zone_shape(zones, p.shape[1], depth) for p in parts[:zoned]]
        self.out_shape += [jax.ShapeDtypeStruct(p.shape[1:], BF) for p in parts[zoned:]]
        self.out_shape += [zone_shape(zones, o.shape[0], depth) for o in owns]
        self.scratch_shapes = []
        for p in parts:
            self.scratch_shapes += cross_scratch(owners, p.shape[1], depth)
        for p in parts[:zoned]:
            self.scratch_shapes += zone_scratch(zones, p.shape[1], depth)
        for o in owns:
            self.scratch_shapes += zone_scratch(zones, o.shape[0], depth)
        copies = len(parts) * cross_copies(owners) + (zoned + len(owns)) * (zones - 1)
        if self.with_rows:
            y, slot_rows = rows
            length = slot_rows.shape[2]
            self.args += [y, slot_rows]
            self.in_specs += [hbm, VMEM_SPEC]
            self.out_shape += [jax.ShapeDtypeStruct((groups - 1, length, depth), BF)]
            self.scratch_shapes += [
                pltpu.VMEM((groups - 1,) + y.shape[:2] + (capacity, depth), BF),
                pltpu.SemaphoreType.DMA((groups - 1,)),
                *[pltpu.VMEM((length, depth), BF)] * (groups - 2),
            ]
            copies += groups - 1
        self.out_specs = [VMEM_SPEC] * len(self.out_shape)
        self.scratch_shapes += [pltpu.SemaphoreType.DMA((copies,)), pltpu.SemaphoreType.DMA((copies,))]
        self.inputs, self.outputs, self.scratch = len(self.args), len(self.out_shape), len(self.scratch_shapes)
        self.params = pltpu.CompilerParams(
            vmem_limit_bytes=61 * 1024 * 1024, collective_id=collective_id, has_side_effects=True
        )

    def board(self, inputs, outputs, scratch, room, spare):
        owner, zone = lax.axis_index("expert"), lax.axis_index("shard")
        owners, zones, count, groups = self.owners, self.zones, self.count, self.zones // 2
        greet(owner, zone, owners, zones)
        post = Post(scratch[-2], scratch[-1])
        plans = [cross_plan(post, inputs[g], *scratch[4 * g:4 * g + 4], owner, zone, owners) for g in range(count)]
        keeps = [scratch[4 * g] for g in range(count)]
        for begin, _ in plans:
            begin()
        zone_plans = []
        for g in range(self.zoned):
            slab, incoming = scratch[4 * count + 2 * g:4 * count + 2 * g + 2]
            zone_plans.append(zone_plan(post, slab, incoming, outputs[g], owner, zone, zones))
        for i in range(self.owns):
            at = 4 * count + 2 * (self.zoned + i)
            start, end = zone_plan(post, scratch[at], scratch[at + 1], outputs[count + i], owner, zone, zones)
            start(inputs[count + i][...])
            zone_plans.append((start, end))
        y_mails = []
        if self.with_rows:
            y_ref, slot_ref = inputs[count + self.owns:count + self.owns + 2]
            at = 4 * count + 2 * (self.zoned + self.owns)
            y_rows, y_sem = scratch[at:at + 2]
            y_part = [spare, *scratch[at + 2:-2]]

            def load(d):
                window = pl.ds(d * self.capacity, self.capacity)
                return pltpu.make_async_copy(y_ref.at[:, :, window, :], y_rows.at[d - 1], y_sem.at[d - 1])

            for d in range(1, groups):
                load(d).start()
                y_mails.append(post.plan(
                    lambda d=d: y_part[d - 1], lambda d=d: outputs[-1].at[d - 1], (owner, (zone + 2 * d) % zones)
                ))

        def rows_turn():
            for d in range(1, groups):
                load(d).wait()
                collect_rows(y_rows.at[d - 1], slot_ref[d], room)
                y_part[d - 1][...] = room[...].astype(BF)
                y_mails[d - 1].start()

        turns = []
        for g in range(count):
            turns.append(lambda g=g: self.run([plans[g - 1][1][1]] if g else [], [plans[g][1][0]]))
        if count == 1:
            turns.append(lambda: self.run([plans[0][1][1]]))
        longest = len(plans[0][1]) if plans else 0

        def finish_part():
            for t in range(1, count + longest - 1):
                for g in reversed(range(count)):
                    at = t - g
                    if 1 <= at < longest and (at > 1 or (g == count - 1 and count > 1)):
                        plans[g][1][at]()
                        if at == longest - 1 and g < self.zoned:
                            zone_plans[g][0](keeps[g][owner // 2])
            for g in range(self.zoned, count):
                outputs[g][...] = keeps[g][owner // 2]
            for _, end in zone_plans:
                end()
            for mail in y_mails:
                mail.wait_recv()
            post.close()

        return turns, rows_turn if self.with_rows else None, finish_part

    def run(self, *groups):
        for acts in groups:
            for act in acts:
                act()


def collect_rows(rows_ref, slots, room):
    owners, local, capacity, width = rows_ref.shape
    span = 2 * local * capacity
    for h in range(owners // 2):
        hits = slot_hits(slots, jnp.int32(h * span), span)
        added = tn(hits[0] + hits[1], rows_ref[2 * h:2 * h + 2].reshape(span, width))
        if h == 0:
            room[...] = added
        else:
            room[...] += added


def finish_kernel(owners, zones, capacity, sizes, *refs):
    refs = list(refs)

    def take(count):
        found = refs[:count]
        del refs[:count]
        return found

    with_rows, chunks = sizes
    early_refs, (down_part, part, small) = take(2), take(3)
    own_refs, peer_refs = take(2), take(2)
    y_ref, slot_ref, x_ref, y_in = take(4) if with_rows else (None, None, None, None)
    *outs, small_out = take(5)
    sum_refs = take(2)
    y_out = take(1)[0] if with_rows else None
    cross_refs = [take(4) for _ in range(2)]
    zone_refs = [take(2) for _ in range(4)]
    small_mine, small_other = take(2)
    stages = [take(3) for _ in range(2)]
    add_sem = take(1)[0]
    if with_rows:
        y_rows, y_sum, y_sem = take(3)
    send_sem, recv_sem = take(2)
    owner, zone = lax.axis_index("expert"), lax.axis_index("shard")
    greet(owner, zone, owners, zones)
    post = Post(send_sem, recv_sem)
    plans = [
        cross_plan(post, p, *r, owner, zone, owners) for p, r in zip((down_part, part), cross_refs)
    ]
    for begin, _ in plans:
        begin()
    down, cross = [stages for _, stages in plans]
    if with_rows:
        y_copy = pltpu.make_async_copy(y_ref.at[:, :, pl.ds(0, capacity), :], y_rows, y_sem)
        y_copy.start()
    zone_starts, zone_ends = zip(
        *[zone_plan(post, r[0], r[1], out, owner, zone, zones) for r, out in zip(zone_refs, outs)]
    )
    for start, ref in zip(zone_starts, early_refs):
        start(ref[...])
    small_peers = [(flip(owner, bit), zone) for bit in bits_below(owners)]
    small_peers += [(owner, flip(zone, bit)) for bit in bits_below(zones)]
    small_mails = [
        post.plan(lambda i=i: small_mine.at[i], lambda i=i: small_other.at[i], peer)
        for i, peer in enumerate(small_peers)
    ]
    small_mine[0] = small[...]
    small_mails[0].start()

    def small_step(i):
        if i < len(small_mails):
            small_mails[i].wait_recv()
            small_mine[i + 1] = small_mine[i] + small_other[i]
            if i + 1 < len(small_mails):
                small_mails[i + 1].start()

    groups = zones // 2

    def add_stage(i):
        mine, theirs, total = stages[i]
        count = chunks[i]
        size = mine.shape[1]

        def loads(k):
            rows = pl.ds(k * size, size)
            return (
                pltpu.make_async_copy(own_refs[i].at[rows, :], mine.at[k % 2], add_sem.at[i, k % 2, 0]),
                pltpu.make_async_copy(peer_refs[i].at[rows, :], theirs.at[k % 2], add_sem.at[i, k % 2, 1]),
            )

        def store(k):
            return pltpu.make_async_copy(
                total.at[k % 2], sum_refs[i].at[pl.ds(k * size, size), :], add_sem.at[i, k % 2, 2]
            )

        for copy in loads(0):
            copy.start()
        for k in range(count):
            if k + 1 < count:
                for copy in loads(k + 1):
                    copy.start()
            for copy in loads(k):
                copy.wait()
            if k >= 2:
                store(k - 2).wait()
            total[k % 2] = mine[k % 2] + theirs[k % 2].astype(F32)
            store(k).start()
        for k in range(max(0, count - 2), count):
            store(k).wait()

    down[0]()
    small_step(0)
    add_stage(0)
    down[1]()
    cross[0]()
    small_step(1)
    if with_rows:
        y_copy.wait()
        collect_rows(y_rows, slot_ref[0], y_sum)
        total = x_ref[...] + y_sum[...]
        for d in range(1, groups):
            total = total + y_in[d - 1].astype(F32)
        y_out[...] = total.astype(BF)
    small_step(2)
    for act in down[2:]:
        act()
    zone_starts[2](cross_refs[0][0][owner // 2])
    for act in cross[1:-1]:
        act()
    zone_ends[0]()
    zone_ends[1]()
    small_step(3)
    cross[-1]()
    zone_starts[3](cross_refs[1][0][owner // 2])
    small_step(4)
    add_stage(1)
    for i in range(5, len(small_mails)):
        small_step(i)
    small_out[...] = small_mine[len(small_mails)]
    zone_ends[2]()
    zone_ends[3]()
    post.close()


def finish(early, down_part, first_part, small, owns, peers, owners, zones, capacity, rows=None):
    depth = first_part.shape[2]
    chips = owners // 2
    used = tuple(o.shape[0] for o in early) + (down_part.shape[1], first_part.shape[1])
    cross_parts = [p.reshape(chips, 2, p.shape[1], depth) for p in (down_part, first_part)]
    flat = [o.reshape(-1, o.shape[-1]) for o in owns]
    flat_peers = [p.reshape(-1, p.shape[-1]) for p in peers]
    chunk = 256
    chunks = tuple(f.shape[0] // chunk for f in flat)
    rounds = len(bits_below(owners)) + len(bits_below(zones))
    copies = 2 * cross_copies(owners) + 4 * (zones - 1) + rounds
    hbm = pl.BlockSpec(memory_space=pltpu.HBM)
    args = [*early, *cross_parts, small, *flat, *flat_peers]
    in_specs = [VMEM_SPEC, VMEM_SPEC, hbm, hbm, VMEM_SPEC] + [hbm] * 4
    out_shape = [zone_shape(zones, u, depth) for u in used] + [jax.ShapeDtypeStruct(small.shape, F32)]
    out_shape += [jax.ShapeDtypeStruct(f.shape, F32) for f in flat]
    out_specs = [VMEM_SPEC] * 5 + [hbm] * 2
    scratch = cross_scratch(owners, used[2], depth) + cross_scratch(owners, used[3], depth)
    for u in used:
        scratch += zone_scratch(zones, u, depth)
    scratch += [pltpu.VMEM((rounds + 1,) + small.shape, F32), pltpu.VMEM((rounds,) + small.shape, F32)]
    for f in flat:
        shape = (2, chunk, f.shape[1])
        scratch += [pltpu.VMEM(shape, F32), pltpu.VMEM(shape, BF), pltpu.VMEM(shape, F32)]
    scratch += [pltpu.SemaphoreType.DMA((2, 2, 3))]
    if rows is not None:
        y, slot_rows, x, y_near = rows
        args += [y, slot_rows, x, y_near]
        in_specs += [hbm, VMEM_SPEC, VMEM_SPEC, VMEM_SPEC]
        out_shape += [jax.ShapeDtypeStruct(x.shape, BF)]
        out_specs += [VMEM_SPEC]
        scratch += [
            pltpu.VMEM(y.shape[:2] + (capacity, depth), BF), pltpu.VMEM(x.shape, F32), pltpu.SemaphoreType.DMA,
        ]
    scratch += [pltpu.SemaphoreType.DMA((copies,)), pltpu.SemaphoreType.DMA((copies,))]
    sizes = (rows is not None, chunks)
    return pl.pallas_call(
        lambda *refs: finish_kernel(owners, zones, capacity, sizes, *refs),
        out_shape=tuple(out_shape),
        in_specs=in_specs,
        out_specs=tuple(out_specs),
        scratch_shapes=scratch,
        compiler_params=pltpu.CompilerParams(
            vmem_limit_bytes=61 * 1024 * 1024, collective_id=2, has_side_effects=True
        ),
        name="finish",
    )(*args)


def three_pieces(row):
    top = row.astype(BF)
    rest = row - top.astype(F32)
    middle = rest.astype(BF)
    low = (rest - middle.astype(F32)).astype(BF)
    return jnp.concatenate([top, middle, low, jnp.zeros((5, row.shape[1]), BF)], axis=0)


def sum_pieces(rows):
    return rows[0:1] + rows[1:2] + rows[2:3]


def token_slots(route_rows, experts, capacity):
    length = route_rows.shape[1]
    ids = lax.broadcasted_iota(jnp.int32, (experts, length), 0)
    first, second = route_rows[0:1] == ids, route_rows[1:2] == ids
    named = jnp.where(first | second, 1.0, 0.0).astype(BF)
    earlier = (
        lax.broadcasted_iota(jnp.int32, (length, length), 0) < lax.broadcasted_iota(jnp.int32, (length, length), 1)
    )
    place = nn(named, jnp.where(earlier, 1.0, 0.0).astype(BF)) + (ids * capacity).astype(F32)
    rows = [jnp.sum(jnp.where(hit, place, 0.0), axis=0, keepdims=True) for hit in (first, second)]
    return jnp.concatenate(rows + [jnp.zeros((6, length), F32)], axis=0)


def slot_hits(slots, start, count):
    place = lax.broadcasted_iota(jnp.int32, (count, slots.shape[1]), 0).astype(F32) + start.astype(F32)
    one, zero = jnp.asarray(1.0, F32), jnp.asarray(0.0, F32)
    return [jnp.where(place == slots[k:k + 1], one, zero).astype(BF) for k in range(2)]


def greet_plane(owner, zone, owners, zones):
    barrier = pltpu.get_barrier_semaphore()
    peers = [(flip(owner, mask), zone) for mask in range(1, owners)]
    peers += [(owner, (zone + d) % zones) for d in range(2, zones, 2)] + [(owner, flip(zone, 1))]
    for peer in peers:
        pl.semaphore_signal(barrier, inc=1, device_id=peer, device_id_type=MESH)
    pl.semaphore_wait(barrier, len(peers))


def peer_order(owners):
    return list(range(2, owners)) + [1, 0]


def softmax_pair(logits, route_rows):
    ids = lax.broadcasted_iota(jnp.int32, logits.shape, 0)
    a, b = [jnp.sum(jnp.where(route_rows[k:k + 1] == ids, logits, 0.0), axis=0, keepdims=True) for k in range(2)]
    peak = jnp.maximum(a, b)
    ea, eb = jnp.exp(a - peak), jnp.exp(b - peak)
    return ea / (ea + eb), eb / (ea + eb)


def send_rows_kernel(
    owners, zones, capacity, x_ref, gain_ref, router_ref, route_ref, slot_ref, slices_ref,
    normed_ref, gates_ref, rows_ref, gate_ref, other_ref,
    near_ref, near_gates_ref, packed_ref, tags_ref, tags_in_ref, send_sem, recv_sem, local_sem,
):
    owner, zone = lax.axis_index("expert"), lax.axis_index("shard")
    tags_ref[...] = jnp.zeros_like(tags_ref)
    greet_plane(owner, zone, owners, zones)
    send = sender(send_sem, recv_sem)
    groups = zones // 2
    local = rows_ref.shape[1]
    span = local * capacity
    field = x_ref[...]
    normed_ref[...] = (field * inverse_rms(field) * gain_ref[...]).astype(BF)
    cut = normed_ref.shape[1] // 2
    lanes = [pl.ds(0, cut), pl.ds(cut, cut)]
    copies = {}
    for half in range(2):
        for d in range(1, groups):
            device = (owner, (zone + zones - 2 * d) % zones)
            copies[d, half] = send(normed_ref.at[:, lanes[half]], near_ref.at[d - 1, :, lanes[half]], device)
    gates = softmax_pair(nt(router_ref[...], normed_ref[...]), route_ref[...])
    gates_ref[...] = jnp.concatenate(list(gates) + [jnp.zeros((6, gates[0].shape[1]), F32)], axis=0)
    for d in range(1, groups):
        copies[d, 2] = send(gates_ref, near_gates_ref.at[d - 1], (owner, (zone + zones - 2 * d) % zones))
    arrivals, stays = [], []
    for part in range(local):
        arrivals.append(send(slices_ref.at[part], other_ref.at[part], (owner, flip(zone, 1))))
    def ship(d, mask, target, half):
        columns = slice(None) if half is None else lanes[half]
        for part in range(local):
            source = packed_ref.at[d, mask, pl.ds(part * capacity, capacity), columns]
            place = rows_ref.at[owner, part, pl.ds(d * capacity, capacity), columns]
            if mask:
                arrivals.append(send(source, place, (target, zone)))
            else:
                at = (2 * d + (half or 0)) * local + part
                copy = pltpu.make_async_copy(source, place, local_sem.at[at])
                copy.start()
                stays.append(copy)

    for d in range(groups):
        for half in (None,) if d == 0 else (0, 1):
            if d:
                copies[d, half].wait_recv()
                if half == 0:
                    copies[d, 2].wait_recv()
            rows = normed_ref if d == 0 else near_ref.at[d - 1]
            weights = gates_ref[...] if d == 0 else near_gates_ref[d - 1]
            pieces = [three_pieces(weights[k:k + 1]) for k in range(2)]
            slots = slot_ref[d]
            for mask in peer_order(owners):
                target = flip(owner, mask)
                hits = slot_hits(slots, target * span, span)
                both = hits[0] + hits[1]
                if half is None:
                    packed_ref[d, mask] = nn(both, rows[...]).astype(BF)
                else:
                    packed_ref[d, mask, :, lanes[half]] = nn(both, rows[:, lanes[half]]).astype(BF)
                ship(d, mask, target, half)
                if half == 1:
                    continue
                tag = sum_pieces(nt(pieces[0], hits[0]) + nt(pieces[1], hits[1]))
                tags_ref[d, mask, :, 0:span] = jnp.broadcast_to(tag, (8, span))
                if mask:
                    arrivals.append(send(tags_ref.at[d, mask], tags_in_ref.at[d, owner], (target, zone)))
                else:
                    tags_in_ref[d, owner] = tags_ref[d, mask]
    for copy in arrivals:
        copy.wait_recv()
    for d in range(groups):
        for source in range(owners):
            column = tags_in_ref[d, source].T
            for part in range(local):
                gate_ref[source, part, d * capacity:(d + 1) * capacity, :] = column[
                    part * capacity:(part + 1) * capacity, 0:1
                ]
    for copy in stays:
        copy.wait()
    for copy in list(copies.values()) + arrivals:
        copy.wait_send()


def send_rows(x, gain, router, route_rows, slot_rows, slices, owners, zones, local, capacity):
    length, width = x.shape
    groups = zones // 2
    span = local * capacity
    any_spec = pl.BlockSpec(memory_space=pltpu.HBM)
    wide = -(-span // 128) * 128
    copies = local + 3 * (groups - 1) + (owners - 1) * (local + 1 + (groups - 1) * (2 * local + 1))
    return pl.pallas_call(
        lambda *refs: send_rows_kernel(owners, zones, capacity, *refs),
        out_shape=(
            jax.ShapeDtypeStruct((length, width), BF),
            jax.ShapeDtypeStruct((8, length), F32),
            jax.ShapeDtypeStruct((owners, local, groups * capacity, width), BF),
            jax.ShapeDtypeStruct((owners, local, groups * capacity, 1), F32),
            jax.ShapeDtypeStruct(slices.shape, slices.dtype),
        ),
        in_specs=[VMEM_SPEC] * 5 + [any_spec],
        out_specs=(VMEM_SPEC, VMEM_SPEC, any_spec, VMEM_SPEC, any_spec),
        scratch_shapes=[
            pltpu.VMEM((groups - 1, length, width), BF),
            pltpu.VMEM((groups - 1, 8, length), F32),
            pltpu.VMEM((groups, owners, span, width), BF),
            pltpu.VMEM((groups, owners, 8, wide), F32),
            pltpu.VMEM((groups, owners, 8, wide), F32),
            pltpu.SemaphoreType.DMA((copies,)),
            pltpu.SemaphoreType.DMA((copies,)),
            pltpu.SemaphoreType.DMA((2 * groups * local,)),
        ],
        compiler_params=pltpu.CompilerParams(
            vmem_limit_bytes=61 * 1024 * 1024, collective_id=3, has_side_effects=True
        ),
        name="send_rows",
    )(x, gain, router, route_rows, slot_rows, slices)


def return_rows_kernel(
    owners, zones, capacity,
    rows_ref, hidden_in, pre_in, dey_in, sent_in, own_down_in, peer_down_in,
    gate_cols_ref, dgate_ref, slot_ref, gates_ref, route_ref, x_ref, gain_ref, router_ref, normed_ref, top_ref,
    dx_ref, dgain_ref, drouter_ref, *refs,
):
    outs, y_out, refs = (refs[0:2], refs[2:4]), refs[4], refs[5:]
    (hidden_ref, pre_ref, dey_ref, sent_ref, own_ref, peer_ref, load_sem, store_sem), refs = refs[:8], refs[8:]
    (down_ref, y_ref, down_sem, y_sem), refs = refs[:4], refs[4:]
    (back_ref, tags_ref, tags_in_ref, part_ref, part_in_ref, mark_ref, mark_in_ref, sum_ref, send_sem, recv_sem,
     local_sem) = refs
    owner, zone = lax.axis_index("expert"), lax.axis_index("shard")
    tags_ref[...] = jnp.zeros_like(tags_ref)
    greet_plane(owner, zone, owners, zones)
    send = sender(send_sem, recv_sem)
    groups = zones // 2
    local = rows_ref.shape[1]
    span = local * capacity
    chip = owner // 2
    cut = back_ref.shape[3] // 2
    lanes = [pl.ds(0, cut), pl.ds(cut, cut)]
    arrivals, stays, sent = {}, {}, []

    def ship(d, half):
        window = pl.ds(d * capacity, capacity)
        columns = slice(None) if half is None else lanes[half]
        for mask in peer_order(owners):
            target = flip(owner, mask)
            for part in range(local):
                source = rows_ref.at[target, part, window, columns]
                place = back_ref.at[d, owner, pl.ds(part * capacity, capacity), columns]
                if mask:
                    arrivals.setdefault((d, half, mask), []).append(send(source, place, (target, zone)))
                else:
                    at = (2 * d + (half or 0)) * local + part
                    copy = pltpu.make_async_copy(source, place, local_sem.at[at])
                    copy.start()
                    stays.setdefault((d, half), []).append(copy)

    def ship_tags(d):
        for mask in peer_order(owners):
            target = flip(owner, mask)
            columns = [dgate_ref[target, part, d * capacity:(d + 1) * capacity, :] for part in range(local)]
            column = jnp.concatenate(columns, axis=0)
            tags_ref[d, mask, :, 0:span] = jnp.broadcast_to(column, (span, 128)).T[0:8]
            if mask:
                arrivals.setdefault((d, "tags", mask), []).append(
                    send(tags_ref.at[d, mask], tags_in_ref.at[d, owner], (target, zone))
                )
            else:
                tags_in_ref[d, owner] = tags_ref[d, mask]

    def collect_zone(d, half):
        slots = slot_ref[d]
        columns = slice(None) if half is None else lanes[half]
        marks = [jnp.zeros((1, slots.shape[1]), F32) for _ in range(2)]
        for turn, hop in enumerate(list(range(1, owners // 2)) + [0]):
            for mask in (2 * hop, 2 * hop + 1):
                waits = arrivals.get((d, half, mask), [])
                if half != 1:
                    waits = waits + arrivals.get((d, "tags", mask), [])
                for copy in waits:
                    copy.wait_recv()
                if mask == 0:
                    for copy in stays[d, half]:
                        copy.wait()
            peer = flip(chip, hop)
            hits = slot_hits(slots, peer * (2 * span), 2 * span)
            rows = back_ref[d, pl.ds(2 * peer, 2), :, columns]
            added = tn(hits[0] + hits[1], rows.reshape(2 * span, rows.shape[2]))
            if turn == 0:
                sum_ref[:, columns] = added
            else:
                sum_ref[:, columns] += added
            if half == 1:
                continue
            tag = tags_in_ref[d, pl.ds(2 * peer, 2)]
            tag = jnp.concatenate([tag[0, 0:1, 0:span], tag[1, 0:1, 0:span]], axis=1)
            pieces = three_pieces(tag)
            for k in range(2):
                marks[k] = marks[k] + sum_pieces(nn(pieces, hits[k]))
        return marks

    def load(e):
        return [
            pltpu.make_async_copy(source, target.at[e], load_sem.at[e, i])
            for i, (source, target) in enumerate((
                (hidden_in.at[e], hidden_ref), (pre_in.at[e], pre_ref), (dey_in.at[e], dey_ref),
                (sent_in.at[:, e], sent_ref),
            ))
        ]

    def stores(turn):
        e, kind, slot = turn // 2, turn % 2, turn % 2
        return [
            pltpu.make_async_copy(ref.at[slot], out[kind].at[e], store_sem.at[slot, i])
            for i, (ref, out) in enumerate(((own_ref, outs[0]), (peer_ref, outs[1])))
        ]

    size = hidden_ref.shape[2] // 2
    width = dey_ref.shape[2]

    def weight_turn(turn):
        e, kind = turn // 2, turn % 2
        if kind == 0:
            for copy in load(e):
                copy.wait()
        if turn >= 2:
            for copy in stores(turn - 2):
                copy.wait()
        total = width if kind == 0 else size
        step = 256 if total % 256 == 0 else 128
        columns = size if kind == 0 else width

        @pl.loop(0, total // step)
        def _(i):
            at = pl.ds(pl.multiple_of(i * step, step), step)
            if kind == 0:
                rows = sent_ref[e, :, :, at].reshape(-1, step)
                own_ref[turn % 2, at, 0:columns] = tn(rows, pre_ref[e, :, 0:size])
                peer_ref[turn % 2, at, 0:columns] = tn(rows, pre_ref[e, :, size:]).astype(BF)
            else:
                peer_at = pl.ds(pl.multiple_of(i * step + size, step), step)
                own_ref[turn % 2, at, :] = tn(hidden_ref[e, :, at], dey_ref[e])
                peer_ref[turn % 2, at, :] = tn(hidden_ref[e, :, peer_at], dey_ref[e]).astype(BF)

        for copy in stores(turn):
            copy.start()

    def down_load(e):
        return [
            pltpu.make_async_copy(source.at[e], down_ref.at[e, i], down_sem.at[e, i])
            for i, source in enumerate((own_down_in, peer_down_in))
        ]

    group = y_ref.shape[1]
    tiles = owners // group

    def y_store(e, i):
        return pltpu.make_async_copy(
            y_ref.at[i % 2], y_out.at[pl.ds(i * group, group), e], y_sem.at[i % 2]
        )

    def y_turn(e):
        for copy in down_load(e):
            copy.wait()
        rows = group * sent_ref.shape[2]

        @pl.loop(0, tiles)
        def _(i):
            pl.when(i >= 2)(lambda: y_store(e, i - 2).wait())
            at = pl.ds(pl.multiple_of(i * rows, 16), rows)
            y = nn(hidden_ref[e, at, 0:size], down_ref[e, 0]) + nn(hidden_ref[e, at, size:], down_ref[e, 1])
            y = gate_cols_ref[pl.ds(i * group, group), e].reshape(rows, 1) * y
            y_ref[i % 2] = y.astype(BF).reshape(group, sent_ref.shape[2], width)
            y_store(e, i).start()

        for i in range(max(0, tiles - 2), tiles):
            y_store(e, i).wait()

    turns = 2 * hidden_ref.shape[0]
    for e in range(hidden_ref.shape[0]):
        for copy in load(e) + down_load(e):
            copy.start()
    for d in range(1, groups):
        ship(d, 0)
        ship_tags(d)
    incoming = {d: [] for d in range(1, groups)}
    for half in range(2):
        for turn in ((0, 1), (2,))[half]:
            weight_turn(turn)
        if half == 1:
            y_turn(0)
        for d in range(1, groups):
            for mask in peer_order(owners):
                for copy in arrivals.get((d, half, mask), []):
                    copy.wait_send()
            if half == 0:
                ship(d, 1)
        if half == 1:
            ship(0, None)
            ship_tags(0)
        for d in range(1, groups):
            device = (owner, (zone + 2 * d) % zones)
            marks = collect_zone(d, half)
            part_ref[d - 1, :, lanes[half]] = sum_ref[:, lanes[half]].astype(BF)
            incoming[d].append(
                send(part_ref.at[d - 1, :, lanes[half]], part_in_ref.at[d - 1, :, lanes[half]], device)
            )
            if half == 0:
                mark_ref[d - 1] = jnp.concatenate(marks + [jnp.zeros((6, marks[0].shape[1]), F32)], axis=0)
                incoming[d].append(send(mark_ref.at[d - 1], mark_in_ref.at[d - 1], device))
    for turn in range(3, turns):
        weight_turn(turn)
    for e in range(1, hidden_ref.shape[0]):
        y_turn(e)
    marks = collect_zone(0, None)
    for d in range(1, groups):
        for copy in incoming[d]:
            copy.wait_recv()
            sent.append(copy)
        sum_ref[...] += part_in_ref[d - 1].astype(F32)
        marks = [marks[k] + mark_in_ref[d - 1, k:k + 1, :] for k in range(2)]
    gates = [gates_ref[k:k + 1, :] for k in range(2)]
    mean = gates[0] * marks[0] + gates[1] * marks[1]
    ids = lax.broadcasted_iota(jnp.int32, (router_ref.shape[0], mean.shape[1]), 0)
    dlogits = jnp.zeros(ids.shape, F32)
    for k in range(2):
        dlogits = dlogits + jnp.where(route_ref[k:k + 1, :] == ids, gates[k] * (marks[k] - mean), 0.0)
    dlogits = dlogits.astype(BF)
    drouter_ref[...] = nn(dlogits, normed_ref[...])
    sum_ref[...] += tn(dlogits, router_ref[...])
    field = x_ref[...]
    inverse = inverse_rms(field)
    unit = field * inverse
    upper = sum_ref[...]
    scaled = upper * gain_ref[...]
    dgain_ref[...] = jnp.sum(upper * unit, axis=0, keepdims=True)
    dx_ref[...] = top_ref[...].astype(F32) + inverse * (
        scaled - unit * jnp.mean(scaled * unit, axis=1, keepdims=True)
    )
    for (d, half, _), copies in arrivals.items():
        if d == 0 or half == "tags":
            sent.extend(copies)
    for turn in range(max(0, turns - 2), turns):
        for copy in stores(turn):
            copy.wait()
    for copy in sent:
        copy.wait_send()


def return_rows(rows, hidden, pre, dey, sent, own_down, peer_down, gate_cols, dgate, slot_rows, gates, route_rows, x, gain, router, normed, top, zones, capacity):
    length, width = x.shape
    owners, local = rows.shape[:2]
    groups = zones // 2
    size = hidden.shape[2] // 2
    span = local * capacity
    wide = -(-span // 128) * 128
    copies = 3 * (groups - 1) + (owners - 1) * (local + 1 + (groups - 1) * (2 * local + 1))
    return pl.pallas_call(
        lambda *refs: return_rows_kernel(owners, zones, capacity, *refs),
        out_shape=(
            jax.ShapeDtypeStruct((length, width), F32),
            jax.ShapeDtypeStruct((1, width), F32),
            jax.ShapeDtypeStruct(router.shape, F32),
            jax.ShapeDtypeStruct((local, width, size), F32),
            jax.ShapeDtypeStruct((local, size, width), F32),
            jax.ShapeDtypeStruct((local, width, size), BF),
            jax.ShapeDtypeStruct((local, size, width), BF),
            jax.ShapeDtypeStruct(sent.shape, BF),
        ),
        in_specs=[HBM_SPEC] * 7 + [VMEM_SPEC] * 10,
        out_specs=[VMEM_SPEC] * 3 + [HBM_SPEC] * 5,
        scratch_shapes=[
            pltpu.VMEM(hidden.shape, BF),
            pltpu.VMEM(pre.shape, BF),
            pltpu.VMEM(dey.shape, BF),
            pltpu.VMEM((local, owners) + sent.shape[2:], BF),
            pltpu.VMEM((2, max(width, size), width), F32),
            pltpu.VMEM((2, max(width, size), width), BF),
            pltpu.SemaphoreType.DMA((local, 4)),
            pltpu.SemaphoreType.DMA((2, 2)),
            pltpu.VMEM((local, 2, size, width), BF),
            pltpu.VMEM((2, max(1, 384 // sent.shape[2])) + sent.shape[2:], BF),
            pltpu.SemaphoreType.DMA((local, 2)),
            pltpu.SemaphoreType.DMA((2,)),
            pltpu.VMEM((groups, owners, span, width), BF),
            pltpu.VMEM((groups, owners, 8, wide), F32),
            pltpu.VMEM((groups, owners, 8, wide), F32),
            pltpu.VMEM((groups - 1, length, width), BF),
            pltpu.VMEM((groups - 1, length, width), BF),
            pltpu.VMEM((groups - 1, 8, length), F32),
            pltpu.VMEM((groups - 1, 8, length), F32),
            pltpu.VMEM((length, width), F32),
            pltpu.SemaphoreType.DMA((copies,)),
            pltpu.SemaphoreType.DMA((copies,)),
            pltpu.SemaphoreType.DMA((2 * groups * local,)),
        ],
        compiler_params=pltpu.CompilerParams(
            vmem_limit_bytes=61 * 1024 * 1024, collective_id=4, has_side_effects=True
        ),
        name="return_rows",
    )(rows, hidden, pre, dey, sent, own_down, peer_down, gate_cols, dgate, slot_rows, gates, route_rows, x, gain, router, normed, top)


def experts_kernel(
    x_ref, c_ref, gate_ref, own_up_in, own_down_in, peer_up_in, peer_down_in,
    y_ref, dx_ref, dgate_ref, own_up_ref, own_down_ref, peer_up_ref, peer_down_ref,
    hidden_ref, pre_ref, dey_ref,
):
    sources, _, span, width = x_ref.shape
    size = own_up_in.shape[1]
    group = max(1, 384 // span)
    rows = group * span

    @pl.loop(0, sources // group)
    def _(i):
        at = pl.ds(i * group, group)
        rows_at = pl.ds(pl.multiple_of(i * rows, 16), rows)
        x = x_ref[at, 0].reshape(rows, width)
        c = c_ref[at, 0].reshape(rows, width)
        gate = gate_ref[at, 0].reshape(rows, 1)
        dey_ref[rows_at, :] = (gate * c.astype(F32)).astype(BF)
        dgate = jnp.zeros((rows, 1), F32)
        for part, (up_ref, down_ref) in enumerate(((own_up_in, own_down_in), (peer_up_in, peer_down_in))):
            cols = slice(part * size, part * size + size)
            hidden, slope = gelu_parts(nn(x, up_ref[...]))
            hidden = hidden.astype(BF)
            hidden_ref[rows_at, cols] = hidden
            back = nt(c, down_ref[...])
            dgate = dgate + jnp.sum(hidden.astype(F32) * back, axis=1, keepdims=True)
            pre_ref[rows_at, cols] = (gate * back * slope).astype(BF)
        y = nn(hidden_ref[rows_at, 0:size], own_down_in[...]) + nn(hidden_ref[rows_at, size:], peer_down_in[...])
        y_ref[at, 0] = (gate * y).astype(BF).reshape(group, span, width)
        dx = nt(pre_ref[rows_at, 0:size], own_up_in[...]) + nt(pre_ref[rows_at, size:], peer_up_in[...])
        dx_ref[at, 0] = dx.astype(BF).reshape(group, span, width)
        dgate_ref[at, 0] = dgate.reshape(group, span, 1)

    step = 256 if width % 256 == 0 else 128

    @pl.loop(0, width // step)
    def _(i):
        at = pl.ds(pl.multiple_of(i * step, step), step)
        x = x_ref[:, 0, :, at].reshape(sources * span, step)
        own_up_ref[at, :] = tn(x, pre_ref[:, 0:size])
        peer_up_ref[at, :] = tn(x, pre_ref[:, size:]).astype(BF)

    step = 256 if size % 256 == 0 else 128

    @pl.loop(0, size // step)
    def _(i):
        at = pl.ds(pl.multiple_of(i * step, step), step)
        own_down_ref[at, :] = tn(hidden_ref[:, at], dey_ref[...])
        peer_at = pl.ds(pl.multiple_of(i * step + size, step), step)
        peer_down_ref[at, :] = tn(hidden_ref[:, peer_at], dey_ref[...]).astype(BF)


def experts_rows_kernel(
    x_ref, c_ref, gate_ref, own_up_in, own_down_in, peer_up_in, peer_down_in,
    dx_ref, dgate_ref, hidden_ref, pre_ref, dey_ref,
):
    group, _, span, width = x_ref.shape
    size = own_up_in.shape[1]
    rows = group * span
    x = x_ref[:, 0].reshape(rows, width)
    c = c_ref[:, 0].reshape(rows, width)
    gate = gate_ref[:, 0].reshape(rows, 1)
    dey_ref[...] = (gate * c.astype(F32)).astype(BF)
    dgate = jnp.zeros((rows, 1), F32)
    for part, (up_ref, down_ref) in enumerate(((own_up_in, own_down_in), (peer_up_in, peer_down_in))):
        cols = slice(part * size, part * size + size)
        hidden, slope = gelu_parts(nn(x, up_ref[...]))
        hidden = hidden.astype(BF)
        hidden_ref[:, cols] = hidden
        back = nt(c, down_ref[...])
        dgate = dgate + jnp.sum(hidden.astype(F32) * back, axis=1, keepdims=True)
        pre_ref[:, cols] = (gate * back * slope).astype(BF)
    dx = nt(pre_ref[:, 0:size], own_up_in[...]) + nt(pre_ref[:, size:], peer_up_in[...])
    dx_ref[:, 0] = dx.astype(BF).reshape(group, span, width)
    dgate_ref[:, 0] = dgate.reshape(group, span, 1)


def run_experts(x, c, gate, own_up, own_down, peer_up, peer_down):
    sources, local, span, width = x.shape
    hidden = own_up.shape[2]
    lean = sources * span > 2048
    once = dict(pipeline_mode=pl.Buffered(1)) if lean else {}
    row_spec = pl.BlockSpec((sources, 1, span, width), lambda e: (0, e, 0, 0), **once)
    gate_spec = pl.BlockSpec((sources, 1, span, 1), lambda e: (0, e, 0, 0), **once)
    late_spec = pl.BlockSpec((sources, 1, span, width), lambda e: (0, e, 0, 0), pipeline_mode=pl.Buffered(1))
    sq = pl.Squeezed()
    gup_spec = pl.BlockSpec((sq, width, hidden), lambda e: (e, 0, 0))
    gdown_spec = pl.BlockSpec((sq, hidden, width), lambda e: (e, 0, 0))
    rows = local * sources * span
    return pl.pallas_call(
        experts_kernel,
        grid=(local,),
        out_shape=(
            jax.ShapeDtypeStruct(x.shape, BF),
            jax.ShapeDtypeStruct(x.shape, BF),
            jax.ShapeDtypeStruct(gate.shape, F32),
            jax.ShapeDtypeStruct((local, width, hidden), F32),
            jax.ShapeDtypeStruct((local, hidden, width), F32),
            jax.ShapeDtypeStruct((local, width, hidden), BF),
            jax.ShapeDtypeStruct((local, hidden, width), BF),
        ),
        in_specs=[row_spec, late_spec, gate_spec, gup_spec, gdown_spec, gup_spec, gdown_spec],
        out_specs=[late_spec, row_spec, gate_spec, gup_spec, gdown_spec, gup_spec, gdown_spec],
        scratch_shapes=[
            pltpu.VMEM((sources * span, 2 * hidden), BF),
            pltpu.VMEM((sources * span, 2 * hidden), BF),
            pltpu.VMEM((sources * span, width), BF),
        ],
        compiler_params=pltpu.CompilerParams(vmem_limit_bytes=60 * 1024 * 1024),
        cost_estimate=pl.CostEstimate(
            flops=24 * rows * width * hidden, bytes_accessed=16 * rows * width, transcendentals=2 * rows * hidden,
        ),
        name="experts",
    )(x, c, gate, own_up, own_down, peer_up, peer_down)


def run_expert_rows(x, c, gate, own_up, own_down, peer_up, peer_down):
    sources, local, span, width = x.shape
    hidden = own_up.shape[2]
    group = max(1, 384 // span)
    rows = group * span
    tiles = sources // group
    row_spec = pl.BlockSpec((group, 1, span, width), lambda e, i: (i, e, 0, 0))
    gate_spec = pl.BlockSpec((group, 1, span, 1), lambda e, i: (i, e, 0, 0))
    sq = pl.Squeezed()
    up_spec = pl.BlockSpec((sq, width, hidden), lambda e, i: (e, 0, 0))
    down_spec = pl.BlockSpec((sq, hidden, width), lambda e, i: (e, 0, 0))
    wide_spec = pl.BlockSpec((sq, rows, 2 * hidden), lambda e, i: (e, i, 0))
    dey_spec = pl.BlockSpec((sq, rows, width), lambda e, i: (e, i, 0))
    everything = local * sources * span
    return pl.pallas_call(
        experts_rows_kernel,
        grid=(local, tiles),
        out_shape=(
            jax.ShapeDtypeStruct(x.shape, BF),
            jax.ShapeDtypeStruct(gate.shape, F32),
            jax.ShapeDtypeStruct((local, sources * span, 2 * hidden), BF),
            jax.ShapeDtypeStruct((local, sources * span, 2 * hidden), BF),
            jax.ShapeDtypeStruct((local, sources * span, width), BF),
        ),
        in_specs=[row_spec, row_spec, gate_spec, up_spec, down_spec, up_spec, down_spec],
        out_specs=[row_spec, gate_spec, wide_spec, wide_spec, dey_spec],
        compiler_params=pltpu.CompilerParams(vmem_limit_bytes=60 * 1024 * 1024),
        cost_estimate=pl.CostEstimate(
            flops=12 * everything * width * hidden, bytes_accessed=16 * everything * width,
            transcendentals=2 * everything * hidden,
        ),
        name="expert_rows",
    )(x, c, gate, own_up, own_down, peer_up, peer_down)


def spread_kernel(slot_ref, rows_ref, out_ref):
    experts, zones, capacity, width = out_ref.shape
    take = max(1, 384 // capacity)

    def chunk(i, _):
        for zone in range(zones):
            hits = slot_hits(slot_ref[zone], i * (take * capacity), take * capacity)
            picked = nn(hits[0] + hits[1], rows_ref[zone])
            out_ref[pl.ds(i * take, take), zone] = picked.reshape(take, capacity, width).astype(BF)
        return 0

    lax.fori_loop(0, experts // take, chunk, 0)


def spread(slot_rows, rows, experts, capacity):
    zones, length, width = rows.shape
    return pl.pallas_call(
        spread_kernel,
        out_shape=jax.ShapeDtypeStruct((experts, zones, capacity, width), BF),
        in_specs=[VMEM_SPEC] * 2,
        out_specs=VMEM_SPEC,
        compiler_params=pltpu.CompilerParams(vmem_limit_bytes=VMEM_BYTES),
        cost_estimate=pl.CostEstimate(
            flops=2 * zones * experts * capacity * length * width,
            bytes_accessed=2 * zones * (experts * capacity + length) * width, transcendentals=0,
        ),
        name="spread",
    )(slot_rows, rows)


def collect_kernel(first, slot_ref, rows_ref, out_ref):
    experts, zones, capacity, width = rows_ref.shape
    length = out_ref.shape[1]
    take = max(1, 384 // capacity)
    out_ref[...] = jnp.zeros_like(out_ref)

    def chunk(i, _):
        for zone in range(first, zones):
            hits = slot_hits(slot_ref[zone], i * (take * capacity), take * capacity)
            rows = rows_ref[pl.ds(i * take, take), zone].reshape(take * capacity, width)
            out_ref[zone - first] += tn(hits[0] + hits[1], rows)
        return 0

    lax.fori_loop(0, experts // take, chunk, 0)


def collect(slot_rows, rows, first=0):
    experts, zones, capacity, width = rows.shape
    length = slot_rows.shape[2]
    return pl.pallas_call(
        lambda *refs: collect_kernel(first, *refs),
        out_shape=jax.ShapeDtypeStruct((zones - first, length, width), F32),
        in_specs=[VMEM_SPEC] * 2,
        out_specs=VMEM_SPEC,
        compiler_params=pltpu.CompilerParams(vmem_limit_bytes=VMEM_BYTES),
        cost_estimate=pl.CostEstimate(
            flops=2 * zones * experts * capacity * length * width,
            bytes_accessed=2 * zones * (experts * capacity + 2 * length) * width, transcendentals=0,
        ),
        name="collect",
    )(slot_rows, rows)


bucket_edges = (1, 2, 3, 4, 6, 8, 12, 16, 24, 32, 48, 64, 96, 128, 192, 256, 384, 512, 768, 1024, 1536)


def bucket_onehot(length, buckets):
    distance = (length - 1) - jnp.arange(2 * length, dtype=jnp.int32)
    edge_list = jnp.array(bucket_edges, dtype=jnp.int32)
    magnitude = jnp.sum(
        (jnp.abs(distance)[:, None] >= edge_list[None, :]).astype(jnp.int32), axis=1, dtype=jnp.int32
    )
    bucket = magnitude + buckets // 2 * (distance > 0).astype(jnp.int32)
    real = jnp.arange(2 * length)[:, None] < 2 * length - 1
    hit = (bucket[:, None] == jnp.arange(buckets, dtype=jnp.int32)[None, :]) & real
    return hit.astype(F32)


def shift_from(value, distance):
    size = lax.axis_size("shard")
    return lax.ppermute(value, "shard", [((z + distance) % size, z) for z in range(size)])


def shift_to(value, distance):
    size = lax.axis_size("shard")
    return lax.ppermute(value, "shard", [(z, (z + distance) % size) for z in range(size)])


def swap_pair(value):
    return lax.ppermute(value, "shard", [(z, z ^ 1) for z in range(lax.axis_size("shard"))])


def exchange(value):
    return lax.all_to_all(value, "expert", split_axis=0, concat_axis=0, tiled=True)


def per_device(
    tokens, piece_start, routes, norm_gains, bias_tables, qkv_weight, out_weight, mlp_up, mlp_down, router,
    expert_up, expert_down, cotangent,
):
    length, width = tokens.shape
    owners = lax.axis_size("expert")
    zones = lax.axis_size("shard") // 2
    local = expert_up.shape[0]
    experts_all = local * owners
    capacity = 3 * routes.shape[1] * length // (2 * experts_all)
    qkv_cols, out_cols = qkv_weight.shape[2], out_weight.shape[2]
    zones_all = 2 * zones
    router_pad = 16
    direct = capacity % 16 == 0
    parts = mlp_down.shape[0] // qkv_weight.shape[1]
    aligned = qkv_cols % 16 == 0 and out_cols % 16 == 0 and qkv_cols % out_cols == 0

    def padded(block):
        return jnp.pad(block, ((0, 0), (0, -block.shape[1] % 128)))

    down_block = mlp_down.reshape(parts, -1, mlp_down.shape[1]).transpose(1, 0, 2).reshape(qkv_weight.shape[1], -1)
    router_block = jnp.pad(router, ((0, 0), (0, router_pad - router.shape[1])))
    route_rows = routes.T
    first, up_full, down_full, last, slot_rows, cotangent_rows = gather_weights(
        [
            padded(jnp.concatenate([qkv_weight[0], out_weight[0]], axis=1)),
            padded(mlp_up),
            padded(down_block),
            padded(jnp.concatenate([qkv_weight[1], out_weight[1], router_block], axis=1)),
        ],
        (qkv_cols + out_cols, mlp_up.shape[1], parts * mlp_down.shape[1], qkv_cols + out_cols + router_pad),
        cotangent, route_rows, owners, zones_all, experts_all, capacity,
    )

    def layer_weights(block):
        if aligned:
            return (block, qkv_cols, out_cols)
        flat = (block[:, :qkv_cols].reshape(1, -1, width), block[:, qkv_cols:qkv_cols + out_cols].reshape(1, -1, width))
        return (flat, 3 * width, width)

    up_full = up_full.reshape(-1, width)
    if mlp_down.shape[1] % 16:
        down_full = down_full.reshape(owners, parts, -1, width).transpose(1, 0, 2, 3).reshape(1, -1, width)
    router_full = last[:, qkv_cols + out_cols:qkv_cols + out_cols + router.shape[1]].reshape(experts_all, width)

    first, up_late = lax.optimization_barrier((first, expert_up))
    weights0, weights1 = layer_weights(first), layer_weights(last)
    up_other = swap_pair(up_late)

    def dispatch(rows):
        packed = spread(slot_rows, rows, experts_all, capacity)
        return exchange(packed.reshape(owners, local, zones * capacity, width))

    if direct:
        cotangent_rows = exchange(cotangent_rows.reshape(owners, local, zones * capacity, width))
    else:
        cotangent_rows = dispatch(jnp.concatenate([cotangent[None], cotangent_rows]))

    def undo(rows):
        back = exchange(rows).reshape(experts_all, zones, capacity, width)
        return collect(slot_rows, back)


    onehot = bucket_onehot(length, bias_tables.shape[2])
    vectors = lax.dot_general(
        bias_tables, onehot, (((2,), (1,)), ((), ())), precision=lax.Precision.HIGHEST
    )
    gains = [norm_gains[i:i + 1] for i in range(4)]
    x0 = tokens
    x1, ah0, qkv0, o0, lse0 = attend(piece_start, x0, gains[0], weights0, vectors[0])
    x2, mh = mlp(x1, gains[1], up_full, down_full, parts, zones_all)
    x3, ah1, qkv1, o1, lse1 = attend(piece_start, x2, gains[2], weights1, vectors[1])

    x3, up_other, cotangent_rows = lax.optimization_barrier((x3, up_other, cotangent_rows))
    if direct:
        eh, gates, eh_rows, gate_rows, down_other = send_rows(
            x3, gains[3], router_full, route_rows, slot_rows, expert_down, owners, zones_all, local, capacity
        )
    else:
        down_other = swap_pair(expert_down)
        eh = (x3 * inverse_rms(x3) * gains[3]).astype(BF)
        gates = jnp.concatenate(softmax_pair(nt(router_full, eh), route_rows))
        eh_rows = dispatch(jnp.stack([eh] + [shift_from(eh, 2 * d) for d in range(1, zones)]))
        slot_ids = jnp.arange(experts_all * capacity, dtype=jnp.int32).astype(F32)
        marks = [slot_rows[d, :2][None] == slot_ids[:, None, None] for d in range(zones)]

        def gate_slots(d):
            held = gates if d == 0 else shift_from(gates, 2 * d)
            return jnp.sum(jnp.where(marks[d], held[None], 0.0), axis=(1, 2)).reshape(experts_all, capacity)

        gate_rows = exchange(
            jnp.stack([gate_slots(d) for d in range(zones)], axis=1).reshape(owners, local, zones * capacity)
        )[..., None]
    expert_weights = (expert_up, expert_down, up_other, down_other)
    if direct:
        dx_rows, dgate_rows, hidden_rows, pre_rows, dey_rows = run_expert_rows(
            eh_rows, cotangent_rows, gate_rows, *expert_weights
        )
        dx3, dgain3, grad_router, own_up, own_down, peer_up, peer_down, y_rows = return_rows(
            dx_rows, hidden_rows, pre_rows, dey_rows, eh_rows, expert_down, down_other, gate_rows, dgate_rows,
            slot_rows, gates, route_rows, x3, gains[3], router_full, eh, cotangent, zones_all, capacity,
        )
    else:
        y_rows, dx_rows, dgate_rows, own_up, own_down, peer_up, peer_down = run_experts(
            eh_rows, cotangent_rows, gate_rows, *expert_weights
        )
        dx_back = undo(dx_rows)
        dgate_back = exchange(dgate_rows[..., 0]).reshape(experts_all, zones, capacity)
        token_grad, gate_grad = dx_back[0], 0.0
        for d in range(zones):
            part = jnp.sum(jnp.where(marks[d], dgate_back[:, d].reshape(-1)[:, None, None], 0.0), axis=0)
            gate_grad = gate_grad + (part if d == 0 else shift_to(part, 2 * d))
        for d in range(1, zones):
            token_grad = token_grad + shift_to(dx_back[d].astype(BF), 2 * d).astype(F32)
        dchoice = gates * (gate_grad - jnp.sum(gates * gate_grad, axis=0, keepdims=True))
        chosen = route_rows[:, None, :] == jnp.arange(experts_all, dtype=jnp.int32)[None, :, None]
        dlogits = jnp.sum(jnp.where(chosen, dchoice[:, None, :], 0.0), axis=0).astype(BF)
        grad_router = nn(dlogits, eh)
        deh = token_grad + tn(dlogits, router_full)
        unit3 = x3 * inverse_rms(x3)
        scaled = deh * gains[3]
        dx3 = cotangent.astype(F32) + inverse_rms(x3) * (
            scaled - unit3 * jnp.mean(scaled * unit3, axis=1, keepdims=True)
        )
        dgain3 = jnp.sum(deh * unit3, axis=0)[None]
    router_rows = jnp.pad(
        grad_router.astype(BF).reshape(owners, local, width), ((0, 0), (0, router_pad - local), (0, 0))
    )

    def layer_grads(results, tail=None):
        grads = results[1:-2]
        if not aligned:
            pieces = [g.reshape(owners, -1, width) for g in grads] + ([] if tail is None else [tail])
            grads = [jnp.concatenate(pieces, axis=1)]
        return results[0], grads[0], results[-2], results[-1]

    dx3, y_rows = lax.optimization_barrier((dx3, y_rows))
    y_back = exchange(y_rows)
    dx2, last_part, dvec1, dgain2 = layer_grads(
        attend_back(
            piece_start, x2, gains[2], weights1, vectors[1], ah1, qkv1, o1, lse1, dx3, router_rows if aligned else None,
        ),
        router_rows,
    )
    peer_up = swap_pair(peer_up)
    dx2, peer_down = lax.optimization_barrier((dx2, peer_down))
    peer_down = swap_pair(peer_down)
    dx1, up_part, down_part, dgain1 = mlp_back(
        x1, gains[1], up_full, down_full, mh, dx2, parts, zones_all
    )
    if mlp_down.shape[1] % 16:
        down_part = down_part.reshape(parts, owners, -1, width).transpose(1, 0, 2, 3)
    dx1, y_back, peer_up = lax.optimization_barrier((dx1, y_back, peer_up))
    ride = Ride(
        [last_part, up_part.reshape(owners, -1, width)], 0, [], (y_back, slot_rows) if direct else None,
        owners, zones_all, capacity, width, 6,
    )
    last_own, up_own, *results = attend_back(
        piece_start, x0, gains[0], weights0, vectors[0], ah0, qkv0, o0, lse0, dx1, None, ride
    )
    y_near = results.pop(0) if direct else None
    dx0, first_part, dvec0, dgain0 = layer_grads(results)
    dx0, peer_down = lax.optimization_barrier((dx0, peer_down))
    dtables = lax.dot_general(
        jnp.stack([dvec0, dvec1]), onehot, (((2,), (0,)), ((), ())), precision=lax.Precision.HIGHEST
    )
    dgains = jnp.concatenate([dgain0, dgain1, dgain2, dgain3])
    small = jnp.concatenate([dgains.reshape(-1), dtables.reshape(-1)])
    small = jnp.pad(small, (0, -small.size % 1024)).reshape(-1, 128)
    last_grad, up_grad, down_grad, first_grad, small, grad_up, grad_down, *finals = finish(
        (last_own, up_own), down_part.reshape(owners, -1, width), first_part, small, (own_up, own_down), (peer_up, peer_down), owners, zones_all, capacity,
        (y_back, slot_rows, x3, y_near) if direct else None,
    )
    grad_up, grad_down = grad_up.reshape(own_up.shape), grad_down.reshape(own_down.shape)
    if direct:
        output = finals[0]
    else:
        y_zones = collect(slot_rows, y_back.reshape(experts_all, zones, capacity, width))
        output = x3 + y_zones[0]
        for d in range(1, zones):
            output = output + shift_to(y_zones[d].astype(BF), 2 * d).astype(F32)
        output = output.astype(BF)
    small = small.reshape(-1)
    grad_qkv = jnp.stack([first_grad[:, :qkv_cols], last_grad[:, :qkv_cols]])
    grad_out = jnp.stack(
        [first_grad[:, qkv_cols:qkv_cols + out_cols], last_grad[:, qkv_cols:qkv_cols + out_cols]]
    )
    grad_router_out = last_grad[:, qkv_cols + out_cols:qkv_cols + out_cols + local]
    grad_mlp_up = up_grad[:, :mlp_up.shape[1]]
    down_cols = mlp_down.shape[1]
    grad_mlp_down = down_grad[:, :parts * down_cols].reshape(-1, parts, down_cols).transpose(1, 0, 2)
    grad_mlp_down = grad_mlp_down.reshape(mlp_down.shape)
    return (
        output,
        dx0,
        small[:dgains.size].reshape(dgains.shape),
        small[dgains.size:dgains.size + dtables.size].reshape(dtables.shape),
        grad_qkv,
        grad_out,
        grad_mlp_up,
        grad_mlp_down,
        grad_router_out,
        grad_up,
        grad_down,
    )


def solution(mesh):
    both = P(("expert", "shard"), None)
    split3, split2 = P(None, "shard", "expert"), P("shard", "expert")
    up_spec, down_spec = P("expert", None, "shard"), P("expert", "shard", None)
    in_specs = (
        both, P(("expert", "shard")), both, P(), P(), split3, split3, split2, split2, split2, up_spec, down_spec, both
    )
    out_specs = (both, both, P(), P(), split3, split3, split2, split2, split2, up_spec, down_spec)
    return jax.shard_map(per_device, mesh=mesh, in_specs=in_specs, out_specs=out_specs, check_vma=False)
```
